32 devices in a mesh: grp: 16 (over z, x, core), uly: 2 (over y).
Axes of the slice: x: 2, y: 2, z: 4, core: 2. Of those that a mesh axis runs over, the one named last changes fastest.
Arguments:
- queries: bfloat16 [4096, 32, 128], P(('grp', 'uly')), may hold values from -16 to 16
- keys: bfloat16 [4096, 4, 128], P(('grp', 'uly')), may hold values from -8 to 8
- values: bfloat16 [4096, 4, 128], P(('grp', 'uly')), may hold values from -6 to 6
- output_cotangent: bfloat16 [4096, 32, 128], P(('grp', 'uly')), may hold values from -6 to 6
- block_lists: int32 [128, 1], replicated, may hold values from 0 to 127, as said below
- list_counts: int32 [128], replicated, may hold values from 0 to 1, as said below
Outputs:
- attended: bfloat16 [4096, 32, 128], P(('grp', 'uly'))
- query_grad: bfloat16 [4096, 32, 128], P(('grp', 'uly'))
- key_gradient: bfloat16 [4096, 4, 128], P(('grp', 'uly'))
- value_gradient: bfloat16 [4096, 4, 128], P(('grp', 'uly'))
The draws below stay inside these ranges and needn't reach their ends.
Inputs may be any that keep to these rules, and one draw needn't show every extreme that they name: `block_lists`: calling an aligned run of 8 blocks a group: every entry of block b's list is a block of another group than b's, and the entries of all lists of one group, counted or not, lie in pairwise different groups. `list_counts`: some block counts all 1 entries in every draw.
All inputs are finite; a program needn't handle non-finite values.
Results may differ from the reference program's by a relative error of at most 0.039.
Values may be sent and summed in bfloat16 or wider, within the bound.
No kernel may reach another device: no remote copies, remote signals or barrier semaphores. Data moves between devices by JAX's collectives and lax.ppermute only.
A program may use at most 128 MiB of HBM per device.

```python
import jax
import jax.numpy as jnp
from jax import lax

QUERY_HEADS_HALF = 32
KEY_VALUE_HEADS = 4
HEAD_SIZE = 128
MASK_BLOCKS = 128
SEQUENCE_TOKENS = 4096
BLOCK_TOKENS = 32
BPG = 8
REMOTE = 1
N_GRP = 16


def draw_queries(key, part):
    unmasked_result = jnp.clip(jax.random.normal(jax.random.fold_in(key, 1), (SEQUENCE_TOKENS, QUERY_HEADS_HALF, HEAD_SIZE), jnp.float32), -6.0, 6.0)
    return unmasked_result.astype(jnp.bfloat16)


def draw_keys(key, part):
    unmasked_result = jnp.clip(jax.random.normal(jax.random.fold_in(key, 2), (SEQUENCE_TOKENS, KEY_VALUE_HEADS, HEAD_SIZE), jnp.float32), -6.0, 6.0)
    return unmasked_result.astype(jnp.bfloat16)


def one_order(order_key):
    return jax.random.permutation(order_key, N_GRP - 1)


def block_tables(key):
    random_seed_key = jax.random.fold_in(key, 5)
    group_keys = jax.random.split(jax.random.fold_in(random_seed_key, 1), N_GRP)
    offsets = jax.vmap(one_order)(group_keys) + 1
    offsets = offsets[:, :BPG * REMOTE].reshape(N_GRP, BPG, REMOTE)
    source = (jnp.arange(N_GRP)[:, None, None] + offsets) % N_GRP
    within = jax.random.randint(jax.random.fold_in(random_seed_key, 2), (N_GRP, BPG, REMOTE), 0, BPG)
    lists = (source * BPG + within).reshape(MASK_BLOCKS, REMOTE).astype(jnp.int32)
    counts = jax.random.randint(jax.random.fold_in(random_seed_key, 3), (MASK_BLOCKS,), 0, REMOTE + 1)
    fullest = jax.random.randint(jax.random.fold_in(random_seed_key, 4), (), 0, MASK_BLOCKS)
    counts = jnp.where(jnp.arange(MASK_BLOCKS) == fullest, REMOTE, counts).astype(jnp.int32)
    return (lists, counts)


def draw_block_lists(key, part):
    return block_tables(key)[0]


def draw_list_counts(key, part):
    return block_tables(key)[1]


def levels(own_key, shape, pieces, smallest, high):
    loudness, own = 1.0, jax.random.fold_in(own_key, 6)
    for dim, shards_of in pieces:
        heights = jnp.exp(jax.random.uniform(jax.random.fold_in(own, dim), (shards_of,), jnp.float32, smallest / len(pieces), high / len(pieces)))
        loudness = loudness * jnp.repeat(heights, shape[dim] // shards_of).reshape([-1 if axis == dim else 1 for axis in range(len(shape))])
    return loudness


def scatter_about(rng, shape, scale, reach, pieces=(), kind=jnp.bfloat16):
    array = scale * jax.random.normal(rng, shape, jnp.float32)
    if pieces:
        array = array * levels(rng, shape, pieces, -0.22, 0.18)
    return jnp.clip(array, -reach, reach).astype(kind)


def setup_inputs(seed: int = 0) -> dict:
    arg_keys = jax.random.split(jax.random.key(seed), 7)
    return {
        "queries": draw_queries(jax.random.fold_in(arg_keys[6], 71), 0),
        "keys": draw_keys(jax.random.fold_in(arg_keys[6], 71), 0),
        "values": scatter_about(arg_keys[2], (SEQUENCE_TOKENS, KEY_VALUE_HEADS, HEAD_SIZE), 1.0, 6.0, ((0, 32),)),
        "output_cotangent": scatter_about(arg_keys[3], (SEQUENCE_TOKENS, QUERY_HEADS_HALF, HEAD_SIZE), 1.0, 6.0, ((0, 32),)),
        "block_lists": draw_block_lists(jax.random.fold_in(arg_keys[6], 71), 0),
        "list_counts": draw_list_counts(jax.random.fold_in(arg_keys[6], 71), 0),
    }


def reference(queries, keys, values, output_cotangent, block_lists, list_counts):
    heads_per_group = QUERY_HEADS_HALF // KEY_VALUE_HEADS
    score_scale = HEAD_SIZE ** -0.5
    blocked_queries = queries.astype(jnp.float32).reshape(MASK_BLOCKS, BLOCK_TOKENS, KEY_VALUE_HEADS, heads_per_group, HEAD_SIZE)
    gradient_blocks = output_cotangent.astype(jnp.float32).reshape(MASK_BLOCKS, BLOCK_TOKENS, KEY_VALUE_HEADS, heads_per_group, HEAD_SIZE)
    blocked_keys = keys.astype(jnp.float32).reshape(MASK_BLOCKS, BLOCK_TOKENS, KEY_VALUE_HEADS, HEAD_SIZE)
    blocked_values = values.astype(jnp.float32).reshape(MASK_BLOCKS, BLOCK_TOKENS, KEY_VALUE_HEADS, HEAD_SIZE)
    causal = jnp.arange(BLOCK_TOKENS)[:, None] >= jnp.arange(BLOCK_TOKENS)[None, :]
    list_slots = jnp.arange(REMOTE)
    first_slot = (jnp.arange(REMOTE + 1) == 0)[None, :, None]

    def one_block(state_pair, block_index):
        key_running_total, value_running_total = state_pair
        chosen = jnp.concatenate([block_index[None].astype(jnp.int32), block_lists[block_index].astype(jnp.int32)])
        counted_slot = jnp.concatenate([jnp.ones((1,), bool), list_slots < list_counts[block_index]])
        query_rows = blocked_queries[block_index]
        grad_rows = gradient_blocks[block_index]
        near_keys = blocked_keys[chosen]
        near_values = blocked_values[chosen]
        scores = jnp.einsum('qkgd,rjkd->kgqrj', query_rows, near_keys) * score_scale
        visible = jnp.where(first_slot, causal[:, None, :], counted_slot[None, :, None])
        scores = jnp.where(visible, scores, -jnp.inf)
        highest = jnp.max(scores, axis=(3, 4), keepdims=True)
        log_total = highest + jnp.log(jnp.sum(jnp.exp(scores - highest), axis=(3, 4), keepdims=True))
        probs = jnp.exp(scores - log_total)
        weights = lax.optimization_barrier(probs.astype(jnp.bfloat16)).astype(jnp.float32)
        attended_rows = jnp.einsum('kgqrj,rjkd->qkgd', weights, near_values).astype(jnp.bfloat16)
        row_delta = jnp.sum(grad_rows * attended_rows.astype(jnp.float32), axis=-1)
        dprobs = jnp.einsum('qkgd,rjkd->kgqrj', grad_rows, near_values)
        dscores = probs * (dprobs - jnp.transpose(row_delta, (1, 2, 0))[..., None, None])
        dscores = lax.optimization_barrier(dscores.astype(jnp.bfloat16)).astype(jnp.float32)
        query_rows_grad = (jnp.einsum('kgqrj,rjkd->qkgd', dscores, near_keys) * score_scale).astype(jnp.bfloat16)
        key_terms = jnp.einsum('kgqrj,qkgd->rjkd', dscores, query_rows) * score_scale
        value_terms = jnp.einsum('kgqrj,qkgd->rjkd', weights, grad_rows)
        key_running_total = key_running_total.at[chosen].add(key_terms)
        value_running_total = value_running_total.at[chosen].add(value_terms)
        return (key_running_total, value_running_total), (attended_rows, query_rows_grad)

    start_offset = (jnp.zeros((MASK_BLOCKS, BLOCK_TOKENS, KEY_VALUE_HEADS, HEAD_SIZE), jnp.float32), jnp.zeros((MASK_BLOCKS, BLOCK_TOKENS, KEY_VALUE_HEADS, HEAD_SIZE), jnp.float32))
    (key_running_total, value_running_total), (attended, query_grad) = lax.scan(one_block, start_offset, jnp.arange(MASK_BLOCKS, dtype=jnp.int32))
    attended = attended.reshape(SEQUENCE_TOKENS, QUERY_HEADS_HALF, HEAD_SIZE)
    query_grad = query_grad.reshape(SEQUENCE_TOKENS, QUERY_HEADS_HALF, HEAD_SIZE)
    key_gradient = key_running_total.reshape(SEQUENCE_TOKENS, KEY_VALUE_HEADS, HEAD_SIZE).astype(jnp.bfloat16)
    value_gradient = value_running_total.reshape(SEQUENCE_TOKENS, KEY_VALUE_HEADS, HEAD_SIZE).astype(jnp.bfloat16)
    return (attended, query_grad, key_gradient, value_gradient)
```

```python
import jax
import jax.numpy as jnp
from jax import lax
from jax.experimental import pallas as pl
from jax.experimental.pallas import tpu as pltpu
from jax.sharding import PartitionSpec as P


def spread_blocks(queries, keys, values, output_cotangent, block_lists, list_counts):
    uly_count = lax.axis_size("uly")
    grp_count = lax.axis_size("grp")
    my_group = lax.axis_index("grp")
    tokens, head_count, head_width = queries.shape
    kv_heads = keys.shape[1]
    copies = max(1, uly_count // kv_heads)
    blocks_all, remote = block_lists.shape
    per_group = blocks_all // grp_count
    block_tok = tokens * uly_count // per_group
    group_tok = tokens * uly_count
    score_scale = head_width ** (-0.5)
    lists = block_lists.reshape(grp_count, per_group, remote)
    counted = (jnp.arange(remote)[None, :] < list_counts[:, None]).reshape(
        grp_count, per_group, remote
    )
    wanted = (lists // per_group == my_group) & counted
    send_place = jnp.sum(jnp.where(wanted, lists % per_group, 0), axis=(1, 2))
    sending = jnp.any(wanted, axis=(1, 2))
    mine_source = lax.dynamic_index_in_dim(lists, my_group, 0, keepdims=False) // per_group
    mine_counted = lax.dynamic_index_in_dim(counted, my_group, 0, keepdims=False)
    trip_count = jnp.max(jnp.sum(mine_counted.astype(jnp.int32), axis=1))

    def to_blocks(array_in):
        return array_in.reshape((per_group, block_tok) + array_in.shape[1:])

    keys_wide = jnp.repeat(keys, copies, axis=1)
    values_wide = jnp.repeat(values, copies, axis=1)
    query_heads, grad_heads, key_heads, value_heads = (
        lax.all_to_all(queries, "uly", split_axis=1, concat_axis=0, tiled=True),
        lax.all_to_all(output_cotangent, "uly", split_axis=1, concat_axis=0, tiled=True),
        lax.all_to_all(keys_wide, "uly", split_axis=1, concat_axis=0, tiled=True),
        lax.all_to_all(values_wide, "uly", split_axis=1, concat_axis=0, tiled=True),
    )
    stacked = jnp.stack([to_blocks(key_heads), to_blocks(value_heads)])
    outgoing = jnp.take(stacked, send_place, axis=1)
    arrived = lax.all_to_all(outgoing, "grp", split_axis=1, concat_axis=1, tiled=True)
    kv_local = key_heads.shape[1]
    heads_local = query_heads.shape[1]
    heads_per_group = heads_local // kv_local
    query_blk = query_heads.reshape(per_group, block_tok, kv_local, heads_per_group, head_width)
    grad_blk = grad_heads.reshape(per_group, block_tok, kv_local, heads_per_group, head_width)
    key_blk = to_blocks(key_heads)
    value_blk = to_blocks(value_heads)
    far_keys = arrived[0]
    far_values = arrived[1]
    causal = jnp.arange(block_tok)[:, None] >= jnp.arange(block_tok)[None, :]

    def logits(key_rows):
        return (
            jnp.einsum("pqkgd,pjkd->pkgqj", query_blk, key_rows, preferred_element_type=jnp.float32)
            * score_scale
        )

    def slot_rows(slot_index):
        source = lax.dynamic_index_in_dim(mine_source, slot_index, 1, keepdims=False)
        counted_slot = lax.dynamic_index_in_dim(mine_counted, slot_index, 1, keepdims=False)
        return (
            jnp.take(far_keys, source, axis=0),
            jnp.take(far_values, source, axis=0),
            counted_slot,
            source,
        )

    def masked(scores, counted_slot):
        return jnp.where(counted_slot[:, None, None, None, None], scores, -jnp.inf)

    near_scores = jnp.where(causal, logits(key_blk), -jnp.inf)
    highest = jnp.max(near_scores, axis=-1)
    denominator = jnp.sum(jnp.exp(near_scores - highest[..., None]), axis=-1)

    def max_sweep(slot_index, state_pair):
        highest, denominator = state_pair
        key_rows, value_rows, counted_slot, source = slot_rows(slot_index)
        scores = masked(logits(key_rows), counted_slot)
        new_highest = jnp.maximum(highest, jnp.max(scores, axis=-1))
        denominator = denominator * jnp.exp(highest - new_highest) + jnp.sum(
            jnp.exp(scores - new_highest[..., None]), axis=-1
        )
        return (new_highest, denominator)

    highest, denominator = lax.fori_loop(0, trip_count, max_sweep, (highest, denominator))
    log_total = highest + jnp.log(denominator)

    def softmax_weights(scores):
        return jnp.exp(scores - log_total[..., None])

    summed = jnp.einsum(
        "pkgqj,pjkd->pqkgd",
        softmax_weights(near_scores).astype(jnp.bfloat16),
        value_blk,
        preferred_element_type=jnp.float32,
    )

    def value_sweep(slot_index, summed):
        key_rows, value_rows, counted_slot, source = slot_rows(slot_index)
        weights = softmax_weights(masked(logits(key_rows), counted_slot)).astype(jnp.bfloat16)
        return summed + jnp.einsum(
            "pkgqj,pjkd->pqkgd", weights, value_rows, preferred_element_type=jnp.float32
        )

    summed = lax.fori_loop(0, trip_count, value_sweep, summed)
    attended_blk = summed.astype(jnp.bfloat16)
    row_delta = jnp.transpose(
        jnp.sum(grad_blk.astype(jnp.float32) * attended_blk.astype(jnp.float32), axis=-1),
        (0, 2, 3, 1),
    )

    def backward(scores, key_rows, value_rows):
        probs = softmax_weights(scores)
        weights = probs.astype(jnp.bfloat16)
        dprobs = jnp.einsum(
            "pqkgd,pjkd->pkgqj", grad_blk, value_rows, preferred_element_type=jnp.float32
        )
        dscores = (probs * (dprobs - row_delta[..., None])).astype(jnp.bfloat16)
        query_term = jnp.einsum(
            "pkgqj,pjkd->pqkgd", dscores, key_rows, preferred_element_type=jnp.float32
        )
        key_term = (
            jnp.einsum("pkgqj,pqkgd->pjkd", dscores, query_blk, preferred_element_type=jnp.float32)
            * score_scale
        )
        value_term = jnp.einsum(
            "pkgqj,pqkgd->pjkd", weights, grad_blk, preferred_element_type=jnp.float32
        )
        return (query_term, key_term, value_term)

    query_sum, key_near, value_near = backward(near_scores, key_blk, value_blk)
    far_grads = jnp.zeros((2, grp_count, block_tok, kv_local, head_width), jnp.float32)

    def grad_sweep(slot_index, state_pair):
        query_sum, far_grads = state_pair
        key_rows, value_rows, counted_slot, source = slot_rows(slot_index)
        query_term, key_term, value_term = backward(
            masked(logits(key_rows), counted_slot), key_rows, value_rows
        )
        routing = (
            (source[:, None] == jnp.arange(grp_count)[None, :]) & counted_slot[:, None]
        ).astype(jnp.float32)
        routed = jnp.einsum(
            "ps,xpjkd->xsjkd",
            routing,
            jnp.stack([key_term, value_term]),
            precision=lax.Precision.HIGHEST,
        )
        return (query_sum + query_term, far_grads + routed)

    query_sum, far_grads = lax.fori_loop(0, trip_count, grad_sweep, (query_sum, far_grads))
    owners = ((send_place[:, None] == jnp.arange(per_group)[None, :]) & sending[:, None]).astype(
        jnp.float32
    )
    returned = lax.all_to_all(far_grads, "grp", split_axis=1, concat_axis=1, tiled=True)
    landed = jnp.einsum("sp,xsjkd->xpjkd", owners, returned, precision=lax.Precision.HIGHEST)
    key_local = (key_near + landed[0]).reshape(group_tok, kv_local, head_width)
    value_local = (value_near + landed[1]).reshape(group_tok, kv_local, head_width)
    attended_rows = attended_blk.reshape(group_tok, heads_local, head_width)
    query_rows = (
        (query_sum * score_scale).astype(jnp.bfloat16).reshape(group_tok, heads_local, head_width)
    )
    attended, query_grad = (
        lax.all_to_all(attended_rows, "uly", split_axis=0, concat_axis=1, tiled=True),
        lax.all_to_all(query_rows, "uly", split_axis=0, concat_axis=1, tiled=True),
    )
    key_parts, value_parts = (
        lax.all_to_all(key_local, "uly", split_axis=0, concat_axis=1, tiled=True),
        lax.all_to_all(value_local, "uly", split_axis=0, concat_axis=1, tiled=True),
    )
    key_gradient = jnp.sum(key_parts.reshape(tokens, kv_heads, copies, head_width), axis=2).astype(
        jnp.bfloat16
    )
    value_gradient = jnp.sum(
        value_parts.reshape(tokens, kv_heads, copies, head_width), axis=2
    ).astype(jnp.bfloat16)
    return (attended, query_grad, key_gradient, value_gradient)


HIDDEN = -1e30


def attention_kernel(
    source_ref, seen_ref, q_ref, g_ref, k_ref, v_ref, mine_ref, other_ref,
    att_ref, dq_ref, dk_ref, dv_ref, far_mine_ref, far_other_ref, bias_ref,
    *, heads, kv_heads, score_scale
):
    step = pl.program_id(0)
    rows = q_ref.shape[0]
    cols = k_ref.shape[0]
    half = mine_ref.shape[2]

    @pl.when(step == 0)
    def _():
        row = lax.broadcasted_iota(jnp.int32, (rows, cols), 0)
        col = lax.broadcasted_iota(jnp.int32, (rows, cols), 1)
        same = (row % heads) // (heads // kv_heads) == col % kv_heads
        causal = col // kv_heads <= row // heads
        bias_ref[:, :cols] = jnp.where(same & causal, 0.0, HIDDEN)
        bias_ref[:, cols:] = jnp.where(same, 0.0, HIDDEN)

    far_bias = jnp.where(seen_ref[step] > 0, 0.0, HIDDEN)
    k_all = jnp.concatenate([k_ref[...], mine_ref[0, 0], other_ref[0, 0]], axis=0)
    v_all = jnp.concatenate([v_ref[...], mine_ref[0, 1], other_ref[0, 1]], axis=0)
    q = q_ref[...]
    g = g_ref[...]
    last = (((1,), (1,)), ((), ()))
    first = (((0,), (0,)), ((), ()))
    scores = lax.dot_general(q, k_all, last, preferred_element_type=jnp.float32) * score_scale
    scores = scores + bias_ref[...]
    scores = jnp.concatenate([scores[:, :cols], scores[:, cols:] + far_bias], axis=1)
    highest = jnp.max(scores, axis=1, keepdims=True)
    raised = jnp.exp(scores - highest)
    total = jnp.sum(raised, axis=1, keepdims=True)
    probs = raised * (1.0 / total)
    weights = probs.astype(jnp.bfloat16)
    attended = jnp.dot(weights, v_all, preferred_element_type=jnp.float32).astype(jnp.bfloat16)
    att_ref[...] = attended
    delta = jnp.sum(g.astype(jnp.float32) * attended.astype(jnp.float32), axis=1, keepdims=True)
    dprobs = lax.dot_general(g, v_all, last, preferred_element_type=jnp.float32)
    dscores = (probs * (dprobs - delta)).astype(jnp.bfloat16)
    dq = jnp.dot(dscores, k_all, preferred_element_type=jnp.float32) * score_scale
    dq_ref[...] = dq.astype(jnp.bfloat16)
    dk = lax.dot_general(dscores, q, first, preferred_element_type=jnp.float32) * score_scale
    dv = lax.dot_general(weights, g, first, preferred_element_type=jnp.float32)
    dk_ref[...] = dk[:cols]
    dv_ref[...] = dv[:cols]
    far_mine_ref[0, 0] = dk[cols:cols + half].astype(jnp.bfloat16)
    far_mine_ref[0, 1] = dv[cols:cols + half].astype(jnp.bfloat16)
    far_other_ref[0, 0] = dk[cols + half:].astype(jnp.bfloat16)
    far_other_ref[0, 1] = dv[cols + half:].astype(jnp.bfloat16)


def whole_blocks(queries, keys, values, output_cotangent, block_lists, list_counts):
    grp_count = lax.axis_size("grp")
    uly_count = lax.axis_size("uly")
    my_group = lax.axis_index("grp")
    my_half = lax.axis_index("uly")
    tokens, heads, width = queries.shape
    kv_heads = keys.shape[1]
    per_group = block_lists.shape[0] // grp_count
    block_tok = tokens * uly_count // per_group
    mine_blocks = tokens // block_tok
    rows = block_tok * heads
    cols = block_tok * kv_heads
    half = cols // 2
    score_scale = width ** (-0.5)
    swap = [(0, 1), (1, 0)]

    lists = block_lists.reshape(grp_count, per_group)
    counted = (list_counts > 0).reshape(grp_count, per_group)
    wanted = (lists // per_group == my_group) & counted
    send_place = jnp.sum(jnp.where(wanted, lists % per_group, 0), axis=1)
    sending = jnp.any(wanted, axis=1)
    my_lists = lax.dynamic_index_in_dim(lists, my_group, 0, keepdims=False)
    my_seen = lax.dynamic_index_in_dim(counted, my_group, 0, keepdims=False).astype(jnp.int32)
    source = my_lists // per_group

    def by_owner(vector):
        both = vector.reshape(2, mine_blocks)
        return (
            lax.dynamic_index_in_dim(both, my_half, 0, keepdims=False),
            lax.dynamic_index_in_dim(both, 1 - my_half, 0, keepdims=False),
        )

    source_own, source_sib = by_owner(source)
    seen_own, seen_sib = by_owner(my_seen)
    owner_first = jnp.where(
        send_place // mine_blocks == my_half,
        send_place % mine_blocks,
        send_place % mine_blocks + mine_blocks,
    )

    parts = jnp.stack(
        [keys.reshape(mine_blocks, 2, half, width), values.reshape(mine_blocks, 2, half, width)],
        axis=2,
    )
    kept = lax.dynamic_index_in_dim(parts, my_half, 1, keepdims=False)
    given = lax.dynamic_index_in_dim(parts, 1 - my_half, 1, keepdims=False)
    gotten = lax.ppermute(given, "uly", swap)
    outgoing = jnp.take(jnp.concatenate([kept, gotten]), owner_first, axis=0)
    arrived = lax.all_to_all(outgoing, "grp", split_axis=0, concat_axis=0, tiled=True)
    other = lax.ppermute(jnp.take(arrived, source_sib, axis=0), "uly", swap)

    q2 = queries.reshape(tokens * heads, width)
    g2 = output_cotangent.reshape(tokens * heads, width)
    k2 = keys.reshape(tokens * kv_heads, width)
    v2 = values.reshape(tokens * kv_heads, width)

    def step_rows(i, *_):
        return (i, 0)

    def step_part(i, *_):
        return (i, 0, 0, 0)

    def from_source(i, source_ref, seen_ref):
        return (source_ref[i], 0, 0, 0)

    def far_spec(index_map):
        return pl.BlockSpec((1, 2, half, width), index_map)

    row_spec = pl.BlockSpec((rows, width), step_rows)
    col_spec = pl.BlockSpec((cols, width), step_rows)
    f32 = jnp.float32
    bf16 = jnp.bfloat16
    attended, dq, dk_near, dv_near, far_mine, far_other = pl.pallas_call(
        lambda *refs: attention_kernel(
            *refs, heads=heads, kv_heads=kv_heads, score_scale=score_scale
        ),
        grid_spec=pltpu.PrefetchScalarGridSpec(
            num_scalar_prefetch=2,
            grid=(mine_blocks,),
            in_specs=[
                row_spec, row_spec, col_spec, col_spec, far_spec(from_source), far_spec(step_part)
            ],
            out_specs=[
                row_spec, row_spec, col_spec, col_spec, far_spec(step_part), far_spec(step_part)
            ],
            scratch_shapes=[pltpu.VMEM((rows, 2 * cols), f32)],
        ),
        out_shape=[
            jax.ShapeDtypeStruct(q2.shape, bf16),
            jax.ShapeDtypeStruct(q2.shape, bf16),
            jax.ShapeDtypeStruct(k2.shape, f32),
            jax.ShapeDtypeStruct(k2.shape, f32),
            jax.ShapeDtypeStruct((mine_blocks, 2, half, width), bf16),
            jax.ShapeDtypeStruct((mine_blocks, 2, half, width), bf16),
        ],
        compiler_params=pltpu.CompilerParams(vmem_limit_bytes=48 * 1024 * 1024),
        name="attention",
    )(source_own, seen_own, q2, g2, k2, v2, arrived, other)

    from_sib = lax.ppermute(far_other, "uly", swap)
    groups = jnp.arange(grp_count)
    source_both = jnp.concatenate([source_own, source_sib])
    asked = jnp.argmax(source_both[None, :] == groups[:, None], axis=1)
    returning = jnp.take(jnp.concatenate([far_mine, from_sib]), asked, axis=0)
    landed = lax.all_to_all(returning, "grp", split_axis=0, concat_axis=0, tiled=True)
    routing = ((owner_first[:, None] == jnp.arange(per_group)[None, :]) & sending[:, None]).astype(
        bf16
    )
    summed = jnp.einsum("sp,sxrd->pxrd", routing, landed, preferred_element_type=f32)
    summed_own = summed[:mine_blocks]
    back = lax.ppermute(summed[mine_blocks:].astype(bf16), "uly", swap)
    first_half = jnp.where(my_half == 0, summed_own, back.astype(f32))
    second_half = jnp.where(my_half == 0, back.astype(f32), summed_own)
    far_sum = jnp.stack([first_half, second_half], axis=1)
    near_shape = (mine_blocks, 2, half, width)
    dk = (dk_near.reshape(near_shape) + far_sum[:, :, 0]).astype(bf16).reshape(keys.shape)
    dv = (dv_near.reshape(near_shape) + far_sum[:, :, 1]).astype(bf16).reshape(keys.shape)
    return (attended.reshape(queries.shape), dq.reshape(queries.shape), dk, dv)


def on_device(queries, keys, values, output_cotangent, block_lists, list_counts):
    uly_count = lax.axis_size("uly")
    grp_count = lax.axis_size("grp")
    blocks_all, remote = block_lists.shape
    block_tok = queries.shape[0] * uly_count * grp_count // blocks_all
    held_whole = queries.shape[0] % block_tok == 0
    run = whole_blocks if held_whole and remote == 1 and uly_count == 2 else spread_blocks
    return run(queries, keys, values, output_cotangent, block_lists, list_counts)


def solution(mesh):
    placed = (
        P(("grp", "uly"), None, None),
        P(("grp", "uly"), None, None),
        P(("grp", "uly"), None, None),
        P(("grp", "uly"), None, None),
        P(),
        P(),
    )
    return jax.shard_map(
        on_device,
        mesh=mesh,
        in_specs=placed,
        out_specs=(
            P(("grp", "uly"), None, None),
            P(("grp", "uly"), None, None),
            P(("grp", "uly"), None, None),
            P(("grp", "uly"), None, None),
        ),
        check_vma=False,
    )
```

```python
import jax
import jax.numpy as jnp
from jax import lax
from jax.experimental import pallas as pl
from jax.experimental.pallas import tpu as pltpu
from jax.sharding import PartitionSpec as P


def spread_blocks(queries, keys, values, output_cotangent, block_lists, list_counts):
    uly_count = lax.axis_size("uly")
    grp_count = lax.axis_size("grp")
    my_group = lax.axis_index("grp")
    tokens, head_count, head_width = queries.shape
    kv_heads = keys.shape[1]
    copies = max(1, uly_count // kv_heads)
    blocks_all, remote = block_lists.shape
    per_group = blocks_all // grp_count
    block_tok = tokens * uly_count // per_group
    group_tok = tokens * uly_count
    score_scale = head_width ** (-0.5)
    lists = block_lists.reshape(grp_count, per_group, remote)
    counted = (jnp.arange(remote)[None, :] < list_counts[:, None]).reshape(
        grp_count, per_group, remote
    )
    wanted = (lists // per_group == my_group) & counted
    send_place = jnp.sum(jnp.where(wanted, lists % per_group, 0), axis=(1, 2))
    sending = jnp.any(wanted, axis=(1, 2))
    mine_source = lax.dynamic_index_in_dim(lists, my_group, 0, keepdims=False) // per_group
    mine_counted = lax.dynamic_index_in_dim(counted, my_group, 0, keepdims=False)
    trip_count = jnp.max(jnp.sum(mine_counted.astype(jnp.int32), axis=1))

    def to_blocks(array_in):
        return array_in.reshape((per_group, block_tok) + array_in.shape[1:])

    keys_wide = jnp.repeat(keys, copies, axis=1)
    values_wide = jnp.repeat(values, copies, axis=1)
    query_heads, grad_heads, key_heads, value_heads = (
        lax.all_to_all(queries, "uly", split_axis=1, concat_axis=0, tiled=True),
        lax.all_to_all(output_cotangent, "uly", split_axis=1, concat_axis=0, tiled=True),
        lax.all_to_all(keys_wide, "uly", split_axis=1, concat_axis=0, tiled=True),
        lax.all_to_all(values_wide, "uly", split_axis=1, concat_axis=0, tiled=True),
    )
    stacked = jnp.stack([to_blocks(key_heads), to_blocks(value_heads)])
    outgoing = jnp.take(stacked, send_place, axis=1)
    arrived = lax.all_to_all(outgoing, "grp", split_axis=1, concat_axis=1, tiled=True)
    kv_local = key_heads.shape[1]
    heads_local = query_heads.shape[1]
    heads_per_group = heads_local // kv_local
    query_blk = query_heads.reshape(per_group, block_tok, kv_local, heads_per_group, head_width)
    grad_blk = grad_heads.reshape(per_group, block_tok, kv_local, heads_per_group, head_width)
    key_blk = to_blocks(key_heads)
    value_blk = to_blocks(value_heads)
    far_keys = arrived[0]
    far_values = arrived[1]
    causal = jnp.arange(block_tok)[:, None] >= jnp.arange(block_tok)[None, :]

    def logits(key_rows):
        return (
            jnp.einsum("pqkgd,pjkd->pkgqj", query_blk, key_rows, preferred_element_type=jnp.float32)
            * score_scale
        )

    def slot_rows(slot_index):
        source = lax.dynamic_index_in_dim(mine_source, slot_index, 1, keepdims=False)
        counted_slot = lax.dynamic_index_in_dim(mine_counted, slot_index, 1, keepdims=False)
        return (
            jnp.take(far_keys, source, axis=0),
            jnp.take(far_values, source, axis=0),
            counted_slot,
            source,
        )

    def masked(scores, counted_slot):
        return jnp.where(counted_slot[:, None, None, None, None], scores, -jnp.inf)

    near_scores = jnp.where(causal, logits(key_blk), -jnp.inf)
    highest = jnp.max(near_scores, axis=-1)
    denominator = jnp.sum(jnp.exp(near_scores - highest[..., None]), axis=-1)

    def max_sweep(slot_index, state_pair):
        highest, denominator = state_pair
        key_rows, value_rows, counted_slot, source = slot_rows(slot_index)
        scores = masked(logits(key_rows), counted_slot)
        new_highest = jnp.maximum(highest, jnp.max(scores, axis=-1))
        denominator = denominator * jnp.exp(highest - new_highest) + jnp.sum(
            jnp.exp(scores - new_highest[..., None]), axis=-1
        )
        return (new_highest, denominator)

    highest, denominator = lax.fori_loop(0, trip_count, max_sweep, (highest, denominator))
    log_total = highest + jnp.log(denominator)

    def softmax_weights(scores):
        return jnp.exp(scores - log_total[..., None])

    summed = jnp.einsum(
        "pkgqj,pjkd->pqkgd",
        softmax_weights(near_scores).astype(jnp.bfloat16),
        value_blk,
        preferred_element_type=jnp.float32,
    )

    def value_sweep(slot_index, summed):
        key_rows, value_rows, counted_slot, source = slot_rows(slot_index)
        weights = softmax_weights(masked(logits(key_rows), counted_slot)).astype(jnp.bfloat16)
        return summed + jnp.einsum(
            "pkgqj,pjkd->pqkgd", weights, value_rows, preferred_element_type=jnp.float32
        )

    summed = lax.fori_loop(0, trip_count, value_sweep, summed)
    attended_blk = summed.astype(jnp.bfloat16)
    row_delta = jnp.transpose(
        jnp.sum(grad_blk.astype(jnp.float32) * attended_blk.astype(jnp.float32), axis=-1),
        (0, 2, 3, 1),
    )

    def backward(scores, key_rows, value_rows):
        probs = softmax_weights(scores)
        weights = probs.astype(jnp.bfloat16)
        dprobs = jnp.einsum(
            "pqkgd,pjkd->pkgqj", grad_blk, value_rows, preferred_element_type=jnp.float32
        )
        dscores = (probs * (dprobs - row_delta[..., None])).astype(jnp.bfloat16)
        query_term = jnp.einsum(
            "pkgqj,pjkd->pqkgd", dscores, key_rows, preferred_element_type=jnp.float32
        )
        key_term = (
            jnp.einsum("pkgqj,pqkgd->pjkd", dscores, query_blk, preferred_element_type=jnp.float32)
            * score_scale
        )
        value_term = jnp.einsum(
            "pkgqj,pqkgd->pjkd", weights, grad_blk, preferred_element_type=jnp.float32
        )
        return (query_term, key_term, value_term)

    query_sum, key_near, value_near = backward(near_scores, key_blk, value_blk)
    far_grads = jnp.zeros((2, grp_count, block_tok, kv_local, head_width), jnp.float32)

    def grad_sweep(slot_index, state_pair):
        query_sum, far_grads = state_pair
        key_rows, value_rows, counted_slot, source = slot_rows(slot_index)
        query_term, key_term, value_term = backward(
            masked(logits(key_rows), counted_slot), key_rows, value_rows
        )
        routing = (
            (source[:, None] == jnp.arange(grp_count)[None, :]) & counted_slot[:, None]
        ).astype(jnp.float32)
        routed = jnp.einsum(
            "ps,xpjkd->xsjkd",
            routing,
            jnp.stack([key_term, value_term]),
            precision=lax.Precision.HIGHEST,
        )
        return (query_sum + query_term, far_grads + routed)

    query_sum, far_grads = lax.fori_loop(0, trip_count, grad_sweep, (query_sum, far_grads))
    owners = ((send_place[:, None] == jnp.arange(per_group)[None, :]) & sending[:, None]).astype(
        jnp.float32
    )
    returned = lax.all_to_all(far_grads, "grp", split_axis=1, concat_axis=1, tiled=True)
    landed = jnp.einsum("sp,xsjkd->xpjkd", owners, returned, precision=lax.Precision.HIGHEST)
    key_local = (key_near + landed[0]).reshape(group_tok, kv_local, head_width)
    value_local = (value_near + landed[1]).reshape(group_tok, kv_local, head_width)
    attended_rows = attended_blk.reshape(group_tok, heads_local, head_width)
    query_rows = (
        (query_sum * score_scale).astype(jnp.bfloat16).reshape(group_tok, heads_local, head_width)
    )
    attended, query_grad = (
        lax.all_to_all(attended_rows, "uly", split_axis=0, concat_axis=1, tiled=True),
        lax.all_to_all(query_rows, "uly", split_axis=0, concat_axis=1, tiled=True),
    )
    key_parts, value_parts = (
        lax.all_to_all(key_local, "uly", split_axis=0, concat_axis=1, tiled=True),
        lax.all_to_all(value_local, "uly", split_axis=0, concat_axis=1, tiled=True),
    )
    key_gradient = jnp.sum(key_parts.reshape(tokens, kv_heads, copies, head_width), axis=2).astype(
        jnp.bfloat16
    )
    value_gradient = jnp.sum(
        value_parts.reshape(tokens, kv_heads, copies, head_width), axis=2
    ).astype(jnp.bfloat16)
    return (attended, query_grad, key_gradient, value_gradient)


HIDDEN = -1e30
LAST = (((1,), (1,)), ((), ()))
FIRST = (((0,), (0,)), ((), ()))
F32 = jnp.float32
BF16 = jnp.bfloat16


def dot_last(left, right):
    return lax.dot_general(left, right, LAST, preferred_element_type=F32)


def dot_first(left, right):
    return lax.dot_general(left, right, FIRST, preferred_element_type=F32)


def same_head(rows, cols, heads, kv_heads):
    row = lax.broadcasted_iota(jnp.int32, (rows, cols), 0)
    col = lax.broadcasted_iota(jnp.int32, (rows, cols), 1)
    same = (row % heads) // (heads // kv_heads) == col % kv_heads
    causal = col // kv_heads <= row // heads
    return same, causal


def near_kernel(q_ref, g_ref, k_ref, v_ref, stat_ref, bias_ref, *, heads, kv_heads, score_scale):
    rows = q_ref.shape[0]
    cols = k_ref.shape[0]

    @pl.when(pl.program_id(0) == 0)
    def _():
        same, causal = same_head(rows, cols, heads, kv_heads)
        bias_ref[...] = jnp.where(same & causal, 0.0, HIDDEN)

    scores = dot_last(q_ref[...], k_ref[...]) * score_scale + bias_ref[...]
    highest = jnp.max(scores, axis=1, keepdims=True)
    raised = jnp.exp(scores - highest)
    total = jnp.sum(raised, axis=1, keepdims=True)
    delta = jnp.sum(raised * dot_last(g_ref[...], v_ref[...]), axis=1, keepdims=True)
    lane = lax.broadcasted_iota(jnp.int32, stat_ref.shape, 1)
    stat_ref[...] = jnp.where(lane == 0, highest, jnp.where(lane == 1, total, delta))


def far_kernel(
    source_ref, seen_ref, q_ref, g_ref, stat_ref, mine_ref, other_ref,
    far_mine_ref, far_other_ref, bias_ref, *, heads, kv_heads, score_scale
):
    step = pl.program_id(0)
    rows = q_ref.shape[0]
    half = mine_ref.shape[2]

    @pl.when(step == 0)
    def _():
        same, _ = same_head(rows, 2 * half, heads, kv_heads)
        bias_ref[...] = jnp.where(same, 0.0, HIDDEN)

    seen_bias = jnp.where(seen_ref[step] > 0, 0.0, HIDDEN)
    q = q_ref[...]
    g = g_ref[...]
    k_far = jnp.concatenate([mine_ref[0, 0], other_ref[0, 0]], axis=0)
    v_far = jnp.concatenate([mine_ref[0, 1], other_ref[0, 1]], axis=0)
    stat = stat_ref[...]
    scores = dot_last(q, k_far) * score_scale + (bias_ref[...] + seen_bias)
    near_highest = stat[:, 0:1]
    highest = jnp.maximum(near_highest, jnp.max(scores, axis=1, keepdims=True))
    raised = jnp.exp(scores - highest)
    shrink = jnp.exp(near_highest - highest)
    dprobs = dot_last(g, v_far)
    total = shrink * stat[:, 1:2] + jnp.sum(raised, axis=1, keepdims=True)
    inverse = 1.0 / total
    delta = (shrink * stat[:, 2:3] + jnp.sum(raised * dprobs, axis=1, keepdims=True)) * inverse
    probs = raised * inverse
    dscores = (probs * (dprobs - delta)).astype(BF16)
    dk = (dot_first(dscores, q) * score_scale).astype(BF16)
    dv = dot_first(probs.astype(BF16), g).astype(BF16)
    far_mine_ref[0, 0] = dk[:half]
    far_mine_ref[0, 1] = dv[:half]
    far_other_ref[0, 0] = dk[half:]
    far_other_ref[0, 1] = dv[half:]


def local_kernel(
    source_ref, seen_ref, q_ref, g_ref, k_ref, v_ref, mine_ref, other_ref,
    att_ref, dq_ref, dk_ref, dv_ref, bias_ref, *, heads, kv_heads, score_scale
):
    step = pl.program_id(0)
    rows = q_ref.shape[0]
    cols = k_ref.shape[0]

    @pl.when(step == 0)
    def _():
        same, causal = same_head(rows, cols, heads, kv_heads)
        bias_ref[:, :cols] = jnp.where(same & causal, 0.0, HIDDEN)
        bias_ref[:, cols:] = jnp.where(same, 0.0, HIDDEN)

    far_bias = jnp.where(seen_ref[step] > 0, 0.0, HIDDEN)
    k_all = jnp.concatenate([k_ref[...], mine_ref[0, 0], other_ref[0, 0]], axis=0)
    v_all = jnp.concatenate([v_ref[...], mine_ref[0, 1], other_ref[0, 1]], axis=0)
    q = q_ref[...]
    g = g_ref[...]
    scores = dot_last(q, k_all) * score_scale + bias_ref[...]
    scores = jnp.concatenate([scores[:, :cols], scores[:, cols:] + far_bias], axis=1)
    highest = jnp.max(scores, axis=1, keepdims=True)
    raised = jnp.exp(scores - highest)
    total = jnp.sum(raised, axis=1, keepdims=True)
    probs = raised * (1.0 / total)
    weights = probs.astype(BF16)
    attended = jnp.dot(weights, v_all, preferred_element_type=F32).astype(BF16)
    att_ref[...] = attended
    delta = jnp.sum(g.astype(F32) * attended.astype(F32), axis=1, keepdims=True)
    dscores = (probs * (dot_last(g, v_all) - delta)).astype(BF16)
    dq = jnp.dot(dscores, k_all, preferred_element_type=F32) * score_scale
    dq_ref[...] = dq.astype(BF16)
    dk_ref[...] = dot_first(dscores[:, :cols], q) * score_scale
    dv_ref[...] = dot_first(weights[:, :cols], g)


def take_rows(array, index):
    return array.at[index].get(mode="promise_in_bounds")


def whole_blocks(queries, keys, values, output_cotangent, block_lists, list_counts):
    grp_count = lax.axis_size("grp")
    uly_count = lax.axis_size("uly")
    my_group = lax.axis_index("grp")
    my_half = lax.axis_index("uly")
    tokens, heads, width = queries.shape
    kv_heads = keys.shape[1]
    per_group = block_lists.shape[0] // grp_count
    block_tok = tokens * uly_count // per_group
    mine_blocks = tokens // block_tok
    rows = block_tok * heads
    cols = block_tok * kv_heads
    half = cols // 2
    sizes = dict(heads=heads, kv_heads=kv_heads, score_scale=width ** (-0.5))
    swap = [(0, 1), (1, 0)]

    lists = block_lists.reshape(grp_count, per_group)
    counted = (list_counts > 0).reshape(grp_count, per_group)
    wanted = (lists // per_group == my_group) & counted
    send_place = jnp.sum(jnp.where(wanted, lists % per_group, 0), axis=1)
    sending = jnp.any(wanted, axis=1)
    my_lists = lax.dynamic_index_in_dim(lists, my_group, 0, keepdims=False)
    my_seen = lax.dynamic_index_in_dim(counted, my_group, 0, keepdims=False).astype(jnp.int32)
    source = my_lists // per_group

    def by_owner(vector):
        both = vector.reshape(2, mine_blocks)
        return (
            lax.dynamic_index_in_dim(both, my_half, 0, keepdims=False),
            lax.dynamic_index_in_dim(both, 1 - my_half, 0, keepdims=False),
        )

    source_own, source_sib = by_owner(source)
    seen_own, seen_sib = by_owner(my_seen)
    owner_first = jnp.where(
        send_place // mine_blocks == my_half,
        send_place % mine_blocks,
        send_place % mine_blocks + mine_blocks,
    )

    q2 = queries.reshape(tokens * heads, width)
    g2 = output_cotangent.reshape(tokens * heads, width)
    k2 = keys.reshape(tokens * kv_heads, width)
    v2 = values.reshape(tokens * kv_heads, width)

    def step_rows(i, *_):
        return (i, 0)

    def step_part(i, *_):
        return (i, 0, 0, 0)

    def from_source(i, source_ref, seen_ref):
        return (source_ref[i], 0, 0, 0)

    def far_spec(index_map):
        return pl.BlockSpec((1, 2, half, width), index_map)

    row_spec = pl.BlockSpec((rows, width), step_rows)
    col_spec = pl.BlockSpec((cols, width), step_rows)
    far_shape = jax.ShapeDtypeStruct((mine_blocks, 2, half, width), BF16)

    def call(kernel, scalars, in_specs, out_specs, out_shape, bias_cols, name, operands):
        return pl.pallas_call(
            lambda *refs: kernel(*refs, **sizes),
            grid_spec=pltpu.PrefetchScalarGridSpec(
                num_scalar_prefetch=len(scalars),
                grid=(mine_blocks,),
                in_specs=in_specs,
                out_specs=out_specs,
                scratch_shapes=[pltpu.VMEM((rows, bias_cols), F32)],
            ),
            out_shape=out_shape,
            compiler_params=pltpu.CompilerParams(vmem_limit_bytes=48 * 1024 * 1024),
            name=name,
        )(*scalars, *operands)

    parts = jnp.stack(
        [keys.reshape(mine_blocks, 2, half, width), values.reshape(mine_blocks, 2, half, width)],
        axis=2,
    )
    kept = lax.dynamic_index_in_dim(parts, my_half, 1, keepdims=False)
    given = lax.dynamic_index_in_dim(parts, 1 - my_half, 1, keepdims=False)
    gotten = lax.ppermute(given, "uly", swap)
    outgoing = take_rows(jnp.concatenate([kept, gotten]), owner_first)
    outgoing, k2n = lax.optimization_barrier((outgoing, k2))
    arrived = lax.all_to_all(outgoing, "grp", split_axis=0, concat_axis=0, tiled=True)
    stats = call(
        near_kernel, (), [row_spec, row_spec, col_spec, col_spec], row_spec,
        jax.ShapeDtypeStruct((tokens * heads, width), F32), cols, "near", (q2, g2, k2n, v2),
    )
    arrived, stats = lax.optimization_barrier((arrived, stats))
    other = lax.ppermute(take_rows(arrived, source_sib), "uly", swap)

    far_mine, far_other = call(
        far_kernel, (source_own, seen_own),
        [row_spec, row_spec, row_spec, far_spec(from_source), far_spec(step_part)],
        [far_spec(step_part), far_spec(step_part)], [far_shape, far_shape], cols, "far",
        (q2, g2, stats, arrived, other),
    )

    from_sib = lax.ppermute(far_other, "uly", swap)
    groups = jnp.arange(grp_count)
    source_both = jnp.concatenate([source_own, source_sib])
    asked = jnp.argmax(source_both[None, :] == groups[:, None], axis=1)
    returning = take_rows(jnp.concatenate([far_mine, from_sib]), asked)
    returning, k2l = lax.optimization_barrier((returning, k2))
    landed = lax.all_to_all(returning, "grp", split_axis=0, concat_axis=0, tiled=True)
    row_shape = jax.ShapeDtypeStruct(q2.shape, BF16)
    near_shape = jax.ShapeDtypeStruct(k2.shape, F32)
    attended, dq, dk_near, dv_near = call(
        local_kernel, (source_own, seen_own),
        [row_spec, row_spec, col_spec, col_spec, far_spec(from_source), far_spec(step_part)],
        [row_spec, row_spec, col_spec, col_spec],
        [row_shape, row_shape, near_shape, near_shape], 2 * cols, "local",
        (q2, g2, k2l, v2, arrived, other),
    )
    landed, dk_near = lax.optimization_barrier((landed, dk_near))
    routing = ((owner_first[:, None] == jnp.arange(per_group)[None, :]) & sending[:, None]).astype(
        BF16
    )
    summed = jnp.einsum("sp,sxrd->pxrd", routing, landed, preferred_element_type=F32)
    summed_own = summed[:mine_blocks]
    back = lax.ppermute(summed[mine_blocks:].astype(BF16), "uly", swap)
    first_half = jnp.where(my_half == 0, summed_own, back.astype(F32))
    second_half = jnp.where(my_half == 0, back.astype(F32), summed_own)
    far_sum = jnp.stack([first_half, second_half], axis=1)
    split = (mine_blocks, 2, half, width)
    dk = (dk_near.reshape(split) + far_sum[:, :, 0]).astype(BF16).reshape(keys.shape)
    dv = (dv_near.reshape(split) + far_sum[:, :, 1]).astype(BF16).reshape(keys.shape)
    return (attended.reshape(queries.shape), dq.reshape(queries.shape), dk, dv)


def on_device(queries, keys, values, output_cotangent, block_lists, list_counts):
    uly_count = lax.axis_size("uly")
    grp_count = lax.axis_size("grp")
    blocks_all, remote = block_lists.shape
    block_tok = queries.shape[0] * uly_count * grp_count // blocks_all
    held_whole = queries.shape[0] % block_tok == 0
    run = whole_blocks if held_whole and remote == 1 and uly_count == 2 else spread_blocks
    return run(queries, keys, values, output_cotangent, block_lists, list_counts)


def solution(mesh):
    placed = (
        P(("grp", "uly"), None, None),
        P(("grp", "uly"), None, None),
        P(("grp", "uly"), None, None),
        P(("grp", "uly"), None, None),
        P(),
        P(),
    )
    return jax.shard_map(
        on_device,
        mesh=mesh,
        in_specs=placed,
        out_specs=(
            P(("grp", "uly"), None, None),
            P(("grp", "uly"), None, None),
            P(("grp", "uly"), None, None),
            P(("grp", "uly"), None, None),
        ),
        check_vma=False,
    )
```

```python
from functools import partial

import jax
import jax.numpy as jnp
from jax import lax
from jax.experimental import pallas as pl
from jax.experimental.pallas import tpu as pltpu
from jax.sharding import PartitionSpec as P


def spread_blocks(queries, keys, values, output_cotangent, block_lists, list_counts):
    uly_count = lax.axis_size("uly")
    grp_count = lax.axis_size("grp")
    my_group = lax.axis_index("grp")
    tokens, head_count, head_width = queries.shape
    kv_heads = keys.shape[1]
    copies = max(1, uly_count // kv_heads)
    blocks_all, remote = block_lists.shape
    per_group = blocks_all // grp_count
    block_tok = tokens * uly_count // per_group
    group_tok = tokens * uly_count
    score_scale = head_width ** (-0.5)
    lists = block_lists.reshape(grp_count, per_group, remote)
    counted = (jnp.arange(remote)[None, :] < list_counts[:, None]).reshape(
        grp_count, per_group, remote
    )
    wanted = (lists // per_group == my_group) & counted
    send_place = jnp.sum(jnp.where(wanted, lists % per_group, 0), axis=(1, 2))
    sending = jnp.any(wanted, axis=(1, 2))
    mine_source = lax.dynamic_index_in_dim(lists, my_group, 0, keepdims=False) // per_group
    mine_counted = lax.dynamic_index_in_dim(counted, my_group, 0, keepdims=False)
    trip_count = jnp.max(jnp.sum(mine_counted.astype(jnp.int32), axis=1))

    def to_blocks(array_in):
        return array_in.reshape((per_group, block_tok) + array_in.shape[1:])

    keys_wide = jnp.repeat(keys, copies, axis=1)
    values_wide = jnp.repeat(values, copies, axis=1)
    query_heads, grad_heads, key_heads, value_heads = (
        lax.all_to_all(queries, "uly", split_axis=1, concat_axis=0, tiled=True),
        lax.all_to_all(output_cotangent, "uly", split_axis=1, concat_axis=0, tiled=True),
        lax.all_to_all(keys_wide, "uly", split_axis=1, concat_axis=0, tiled=True),
        lax.all_to_all(values_wide, "uly", split_axis=1, concat_axis=0, tiled=True),
    )
    stacked = jnp.stack([to_blocks(key_heads), to_blocks(value_heads)])
    outgoing = jnp.take(stacked, send_place, axis=1)
    arrived = lax.all_to_all(outgoing, "grp", split_axis=1, concat_axis=1, tiled=True)
    kv_local = key_heads.shape[1]
    heads_local = query_heads.shape[1]
    heads_per_group = heads_local // kv_local
    query_blk = query_heads.reshape(per_group, block_tok, kv_local, heads_per_group, head_width)
    grad_blk = grad_heads.reshape(per_group, block_tok, kv_local, heads_per_group, head_width)
    key_blk = to_blocks(key_heads)
    value_blk = to_blocks(value_heads)
    far_keys = arrived[0]
    far_values = arrived[1]
    causal = jnp.arange(block_tok)[:, None] >= jnp.arange(block_tok)[None, :]

    def logits(key_rows):
        return (
            jnp.einsum("pqkgd,pjkd->pkgqj", query_blk, key_rows, preferred_element_type=jnp.float32)
            * score_scale
        )

    def slot_rows(slot_index):
        source = lax.dynamic_index_in_dim(mine_source, slot_index, 1, keepdims=False)
        counted_slot = lax.dynamic_index_in_dim(mine_counted, slot_index, 1, keepdims=False)
        return (
            jnp.take(far_keys, source, axis=0),
            jnp.take(far_values, source, axis=0),
            counted_slot,
            source,
        )

    def masked(scores, counted_slot):
        return jnp.where(counted_slot[:, None, None, None, None], scores, -jnp.inf)

    near_scores = jnp.where(causal, logits(key_blk), -jnp.inf)
    highest = jnp.max(near_scores, axis=-1)
    denominator = jnp.sum(jnp.exp(near_scores - highest[..., None]), axis=-1)

    def max_sweep(slot_index, state_pair):
        highest, denominator = state_pair
        key_rows, value_rows, counted_slot, source = slot_rows(slot_index)
        scores = masked(logits(key_rows), counted_slot)
        new_highest = jnp.maximum(highest, jnp.max(scores, axis=-1))
        denominator = denominator * jnp.exp(highest - new_highest) + jnp.sum(
            jnp.exp(scores - new_highest[..., None]), axis=-1
        )
        return (new_highest, denominator)

    highest, denominator = lax.fori_loop(0, trip_count, max_sweep, (highest, denominator))
    log_total = highest + jnp.log(denominator)

    def softmax_weights(scores):
        return jnp.exp(scores - log_total[..., None])

    summed = jnp.einsum(
        "pkgqj,pjkd->pqkgd",
        softmax_weights(near_scores).astype(jnp.bfloat16),
        value_blk,
        preferred_element_type=jnp.float32,
    )

    def value_sweep(slot_index, summed):
        key_rows, value_rows, counted_slot, source = slot_rows(slot_index)
        weights = softmax_weights(masked(logits(key_rows), counted_slot)).astype(jnp.bfloat16)
        return summed + jnp.einsum(
            "pkgqj,pjkd->pqkgd", weights, value_rows, preferred_element_type=jnp.float32
        )

    summed = lax.fori_loop(0, trip_count, value_sweep, summed)
    attended_blk = summed.astype(jnp.bfloat16)
    row_delta = jnp.transpose(
        jnp.sum(grad_blk.astype(jnp.float32) * attended_blk.astype(jnp.float32), axis=-1),
        (0, 2, 3, 1),
    )

    def backward(scores, key_rows, value_rows):
        probs = softmax_weights(scores)
        weights = probs.astype(jnp.bfloat16)
        dprobs = jnp.einsum(
            "pqkgd,pjkd->pkgqj", grad_blk, value_rows, preferred_element_type=jnp.float32
        )
        dscores = (probs * (dprobs - row_delta[..., None])).astype(jnp.bfloat16)
        query_term = jnp.einsum(
            "pkgqj,pjkd->pqkgd", dscores, key_rows, preferred_element_type=jnp.float32
        )
        key_term = (
            jnp.einsum("pkgqj,pqkgd->pjkd", dscores, query_blk, preferred_element_type=jnp.float32)
            * score_scale
        )
        value_term = jnp.einsum(
            "pkgqj,pqkgd->pjkd", weights, grad_blk, preferred_element_type=jnp.float32
        )
        return (query_term, key_term, value_term)

    query_sum, key_near, value_near = backward(near_scores, key_blk, value_blk)
    far_grads = jnp.zeros((2, grp_count, block_tok, kv_local, head_width), jnp.float32)

    def grad_sweep(slot_index, state_pair):
        query_sum, far_grads = state_pair
        key_rows, value_rows, counted_slot, source = slot_rows(slot_index)
        query_term, key_term, value_term = backward(
            masked(logits(key_rows), counted_slot), key_rows, value_rows
        )
        routing = (
            (source[:, None] == jnp.arange(grp_count)[None, :]) & counted_slot[:, None]
        ).astype(jnp.float32)
        routed = jnp.einsum(
            "ps,xpjkd->xsjkd",
            routing,
            jnp.stack([key_term, value_term]),
            precision=lax.Precision.HIGHEST,
        )
        return (query_sum + query_term, far_grads + routed)

    query_sum, far_grads = lax.fori_loop(0, trip_count, grad_sweep, (query_sum, far_grads))
    owners = ((send_place[:, None] == jnp.arange(per_group)[None, :]) & sending[:, None]).astype(
        jnp.float32
    )
    returned = lax.all_to_all(far_grads, "grp", split_axis=1, concat_axis=1, tiled=True)
    landed = jnp.einsum("sp,xsjkd->xpjkd", owners, returned, precision=lax.Precision.HIGHEST)
    key_local = (key_near + landed[0]).reshape(group_tok, kv_local, head_width)
    value_local = (value_near + landed[1]).reshape(group_tok, kv_local, head_width)
    attended_rows = attended_blk.reshape(group_tok, heads_local, head_width)
    query_rows = (
        (query_sum * score_scale).astype(jnp.bfloat16).reshape(group_tok, heads_local, head_width)
    )
    attended, query_grad = (
        lax.all_to_all(attended_rows, "uly", split_axis=0, concat_axis=1, tiled=True),
        lax.all_to_all(query_rows, "uly", split_axis=0, concat_axis=1, tiled=True),
    )
    key_parts, value_parts = (
        lax.all_to_all(key_local, "uly", split_axis=0, concat_axis=1, tiled=True),
        lax.all_to_all(value_local, "uly", split_axis=0, concat_axis=1, tiled=True),
    )
    key_gradient = jnp.sum(key_parts.reshape(tokens, kv_heads, copies, head_width), axis=2).astype(
        jnp.bfloat16
    )
    value_gradient = jnp.sum(
        value_parts.reshape(tokens, kv_heads, copies, head_width), axis=2
    ).astype(jnp.bfloat16)
    return (attended, query_grad, key_gradient, value_gradient)


HIDDEN = -1e30
LAST = (((1,), (1,)), ((), ()))
FIRST = (((0,), (0,)), ((), ()))
F32 = jnp.float32
BF16 = jnp.bfloat16


def dot_last(left, right):
    return lax.dot_general(left, right, LAST, preferred_element_type=F32)


def dot_first(left, right):
    return lax.dot_general(left, right, FIRST, preferred_element_type=F32)


def same_head(rows, cols, heads, kv_heads):
    row = lax.broadcasted_iota(jnp.int32, (rows, cols), 0)
    col = lax.broadcasted_iota(jnp.int32, (rows, cols), 1)
    same = (row % heads) // (heads // kv_heads) == col % kv_heads
    causal = col // kv_heads <= row // heads
    return same, causal


def head_major(cols, kv_heads):
    row = lax.broadcasted_iota(jnp.int32, (cols, cols), 0)
    col = lax.broadcasted_iota(jnp.int32, (cols, cols), 1)
    place = cols // kv_heads
    return jnp.where(col == (row % place) * kv_heads + row // place, 1.0, 0.0).astype(BF16)


def reorder(one_hot, array):
    return jnp.dot(one_hot, array, preferred_element_type=F32).astype(BF16)


def own_head(scores, lane_head, kv_heads):
    place = scores.shape[0] // kv_heads
    kept = scores[:place]
    for head in range(1, kv_heads):
        kept = jnp.where(lane_head == head, scores[head * place:(head + 1) * place], kept)
    return kept


def all_heads(kept, lane_head, kv_heads):
    none = jnp.zeros_like(kept)
    return jnp.concatenate(
        [jnp.where(lane_head == head, kept, none) for head in range(kv_heads)], axis=0
    )


def near_kernel(q_ref, g_ref, k_ref, v_ref, stat_ref, *, heads, kv_heads, score_scale):
    blocks = stat_ref.shape[0]
    rows = q_ref.shape[0] // blocks
    cols = k_ref.shape[0] // blocks
    place = cols // kv_heads
    order = head_major(cols, kv_heads)
    lane = lax.broadcasted_iota(jnp.int32, (1, rows), 1)
    lane_head = lane % heads // (heads // kv_heads)
    causal = lax.broadcasted_iota(jnp.int32, (place, rows), 0) <= lane // heads
    for block in range(blocks):
        span = slice(block * rows, (block + 1) * rows)
        narrow = slice(block * cols, (block + 1) * cols)
        k_near = reorder(order, k_ref[narrow])
        v_near = reorder(order, v_ref[narrow])
        scores = own_head(dot_last(k_near, q_ref[span]), lane_head, kv_heads) * score_scale
        scores = jnp.where(causal, scores, HIDDEN)
        highest = jnp.max(scores, axis=0, keepdims=True)
        raised = jnp.exp(scores - highest)
        dprobs = own_head(dot_last(v_near, g_ref[span]), lane_head, kv_heads)
        stat_ref[block, 0:1] = highest
        stat_ref[block, 1:2] = jnp.sum(raised, axis=0, keepdims=True)
        stat_ref[block, 2:3] = jnp.sum(raised * dprobs, axis=0, keepdims=True)


def far_kernel(
    source_ref, seen_ref, q_ref, g_ref, stat_ref, arrived_ref, other_ref,
    far_mine_ref, far_other_ref, *, heads, kv_heads, score_scale
):
    blocks = stat_ref.shape[0]
    rows = q_ref.shape[0] // blocks
    half = other_ref.shape[2]
    order = head_major(2 * half, kv_heads)
    lane = lax.broadcasted_iota(jnp.int32, (1, rows), 1)
    lane_head = lane % heads // (heads // kv_heads)
    for block in range(blocks):
        span = slice(block * rows, (block + 1) * rows)
        source = source_ref[block]
        q = q_ref[span]
        g = g_ref[span]
        k_far = reorder(
            order, jnp.concatenate([arrived_ref[source, 0], other_ref[block, 0]], axis=0)
        )
        v_far = reorder(
            order, jnp.concatenate([arrived_ref[source, 1], other_ref[block, 1]], axis=0)
        )
        hidden = jnp.where(seen_ref[block] > 0, 0.0, HIDDEN)
        scores = own_head(dot_last(k_far, q), lane_head, kv_heads) * score_scale + hidden
        near_highest = stat_ref[block, 0:1]
        highest = jnp.maximum(near_highest, jnp.max(scores, axis=0, keepdims=True))
        raised = jnp.exp(scores - highest)
        shrink = jnp.exp(near_highest - highest)
        dprobs = own_head(dot_last(v_far, g), lane_head, kv_heads)
        total = shrink * stat_ref[block, 1:2] + jnp.sum(raised, axis=0, keepdims=True)
        inverse = 1.0 / total
        delta = shrink * stat_ref[block, 2:3] + jnp.sum(raised * dprobs, axis=0, keepdims=True)
        probs = raised * inverse
        dscores = (probs * (dprobs - delta * inverse)).astype(BF16)
        dk = jnp.dot(all_heads(dscores, lane_head, kv_heads), q, preferred_element_type=F32)
        dv = jnp.dot(
            all_heads(probs.astype(BF16), lane_head, kv_heads), g, preferred_element_type=F32
        )
        dk = dot_first(order, (dk * score_scale).astype(BF16)).astype(BF16)
        dv = dot_first(order, dv.astype(BF16)).astype(BF16)
        far_mine_ref[block, 0] = dk[:half]
        far_mine_ref[block, 1] = dv[:half]
        far_other_ref[block, 0] = dk[half:]
        far_other_ref[block, 1] = dv[half:]


def land_kernel(place_ref, sending_ref, landed_ref, own_ref, give_ref, sum_ref):
    blocks = own_ref.shape[0]
    sum_ref[...] = jnp.zeros_like(sum_ref)
    for group in range(landed_ref.shape[0]):

        @pl.when(sending_ref[group] > 0)
        def _():
            place = place_ref[group]
            sum_ref[place] = sum_ref[place] + landed_ref[group].astype(F32)

    own_ref[...] = sum_ref[:blocks]
    give_ref[...] = sum_ref[blocks:].astype(BF16)


def finish_kernel(half_ref, dk_near_ref, dv_near_ref, own_ref, back_ref, dk_ref, dv_ref):
    blocks, _, half, _ = back_ref.shape
    mine = half_ref[0]
    for block in range(blocks):
        for near_ref, out_ref, which in ((dk_near_ref, dk_ref, 0), (dv_near_ref, dv_ref, 1)):
            for sums_ref, place in ((own_ref, mine), (back_ref, 1 - mine)):
                span = pl.ds(pl.multiple_of(block * 2 * half + place * half, half), half)
                far = sums_ref[block, which].astype(F32)
                out_ref[span] = (near_ref[span] + far).astype(BF16)


def local_kernel(
    source_ref, seen_ref, q_ref, g_ref, k_ref, v_ref, mine_ref, other_ref,
    att_ref, dq_ref, dk_ref, dv_ref, bias_ref, *, heads, kv_heads, score_scale
):
    step = pl.program_id(0)
    rows = q_ref.shape[0]
    cols = k_ref.shape[0]

    @pl.when(step == 0)
    def _():
        same, causal = same_head(rows, cols, heads, kv_heads)
        bias_ref[:, :cols] = jnp.where(same & causal, 0.0, HIDDEN)
        bias_ref[:, cols:] = jnp.where(same, 0.0, HIDDEN)

    far_bias = jnp.where(seen_ref[step] > 0, 0.0, HIDDEN)
    k_all = jnp.concatenate([k_ref[...], mine_ref[0, 0], other_ref[0, 0]], axis=0)
    v_all = jnp.concatenate([v_ref[...], mine_ref[0, 1], other_ref[0, 1]], axis=0)
    q = q_ref[...]
    g = g_ref[...]
    scores = dot_last(q, k_all) * score_scale + bias_ref[...]
    scores = jnp.concatenate([scores[:, :cols], scores[:, cols:] + far_bias], axis=1)
    highest = jnp.max(scores, axis=1, keepdims=True)
    raised = jnp.exp(scores - highest)
    total = jnp.sum(raised, axis=1, keepdims=True)
    probs = raised * (1.0 / total)
    weights = probs.astype(BF16)
    attended = jnp.dot(weights, v_all, preferred_element_type=F32).astype(BF16)
    att_ref[...] = attended
    delta = jnp.sum(g.astype(F32) * attended.astype(F32), axis=1, keepdims=True)
    dscores = (probs * (dot_last(g, v_all) - delta)).astype(BF16)
    dq = jnp.dot(dscores, k_all, preferred_element_type=F32) * score_scale
    dq_ref[...] = dq.astype(BF16)
    dk_ref[...] = dot_first(dscores[:, :cols], q) * score_scale
    dv_ref[...] = dot_first(weights[:, :cols], g)


def take_rows(array, index):
    return array.at[index].get(mode="promise_in_bounds")


def whole_blocks(queries, keys, values, output_cotangent, block_lists, list_counts):
    grp_count = lax.axis_size("grp")
    uly_count = lax.axis_size("uly")
    my_group = lax.axis_index("grp")
    my_half = lax.axis_index("uly")
    tokens, heads, width = queries.shape
    kv_heads = keys.shape[1]
    per_group = block_lists.shape[0] // grp_count
    block_tok = tokens * uly_count // per_group
    mine_blocks = tokens // block_tok
    rows = block_tok * heads
    cols = block_tok * kv_heads
    half = cols // 2
    sizes = dict(heads=heads, kv_heads=kv_heads, score_scale=width ** (-0.5))
    swap = [(0, 1), (1, 0)]

    lists = block_lists.reshape(grp_count, per_group)
    counted = (list_counts > 0).reshape(grp_count, per_group)
    wanted = (lists // per_group == my_group) & counted
    send_place = jnp.sum(jnp.where(wanted, lists % per_group, 0), axis=1)
    sending = jnp.any(wanted, axis=1)
    my_lists = lax.dynamic_index_in_dim(lists, my_group, 0, keepdims=False)
    my_seen = lax.dynamic_index_in_dim(counted, my_group, 0, keepdims=False).astype(jnp.int32)
    source = my_lists // per_group

    def by_owner(vector):
        both = vector.reshape(2, mine_blocks)
        return (
            lax.dynamic_index_in_dim(both, my_half, 0, keepdims=False),
            lax.dynamic_index_in_dim(both, 1 - my_half, 0, keepdims=False),
        )

    source_own, source_sib = by_owner(source)
    seen_own, seen_sib = by_owner(my_seen)
    owner_first = jnp.where(
        send_place // mine_blocks == my_half,
        send_place % mine_blocks,
        send_place % mine_blocks + mine_blocks,
    )

    q2 = queries.reshape(tokens * heads, width)
    g2 = output_cotangent.reshape(tokens * heads, width)
    k2 = keys.reshape(tokens * kv_heads, width)
    v2 = values.reshape(tokens * kv_heads, width)

    def step_rows(i, *_):
        return (i, 0)

    def step_part(i, *_):
        return (i, 0, 0, 0)

    def from_source(i, source_ref, seen_ref):
        return (source_ref[i], 0, 0, 0)

    def far_spec(index_map):
        return pl.BlockSpec((1, 2, half, width), index_map)

    row_spec = pl.BlockSpec((rows, width), step_rows)
    col_spec = pl.BlockSpec((cols, width), step_rows)
    far_shape = jax.ShapeDtypeStruct((mine_blocks, 2, half, width), BF16)

    limit = pltpu.CompilerParams(vmem_limit_bytes=24 * 1024 * 1024)

    def call(kernel, scalars, operands, out_shape, name, scratch=()):
        whole = pl.BlockSpec(memory_space=pltpu.VMEM)
        return pl.pallas_call(
            kernel,
            in_specs=[pl.BlockSpec(memory_space=pltpu.SMEM)] * len(scalars) + [whole] * len(operands),
            out_specs=jax.tree.map(lambda _: whole, out_shape),
            out_shape=out_shape,
            scratch_shapes=scratch,
            compiler_params=limit,
            name=name,
        )(*scalars, *operands)

    parts = jnp.stack(
        [keys.reshape(mine_blocks, 2, half, width), values.reshape(mine_blocks, 2, half, width)],
        axis=2,
    )
    kept = lax.dynamic_index_in_dim(parts, my_half, 1, keepdims=False)
    given = lax.dynamic_index_in_dim(parts, 1 - my_half, 1, keepdims=False)
    gotten = lax.ppermute(given, "uly", swap)
    outgoing = take_rows(jnp.concatenate([kept, gotten]), owner_first)
    outgoing, k2n = lax.optimization_barrier((outgoing, k2))
    arrived = lax.all_to_all(outgoing, "grp", split_axis=0, concat_axis=0, tiled=True)
    stats = call(
        partial(near_kernel, **sizes), (), (q2, g2, k2n, v2),
        jax.ShapeDtypeStruct((mine_blocks, 8, rows), F32), "near",
    )
    arrived, stats = lax.optimization_barrier((arrived, stats))
    other = lax.ppermute(take_rows(arrived, source_sib), "uly", swap)

    far_mine, far_other = call(
        partial(far_kernel, **sizes), (source_own, seen_own), (q2, g2, stats, arrived, other),
        [far_shape, far_shape], "far",
    )
    from_sib = lax.ppermute(far_other, "uly", swap)
    groups = jnp.arange(grp_count)
    source_both = jnp.concatenate([source_own, source_sib])
    asked = jnp.argmax(source_both[None, :] == groups[:, None], axis=1)
    returning = take_rows(jnp.concatenate([far_mine, from_sib]), asked)
    returning, k2l = lax.optimization_barrier((returning, k2))
    landed = lax.all_to_all(returning, "grp", split_axis=0, concat_axis=0, tiled=True)
    row_shape = jax.ShapeDtypeStruct(q2.shape, BF16)
    near_shape = jax.ShapeDtypeStruct(k2.shape, F32)
    attended, dq, dk_near, dv_near = pl.pallas_call(
        partial(local_kernel, **sizes),
        grid_spec=pltpu.PrefetchScalarGridSpec(
            num_scalar_prefetch=2,
            grid=(mine_blocks,),
            in_specs=[
                row_spec, row_spec, col_spec, col_spec, far_spec(from_source), far_spec(step_part)
            ],
            out_specs=[row_spec, row_spec, col_spec, col_spec],
            scratch_shapes=[pltpu.VMEM((rows, 2 * cols), F32)],
        ),
        out_shape=[row_shape, row_shape, near_shape, near_shape],
        compiler_params=limit,
        name="local",
    )(source_own, seen_own, q2, g2, k2l, v2, arrived, other)
    landed, dk_near = lax.optimization_barrier((landed, dk_near))
    own, give = call(
        land_kernel, (owner_first, sending.astype(jnp.int32)), (landed,),
        [jax.ShapeDtypeStruct(far_shape.shape, F32), far_shape], "land",
        [pltpu.VMEM((per_group, 2, half, width), F32)],
    )
    back = lax.ppermute(give, "uly", swap)
    small = jax.ShapeDtypeStruct(k2.shape, BF16)
    dk, dv = call(
        finish_kernel, (my_half.reshape(1),), (dk_near, dv_near, own, back),
        [small, small], "finish",
    )
    dk = dk.reshape(keys.shape)
    dv = dv.reshape(keys.shape)
    return (attended.reshape(queries.shape), dq.reshape(queries.shape), dk, dv)


def on_device(queries, keys, values, output_cotangent, block_lists, list_counts):
    uly_count = lax.axis_size("uly")
    grp_count = lax.axis_size("grp")
    blocks_all, remote = block_lists.shape
    block_tok = queries.shape[0] * uly_count * grp_count // blocks_all
    held_whole = queries.shape[0] % block_tok == 0
    run = whole_blocks if held_whole and remote == 1 and uly_count == 2 else spread_blocks
    return run(queries, keys, values, output_cotangent, block_lists, list_counts)


def solution(mesh):
    placed = (
        P(("grp", "uly"), None, None),
        P(("grp", "uly"), None, None),
        P(("grp", "uly"), None, None),
        P(("grp", "uly"), None, None),
        P(),
        P(),
    )
    return jax.shard_map(
        on_device,
        mesh=mesh,
        in_specs=placed,
        out_specs=(
            P(("grp", "uly"), None, None),
            P(("grp", "uly"), None, None),
            P(("grp", "uly"), None, None),
            P(("grp", "uly"), None, None),
        ),
        check_vma=False,
    )
```

```python
from functools import partial

import jax
import jax.numpy as jnp
from jax import lax
from jax.experimental import pallas as pl
from jax.experimental.pallas import tpu as pltpu
from jax.sharding import PartitionSpec as P


def spread_blocks(queries, keys, values, output_cotangent, block_lists, list_counts):
    uly_count = lax.axis_size("uly")
    grp_count = lax.axis_size("grp")
    my_group = lax.axis_index("grp")
    tokens, head_count, head_width = queries.shape
    kv_heads = keys.shape[1]
    copies = max(1, uly_count // kv_heads)
    blocks_all, remote = block_lists.shape
    per_group = blocks_all // grp_count
    block_tok = tokens * uly_count // per_group
    group_tok = tokens * uly_count
    score_scale = head_width ** (-0.5)
    lists = block_lists.reshape(grp_count, per_group, remote)
    counted = (jnp.arange(remote)[None, :] < list_counts[:, None]).reshape(
        grp_count, per_group, remote
    )
    wanted = (lists // per_group == my_group) & counted
    send_place = jnp.sum(jnp.where(wanted, lists % per_group, 0), axis=(1, 2))
    sending = jnp.any(wanted, axis=(1, 2))
    mine_source = lax.dynamic_index_in_dim(lists, my_group, 0, keepdims=False) // per_group
    mine_counted = lax.dynamic_index_in_dim(counted, my_group, 0, keepdims=False)
    trip_count = jnp.max(jnp.sum(mine_counted.astype(jnp.int32), axis=1))

    def to_blocks(array_in):
        return array_in.reshape((per_group, block_tok) + array_in.shape[1:])

    keys_wide = jnp.repeat(keys, copies, axis=1)
    values_wide = jnp.repeat(values, copies, axis=1)
    query_heads, grad_heads, key_heads, value_heads = (
        lax.all_to_all(queries, "uly", split_axis=1, concat_axis=0, tiled=True),
        lax.all_to_all(output_cotangent, "uly", split_axis=1, concat_axis=0, tiled=True),
        lax.all_to_all(keys_wide, "uly", split_axis=1, concat_axis=0, tiled=True),
        lax.all_to_all(values_wide, "uly", split_axis=1, concat_axis=0, tiled=True),
    )
    stacked = jnp.stack([to_blocks(key_heads), to_blocks(value_heads)])
    outgoing = jnp.take(stacked, send_place, axis=1)
    arrived = lax.all_to_all(outgoing, "grp", split_axis=1, concat_axis=1, tiled=True)
    kv_local = key_heads.shape[1]
    heads_local = query_heads.shape[1]
    heads_per_group = heads_local // kv_local
    query_blk = query_heads.reshape(per_group, block_tok, kv_local, heads_per_group, head_width)
    grad_blk = grad_heads.reshape(per_group, block_tok, kv_local, heads_per_group, head_width)
    key_blk = to_blocks(key_heads)
    value_blk = to_blocks(value_heads)
    far_keys = arrived[0]
    far_values = arrived[1]
    causal = jnp.arange(block_tok)[:, None] >= jnp.arange(block_tok)[None, :]

    def logits(key_rows):
        return (
            jnp.einsum("pqkgd,pjkd->pkgqj", query_blk, key_rows, preferred_element_type=jnp.float32)
            * score_scale
        )

    def slot_rows(slot_index):
        source = lax.dynamic_index_in_dim(mine_source, slot_index, 1, keepdims=False)
        counted_slot = lax.dynamic_index_in_dim(mine_counted, slot_index, 1, keepdims=False)
        return (
            jnp.take(far_keys, source, axis=0),
            jnp.take(far_values, source, axis=0),
            counted_slot,
            source,
        )

    def masked(scores, counted_slot):
        return jnp.where(counted_slot[:, None, None, None, None], scores, -jnp.inf)

    near_scores = jnp.where(causal, logits(key_blk), -jnp.inf)
    highest = jnp.max(near_scores, axis=-1)
    denominator = jnp.sum(jnp.exp(near_scores - highest[..., None]), axis=-1)

    def max_sweep(slot_index, state_pair):
        highest, denominator = state_pair
        key_rows, value_rows, counted_slot, source = slot_rows(slot_index)
        scores = masked(logits(key_rows), counted_slot)
        new_highest = jnp.maximum(highest, jnp.max(scores, axis=-1))
        denominator = denominator * jnp.exp(highest - new_highest) + jnp.sum(
            jnp.exp(scores - new_highest[..., None]), axis=-1
        )
        return (new_highest, denominator)

    highest, denominator = lax.fori_loop(0, trip_count, max_sweep, (highest, denominator))
    log_total = highest + jnp.log(denominator)

    def softmax_weights(scores):
        return jnp.exp(scores - log_total[..., None])

    summed = jnp.einsum(
        "pkgqj,pjkd->pqkgd",
        softmax_weights(near_scores).astype(jnp.bfloat16),
        value_blk,
        preferred_element_type=jnp.float32,
    )

    def value_sweep(slot_index, summed):
        key_rows, value_rows, counted_slot, source = slot_rows(slot_index)
        weights = softmax_weights(masked(logits(key_rows), counted_slot)).astype(jnp.bfloat16)
        return summed + jnp.einsum(
            "pkgqj,pjkd->pqkgd", weights, value_rows, preferred_element_type=jnp.float32
        )

    summed = lax.fori_loop(0, trip_count, value_sweep, summed)
    attended_blk = summed.astype(jnp.bfloat16)
    row_delta = jnp.transpose(
        jnp.sum(grad_blk.astype(jnp.float32) * attended_blk.astype(jnp.float32), axis=-1),
        (0, 2, 3, 1),
    )

    def backward(scores, key_rows, value_rows):
        probs = softmax_weights(scores)
        weights = probs.astype(jnp.bfloat16)
        dprobs = jnp.einsum(
            "pqkgd,pjkd->pkgqj", grad_blk, value_rows, preferred_element_type=jnp.float32
        )
        dscores = (probs * (dprobs - row_delta[..., None])).astype(jnp.bfloat16)
        query_term = jnp.einsum(
            "pkgqj,pjkd->pqkgd", dscores, key_rows, preferred_element_type=jnp.float32
        )
        key_term = (
            jnp.einsum("pkgqj,pqkgd->pjkd", dscores, query_blk, preferred_element_type=jnp.float32)
            * score_scale
        )
        value_term = jnp.einsum(
            "pkgqj,pqkgd->pjkd", weights, grad_blk, preferred_element_type=jnp.float32
        )
        return (query_term, key_term, value_term)

    query_sum, key_near, value_near = backward(near_scores, key_blk, value_blk)
    far_grads = jnp.zeros((2, grp_count, block_tok, kv_local, head_width), jnp.float32)

    def grad_sweep(slot_index, state_pair):
        query_sum, far_grads = state_pair
        key_rows, value_rows, counted_slot, source = slot_rows(slot_index)
        query_term, key_term, value_term = backward(
            masked(logits(key_rows), counted_slot), key_rows, value_rows
        )
        routing = (
            (source[:, None] == jnp.arange(grp_count)[None, :]) & counted_slot[:, None]
        ).astype(jnp.float32)
        routed = jnp.einsum(
            "ps,xpjkd->xsjkd",
            routing,
            jnp.stack([key_term, value_term]),
            precision=lax.Precision.HIGHEST,
        )
        return (query_sum + query_term, far_grads + routed)

    query_sum, far_grads = lax.fori_loop(0, trip_count, grad_sweep, (query_sum, far_grads))
    owners = ((send_place[:, None] == jnp.arange(per_group)[None, :]) & sending[:, None]).astype(
        jnp.float32
    )
    returned = lax.all_to_all(far_grads, "grp", split_axis=1, concat_axis=1, tiled=True)
    landed = jnp.einsum("sp,xsjkd->xpjkd", owners, returned, precision=lax.Precision.HIGHEST)
    key_local = (key_near + landed[0]).reshape(group_tok, kv_local, head_width)
    value_local = (value_near + landed[1]).reshape(group_tok, kv_local, head_width)
    attended_rows = attended_blk.reshape(group_tok, heads_local, head_width)
    query_rows = (
        (query_sum * score_scale).astype(jnp.bfloat16).reshape(group_tok, heads_local, head_width)
    )
    attended, query_grad = (
        lax.all_to_all(attended_rows, "uly", split_axis=0, concat_axis=1, tiled=True),
        lax.all_to_all(query_rows, "uly", split_axis=0, concat_axis=1, tiled=True),
    )
    key_parts, value_parts = (
        lax.all_to_all(key_local, "uly", split_axis=0, concat_axis=1, tiled=True),
        lax.all_to_all(value_local, "uly", split_axis=0, concat_axis=1, tiled=True),
    )
    key_gradient = jnp.sum(key_parts.reshape(tokens, kv_heads, copies, head_width), axis=2).astype(
        jnp.bfloat16
    )
    value_gradient = jnp.sum(
        value_parts.reshape(tokens, kv_heads, copies, head_width), axis=2
    ).astype(jnp.bfloat16)
    return (attended, query_grad, key_gradient, value_gradient)


HIDDEN = -1e30
LAST = (((1,), (1,)), ((), ()))
FIRST = (((0,), (0,)), ((), ()))
F32 = jnp.float32
BF16 = jnp.bfloat16


def dot_last(left, right):
    return lax.dot_general(left, right, LAST, preferred_element_type=F32)


def dot_first(left, right):
    return lax.dot_general(left, right, FIRST, preferred_element_type=F32)


def head_major(cols, kv_heads):
    half = cols // 2
    place = half // kv_heads
    row = lax.broadcasted_iota(jnp.int32, (cols, cols), 0)
    col = lax.broadcasted_iota(jnp.int32, (cols, cols), 1)
    token = row // half * place + row % place
    return jnp.where(col == token * kv_heads + row % half // place, 1.0, 0.0).astype(BF16)


def reorder(one_hot, array):
    return jnp.dot(one_hot, array, preferred_element_type=F32).astype(BF16)


def own_head(scores, lane_head, kv_heads):
    place = scores.shape[0] // kv_heads
    kept = scores[:place]
    for head in range(1, kv_heads):
        kept = jnp.where(lane_head == head, scores[head * place:(head + 1) * place], kept)
    return kept


def all_heads(kept, lane_head, kv_heads):
    none = jnp.zeros_like(kept)
    return jnp.concatenate(
        [jnp.where(lane_head == head, kept, none) for head in range(kv_heads)], axis=0
    )


def lanes(rows, heads, kv_heads):
    lane = lax.broadcasted_iota(jnp.int32, (1, rows), 1)
    return lane // heads, lane % heads // (heads // kv_heads)


def pack_kernel(half_ref, k_ref, v_ref, kept_ref, given_ref, *, kv_heads):
    blocks, _, half, _ = kept_ref.shape
    mine = half_ref[0] == 0
    order = head_major(2 * half, kv_heads)
    for block in range(blocks):
        for which, ref in enumerate((k_ref, v_ref)):
            ordered = reorder(order, ref[block * 2 * half:(block + 1) * 2 * half])
            kept_ref[block, which] = jnp.where(mine, ordered[:half], ordered[half:])
            given_ref[block, which] = jnp.where(mine, ordered[half:], ordered[:half])


def outgoing_kernel(place_ref, sending_ref, blocks_ref, *refs, first):
    out_ref, sems = refs[-2:]
    blocks = blocks_ref.shape[0]
    copies = []
    for group in range(out_ref.shape[0]):
        place = place_ref[group] - first
        wanted = (sending_ref[group] > 0) & (place >= 0) & (place < blocks)
        block = jnp.clip(place, 0, blocks - 1)
        copies.append(
            (wanted, pltpu.make_async_copy(blocks_ref.at[block], out_ref.at[group], sems.at[group]))
        )
    for wanted, copy in copies:
        pl.when(wanted)(copy.start)
    for wanted, copy in copies:
        pl.when(wanted)(copy.wait)


def returning_kernel(source_ref, blocks_ref, _, out_ref, sems):
    copies = [
        pltpu.make_async_copy(blocks_ref.at[block], out_ref.at[source_ref[block]], sems.at[block])
        for block in range(blocks_ref.shape[0])
    ]
    for copy in copies:
        copy.start()
    for copy in copies:
        copy.wait()


def near_kernel(
    half_ref, q_ref, g_ref, kept_ref, given_ref, stat_ref, *, heads, kv_heads, score_scale
):
    blocks = stat_ref.shape[0]
    rows = q_ref.shape[0] // blocks
    place = kept_ref.shape[2] // kv_heads
    token, lane_head = lanes(rows, heads, kv_heads)
    key = lax.broadcasted_iota(jnp.int32, (2 * place, rows), 0)
    part = jnp.where(key < place, half_ref[0], 1 - half_ref[0])
    causal = key % place + part * place <= token
    for block in range(blocks):
        span = slice(block * rows, (block + 1) * rows)
        pieces = []
        for which, ref in enumerate((q_ref, g_ref)):
            both = jnp.concatenate([kept_ref[block, which], given_ref[block, which]], axis=0)
            full = dot_last(both, ref[span])
            half = full.shape[0] // 2
            pieces.append(
                jnp.concatenate(
                    [
                        own_head(full[:half], lane_head, kv_heads),
                        own_head(full[half:], lane_head, kv_heads),
                    ],
                    axis=0,
                )
            )
        scores = jnp.where(causal, pieces[0] * score_scale, HIDDEN)
        highest = jnp.max(scores, axis=0, keepdims=True)
        raised = jnp.exp(scores - highest)
        stat_ref[block, 0:1] = highest
        stat_ref[block, 1:2] = jnp.sum(raised, axis=0, keepdims=True)
        stat_ref[block, 2:3] = jnp.sum(raised * pieces[1], axis=0, keepdims=True)


def far_scores(part_ref, at, q, g, seen, lane_head, kv_heads, score_scale):
    hidden = jnp.where(seen > 0, 0.0, HIDDEN)
    scores = own_head(dot_last(part_ref[at, 0], q), lane_head, kv_heads) * score_scale + hidden
    return scores, own_head(dot_last(part_ref[at, 1], g), lane_head, kv_heads)


def merged(stat_ref, block, scores, dprobs):
    before = stat_ref[block, 0:1]
    highest = jnp.maximum(before, jnp.max(scores, axis=0, keepdims=True))
    raised = jnp.exp(scores - highest)
    shrink = jnp.exp(before - highest)
    total = shrink * stat_ref[block, 1:2] + jnp.sum(raised, axis=0, keepdims=True)
    delta = shrink * stat_ref[block, 2:3] + jnp.sum(raised * dprobs, axis=0, keepdims=True)
    return highest, raised, total, delta


def far_gradients(probs, dprobs, delta, q, g, lane_head, kv_heads, score_scale):
    dscores = (probs * (dprobs - delta)).astype(BF16)
    dk = jnp.dot(all_heads(dscores, lane_head, kv_heads), q, preferred_element_type=F32)
    dv = jnp.dot(all_heads(probs.astype(BF16), lane_head, kv_heads), g, preferred_element_type=F32)
    return (dk * score_scale).astype(BF16), dv.astype(BF16)


def mid_kernel(
    source_ref, seen_ref, q_ref, g_ref, stat_ref, arrived_ref, out_ref,
    *, heads, kv_heads, score_scale
):
    blocks = stat_ref.shape[0]
    rows = q_ref.shape[0] // blocks
    _, lane_head = lanes(rows, heads, kv_heads)
    for block in range(blocks):
        span = slice(block * rows, (block + 1) * rows)
        scores, dprobs = far_scores(
            arrived_ref, source_ref[block], q_ref[span], g_ref[span], seen_ref[block],
            lane_head, kv_heads, score_scale,
        )
        highest, _, total, delta = merged(stat_ref, block, scores, dprobs)
        out_ref[block, 0:1] = highest
        out_ref[block, 1:2] = total
        out_ref[block, 2:3] = delta


def far_kernel(
    seen_ref, q_ref, g_ref, stat_ref, other_ref, grad_ref, out_ref,
    *, heads, kv_heads, score_scale
):
    blocks = stat_ref.shape[0]
    rows = q_ref.shape[0] // blocks
    _, lane_head = lanes(rows, heads, kv_heads)
    for block in range(blocks):
        span = slice(block * rows, (block + 1) * rows)
        q = q_ref[span]
        g = g_ref[span]
        scores, dprobs = far_scores(
            other_ref, block, q, g, seen_ref[block], lane_head, kv_heads, score_scale
        )
        highest, raised, total, delta = merged(stat_ref, block, scores, dprobs)
        inverse = 1.0 / total
        delta = delta * inverse
        grad_ref[block, 0], grad_ref[block, 1] = far_gradients(
            raised * inverse, dprobs, delta, q, g, lane_head, kv_heads, score_scale
        )
        out_ref[block, 0:1] = highest
        out_ref[block, 1:2] = inverse
        out_ref[block, 2:3] = delta


def mine_kernel(
    source_ref, seen_ref, q_ref, g_ref, stat_ref, arrived_ref, out_ref, grad_ref, sems,
    *, heads, kv_heads, score_scale
):
    blocks = stat_ref.shape[0]
    rows = q_ref.shape[0] // blocks
    _, lane_head = lanes(rows, heads, kv_heads)
    copies = []
    for block in range(blocks):
        span = slice(block * rows, (block + 1) * rows)
        q = q_ref[span]
        g = g_ref[span]
        source = source_ref[block]
        scores, dprobs = far_scores(
            arrived_ref, source, q, g, seen_ref[block], lane_head, kv_heads, score_scale
        )
        probs = jnp.exp(scores - stat_ref[block, 0:1]) * stat_ref[block, 1:2]
        grad_ref[block, 0], grad_ref[block, 1] = far_gradients(
            probs, dprobs, stat_ref[block, 2:3], q, g, lane_head, kv_heads, score_scale
        )
        copies.append(
            pltpu.make_async_copy(grad_ref.at[block], out_ref.at[source], sems.at[block])
        )
        copies[-1].start()
    for copy in copies:
        copy.wait()


def local_kernel(
    source_ref, seen_ref, q_ref, g_ref, k_ref, v_ref, mine_ref, other_ref,
    att_ref, dq_ref, dk_ref, dv_ref, bias_ref, *, heads, kv_heads, score_scale
):
    step = pl.program_id(0)
    rows = q_ref.shape[0]
    cols = k_ref.shape[0]

    @pl.when(step == 0)
    def _():
        half = cols // 2
        place = half // kv_heads
        row = lax.broadcasted_iota(jnp.int32, (rows, cols), 0)
        col = lax.broadcasted_iota(jnp.int32, (rows, cols), 1)
        same = row % heads // (heads // kv_heads) == col % half // place
        causal = col // half * place + col % place <= row // heads
        bias_ref[:, :cols] = jnp.where(same & causal, 0.0, HIDDEN)
        bias_ref[:, cols:] = jnp.where(same, 0.0, HIDDEN)

    far_bias = jnp.where(seen_ref[step] > 0, 0.0, HIDDEN)
    order = head_major(cols, kv_heads)
    k_near = reorder(order, k_ref[...])
    v_near = reorder(order, v_ref[...])
    k_all = jnp.concatenate([k_near, mine_ref[0, 0], other_ref[0, 0]], axis=0)
    v_all = jnp.concatenate([v_near, mine_ref[0, 1], other_ref[0, 1]], axis=0)
    q = q_ref[...]
    g = g_ref[...]
    scores = dot_last(q, k_all) * score_scale + bias_ref[...]
    scores = jnp.concatenate([scores[:, :cols], scores[:, cols:] + far_bias], axis=1)
    highest = jnp.max(scores, axis=1, keepdims=True)
    raised = jnp.exp(scores - highest)
    total = jnp.sum(raised, axis=1, keepdims=True)
    probs = raised * (1.0 / total)
    weights = probs.astype(BF16)
    attended = jnp.dot(weights, v_all, preferred_element_type=F32).astype(BF16)
    att_ref[...] = attended
    delta = jnp.sum(g.astype(F32) * attended.astype(F32), axis=1, keepdims=True)
    dscores = (probs * (dot_last(g, v_all) - delta)).astype(BF16)
    dq = jnp.dot(dscores, k_all, preferred_element_type=F32) * score_scale
    dq_ref[...] = dq.astype(BF16)
    dk_ref[...] = dot_first(dscores[:, :cols], q) * score_scale
    dv_ref[...] = dot_first(weights[:, :cols], g)


def landing_kernel(place_ref, sending_ref, landed_ref, out_ref, sum_ref, *, first):
    blocks = sum_ref.shape[0]
    sum_ref[...] = jnp.zeros_like(sum_ref)
    for group in range(landed_ref.shape[0]):
        place = place_ref[group] - first

        @pl.when((sending_ref[group] > 0) & (place >= 0) & (place < blocks))
        def _():
            sum_ref[place] = sum_ref[place] + landed_ref[group].astype(F32)

    out_ref[...] = sum_ref[...].astype(out_ref.dtype)


def finish_kernel(
    half_ref, dk_near_ref, dv_near_ref, own_ref, back_ref, dk_ref, dv_ref, *, kv_heads
):
    blocks, _, half, _ = back_ref.shape
    mine = half_ref[0] == 0
    order = head_major(2 * half, kv_heads)
    for block in range(blocks):
        span = slice(block * 2 * half, (block + 1) * 2 * half)
        for near_ref, out_ref, which in ((dk_near_ref, dk_ref, 0), (dv_near_ref, dv_ref, 1)):
            own = own_ref[block, which]
            back = back_ref[block, which].astype(F32)
            far = jnp.concatenate([jnp.where(mine, own, back), jnp.where(mine, back, own)], axis=0)
            summed = (near_ref[span] + far).astype(BF16)
            out_ref[span] = dot_first(order, summed).astype(BF16)


def take_rows(array, index):
    return array.at[index].get(mode="promise_in_bounds")


def whole_blocks(queries, keys, values, output_cotangent, block_lists, list_counts):
    grp_count = lax.axis_size("grp")
    uly_count = lax.axis_size("uly")
    my_group = lax.axis_index("grp")
    my_half = lax.axis_index("uly")
    tokens, heads, width = queries.shape
    kv_heads = keys.shape[1]
    per_group = block_lists.shape[0] // grp_count
    block_tok = tokens * uly_count // per_group
    mine_blocks = tokens // block_tok
    rows = block_tok * heads
    cols = block_tok * kv_heads
    half = cols // 2
    sizes = dict(heads=heads, kv_heads=kv_heads, score_scale=width ** (-0.5))
    swap = [(0, 1), (1, 0)]

    lists = block_lists.reshape(grp_count, per_group)
    counted = (list_counts > 0).reshape(grp_count, per_group)
    wanted = (lists // per_group == my_group) & counted
    send_place = jnp.sum(jnp.where(wanted, lists % per_group, 0), axis=1)
    sending = jnp.any(wanted, axis=1).astype(jnp.int32)
    my_lists = lax.dynamic_index_in_dim(lists, my_group, 0, keepdims=False)
    my_seen = lax.dynamic_index_in_dim(counted, my_group, 0, keepdims=False).astype(jnp.int32)
    source = my_lists // per_group

    def by_owner(vector):
        both = vector.reshape(2, mine_blocks)
        return (
            lax.dynamic_index_in_dim(both, my_half, 0, keepdims=False),
            lax.dynamic_index_in_dim(both, 1 - my_half, 0, keepdims=False),
        )

    source_own, source_sib = by_owner(source)
    seen_own, _ = by_owner(my_seen)
    owner_first = jnp.where(
        send_place // mine_blocks == my_half,
        send_place % mine_blocks,
        send_place % mine_blocks + mine_blocks,
    )
    half_id = my_half.reshape(1)

    q2 = queries.reshape(tokens * heads, width)
    g2 = output_cotangent.reshape(tokens * heads, width)
    k2 = keys.reshape(tokens * kv_heads, width)
    v2 = values.reshape(tokens * kv_heads, width)

    part_shape = jax.ShapeDtypeStruct((mine_blocks, 2, half, width), BF16)
    slot_shape = jax.ShapeDtypeStruct((grp_count, 2, half, width), BF16)
    stat_shape = jax.ShapeDtypeStruct((mine_blocks, 8, rows), F32)
    row_shape = jax.ShapeDtypeStruct(q2.shape, BF16)
    near_shape = jax.ShapeDtypeStruct(k2.shape, F32)
    small_shape = jax.ShapeDtypeStruct(k2.shape, BF16)
    sum_scratch = [pltpu.VMEM((mine_blocks, 2, half, width), F32)]
    slot_sems = [pltpu.SemaphoreType.DMA((grp_count,))]
    limit = pltpu.CompilerParams(vmem_limit_bytes=24 * 1024 * 1024)
    vmem = pl.BlockSpec(memory_space=pltpu.VMEM)
    smem = pl.BlockSpec(memory_space=pltpu.SMEM)
    anywhere = pl.BlockSpec(memory_space=pltpu.HBM)

    def call(kernel, name, scalars, operands, out_shape, scratch=(), into=None, out_spec=vmem):
        extra = () if into is None else (into,)
        return pl.pallas_call(
            kernel,
            in_specs=[smem] * len(scalars) + [vmem] * len(operands) + [anywhere] * len(extra),
            out_specs=jax.tree.map(lambda _: out_spec, out_shape),
            out_shape=out_shape,
            scratch_shapes=scratch,
            input_output_aliases={len(scalars) + len(operands): 0} if extra else {},
            compiler_params=limit,
            name=name,
        )(*scalars, *operands, *extra)

    kept, given = call(
        partial(pack_kernel, kv_heads=kv_heads), "pack", (half_id,), (k2, v2),
        [part_shape, part_shape],
    )
    gotten = lax.ppermute(given, "uly", swap)
    outgoing = call(
        partial(outgoing_kernel, first=0), "send_own", (owner_first, sending), (kept,),
        slot_shape, slot_sems, out_spec=anywhere,
    )
    outgoing = call(
        partial(outgoing_kernel, first=mine_blocks), "send_sibling", (owner_first, sending),
        (gotten,), slot_shape, slot_sems, into=outgoing, out_spec=anywhere,
    )
    outgoing, given = lax.optimization_barrier((outgoing, given))
    arrived = lax.all_to_all(outgoing, "grp", split_axis=0, concat_axis=0, tiled=True)
    stats = call(
        partial(near_kernel, **sizes), "near", (half_id,), (q2, g2, kept, given), stat_shape
    )
    arrived, stats = lax.optimization_barrier((arrived, stats))
    other = lax.ppermute(take_rows(arrived, source_sib), "uly", swap)
    stats = call(
        partial(mid_kernel, **sizes), "mid", (source_own, seen_own), (q2, g2, stats, arrived),
        stat_shape,
    )
    far_other, stats = call(
        partial(far_kernel, **sizes), "far", (seen_own,), (q2, g2, stats, other),
        [part_shape, stat_shape],
    )
    from_sib = lax.ppermute(far_other, "uly", swap)
    returning = call(
        partial(mine_kernel, **sizes), "mine", (source_own, seen_own), (q2, g2, stats, arrived),
        slot_shape,
        [pltpu.VMEM(part_shape.shape, BF16), pltpu.SemaphoreType.DMA((mine_blocks,))],
        out_spec=anywhere,
    )
    returning = call(
        returning_kernel, "return_sibling", (source_sib,), (from_sib,), slot_shape,
        [pltpu.SemaphoreType.DMA((mine_blocks,))], into=returning, out_spec=anywhere,
    )
    returning, k2l = lax.optimization_barrier((returning, k2))
    landed = lax.all_to_all(returning, "grp", split_axis=0, concat_axis=0, tiled=True)

    def step_rows(i, *_):
        return (i, 0)

    def step_part(i, *_):
        return (i, 0, 0, 0)

    def from_source(i, source_ref, seen_ref):
        return (source_ref[i], 0, 0, 0)

    row_spec = pl.BlockSpec((rows, width), step_rows)
    col_spec = pl.BlockSpec((cols, width), step_rows)
    attended, dq, dk_near, dv_near = pl.pallas_call(
        partial(local_kernel, **sizes),
        grid_spec=pltpu.PrefetchScalarGridSpec(
            num_scalar_prefetch=2,
            grid=(mine_blocks,),
            in_specs=[
                row_spec, row_spec, col_spec, col_spec,
                pl.BlockSpec((1, 2, half, width), from_source),
                pl.BlockSpec((1, 2, half, width), step_part),
            ],
            out_specs=[row_spec, row_spec, col_spec, col_spec],
            scratch_shapes=[pltpu.VMEM((rows, 2 * cols), F32)],
        ),
        out_shape=[row_shape, row_shape, near_shape, near_shape],
        compiler_params=limit,
        name="local",
    )(source_own, seen_own, q2, g2, k2l, v2, arrived, other)
    landed, dk_near = lax.optimization_barrier((landed, dk_near))
    give = call(
        partial(landing_kernel, first=mine_blocks), "land_sibling", (owner_first, sending),
        (landed,), part_shape, sum_scratch,
    )
    back = lax.ppermute(give, "uly", swap)
    own = call(
        partial(landing_kernel, first=0), "land_own", (owner_first, sending), (landed,),
        jax.ShapeDtypeStruct(part_shape.shape, F32), sum_scratch,
    )
    dk, dv = call(
        partial(finish_kernel, kv_heads=kv_heads), "finish", (half_id,),
        (dk_near, dv_near, own, back), [small_shape, small_shape],
    )
    return (
        attended.reshape(queries.shape), dq.reshape(queries.shape),
        dk.reshape(keys.shape), dv.reshape(keys.shape),
    )


def on_device(queries, keys, values, output_cotangent, block_lists, list_counts):
    uly_count = lax.axis_size("uly")
    grp_count = lax.axis_size("grp")
    blocks_all, remote = block_lists.shape
    block_tok = queries.shape[0] * uly_count * grp_count // blocks_all
    held_whole = queries.shape[0] % block_tok == 0
    run = whole_blocks if held_whole and remote == 1 and uly_count == 2 else spread_blocks
    return run(queries, keys, values, output_cotangent, block_lists, list_counts)


def solution(mesh):
    placed = (
        P(("grp", "uly"), None, None),
        P(("grp", "uly"), None, None),
        P(("grp", "uly"), None, None),
        P(("grp", "uly"), None, None),
        P(),
        P(),
    )
    return jax.shard_map(
        on_device,
        mesh=mesh,
        in_specs=placed,
        out_specs=(
            P(("grp", "uly"), None, None),
            P(("grp", "uly"), None, None),
            P(("grp", "uly"), None, None),
            P(("grp", "uly"), None, None),
        ),
        check_vma=False,
    )
```

```python
from functools import partial

import jax
import jax.numpy as jnp
from jax import lax
from jax.experimental import pallas as pl
from jax.experimental.pallas import tpu as pltpu
from jax.sharding import PartitionSpec as P


def spread_blocks(queries, keys, values, output_cotangent, block_lists, list_counts):
    uly_count = lax.axis_size("uly")
    grp_count = lax.axis_size("grp")
    my_group = lax.axis_index("grp")
    tokens, head_count, head_width = queries.shape
    kv_heads = keys.shape[1]
    copies = max(1, uly_count // kv_heads)
    blocks_all, remote = block_lists.shape
    per_group = blocks_all // grp_count
    block_tok = tokens * uly_count // per_group
    group_tok = tokens * uly_count
    score_scale = head_width ** (-0.5)
    lists = block_lists.reshape(grp_count, per_group, remote)
    counted = (jnp.arange(remote)[None, :] < list_counts[:, None]).reshape(
        grp_count, per_group, remote
    )
    wanted = (lists // per_group == my_group) & counted
    send_place = jnp.sum(jnp.where(wanted, lists % per_group, 0), axis=(1, 2))
    sending = jnp.any(wanted, axis=(1, 2))
    mine_source = lax.dynamic_index_in_dim(lists, my_group, 0, keepdims=False) // per_group
    mine_counted = lax.dynamic_index_in_dim(counted, my_group, 0, keepdims=False)
    trip_count = jnp.max(jnp.sum(mine_counted.astype(jnp.int32), axis=1))

    def to_blocks(array_in):
        return array_in.reshape((per_group, block_tok) + array_in.shape[1:])

    keys_wide = jnp.repeat(keys, copies, axis=1)
    values_wide = jnp.repeat(values, copies, axis=1)
    query_heads, grad_heads, key_heads, value_heads = (
        lax.all_to_all(queries, "uly", split_axis=1, concat_axis=0, tiled=True),
        lax.all_to_all(output_cotangent, "uly", split_axis=1, concat_axis=0, tiled=True),
        lax.all_to_all(keys_wide, "uly", split_axis=1, concat_axis=0, tiled=True),
        lax.all_to_all(values_wide, "uly", split_axis=1, concat_axis=0, tiled=True),
    )
    stacked = jnp.stack([to_blocks(key_heads), to_blocks(value_heads)])
    outgoing = jnp.take(stacked, send_place, axis=1)
    arrived = lax.all_to_all(outgoing, "grp", split_axis=1, concat_axis=1, tiled=True)
    kv_local = key_heads.shape[1]
    heads_local = query_heads.shape[1]
    heads_per_group = heads_local // kv_local
    query_blk = query_heads.reshape(per_group, block_tok, kv_local, heads_per_group, head_width)
    grad_blk = grad_heads.reshape(per_group, block_tok, kv_local, heads_per_group, head_width)
    key_blk = to_blocks(key_heads)
    value_blk = to_blocks(value_heads)
    far_keys = arrived[0]
    far_values = arrived[1]
    causal = jnp.arange(block_tok)[:, None] >= jnp.arange(block_tok)[None, :]

    def logits(key_rows):
        return (
            jnp.einsum("pqkgd,pjkd->pkgqj", query_blk, key_rows, preferred_element_type=jnp.float32)
            * score_scale
        )

    def slot_rows(slot_index):
        source = lax.dynamic_index_in_dim(mine_source, slot_index, 1, keepdims=False)
        counted_slot = lax.dynamic_index_in_dim(mine_counted, slot_index, 1, keepdims=False)
        return (
            jnp.take(far_keys, source, axis=0),
            jnp.take(far_values, source, axis=0),
            counted_slot,
            source,
        )

    def masked(scores, counted_slot):
        return jnp.where(counted_slot[:, None, None, None, None], scores, -jnp.inf)

    near_scores = jnp.where(causal, logits(key_blk), -jnp.inf)
    highest = jnp.max(near_scores, axis=-1)
    denominator = jnp.sum(jnp.exp(near_scores - highest[..., None]), axis=-1)

    def max_sweep(slot_index, state_pair):
        highest, denominator = state_pair
        key_rows, value_rows, counted_slot, source = slot_rows(slot_index)
        scores = masked(logits(key_rows), counted_slot)
        new_highest = jnp.maximum(highest, jnp.max(scores, axis=-1))
        denominator = denominator * jnp.exp(highest - new_highest) + jnp.sum(
            jnp.exp(scores - new_highest[..., None]), axis=-1
        )
        return (new_highest, denominator)

    highest, denominator = lax.fori_loop(0, trip_count, max_sweep, (highest, denominator))
    log_total = highest + jnp.log(denominator)

    def softmax_weights(scores):
        return jnp.exp(scores - log_total[..., None])

    summed = jnp.einsum(
        "pkgqj,pjkd->pqkgd",
        softmax_weights(near_scores).astype(jnp.bfloat16),
        value_blk,
        preferred_element_type=jnp.float32,
    )

    def value_sweep(slot_index, summed):
        key_rows, value_rows, counted_slot, source = slot_rows(slot_index)
        weights = softmax_weights(masked(logits(key_rows), counted_slot)).astype(jnp.bfloat16)
        return summed + jnp.einsum(
            "pkgqj,pjkd->pqkgd", weights, value_rows, preferred_element_type=jnp.float32
        )

    summed = lax.fori_loop(0, trip_count, value_sweep, summed)
    attended_blk = summed.astype(jnp.bfloat16)
    row_delta = jnp.transpose(
        jnp.sum(grad_blk.astype(jnp.float32) * attended_blk.astype(jnp.float32), axis=-1),
        (0, 2, 3, 1),
    )

    def backward(scores, key_rows, value_rows):
        probs = softmax_weights(scores)
        weights = probs.astype(jnp.bfloat16)
        dprobs = jnp.einsum(
            "pqkgd,pjkd->pkgqj", grad_blk, value_rows, preferred_element_type=jnp.float32
        )
        dscores = (probs * (dprobs - row_delta[..., None])).astype(jnp.bfloat16)
        query_term = jnp.einsum(
            "pkgqj,pjkd->pqkgd", dscores, key_rows, preferred_element_type=jnp.float32
        )
        key_term = (
            jnp.einsum("pkgqj,pqkgd->pjkd", dscores, query_blk, preferred_element_type=jnp.float32)
            * score_scale
        )
        value_term = jnp.einsum(
            "pkgqj,pqkgd->pjkd", weights, grad_blk, preferred_element_type=jnp.float32
        )
        return (query_term, key_term, value_term)

    query_sum, key_near, value_near = backward(near_scores, key_blk, value_blk)
    far_grads = jnp.zeros((2, grp_count, block_tok, kv_local, head_width), jnp.float32)

    def grad_sweep(slot_index, state_pair):
        query_sum, far_grads = state_pair
        key_rows, value_rows, counted_slot, source = slot_rows(slot_index)
        query_term, key_term, value_term = backward(
            masked(logits(key_rows), counted_slot), key_rows, value_rows
        )
        routing = (
            (source[:, None] == jnp.arange(grp_count)[None, :]) & counted_slot[:, None]
        ).astype(jnp.float32)
        routed = jnp.einsum(
            "ps,xpjkd->xsjkd",
            routing,
            jnp.stack([key_term, value_term]),
            precision=lax.Precision.HIGHEST,
        )
        return (query_sum + query_term, far_grads + routed)

    query_sum, far_grads = lax.fori_loop(0, trip_count, grad_sweep, (query_sum, far_grads))
    owners = ((send_place[:, None] == jnp.arange(per_group)[None, :]) & sending[:, None]).astype(
        jnp.float32
    )
    returned = lax.all_to_all(far_grads, "grp", split_axis=1, concat_axis=1, tiled=True)
    landed = jnp.einsum("sp,xsjkd->xpjkd", owners, returned, precision=lax.Precision.HIGHEST)
    key_local = (key_near + landed[0]).reshape(group_tok, kv_local, head_width)
    value_local = (value_near + landed[1]).reshape(group_tok, kv_local, head_width)
    attended_rows = attended_blk.reshape(group_tok, heads_local, head_width)
    query_rows = (
        (query_sum * score_scale).astype(jnp.bfloat16).reshape(group_tok, heads_local, head_width)
    )
    attended, query_grad = (
        lax.all_to_all(attended_rows, "uly", split_axis=0, concat_axis=1, tiled=True),
        lax.all_to_all(query_rows, "uly", split_axis=0, concat_axis=1, tiled=True),
    )
    key_parts, value_parts = (
        lax.all_to_all(key_local, "uly", split_axis=0, concat_axis=1, tiled=True),
        lax.all_to_all(value_local, "uly", split_axis=0, concat_axis=1, tiled=True),
    )
    key_gradient = jnp.sum(key_parts.reshape(tokens, kv_heads, copies, head_width), axis=2).astype(
        jnp.bfloat16
    )
    value_gradient = jnp.sum(
        value_parts.reshape(tokens, kv_heads, copies, head_width), axis=2
    ).astype(jnp.bfloat16)
    return (attended, query_grad, key_gradient, value_gradient)


HIDDEN = -1e30
LAST = (((1,), (1,)), ((), ()))
FIRST = (((0,), (0,)), ((), ()))
F32 = jnp.float32
BF16 = jnp.bfloat16


def dot_last(left, right):
    return lax.dot_general(left, right, LAST, preferred_element_type=F32)


def dot_first(left, right):
    return lax.dot_general(left, right, FIRST, preferred_element_type=F32)


def head_major(cols, kv_heads):
    half = cols // 2
    place = half // kv_heads
    row = lax.broadcasted_iota(jnp.int32, (cols, cols), 0)
    col = lax.broadcasted_iota(jnp.int32, (cols, cols), 1)
    token = row // half * place + row % place
    return jnp.where(col == token * kv_heads + row % half // place, 1.0, 0.0).astype(BF16)


def reorder(one_hot, array):
    return jnp.dot(one_hot, array, preferred_element_type=F32).astype(BF16)


def own_head(scores, lane_head, kv_heads):
    place = scores.shape[0] // kv_heads
    kept = scores[:place]
    for head in range(1, kv_heads):
        kept = jnp.where(lane_head == head, scores[head * place:(head + 1) * place], kept)
    return kept


def all_heads(kept, lane_head, kv_heads):
    none = jnp.zeros_like(kept)
    return jnp.concatenate(
        [jnp.where(lane_head == head, kept, none) for head in range(kv_heads)], axis=0
    )


def lanes(rows, heads, kv_heads):
    lane = lax.broadcasted_iota(jnp.int32, (1, rows), 1)
    return lane // heads, lane % heads // (heads // kv_heads)


def plan_spans(grp_count, blocks):
    return grp_count, 2 * grp_count, 2 * grp_count + blocks, 2 * grp_count + 2 * blocks


def pack_kernel(
    where_ref, lists_ref, counts_ref, k_hbm, v_hbm, plan_ref, kept_ref, given_ref,
    k_ref, v_ref, sems, *, grp_count, kv_heads
):
    blocks, _, half, _ = kept_ref.shape
    copies = [
        pltpu.make_async_copy(k_hbm, k_ref, sems.at[0]),
        pltpu.make_async_copy(v_hbm, v_ref, sems.at[1]),
    ]
    for copy in copies:
        copy.start()
    group, mine = where_ref[0], where_ref[1]
    per_group = 2 * blocks
    low = group * per_group
    sib_at, source_at, give_at, seen_at = plan_spans(grp_count, blocks)
    for other in range(grp_count):
        place = jnp.int32(-1)
        for at in range(other * per_group, (other + 1) * per_group):
            here = lists_ref[at] - low
            wanted = (here >= 0) & (here < per_group) & (counts_ref[at] > 0)
            place = jnp.where(wanted, here, place)
        own = place - mine * blocks
        sib = place - (1 - mine) * blocks
        plan_ref[other] = jnp.where((own >= 0) & (own < blocks), own, -1)
        plan_ref[sib_at + other] = jnp.where((sib >= 0) & (sib < blocks), sib, -1)
    for block in range(blocks):
        at = low + mine * blocks + block
        plan_ref[source_at + block] = lax.div(lists_ref[at], per_group)
        plan_ref[seen_at + block] = counts_ref[at]
        at = low + (1 - mine) * blocks + block
        plan_ref[give_at + block] = lax.div(lists_ref[at], per_group)
    for copy in copies:
        copy.wait()
    first = mine == 0
    order = head_major(2 * half, kv_heads)
    for block in range(blocks):
        for which, ref in enumerate((k_ref, v_ref)):
            ordered = reorder(order, ref[block * 2 * half:(block + 1) * 2 * half])
            kept_ref[block, which] = jnp.where(first, ordered[:half], ordered[half:])
            given_ref[block, which] = jnp.where(first, ordered[half:], ordered[:half])


def outgoing_kernel(plan_ref, blocks_ref, *refs, first):
    out_ref, sems = refs[-2:]
    copies = []
    for group in range(out_ref.shape[0]):
        place = plan_ref[first + group]
        source = blocks_ref.at[jnp.maximum(place, 0)]
        copy = pltpu.make_async_copy(source, out_ref.at[group], sems.at[group])
        copies.append((place >= 0, copy))
    for wanted, copy in copies:
        pl.when(wanted)(copy.start)
    for wanted, copy in copies:
        pl.when(wanted)(copy.wait)


def returning_kernel(plan_ref, blocks_ref, _, out_ref, sems, *, give_at):
    copies = [
        pltpu.make_async_copy(blocks_ref.at[block], out_ref.at[plan_ref[give_at + block]], sems.at[block])
        for block in range(blocks_ref.shape[0])
    ]
    for copy in copies:
        copy.start()
    for copy in copies:
        copy.wait()


def near_kernel(
    where_ref, q_ref, g_ref, kept_ref, given_ref, stat_ref, *, heads, kv_heads, score_scale
):
    blocks = stat_ref.shape[0]
    rows = q_ref.shape[0] // blocks
    place = kept_ref.shape[2] // kv_heads
    token, lane_head = lanes(rows, heads, kv_heads)
    key = lax.broadcasted_iota(jnp.int32, (2 * place, rows), 0)
    part = jnp.where(key < place, where_ref[1], 1 - where_ref[1])
    causal = key % place + part * place <= token
    for block in range(blocks):
        span = slice(block * rows, (block + 1) * rows)
        pieces = []
        for which, ref in enumerate((q_ref, g_ref)):
            both = jnp.concatenate([kept_ref[block, which], given_ref[block, which]], axis=0)
            full = dot_last(both, ref[span])
            half = full.shape[0] // 2
            pieces.append(
                jnp.concatenate(
                    [
                        own_head(full[:half], lane_head, kv_heads),
                        own_head(full[half:], lane_head, kv_heads),
                    ],
                    axis=0,
                )
            )
        scores = jnp.where(causal, pieces[0] * score_scale, HIDDEN)
        highest = jnp.max(scores, axis=0, keepdims=True)
        raised = jnp.exp(scores - highest)
        stat_ref[block, 0:1] = highest
        stat_ref[block, 1:2] = jnp.sum(raised, axis=0, keepdims=True)
        stat_ref[block, 2:3] = jnp.sum(raised * pieces[1], axis=0, keepdims=True)


def far_scores(part_ref, at, q, g, seen, lane_head, kv_heads, score_scale):
    hidden = jnp.where(seen > 0, 0.0, HIDDEN)
    scores = own_head(dot_last(part_ref[at, 0], q), lane_head, kv_heads) * score_scale + hidden
    return scores, own_head(dot_last(part_ref[at, 1], g), lane_head, kv_heads)


def merged(stat_ref, block, scores, dprobs):
    before = stat_ref[block, 0:1]
    highest = jnp.maximum(before, jnp.max(scores, axis=0, keepdims=True))
    raised = jnp.exp(scores - highest)
    shrink = jnp.exp(before - highest)
    total = shrink * stat_ref[block, 1:2] + jnp.sum(raised, axis=0, keepdims=True)
    delta = shrink * stat_ref[block, 2:3] + jnp.sum(raised * dprobs, axis=0, keepdims=True)
    return highest, raised, total, delta


def far_gradients(probs, dprobs, delta, q, g, lane_head, kv_heads, score_scale):
    dscores = (probs * (dprobs - delta)).astype(BF16)
    dk = jnp.dot(all_heads(dscores, lane_head, kv_heads), q, preferred_element_type=F32)
    dv = jnp.dot(all_heads(probs.astype(BF16), lane_head, kv_heads), g, preferred_element_type=F32)
    return (dk * score_scale).astype(BF16), dv.astype(BF16)


def mid_kernel(
    plan_ref, q_ref, g_ref, stat_ref, arrived_ref, out_ref,
    *, heads, kv_heads, score_scale, source_at, seen_at
):
    blocks = stat_ref.shape[0]
    rows = q_ref.shape[0] // blocks
    _, lane_head = lanes(rows, heads, kv_heads)
    for block in range(blocks):
        span = slice(block * rows, (block + 1) * rows)
        scores, dprobs = far_scores(
            arrived_ref, plan_ref[source_at + block], q_ref[span], g_ref[span],
            plan_ref[seen_at + block],            lane_head, kv_heads, score_scale,
        )
        highest, _, total, delta = merged(stat_ref, block, scores, dprobs)
        out_ref[block, 0:1] = highest
        out_ref[block, 1:2] = total
        out_ref[block, 2:3] = delta


def far_kernel(
    plan_ref, q_ref, g_ref, stat_ref, other_ref, grad_ref, out_ref,
    *, heads, kv_heads, score_scale, seen_at
):
    blocks = stat_ref.shape[0]
    rows = q_ref.shape[0] // blocks
    _, lane_head = lanes(rows, heads, kv_heads)
    for block in range(blocks):
        span = slice(block * rows, (block + 1) * rows)
        q = q_ref[span]
        g = g_ref[span]
        scores, dprobs = far_scores(
            other_ref, block, q, g, plan_ref[seen_at + block], lane_head, kv_heads, score_scale
        )
        highest, raised, total, delta = merged(stat_ref, block, scores, dprobs)
        inverse = 1.0 / total
        delta = delta * inverse
        grad_ref[block, 0], grad_ref[block, 1] = far_gradients(
            raised * inverse, dprobs, delta, q, g, lane_head, kv_heads, score_scale
        )
        out_ref[block, 0:1] = highest
        out_ref[block, 1:2] = inverse
        out_ref[block, 2:3] = delta


def mine_kernel(
    plan_ref, q_ref, g_ref, stat_ref, arrived_ref, out_ref, grad_ref, sems,
    *, heads, kv_heads, score_scale, source_at, seen_at
):
    blocks = stat_ref.shape[0]
    rows = q_ref.shape[0] // blocks
    _, lane_head = lanes(rows, heads, kv_heads)
    copies = []
    for block in range(blocks):
        span = slice(block * rows, (block + 1) * rows)
        q = q_ref[span]
        g = g_ref[span]
        source = plan_ref[source_at + block]
        scores, dprobs = far_scores(
            arrived_ref, source, q, g, plan_ref[seen_at + block], lane_head, kv_heads, score_scale
        )
        probs = jnp.exp(scores - stat_ref[block, 0:1]) * stat_ref[block, 1:2]
        grad_ref[block, 0], grad_ref[block, 1] = far_gradients(
            probs, dprobs, stat_ref[block, 2:3], q, g, lane_head, kv_heads, score_scale
        )
        copies.append(
            pltpu.make_async_copy(grad_ref.at[block], out_ref.at[source], sems.at[block])
        )
        copies[-1].start()
    for copy in copies:
        copy.wait()


def local_kernel(
    plan_ref, q_ref, g_ref, k_ref, v_ref, mine_ref, other_ref,
    att_ref, dq_ref, dk_ref, dv_ref, bias_ref, *, heads, kv_heads, score_scale, seen_at
):
    step = pl.program_id(0)
    rows = q_ref.shape[0]
    cols = k_ref.shape[0]

    @pl.when(step == 0)
    def _():
        half = cols // 2
        place = half // kv_heads
        row = lax.broadcasted_iota(jnp.int32, (rows, cols), 0)
        col = lax.broadcasted_iota(jnp.int32, (rows, cols), 1)
        same = row % heads // (heads // kv_heads) == col % half // place
        causal = col // half * place + col % place <= row // heads
        bias_ref[:, :cols] = jnp.where(same & causal, 0.0, HIDDEN)
        bias_ref[:, cols:] = jnp.where(same, 0.0, HIDDEN)

    far_bias = jnp.where(plan_ref[seen_at + step] > 0, 0.0, HIDDEN)
    order = head_major(cols, kv_heads)
    k_near = reorder(order, k_ref[...])
    v_near = reorder(order, v_ref[...])
    k_all = jnp.concatenate([k_near, mine_ref[0, 0], other_ref[0, 0]], axis=0)
    v_all = jnp.concatenate([v_near, mine_ref[0, 1], other_ref[0, 1]], axis=0)
    q = q_ref[...]
    g = g_ref[...]
    scores = dot_last(q, k_all) * score_scale + bias_ref[...]
    scores = jnp.concatenate([scores[:, :cols], scores[:, cols:] + far_bias], axis=1)
    highest = jnp.max(scores, axis=1, keepdims=True)
    raised = jnp.exp(scores - highest)
    total = jnp.sum(raised, axis=1, keepdims=True)
    probs = raised * (1.0 / total)
    weights = probs.astype(BF16)
    attended = jnp.dot(weights, v_all, preferred_element_type=F32).astype(BF16)
    att_ref[...] = attended
    delta = jnp.sum(g.astype(F32) * attended.astype(F32), axis=1, keepdims=True)
    dscores = (probs * (dot_last(g, v_all) - delta)).astype(BF16)
    dq = jnp.dot(dscores, k_all, preferred_element_type=F32) * score_scale
    dq_ref[...] = dq.astype(BF16)
    dk_ref[...] = dot_first(dscores[:, :cols], q) * score_scale
    dv_ref[...] = dot_first(weights[:, :cols], g)


def landing_kernel(plan_ref, landed_ref, out_ref, sum_ref, *, first):
    sum_ref[...] = jnp.zeros_like(sum_ref)
    for group in range(landed_ref.shape[0]):
        place = plan_ref[first + group]

        @pl.when(place >= 0)
        def _():
            sum_ref[place] = sum_ref[place] + landed_ref[group].astype(F32)

    out_ref[...] = sum_ref[...].astype(out_ref.dtype)


def finish_kernel(
    where_ref, dk_near_ref, dv_near_ref, own_ref, back_ref, dk_ref, dv_ref, *, kv_heads
):
    blocks, _, half, _ = back_ref.shape
    mine = where_ref[1] == 0
    order = head_major(2 * half, kv_heads)
    for block in range(blocks):
        span = slice(block * 2 * half, (block + 1) * 2 * half)
        for near_ref, out_ref, which in ((dk_near_ref, dk_ref, 0), (dv_near_ref, dv_ref, 1)):
            own = own_ref[block, which]
            back = back_ref[block, which].astype(F32)
            far = jnp.concatenate([jnp.where(mine, own, back), jnp.where(mine, back, own)], axis=0)
            summed = (near_ref[span] + far).astype(BF16)
            out_ref[span] = dot_first(order, summed).astype(BF16)


def take_rows(array, index):
    return array.at[index].get(mode="promise_in_bounds")


def whole_blocks(queries, keys, values, output_cotangent, block_lists, list_counts):
    grp_count = lax.axis_size("grp")
    uly_count = lax.axis_size("uly")
    my_group = lax.axis_index("grp")
    my_half = lax.axis_index("uly")
    tokens, heads, width = queries.shape
    kv_heads = keys.shape[1]
    per_group = block_lists.shape[0] // grp_count
    block_tok = tokens * uly_count // per_group
    mine_blocks = tokens // block_tok
    rows = block_tok * heads
    cols = block_tok * kv_heads
    half = cols // 2
    sizes = dict(heads=heads, kv_heads=kv_heads, score_scale=width ** (-0.5))
    swap = [(0, 1), (1, 0)]

    where = jnp.stack([my_group, my_half]).astype(jnp.int32)
    sib_at, source_at, give_at, seen_at = plan_spans(grp_count, mine_blocks)

    q2 = queries.reshape(tokens * heads, width)
    g2 = output_cotangent.reshape(tokens * heads, width)
    k2 = keys.reshape(tokens * kv_heads, width)
    v2 = values.reshape(tokens * kv_heads, width)

    part_shape = jax.ShapeDtypeStruct((mine_blocks, 2, half, width), BF16)
    slot_shape = pltpu.HBM((grp_count, 2, half, width), BF16)
    stat_shape = jax.ShapeDtypeStruct((mine_blocks, 8, rows), F32)
    row_shape = jax.ShapeDtypeStruct(q2.shape, BF16)
    near_shape = jax.ShapeDtypeStruct(k2.shape, F32)
    small_shape = jax.ShapeDtypeStruct(k2.shape, BF16)
    sum_scratch = [pltpu.VMEM((mine_blocks, 2, half, width), F32)]
    slot_sems = [pltpu.SemaphoreType.DMA((grp_count,))]
    limit = pltpu.CompilerParams(vmem_limit_bytes=24 * 1024 * 1024)
    vmem = pl.BlockSpec(memory_space=pltpu.VMEM)
    smem = pl.BlockSpec(memory_space=pltpu.SMEM)
    anywhere = pl.BlockSpec(memory_space=pltpu.HBM)

    def call(kernel, name, scalars, operands, out_shape, scratch=(), into=None, out_spec=vmem):
        extra = () if into is None else (into,)
        return pl.pallas_call(
            kernel,
            in_specs=[smem] * len(scalars) + [vmem] * len(operands) + [anywhere] * len(extra),
            out_specs=jax.tree.map(lambda _: out_spec, out_shape),
            out_shape=out_shape,
            scratch_shapes=scratch,
            input_output_aliases={len(scalars) + len(operands): 0} if extra else {},
            compiler_params=limit,
            name=name,
        )(*scalars, *operands, *extra)

    plan, kept, given = pl.pallas_call(
        partial(pack_kernel, grp_count=grp_count, kv_heads=kv_heads),
        in_specs=[smem, smem, smem, anywhere, anywhere],
        out_specs=[smem, vmem, vmem],
        out_shape=[
            jax.ShapeDtypeStruct((seen_at + mine_blocks,), jnp.int32), part_shape, part_shape
        ],
        scratch_shapes=[
            pltpu.VMEM(k2.shape, BF16), pltpu.VMEM(k2.shape, BF16), pltpu.SemaphoreType.DMA((2,))
        ],
        compiler_params=limit,
        name="pack",
    )(
        where,
        pltpu.with_memory_space_constraint(block_lists.reshape(-1), pltpu.HBM),
        pltpu.with_memory_space_constraint(list_counts, pltpu.HBM),
        pltpu.with_memory_space_constraint(k2, pltpu.HBM),
        pltpu.with_memory_space_constraint(v2, pltpu.HBM),
    )
    gotten = lax.ppermute(given, "uly", swap)
    outgoing = call(
        partial(outgoing_kernel, first=0), "send_own", (plan,), (kept,),
        slot_shape, slot_sems, out_spec=anywhere,
    )
    outgoing = call(
        partial(outgoing_kernel, first=sib_at), "send_sibling", (plan,), (gotten,),
        slot_shape, slot_sems, into=outgoing, out_spec=anywhere,
    )
    outgoing, given = lax.optimization_barrier((outgoing, given))
    arrived = lax.all_to_all(outgoing, "grp", split_axis=0, concat_axis=0, tiled=True)
    stats = call(
        partial(near_kernel, **sizes), "near", (where,), (q2, g2, kept, given), stat_shape
    )
    arrived, stats = lax.optimization_barrier((arrived, stats))
    give_rows = plan[give_at:give_at + mine_blocks]
    other = lax.ppermute(take_rows(arrived, give_rows), "uly", swap)
    stats = call(
        partial(mid_kernel, source_at=source_at, seen_at=seen_at, **sizes), "mid", (plan,),
        (q2, g2, stats, arrived), stat_shape,
    )
    far_other, stats = call(
        partial(far_kernel, seen_at=seen_at, **sizes), "far", (plan,), (q2, g2, stats, other),
        [part_shape, stat_shape],
    )
    from_sib = lax.ppermute(far_other, "uly", swap)
    returning = call(
        partial(mine_kernel, source_at=source_at, seen_at=seen_at, **sizes), "mine", (plan,),
        (q2, g2, stats, arrived), slot_shape,
        [pltpu.VMEM(part_shape.shape, BF16), pltpu.SemaphoreType.DMA((mine_blocks,))],
        out_spec=anywhere,
    )
    returning = call(
        partial(returning_kernel, give_at=give_at), "return_sibling", (plan,), (from_sib,), slot_shape,
        [pltpu.SemaphoreType.DMA((mine_blocks,))], into=returning, out_spec=anywhere,
    )
    returning, k2l = lax.optimization_barrier((returning, k2))
    landed = lax.all_to_all(returning, "grp", split_axis=0, concat_axis=0, tiled=True)

    def step_rows(i, *_):
        return (i, 0)

    def step_part(i, *_):
        return (i, 0, 0, 0)

    def from_source(i, plan_ref):
        return (plan_ref[source_at + i], 0, 0, 0)

    row_spec = pl.BlockSpec((rows, width), step_rows)
    col_spec = pl.BlockSpec((cols, width), step_rows)
    attended, dq, dk_near, dv_near = pl.pallas_call(
        partial(local_kernel, seen_at=seen_at, **sizes),
        grid_spec=pltpu.PrefetchScalarGridSpec(
            num_scalar_prefetch=1,
            grid=(mine_blocks,),
            in_specs=[
                row_spec, row_spec, col_spec, col_spec,
                pl.BlockSpec((1, 2, half, width), from_source),
                pl.BlockSpec((1, 2, half, width), step_part),
            ],
            out_specs=[row_spec, row_spec, col_spec, col_spec],
            scratch_shapes=[pltpu.VMEM((rows, 2 * cols), F32)],
        ),
        out_shape=[row_shape, row_shape, near_shape, near_shape],
        compiler_params=limit,
        name="local",
    )(plan, q2, g2, k2l, v2, arrived, other)
    landed, dk_near = lax.optimization_barrier((landed, dk_near))
    give = call(
        partial(landing_kernel, first=sib_at), "land_sibling", (plan,), (landed,), part_shape,
        sum_scratch,
    )
    back = lax.ppermute(give, "uly", swap)
    own = call(
        partial(landing_kernel, first=0), "land_own", (plan,), (landed,),
        jax.ShapeDtypeStruct(part_shape.shape, F32), sum_scratch,
    )
    dk, dv = call(
        partial(finish_kernel, kv_heads=kv_heads), "finish", (where,),
        (dk_near, dv_near, own, back), [small_shape, small_shape],
    )
    return (
        attended.reshape(queries.shape), dq.reshape(queries.shape),
        dk.reshape(keys.shape), dv.reshape(keys.shape),
    )


def on_device(queries, keys, values, output_cotangent, block_lists, list_counts):
    uly_count = lax.axis_size("uly")
    grp_count = lax.axis_size("grp")
    blocks_all, remote = block_lists.shape
    block_tok = queries.shape[0] * uly_count * grp_count // blocks_all
    held_whole = queries.shape[0] % block_tok == 0
    run = whole_blocks if held_whole and remote == 1 and uly_count == 2 else spread_blocks
    return run(queries, keys, values, output_cotangent, block_lists, list_counts)


def solution(mesh):
    placed = (
        P(("grp", "uly"), None, None),
        P(("grp", "uly"), None, None),
        P(("grp", "uly"), None, None),
        P(("grp", "uly"), None, None),
        P(),
        P(),
    )
    return jax.shard_map(
        on_device,
        mesh=mesh,
        in_specs=placed,
        out_specs=(
            P(("grp", "uly"), None, None),
            P(("grp", "uly"), None, None),
            P(("grp", "uly"), None, None),
            P(("grp", "uly"), None, None),
        ),
        check_vma=False,
    )
```

```python
from functools import partial

import jax
import jax.numpy as jnp
from jax import lax
from jax.experimental import pallas as pl
from jax.experimental.pallas import tpu as pltpu
from jax.sharding import PartitionSpec as P


def spread_blocks(queries, keys, values, output_cotangent, block_lists, list_counts):
    uly_count = lax.axis_size("uly")
    grp_count = lax.axis_size("grp")
    my_group = lax.axis_index("grp")
    tokens, head_count, head_width = queries.shape
    kv_heads = keys.shape[1]
    copies = max(1, uly_count // kv_heads)
    blocks_all, remote = block_lists.shape
    per_group = blocks_all // grp_count
    block_tok = tokens * uly_count // per_group
    group_tok = tokens * uly_count
    score_scale = head_width ** (-0.5)
    lists = block_lists.reshape(grp_count, per_group, remote)
    counted = (jnp.arange(remote)[None, :] < list_counts[:, None]).reshape(
        grp_count, per_group, remote
    )
    wanted = (lists // per_group == my_group) & counted
    send_place = jnp.sum(jnp.where(wanted, lists % per_group, 0), axis=(1, 2))
    sending = jnp.any(wanted, axis=(1, 2))
    mine_source = lax.dynamic_index_in_dim(lists, my_group, 0, keepdims=False) // per_group
    mine_counted = lax.dynamic_index_in_dim(counted, my_group, 0, keepdims=False)
    trip_count = jnp.max(jnp.sum(mine_counted.astype(jnp.int32), axis=1))

    def to_blocks(array_in):
        return array_in.reshape((per_group, block_tok) + array_in.shape[1:])

    keys_wide = jnp.repeat(keys, copies, axis=1)
    values_wide = jnp.repeat(values, copies, axis=1)
    query_heads, grad_heads, key_heads, value_heads = (
        lax.all_to_all(queries, "uly", split_axis=1, concat_axis=0, tiled=True),
        lax.all_to_all(output_cotangent, "uly", split_axis=1, concat_axis=0, tiled=True),
        lax.all_to_all(keys_wide, "uly", split_axis=1, concat_axis=0, tiled=True),
        lax.all_to_all(values_wide, "uly", split_axis=1, concat_axis=0, tiled=True),
    )
    stacked = jnp.stack([to_blocks(key_heads), to_blocks(value_heads)])
    outgoing = jnp.take(stacked, send_place, axis=1)
    arrived = lax.all_to_all(outgoing, "grp", split_axis=1, concat_axis=1, tiled=True)
    kv_local = key_heads.shape[1]
    heads_local = query_heads.shape[1]
    heads_per_group = heads_local // kv_local
    query_blk = query_heads.reshape(per_group, block_tok, kv_local, heads_per_group, head_width)
    grad_blk = grad_heads.reshape(per_group, block_tok, kv_local, heads_per_group, head_width)
    key_blk = to_blocks(key_heads)
    value_blk = to_blocks(value_heads)
    far_keys = arrived[0]
    far_values = arrived[1]
    causal = jnp.arange(block_tok)[:, None] >= jnp.arange(block_tok)[None, :]

    def logits(key_rows):
        return (
            jnp.einsum("pqkgd,pjkd->pkgqj", query_blk, key_rows, preferred_element_type=jnp.float32)
            * score_scale
        )

    def slot_rows(slot_index):
        source = lax.dynamic_index_in_dim(mine_source, slot_index, 1, keepdims=False)
        counted_slot = lax.dynamic_index_in_dim(mine_counted, slot_index, 1, keepdims=False)
        return (
            jnp.take(far_keys, source, axis=0),
            jnp.take(far_values, source, axis=0),
            counted_slot,
            source,
        )

    def masked(scores, counted_slot):
        return jnp.where(counted_slot[:, None, None, None, None], scores, -jnp.inf)

    near_scores = jnp.where(causal, logits(key_blk), -jnp.inf)
    highest = jnp.max(near_scores, axis=-1)
    denominator = jnp.sum(jnp.exp(near_scores - highest[..., None]), axis=-1)

    def max_sweep(slot_index, state_pair):
        highest, denominator = state_pair
        key_rows, value_rows, counted_slot, source = slot_rows(slot_index)
        scores = masked(logits(key_rows), counted_slot)
        new_highest = jnp.maximum(highest, jnp.max(scores, axis=-1))
        denominator = denominator * jnp.exp(highest - new_highest) + jnp.sum(
            jnp.exp(scores - new_highest[..., None]), axis=-1
        )
        return (new_highest, denominator)

    highest, denominator = lax.fori_loop(0, trip_count, max_sweep, (highest, denominator))
    log_total = highest + jnp.log(denominator)

    def softmax_weights(scores):
        return jnp.exp(scores - log_total[..., None])

    summed = jnp.einsum(
        "pkgqj,pjkd->pqkgd",
        softmax_weights(near_scores).astype(jnp.bfloat16),
        value_blk,
        preferred_element_type=jnp.float32,
    )

    def value_sweep(slot_index, summed):
        key_rows, value_rows, counted_slot, source = slot_rows(slot_index)
        weights = softmax_weights(masked(logits(key_rows), counted_slot)).astype(jnp.bfloat16)
        return summed + jnp.einsum(
            "pkgqj,pjkd->pqkgd", weights, value_rows, preferred_element_type=jnp.float32
        )

    summed = lax.fori_loop(0, trip_count, value_sweep, summed)
    attended_blk = summed.astype(jnp.bfloat16)
    row_delta = jnp.transpose(
        jnp.sum(grad_blk.astype(jnp.float32) * attended_blk.astype(jnp.float32), axis=-1),
        (0, 2, 3, 1),
    )

    def backward(scores, key_rows, value_rows):
        probs = softmax_weights(scores)
        weights = probs.astype(jnp.bfloat16)
        dprobs = jnp.einsum(
            "pqkgd,pjkd->pkgqj", grad_blk, value_rows, preferred_element_type=jnp.float32
        )
        dscores = (probs * (dprobs - row_delta[..., None])).astype(jnp.bfloat16)
        query_term = jnp.einsum(
            "pkgqj,pjkd->pqkgd", dscores, key_rows, preferred_element_type=jnp.float32
        )
        key_term = (
            jnp.einsum("pkgqj,pqkgd->pjkd", dscores, query_blk, preferred_element_type=jnp.float32)
            * score_scale
        )
        value_term = jnp.einsum(
            "pkgqj,pqkgd->pjkd", weights, grad_blk, preferred_element_type=jnp.float32
        )
        return (query_term, key_term, value_term)

    query_sum, key_near, value_near = backward(near_scores, key_blk, value_blk)
    far_grads = jnp.zeros((2, grp_count, block_tok, kv_local, head_width), jnp.float32)

    def grad_sweep(slot_index, state_pair):
        query_sum, far_grads = state_pair
        key_rows, value_rows, counted_slot, source = slot_rows(slot_index)
        query_term, key_term, value_term = backward(
            masked(logits(key_rows), counted_slot), key_rows, value_rows
        )
        routing = (
            (source[:, None] == jnp.arange(grp_count)[None, :]) & counted_slot[:, None]
        ).astype(jnp.float32)
        routed = jnp.einsum(
            "ps,xpjkd->xsjkd",
            routing,
            jnp.stack([key_term, value_term]),
            precision=lax.Precision.HIGHEST,
        )
        return (query_sum + query_term, far_grads + routed)

    query_sum, far_grads = lax.fori_loop(0, trip_count, grad_sweep, (query_sum, far_grads))
    owners = ((send_place[:, None] == jnp.arange(per_group)[None, :]) & sending[:, None]).astype(
        jnp.float32
    )
    returned = lax.all_to_all(far_grads, "grp", split_axis=1, concat_axis=1, tiled=True)
    landed = jnp.einsum("sp,xsjkd->xpjkd", owners, returned, precision=lax.Precision.HIGHEST)
    key_local = (key_near + landed[0]).reshape(group_tok, kv_local, head_width)
    value_local = (value_near + landed[1]).reshape(group_tok, kv_local, head_width)
    attended_rows = attended_blk.reshape(group_tok, heads_local, head_width)
    query_rows = (
        (query_sum * score_scale).astype(jnp.bfloat16).reshape(group_tok, heads_local, head_width)
    )
    attended, query_grad = (
        lax.all_to_all(attended_rows, "uly", split_axis=0, concat_axis=1, tiled=True),
        lax.all_to_all(query_rows, "uly", split_axis=0, concat_axis=1, tiled=True),
    )
    key_parts, value_parts = (
        lax.all_to_all(key_local, "uly", split_axis=0, concat_axis=1, tiled=True),
        lax.all_to_all(value_local, "uly", split_axis=0, concat_axis=1, tiled=True),
    )
    key_gradient = jnp.sum(key_parts.reshape(tokens, kv_heads, copies, head_width), axis=2).astype(
        jnp.bfloat16
    )
    value_gradient = jnp.sum(
        value_parts.reshape(tokens, kv_heads, copies, head_width), axis=2
    ).astype(jnp.bfloat16)
    return (attended, query_grad, key_gradient, value_gradient)


HIDDEN = -1e30
LAST = (((1,), (1,)), ((), ()))
FIRST = (((0,), (0,)), ((), ()))
F32 = jnp.float32
BF16 = jnp.bfloat16


def dot_last(left, right):
    return lax.dot_general(left, right, LAST, preferred_element_type=F32)


def dot_first(left, right):
    return lax.dot_general(left, right, FIRST, preferred_element_type=F32)


def head_major(cols, kv_heads):
    half = cols // 2
    place = half // kv_heads
    row = lax.broadcasted_iota(jnp.int32, (cols, cols), 0)
    col = lax.broadcasted_iota(jnp.int32, (cols, cols), 1)
    token = row // half * place + row % place
    return jnp.where(col == token * kv_heads + row % half // place, 1.0, 0.0).astype(BF16)


def reorder(one_hot, array):
    return jnp.dot(one_hot, array, preferred_element_type=F32).astype(BF16)


def own_head(scores, lane_head, kv_heads):
    place = scores.shape[0] // kv_heads
    kept = scores[:place]
    for head in range(1, kv_heads):
        kept = jnp.where(lane_head == head, scores[head * place:(head + 1) * place], kept)
    return kept


def all_heads(kept, lane_head, kv_heads):
    none = jnp.zeros_like(kept)
    return jnp.concatenate(
        [jnp.where(lane_head == head, kept, none) for head in range(kv_heads)], axis=0
    )


def lanes(rows, heads, kv_heads):
    lane = lax.broadcasted_iota(jnp.int32, (1, rows), 1)
    return lane // heads, lane % heads // (heads // kv_heads)


def plan_spans(grp_count, blocks):
    return grp_count, 2 * grp_count, 2 * grp_count + blocks, 2 * grp_count + 2 * blocks


def plan_kernel(lists_ref, counts_ref, plan_ref, *, grp_count, blocks):
    group, mine = lax.axis_index("grp"), lax.axis_index("uly")
    per_group = 2 * blocks
    low = group * per_group
    sib_at, source_at, give_at, seen_at = plan_spans(grp_count, blocks)
    for other in range(grp_count):
        place = jnp.int32(-1)
        for at in range(other * per_group, (other + 1) * per_group):
            here = lists_ref[at] - low
            wanted = (here >= 0) & (here < per_group) & (counts_ref[at] > 0)
            place = jnp.where(wanted, here, place)
        own = place - mine * blocks
        sib = place - (1 - mine) * blocks
        plan_ref[other] = jnp.where((own >= 0) & (own < blocks), own, -1)
        plan_ref[sib_at + other] = jnp.where((sib >= 0) & (sib < blocks), sib, -1)
    for block in range(blocks):
        at = low + mine * blocks + block
        plan_ref[source_at + block] = lax.div(lists_ref[at], per_group)
        plan_ref[seen_at + block] = counts_ref[at]
        at = low + (1 - mine) * blocks + block
        plan_ref[give_at + block] = lax.div(lists_ref[at], per_group)


def pack_kernel(k_hbm, v_hbm, kept_ref, given_ref, k_ref, v_ref, sems, *, kv_heads):
    blocks, _, half, _ = kept_ref.shape
    copies = [
        pltpu.make_async_copy(k_hbm, k_ref, sems.at[0]),
        pltpu.make_async_copy(v_hbm, v_ref, sems.at[1]),
    ]
    for copy in copies:
        copy.start()
    first = lax.axis_index("uly") == 0
    order = head_major(2 * half, kv_heads)
    for which, ref in enumerate((k_ref, v_ref)):
        copies[which].wait()
        for block in range(blocks):
            ordered = reorder(order, ref[block * 2 * half:(block + 1) * 2 * half])
            kept_ref[block, which] = jnp.where(first, ordered[:half], ordered[half:])
            given_ref[block, which] = jnp.where(first, ordered[half:], ordered[:half])


def outgoing_kernel(plan_ref, blocks_ref, *refs, first):
    out_ref, sems = refs[-2:]
    copies = []
    for group in range(out_ref.shape[0]):
        place = plan_ref[first + group]
        source = blocks_ref.at[jnp.maximum(place, 0)]
        copy = pltpu.make_async_copy(source, out_ref.at[group], sems.at[group])
        copies.append((place >= 0, copy))
    for wanted, copy in copies:
        pl.when(wanted)(copy.start)
    for wanted, copy in copies:
        pl.when(wanted)(copy.wait)


def returning_kernel(plan_ref, blocks_ref, _, out_ref, sems, *, give_at):
    copies = [
        pltpu.make_async_copy(blocks_ref.at[block], out_ref.at[plan_ref[give_at + block]], sems.at[block])
        for block in range(blocks_ref.shape[0])
    ]
    for copy in copies:
        copy.start()
    for copy in copies:
        copy.wait()


def near_kernel(
    q_ref, g_ref, kept_ref, given_ref, stat_ref, *, heads, kv_heads, score_scale
):
    blocks = stat_ref.shape[0]
    rows = q_ref.shape[0] // blocks
    place = kept_ref.shape[2] // kv_heads
    token, lane_head = lanes(rows, heads, kv_heads)
    key = lax.broadcasted_iota(jnp.int32, (2 * place, rows), 0)
    mine = lax.axis_index("uly")
    part = jnp.where(key < place, mine, 1 - mine)
    causal = key % place + part * place <= token
    for block in range(blocks):
        span = slice(block * rows, (block + 1) * rows)
        pieces = []
        for which, ref in enumerate((q_ref, g_ref)):
            both = jnp.concatenate([kept_ref[block, which], given_ref[block, which]], axis=0)
            full = dot_last(both, ref[span])
            half = full.shape[0] // 2
            pieces.append(
                jnp.concatenate(
                    [
                        own_head(full[:half], lane_head, kv_heads),
                        own_head(full[half:], lane_head, kv_heads),
                    ],
                    axis=0,
                )
            )
        scores = jnp.where(causal, pieces[0] * score_scale, HIDDEN)
        highest = jnp.max(scores, axis=0, keepdims=True)
        raised = jnp.exp(scores - highest)
        stat_ref[block, 0:1] = highest
        stat_ref[block, 1:2] = jnp.sum(raised, axis=0, keepdims=True)
        stat_ref[block, 2:3] = jnp.sum(raised * pieces[1], axis=0, keepdims=True)


def far_scores(part_ref, at, q, g, seen, lane_head, kv_heads, score_scale):
    hidden = jnp.where(seen > 0, 0.0, HIDDEN)
    scores = own_head(dot_last(part_ref[at, 0], q), lane_head, kv_heads) * score_scale + hidden
    return scores, own_head(dot_last(part_ref[at, 1], g), lane_head, kv_heads)


def merged(stat_ref, block, scores, dprobs):
    before = stat_ref[block, 0:1]
    highest = jnp.maximum(before, jnp.max(scores, axis=0, keepdims=True))
    raised = jnp.exp(scores - highest)
    shrink = jnp.exp(before - highest)
    total = shrink * stat_ref[block, 1:2] + jnp.sum(raised, axis=0, keepdims=True)
    delta = shrink * stat_ref[block, 2:3] + jnp.sum(raised * dprobs, axis=0, keepdims=True)
    return highest, raised, total, delta


def far_gradients(probs, dprobs, delta, q, g, lane_head, kv_heads, score_scale):
    dscores = (probs * (dprobs - delta)).astype(BF16)
    dk = jnp.dot(all_heads(dscores, lane_head, kv_heads), q, preferred_element_type=F32)
    dv = jnp.dot(all_heads(probs.astype(BF16), lane_head, kv_heads), g, preferred_element_type=F32)
    return (dk * score_scale).astype(BF16), dv.astype(BF16)


def mid_kernel(
    plan_ref, q_ref, g_ref, stat_ref, arrived_ref, out_ref,
    *, heads, kv_heads, score_scale, source_at, seen_at
):
    blocks = stat_ref.shape[0]
    rows = q_ref.shape[0] // blocks
    _, lane_head = lanes(rows, heads, kv_heads)
    for block in range(blocks):
        span = slice(block * rows, (block + 1) * rows)
        scores, dprobs = far_scores(
            arrived_ref, plan_ref[source_at + block], q_ref[span], g_ref[span],
            plan_ref[seen_at + block],            lane_head, kv_heads, score_scale,
        )
        highest, _, total, delta = merged(stat_ref, block, scores, dprobs)
        out_ref[block, 0:1] = highest
        out_ref[block, 1:2] = total
        out_ref[block, 2:3] = delta


def far_kernel(
    plan_ref, q_ref, g_ref, stat_ref, other_ref, grad_ref, out_ref,
    *, heads, kv_heads, score_scale, seen_at
):
    blocks = stat_ref.shape[0]
    rows = q_ref.shape[0] // blocks
    _, lane_head = lanes(rows, heads, kv_heads)
    for block in range(blocks):
        span = slice(block * rows, (block + 1) * rows)
        q = q_ref[span]
        g = g_ref[span]
        scores, dprobs = far_scores(
            other_ref, block, q, g, plan_ref[seen_at + block], lane_head, kv_heads, score_scale
        )
        highest, raised, total, delta = merged(stat_ref, block, scores, dprobs)
        inverse = 1.0 / total
        delta = delta * inverse
        grad_ref[block, 0], grad_ref[block, 1] = far_gradients(
            raised * inverse, dprobs, delta, q, g, lane_head, kv_heads, score_scale
        )
        out_ref[block, 0:1] = highest
        out_ref[block, 1:2] = inverse
        out_ref[block, 2:3] = delta


def mine_kernel(
    plan_ref, q_ref, g_ref, stat_ref, arrived_ref, out_ref, grad_ref, sems,
    *, heads, kv_heads, score_scale, source_at, seen_at
):
    blocks = stat_ref.shape[0]
    rows = q_ref.shape[0] // blocks
    _, lane_head = lanes(rows, heads, kv_heads)
    copies = []
    for block in range(blocks):
        span = slice(block * rows, (block + 1) * rows)
        q = q_ref[span]
        g = g_ref[span]
        source = plan_ref[source_at + block]
        scores, dprobs = far_scores(
            arrived_ref, source, q, g, plan_ref[seen_at + block], lane_head, kv_heads, score_scale
        )
        probs = jnp.exp(scores - stat_ref[block, 0:1]) * stat_ref[block, 1:2]
        grad_ref[block, 0], grad_ref[block, 1] = far_gradients(
            probs, dprobs, stat_ref[block, 2:3], q, g, lane_head, kv_heads, score_scale
        )
        copies.append(
            pltpu.make_async_copy(grad_ref.at[block], out_ref.at[source], sems.at[block])
        )
        copies[-1].start()
    for copy in copies:
        copy.wait()


def local_kernel(
    plan_ref, q_ref, g_ref, k_ref, v_ref, mine_ref, other_ref,
    att_ref, dq_ref, dk_ref, dv_ref, bias_ref, *, heads, kv_heads, score_scale, seen_at
):
    step = pl.program_id(0)
    rows = q_ref.shape[0]
    cols = k_ref.shape[0]

    @pl.when(step == 0)
    def _():
        half = cols // 2
        place = half // kv_heads
        row = lax.broadcasted_iota(jnp.int32, (rows, cols), 0)
        col = lax.broadcasted_iota(jnp.int32, (rows, cols), 1)
        same = row % heads // (heads // kv_heads) == col % half // place
        causal = col // half * place + col % place <= row // heads
        bias_ref[:, :cols] = jnp.where(same & causal, 0.0, HIDDEN)
        bias_ref[:, cols:] = jnp.where(same, 0.0, HIDDEN)

    far_bias = jnp.where(plan_ref[seen_at + step] > 0, 0.0, HIDDEN)
    order = head_major(cols, kv_heads)
    k_near = reorder(order, k_ref[...])
    v_near = reorder(order, v_ref[...])
    k_all = jnp.concatenate([k_near, mine_ref[0, 0], other_ref[0, 0]], axis=0)
    v_all = jnp.concatenate([v_near, mine_ref[0, 1], other_ref[0, 1]], axis=0)
    q = q_ref[...]
    g = g_ref[...]
    scores = dot_last(q, k_all) * score_scale + bias_ref[...]
    scores = jnp.concatenate([scores[:, :cols], scores[:, cols:] + far_bias], axis=1)
    highest = jnp.max(scores, axis=1, keepdims=True)
    raised = jnp.exp(scores - highest)
    total = jnp.sum(raised, axis=1, keepdims=True)
    probs = raised * (1.0 / total)
    weights = probs.astype(BF16)
    attended = jnp.dot(weights, v_all, preferred_element_type=F32).astype(BF16)
    att_ref[...] = attended
    delta = jnp.sum(g.astype(F32) * attended.astype(F32), axis=1, keepdims=True)
    dscores = (probs * (dot_last(g, v_all) - delta)).astype(BF16)
    dq = jnp.dot(dscores, k_all, preferred_element_type=F32) * score_scale
    dq_ref[...] = dq.astype(BF16)
    dk_ref[...] = dot_first(dscores[:, :cols], q) * score_scale
    dv_ref[...] = dot_first(weights[:, :cols], g)


def landing_kernel(plan_ref, landed_ref, out_ref, sum_ref, *, first):
    sum_ref[...] = jnp.zeros_like(sum_ref)
    for group in range(landed_ref.shape[0]):
        place = plan_ref[first + group]

        @pl.when(place >= 0)
        def _():
            sum_ref[place] = sum_ref[place] + landed_ref[group].astype(F32)

    out_ref[...] = sum_ref[...].astype(out_ref.dtype)


def finish_kernel(
    dk_near_ref, dv_near_ref, own_ref, back_ref, dk_ref, dv_ref, *, kv_heads
):
    blocks, _, half, _ = back_ref.shape
    mine = lax.axis_index("uly") == 0
    order = head_major(2 * half, kv_heads)
    for block in range(blocks):
        span = slice(block * 2 * half, (block + 1) * 2 * half)
        for near_ref, out_ref, which in ((dk_near_ref, dk_ref, 0), (dv_near_ref, dv_ref, 1)):
            own = own_ref[block, which]
            back = back_ref[block, which].astype(F32)
            far = jnp.concatenate([jnp.where(mine, own, back), jnp.where(mine, back, own)], axis=0)
            summed = (near_ref[span] + far).astype(BF16)
            out_ref[span] = dot_first(order, summed).astype(BF16)


def take_rows(array, index):
    return array.at[index].get(mode="promise_in_bounds")


def whole_blocks(queries, keys, values, output_cotangent, block_lists, list_counts):
    grp_count = lax.axis_size("grp")
    uly_count = lax.axis_size("uly")
    tokens, heads, width = queries.shape
    kv_heads = keys.shape[1]
    per_group = block_lists.shape[0] // grp_count
    block_tok = tokens * uly_count // per_group
    mine_blocks = tokens // block_tok
    rows = block_tok * heads
    cols = block_tok * kv_heads
    half = cols // 2
    sizes = dict(heads=heads, kv_heads=kv_heads, score_scale=width ** (-0.5))
    swap = [(0, 1), (1, 0)]

    sib_at, source_at, give_at, seen_at = plan_spans(grp_count, mine_blocks)

    q2 = queries.reshape(tokens * heads, width)
    g2 = output_cotangent.reshape(tokens * heads, width)
    k2 = keys.reshape(tokens * kv_heads, width)
    v2 = values.reshape(tokens * kv_heads, width)

    part_shape = jax.ShapeDtypeStruct((mine_blocks, 2, half, width), BF16)
    slot_shape = pltpu.HBM((grp_count, 2, half, width), BF16)
    stat_shape = jax.ShapeDtypeStruct((mine_blocks, 8, rows), F32)
    row_shape = jax.ShapeDtypeStruct(q2.shape, BF16)
    near_shape = jax.ShapeDtypeStruct(k2.shape, F32)
    small_shape = jax.ShapeDtypeStruct(k2.shape, BF16)
    sum_scratch = [pltpu.VMEM((mine_blocks, 2, half, width), F32)]
    slot_sems = [pltpu.SemaphoreType.DMA((grp_count,))]
    limit = pltpu.CompilerParams(vmem_limit_bytes=24 * 1024 * 1024)
    vmem = pl.BlockSpec(memory_space=pltpu.VMEM)
    smem = pl.BlockSpec(memory_space=pltpu.SMEM)
    anywhere = pl.BlockSpec(memory_space=pltpu.HBM)

    def call(kernel, name, scalars, operands, out_shape, scratch=(), into=None, out_spec=vmem):
        extra = () if into is None else (into,)
        return pl.pallas_call(
            kernel,
            in_specs=[smem] * len(scalars) + [vmem] * len(operands) + [anywhere] * len(extra),
            out_specs=jax.tree.map(lambda _: out_spec, out_shape),
            out_shape=out_shape,
            scratch_shapes=scratch,
            input_output_aliases={len(scalars) + len(operands): 0} if extra else {},
            compiler_params=limit,
            name=name,
        )(*scalars, *operands, *extra)

    def in_hbm(array):
        return pltpu.with_memory_space_constraint(array, pltpu.HBM)

    kept, given = pl.pallas_call(
        partial(pack_kernel, kv_heads=kv_heads),
        in_specs=[anywhere, anywhere],
        out_specs=[vmem, vmem],
        out_shape=[part_shape, part_shape],
        scratch_shapes=[
            pltpu.VMEM(k2.shape, BF16), pltpu.VMEM(k2.shape, BF16), pltpu.SemaphoreType.DMA((2,))
        ],
        compiler_params=limit,
        name="pack",
    )(in_hbm(k2), in_hbm(v2))
    plan = pl.pallas_call(
        partial(plan_kernel, grp_count=grp_count, blocks=mine_blocks),
        in_specs=[smem, smem],
        out_specs=smem,
        out_shape=pltpu.SMEM((seen_at + mine_blocks,), jnp.int32),
        compiler_params=limit,
        name="plan",
    )(in_hbm(block_lists.reshape(-1)), in_hbm(list_counts))
    gotten = lax.ppermute(given, "uly", swap)
    outgoing = call(
        partial(outgoing_kernel, first=0), "send_own", (plan,), (kept,),
        slot_shape, slot_sems, out_spec=anywhere,
    )
    outgoing = call(
        partial(outgoing_kernel, first=sib_at), "send_sibling", (plan,), (gotten,),
        slot_shape, slot_sems, into=outgoing, out_spec=anywhere,
    )
    outgoing, given = lax.optimization_barrier((outgoing, given))
    arrived = lax.all_to_all(outgoing, "grp", split_axis=0, concat_axis=0, tiled=True)
    stats = call(
        partial(near_kernel, **sizes), "near", (), (q2, g2, kept, given), stat_shape
    )
    arrived, stats = lax.optimization_barrier((arrived, stats))
    give_rows = plan[give_at:give_at + mine_blocks]
    other = lax.ppermute(take_rows(arrived, give_rows), "uly", swap)
    stats = call(
        partial(mid_kernel, source_at=source_at, seen_at=seen_at, **sizes), "mid", (plan,),
        (q2, g2, stats, arrived), stat_shape,
    )
    far_other, stats = call(
        partial(far_kernel, seen_at=seen_at, **sizes), "far", (plan,), (q2, g2, stats, other),
        [part_shape, stat_shape],
    )
    from_sib = lax.ppermute(far_other, "uly", swap)
    returning = call(
        partial(mine_kernel, source_at=source_at, seen_at=seen_at, **sizes), "mine", (plan,),
        (q2, g2, stats, arrived), slot_shape,
        [pltpu.VMEM(part_shape.shape, BF16), pltpu.SemaphoreType.DMA((mine_blocks,))],
        out_spec=anywhere,
    )
    returning = call(
        partial(returning_kernel, give_at=give_at), "return_sibling", (plan,), (from_sib,), slot_shape,
        [pltpu.SemaphoreType.DMA((mine_blocks,))], into=returning, out_spec=anywhere,
    )
    returning, k2l = lax.optimization_barrier((returning, k2))
    landed = lax.all_to_all(returning, "grp", split_axis=0, concat_axis=0, tiled=True)

    def step_rows(i, *_):
        return (i, 0)

    def step_part(i, *_):
        return (i, 0, 0, 0)

    def from_source(i, plan_ref):
        return (plan_ref[source_at + i], 0, 0, 0)

    row_spec = pl.BlockSpec((rows, width), step_rows)
    col_spec = pl.BlockSpec((cols, width), step_rows)
    attended, dq, dk_near, dv_near = pl.pallas_call(
        partial(local_kernel, seen_at=seen_at, **sizes),
        grid_spec=pltpu.PrefetchScalarGridSpec(
            num_scalar_prefetch=1,
            grid=(mine_blocks,),
            in_specs=[
                row_spec, row_spec, col_spec, col_spec,
                pl.BlockSpec((1, 2, half, width), from_source),
                pl.BlockSpec((1, 2, half, width), step_part),
            ],
            out_specs=[row_spec, row_spec, col_spec, col_spec],
            scratch_shapes=[pltpu.VMEM((rows, 2 * cols), F32)],
        ),
        out_shape=[row_shape, row_shape, near_shape, near_shape],
        compiler_params=limit,
        name="local",
    )(plan, q2, g2, k2l, v2, arrived, other)
    landed, dk_near = lax.optimization_barrier((landed, dk_near))
    give = call(
        partial(landing_kernel, first=sib_at), "land_sibling", (plan,), (landed,), part_shape,
        sum_scratch,
    )
    back = lax.ppermute(give, "uly", swap)
    own = call(
        partial(landing_kernel, first=0), "land_own", (plan,), (landed,),
        jax.ShapeDtypeStruct(part_shape.shape, F32), sum_scratch,
    )
    dk, dv = call(
        partial(finish_kernel, kv_heads=kv_heads), "finish", (),
        (dk_near, dv_near, own, back), [small_shape, small_shape],
    )
    return (
        attended.reshape(queries.shape), dq.reshape(queries.shape),
        dk.reshape(keys.shape), dv.reshape(keys.shape),
    )


def on_device(queries, keys, values, output_cotangent, block_lists, list_counts):
    uly_count = lax.axis_size("uly")
    grp_count = lax.axis_size("grp")
    blocks_all, remote = block_lists.shape
    block_tok = queries.shape[0] * uly_count * grp_count // blocks_all
    held_whole = queries.shape[0] % block_tok == 0
    run = whole_blocks if held_whole and remote == 1 and uly_count == 2 else spread_blocks
    return run(queries, keys, values, output_cotangent, block_lists, list_counts)


def solution(mesh):
    placed = (
        P(("grp", "uly"), None, None),
        P(("grp", "uly"), None, None),
        P(("grp", "uly"), None, None),
        P(("grp", "uly"), None, None),
        P(),
        P(),
    )
    return jax.shard_map(
        on_device,
        mesh=mesh,
        in_specs=placed,
        out_specs=(
            P(("grp", "uly"), None, None),
            P(("grp", "uly"), None, None),
            P(("grp", "uly"), None, None),
            P(("grp", "uly"), None, None),
        ),
        check_vma=False,
    )
```

```python
from functools import partial

import jax
import jax.numpy as jnp
from jax import lax
from jax.experimental import pallas as pl
from jax.experimental.pallas import tpu as pltpu
from jax.sharding import PartitionSpec as P


def spread_blocks(queries, keys, values, output_cotangent, block_lists, list_counts):
    uly_count = lax.axis_size("uly")
    grp_count = lax.axis_size("grp")
    my_group = lax.axis_index("grp")
    tokens, head_count, head_width = queries.shape
    kv_heads = keys.shape[1]
    copies = max(1, uly_count // kv_heads)
    blocks_all, remote = block_lists.shape
    per_group = blocks_all // grp_count
    block_tok = tokens * uly_count // per_group
    group_tok = tokens * uly_count
    score_scale = head_width ** (-0.5)
    lists = block_lists.reshape(grp_count, per_group, remote)
    counted = (jnp.arange(remote)[None, :] < list_counts[:, None]).reshape(
        grp_count, per_group, remote
    )
    wanted = (lists // per_group == my_group) & counted
    send_place = jnp.sum(jnp.where(wanted, lists % per_group, 0), axis=(1, 2))
    sending = jnp.any(wanted, axis=(1, 2))
    mine_source = lax.dynamic_index_in_dim(lists, my_group, 0, keepdims=False) // per_group
    mine_counted = lax.dynamic_index_in_dim(counted, my_group, 0, keepdims=False)
    trip_count = jnp.max(jnp.sum(mine_counted.astype(jnp.int32), axis=1))

    def to_blocks(array_in):
        return array_in.reshape((per_group, block_tok) + array_in.shape[1:])

    keys_wide = jnp.repeat(keys, copies, axis=1)
    values_wide = jnp.repeat(values, copies, axis=1)
    query_heads, grad_heads, key_heads, value_heads = (
        lax.all_to_all(queries, "uly", split_axis=1, concat_axis=0, tiled=True),
        lax.all_to_all(output_cotangent, "uly", split_axis=1, concat_axis=0, tiled=True),
        lax.all_to_all(keys_wide, "uly", split_axis=1, concat_axis=0, tiled=True),
        lax.all_to_all(values_wide, "uly", split_axis=1, concat_axis=0, tiled=True),
    )
    stacked = jnp.stack([to_blocks(key_heads), to_blocks(value_heads)])
    outgoing = jnp.take(stacked, send_place, axis=1)
    arrived = lax.all_to_all(outgoing, "grp", split_axis=1, concat_axis=1, tiled=True)
    kv_local = key_heads.shape[1]
    heads_local = query_heads.shape[1]
    heads_per_group = heads_local // kv_local
    query_blk = query_heads.reshape(per_group, block_tok, kv_local, heads_per_group, head_width)
    grad_blk = grad_heads.reshape(per_group, block_tok, kv_local, heads_per_group, head_width)
    key_blk = to_blocks(key_heads)
    value_blk = to_blocks(value_heads)
    far_keys = arrived[0]
    far_values = arrived[1]
    causal = jnp.arange(block_tok)[:, None] >= jnp.arange(block_tok)[None, :]

    def logits(key_rows):
        return (
            jnp.einsum("pqkgd,pjkd->pkgqj", query_blk, key_rows, preferred_element_type=jnp.float32)
            * score_scale
        )

    def slot_rows(slot_index):
        source = lax.dynamic_index_in_dim(mine_source, slot_index, 1, keepdims=False)
        counted_slot = lax.dynamic_index_in_dim(mine_counted, slot_index, 1, keepdims=False)
        return (
            jnp.take(far_keys, source, axis=0),
            jnp.take(far_values, source, axis=0),
            counted_slot,
            source,
        )

    def masked(scores, counted_slot):
        return jnp.where(counted_slot[:, None, None, None, None], scores, -jnp.inf)

    near_scores = jnp.where(causal, logits(key_blk), -jnp.inf)
    highest = jnp.max(near_scores, axis=-1)
    denominator = jnp.sum(jnp.exp(near_scores - highest[..., None]), axis=-1)

    def max_sweep(slot_index, state_pair):
        highest, denominator = state_pair
        key_rows, value_rows, counted_slot, source = slot_rows(slot_index)
        scores = masked(logits(key_rows), counted_slot)
        new_highest = jnp.maximum(highest, jnp.max(scores, axis=-1))
        denominator = denominator * jnp.exp(highest - new_highest) + jnp.sum(
            jnp.exp(scores - new_highest[..., None]), axis=-1
        )
        return (new_highest, denominator)

    highest, denominator = lax.fori_loop(0, trip_count, max_sweep, (highest, denominator))
    log_total = highest + jnp.log(denominator)

    def softmax_weights(scores):
        return jnp.exp(scores - log_total[..., None])

    summed = jnp.einsum(
        "pkgqj,pjkd->pqkgd",
        softmax_weights(near_scores).astype(jnp.bfloat16),
        value_blk,
        preferred_element_type=jnp.float32,
    )

    def value_sweep(slot_index, summed):
        key_rows, value_rows, counted_slot, source = slot_rows(slot_index)
        weights = softmax_weights(masked(logits(key_rows), counted_slot)).astype(jnp.bfloat16)
        return summed + jnp.einsum(
            "pkgqj,pjkd->pqkgd", weights, value_rows, preferred_element_type=jnp.float32
        )

    summed = lax.fori_loop(0, trip_count, value_sweep, summed)
    attended_blk = summed.astype(jnp.bfloat16)
    row_delta = jnp.transpose(
        jnp.sum(grad_blk.astype(jnp.float32) * attended_blk.astype(jnp.float32), axis=-1),
        (0, 2, 3, 1),
    )

    def backward(scores, key_rows, value_rows):
        probs = softmax_weights(scores)
        weights = probs.astype(jnp.bfloat16)
        dprobs = jnp.einsum(
            "pqkgd,pjkd->pkgqj", grad_blk, value_rows, preferred_element_type=jnp.float32
        )
        dscores = (probs * (dprobs - row_delta[..., None])).astype(jnp.bfloat16)
        query_term = jnp.einsum(
            "pkgqj,pjkd->pqkgd", dscores, key_rows, preferred_element_type=jnp.float32
        )
        key_term = (
            jnp.einsum("pkgqj,pqkgd->pjkd", dscores, query_blk, preferred_element_type=jnp.float32)
            * score_scale
        )
        value_term = jnp.einsum(
            "pkgqj,pqkgd->pjkd", weights, grad_blk, preferred_element_type=jnp.float32
        )
        return (query_term, key_term, value_term)

    query_sum, key_near, value_near = backward(near_scores, key_blk, value_blk)
    far_grads = jnp.zeros((2, grp_count, block_tok, kv_local, head_width), jnp.float32)

    def grad_sweep(slot_index, state_pair):
        query_sum, far_grads = state_pair
        key_rows, value_rows, counted_slot, source = slot_rows(slot_index)
        query_term, key_term, value_term = backward(
            masked(logits(key_rows), counted_slot), key_rows, value_rows
        )
        routing = (
            (source[:, None] == jnp.arange(grp_count)[None, :]) & counted_slot[:, None]
        ).astype(jnp.float32)
        routed = jnp.einsum(
            "ps,xpjkd->xsjkd",
            routing,
            jnp.stack([key_term, value_term]),
            precision=lax.Precision.HIGHEST,
        )
        return (query_sum + query_term, far_grads + routed)

    query_sum, far_grads = lax.fori_loop(0, trip_count, grad_sweep, (query_sum, far_grads))
    owners = ((send_place[:, None] == jnp.arange(per_group)[None, :]) & sending[:, None]).astype(
        jnp.float32
    )
    returned = lax.all_to_all(far_grads, "grp", split_axis=1, concat_axis=1, tiled=True)
    landed = jnp.einsum("sp,xsjkd->xpjkd", owners, returned, precision=lax.Precision.HIGHEST)
    key_local = (key_near + landed[0]).reshape(group_tok, kv_local, head_width)
    value_local = (value_near + landed[1]).reshape(group_tok, kv_local, head_width)
    attended_rows = attended_blk.reshape(group_tok, heads_local, head_width)
    query_rows = (
        (query_sum * score_scale).astype(jnp.bfloat16).reshape(group_tok, heads_local, head_width)
    )
    attended, query_grad = (
        lax.all_to_all(attended_rows, "uly", split_axis=0, concat_axis=1, tiled=True),
        lax.all_to_all(query_rows, "uly", split_axis=0, concat_axis=1, tiled=True),
    )
    key_parts, value_parts = (
        lax.all_to_all(key_local, "uly", split_axis=0, concat_axis=1, tiled=True),
        lax.all_to_all(value_local, "uly", split_axis=0, concat_axis=1, tiled=True),
    )
    key_gradient = jnp.sum(key_parts.reshape(tokens, kv_heads, copies, head_width), axis=2).astype(
        jnp.bfloat16
    )
    value_gradient = jnp.sum(
        value_parts.reshape(tokens, kv_heads, copies, head_width), axis=2
    ).astype(jnp.bfloat16)
    return (attended, query_grad, key_gradient, value_gradient)


HIDDEN = -1e30
LAST = (((1,), (1,)), ((), ()))
FIRST = (((0,), (0,)), ((), ()))
F32 = jnp.float32
BF16 = jnp.bfloat16


def dot_last(left, right):
    return lax.dot_general(left, right, LAST, preferred_element_type=F32)


def dot_first(left, right):
    return lax.dot_general(left, right, FIRST, preferred_element_type=F32)


def head_major(cols, kv_heads):
    half = cols // 2
    place = half // kv_heads
    row = lax.broadcasted_iota(jnp.int32, (cols, cols), 0)
    col = lax.broadcasted_iota(jnp.int32, (cols, cols), 1)
    token = row // half * place + row % place
    return jnp.where(col == token * kv_heads + row % half // place, 1.0, 0.0).astype(BF16)


def reorder(one_hot, array):
    return jnp.dot(one_hot, array, preferred_element_type=F32).astype(BF16)


def own_head(scores, lane_head, kv_heads):
    place = scores.shape[0] // kv_heads
    kept = scores[:place]
    for head in range(1, kv_heads):
        kept = jnp.where(lane_head == head, scores[head * place:(head + 1) * place], kept)
    return kept


def all_heads(kept, lane_head, kv_heads):
    none = jnp.zeros_like(kept)
    return jnp.concatenate(
        [jnp.where(lane_head == head, kept, none) for head in range(kv_heads)], axis=0
    )


def lanes(rows, heads, kv_heads):
    lane = lax.broadcasted_iota(jnp.int32, (1, rows), 1)
    return lane // heads, lane % heads // (heads // kv_heads)


def plan_spans(grp_count, blocks):
    return grp_count, 2 * grp_count, 2 * grp_count + blocks, 2 * grp_count + 2 * blocks


def plan_kernel(lists_ref, counts_ref, plan_ref, *, grp_count, blocks):
    group, mine = lax.axis_index("grp"), lax.axis_index("uly")
    per_group = 2 * blocks
    low = group * per_group
    sib_at, source_at, give_at, seen_at = plan_spans(grp_count, blocks)
    for other in range(grp_count):
        place = jnp.int32(-1)
        for at in range(other * per_group, (other + 1) * per_group):
            here = lists_ref[at] - low
            wanted = (here >= 0) & (here < per_group) & (counts_ref[at] > 0)
            place = jnp.where(wanted, here, place)
        own = place - mine * blocks
        sib = place - (1 - mine) * blocks
        plan_ref[other] = jnp.where((own >= 0) & (own < blocks), own, -1)
        plan_ref[sib_at + other] = jnp.where((sib >= 0) & (sib < blocks), sib, -1)
    for block in range(blocks):
        at = low + mine * blocks + block
        plan_ref[source_at + block] = lax.div(lists_ref[at], per_group)
        plan_ref[seen_at + block] = counts_ref[at]
        at = low + (1 - mine) * blocks + block
        plan_ref[give_at + block] = lax.div(lists_ref[at], per_group)


def pack_kernel(k_hbm, v_hbm, kept_ref, given_ref, k_ref, v_ref, sems, *, kv_heads):
    blocks, _, half, _ = kept_ref.shape
    copies = [
        pltpu.make_async_copy(k_hbm, k_ref, sems.at[0]),
        pltpu.make_async_copy(v_hbm, v_ref, sems.at[1]),
    ]
    for copy in copies:
        copy.start()
    first = lax.axis_index("uly") == 0
    order = head_major(2 * half, kv_heads)
    for which, ref in enumerate((k_ref, v_ref)):
        copies[which].wait()
        for block in range(blocks):
            ordered = reorder(order, ref[block * 2 * half:(block + 1) * 2 * half])
            kept_ref[block, which] = jnp.where(first, ordered[:half], ordered[half:])
            given_ref[block, which] = jnp.where(first, ordered[half:], ordered[:half])


def outgoing_kernel(plan_ref, blocks_ref, *refs, first):
    out_ref, sems = refs[-2:]
    copies = []
    for group in range(out_ref.shape[0]):
        place = plan_ref[first + group]
        source = blocks_ref.at[jnp.maximum(place, 0)]
        copy = pltpu.make_async_copy(source, out_ref.at[group], sems.at[group])
        copies.append((place >= 0, copy))
    for wanted, copy in copies:
        pl.when(wanted)(copy.start)
    for wanted, copy in copies:
        pl.when(wanted)(copy.wait)


def giving_kernel(plan_ref, arrived_ref, *out_refs, give_at):
    block = 0
    for out_ref in out_refs:
        for at in range(out_ref.shape[0]):
            out_ref[at] = arrived_ref[plan_ref[give_at + block]]
            block += 1


def returning_kernel(plan_ref, blocks_ref, _, out_ref, sems, *, give_at):
    copies = [
        pltpu.make_async_copy(
            blocks_ref.at[block], out_ref.at[plan_ref[give_at + block]], sems.at[block]
        )
        for block in range(blocks_ref.shape[0])
    ]
    for copy in copies:
        copy.start()
    for copy in copies:
        copy.wait()


def near_kernel(
    q_ref, g_ref, kept_ref, given_ref, stat_ref, *, heads, kv_heads, score_scale
):
    blocks = stat_ref.shape[0]
    rows = q_ref.shape[0] // blocks
    place = kept_ref.shape[2] // kv_heads
    token, lane_head = lanes(rows, heads, kv_heads)
    key = lax.broadcasted_iota(jnp.int32, (2 * place, rows), 0)
    mine = lax.axis_index("uly")
    part = jnp.where(key < place, mine, 1 - mine)
    causal = key % place + part * place <= token
    for block in range(blocks):
        span = slice(block * rows, (block + 1) * rows)
        pieces = []
        for which, ref in enumerate((q_ref, g_ref)):
            both = jnp.concatenate([kept_ref[block, which], given_ref[block, which]], axis=0)
            full = dot_last(both, ref[span])
            half = full.shape[0] // 2
            pieces.append(
                jnp.concatenate(
                    [
                        own_head(full[:half], lane_head, kv_heads),
                        own_head(full[half:], lane_head, kv_heads),
                    ],
                    axis=0,
                )
            )
        scores = jnp.where(causal, pieces[0] * score_scale, HIDDEN)
        highest = jnp.max(scores, axis=0, keepdims=True)
        raised = jnp.exp(scores - highest)
        stat_ref[block, 0:1] = highest
        stat_ref[block, 1:2] = jnp.sum(raised, axis=0, keepdims=True)
        stat_ref[block, 2:3] = jnp.sum(raised * pieces[1], axis=0, keepdims=True)


def far_scores(part_ref, at, q, g, seen, lane_head, kv_heads, score_scale):
    hidden = jnp.where(seen > 0, 0.0, HIDDEN)
    scores = own_head(dot_last(part_ref[at, 0], q), lane_head, kv_heads) * score_scale + hidden
    return scores, own_head(dot_last(part_ref[at, 1], g), lane_head, kv_heads)


def merged(stat_ref, block, scores, dprobs):
    before = stat_ref[block, 0:1]
    highest = jnp.maximum(before, jnp.max(scores, axis=0, keepdims=True))
    raised = jnp.exp(scores - highest)
    shrink = jnp.exp(before - highest)
    total = shrink * stat_ref[block, 1:2] + jnp.sum(raised, axis=0, keepdims=True)
    delta = shrink * stat_ref[block, 2:3] + jnp.sum(raised * dprobs, axis=0, keepdims=True)
    return highest, raised, total, delta


def far_gradients(probs, dprobs, delta, q, g, lane_head, kv_heads, score_scale):
    dscores = (probs * (dprobs - delta)).astype(BF16)
    dk = jnp.dot(all_heads(dscores, lane_head, kv_heads), q, preferred_element_type=F32)
    dv = jnp.dot(all_heads(probs.astype(BF16), lane_head, kv_heads), g, preferred_element_type=F32)
    return (dk * score_scale).astype(BF16), dv.astype(BF16)


def mid_kernel(
    plan_ref, q_ref, g_ref, stat_ref, arrived_ref, out_ref,
    *, heads, kv_heads, score_scale, source_at, seen_at
):
    blocks = stat_ref.shape[0]
    rows = q_ref.shape[0] // blocks
    _, lane_head = lanes(rows, heads, kv_heads)
    for block in range(blocks):
        span = slice(block * rows, (block + 1) * rows)
        scores, dprobs = far_scores(
            arrived_ref, plan_ref[source_at + block], q_ref[span], g_ref[span],
            plan_ref[seen_at + block],            lane_head, kv_heads, score_scale,
        )
        highest, _, total, delta = merged(stat_ref, block, scores, dprobs)
        out_ref[block, 0:1] = highest
        out_ref[block, 1:2] = total
        out_ref[block, 2:3] = delta


def far_kernel(
    plan_ref, q_ref, g_ref, stat_ref, other_ref, grad_ref, out_ref,
    *, heads, kv_heads, score_scale, seen_at, first
):
    rows = q_ref.shape[0] // stat_ref.shape[0]
    _, lane_head = lanes(rows, heads, kv_heads)
    for at in range(other_ref.shape[0]):
        block = first + at
        span = slice(block * rows, (block + 1) * rows)
        q = q_ref[span]
        g = g_ref[span]
        scores, dprobs = far_scores(
            other_ref, at, q, g, plan_ref[seen_at + block], lane_head, kv_heads, score_scale
        )
        highest, raised, total, delta = merged(stat_ref, block, scores, dprobs)
        inverse = 1.0 / total
        delta = delta * inverse
        grad_ref[at, 0], grad_ref[at, 1] = far_gradients(
            raised * inverse, dprobs, delta, q, g, lane_head, kv_heads, score_scale
        )
        out_ref[at, 0:1] = highest
        out_ref[at, 1:2] = inverse
        out_ref[at, 2:3] = delta


def mine_kernel(
    plan_ref, q_ref, g_ref, arrived_ref, *refs, heads, kv_heads, score_scale, source_at, seen_at
):
    stat_refs, (out_ref, grad_ref, sems) = refs[:-3], refs[-3:]
    blocks = grad_ref.shape[0]
    chunk = blocks // len(stat_refs)
    rows = q_ref.shape[0] // blocks
    _, lane_head = lanes(rows, heads, kv_heads)
    copies = []
    for block in range(blocks):
        span = slice(block * rows, (block + 1) * rows)
        q = q_ref[span]
        g = g_ref[span]
        stat_ref = stat_refs[block // chunk]
        at = block % chunk
        source = plan_ref[source_at + block]
        scores, dprobs = far_scores(
            arrived_ref, source, q, g, plan_ref[seen_at + block], lane_head, kv_heads, score_scale
        )
        probs = jnp.exp(scores - stat_ref[at, 0:1]) * stat_ref[at, 1:2]
        grad_ref[block, 0], grad_ref[block, 1] = far_gradients(
            probs, dprobs, stat_ref[at, 2:3], q, g, lane_head, kv_heads, score_scale
        )
        copies.append(
            pltpu.make_async_copy(grad_ref.at[block], out_ref.at[source], sems.at[block])
        )
        copies[-1].start()
    for copy in copies:
        copy.wait()


def local_kernel(
    plan_ref, q_ref, g_ref, k_ref, v_ref, mine_ref, other_ref,
    att_ref, dq_ref, dk_ref, dv_ref, bias_ref, *, heads, kv_heads, score_scale, seen_at
):
    step = pl.program_id(0)
    rows = q_ref.shape[0]
    cols = k_ref.shape[0]

    @pl.when(step == 0)
    def _():
        half = cols // 2
        place = half // kv_heads
        row = lax.broadcasted_iota(jnp.int32, (rows, cols), 0)
        col = lax.broadcasted_iota(jnp.int32, (rows, cols), 1)
        same = row % heads // (heads // kv_heads) == col % half // place
        causal = col // half * place + col % place <= row // heads
        bias_ref[:, :cols] = jnp.where(same & causal, 0.0, HIDDEN)
        bias_ref[:, cols:] = jnp.where(same, 0.0, HIDDEN)

    far_bias = jnp.where(plan_ref[seen_at + step] > 0, 0.0, HIDDEN)
    order = head_major(cols, kv_heads)
    k_near = reorder(order, k_ref[...])
    v_near = reorder(order, v_ref[...])
    k_all = jnp.concatenate([k_near, mine_ref[0, 0], other_ref[0, 0]], axis=0)
    v_all = jnp.concatenate([v_near, mine_ref[0, 1], other_ref[0, 1]], axis=0)
    q = q_ref[...]
    g = g_ref[...]
    scores = dot_last(q, k_all) * score_scale + bias_ref[...]
    scores = jnp.concatenate([scores[:, :cols], scores[:, cols:] + far_bias], axis=1)
    highest = jnp.max(scores, axis=1, keepdims=True)
    raised = jnp.exp(scores - highest)
    total = jnp.sum(raised, axis=1, keepdims=True)
    probs = raised * (1.0 / total)
    weights = probs.astype(BF16)
    attended = jnp.dot(weights, v_all, preferred_element_type=F32).astype(BF16)
    att_ref[...] = attended
    delta = jnp.sum(g.astype(F32) * attended.astype(F32), axis=1, keepdims=True)
    dscores = (probs * (dot_last(g, v_all) - delta)).astype(BF16)
    dq = jnp.dot(dscores, k_all, preferred_element_type=F32) * score_scale
    dq_ref[...] = dq.astype(BF16)
    dk_ref[...] = dot_first(dscores[:, :cols], q) * score_scale
    dv_ref[...] = dot_first(weights[:, :cols], g)


def landing_kernel(plan_ref, landed_ref, out_ref, sum_ref, *, first):
    sum_ref[...] = jnp.zeros_like(sum_ref)
    for group in range(landed_ref.shape[0]):
        place = plan_ref[first + group]

        @pl.when(place >= 0)
        def _():
            sum_ref[place] = sum_ref[place] + landed_ref[group].astype(F32)

    out_ref[...] = sum_ref[...].astype(out_ref.dtype)


def finish_kernel(
    dk_near_ref, dv_near_ref, own_ref, back_ref, dk_ref, dv_ref, *, kv_heads
):
    blocks, _, half, _ = back_ref.shape
    mine = lax.axis_index("uly") == 0
    order = head_major(2 * half, kv_heads)
    for block in range(blocks):
        span = slice(block * 2 * half, (block + 1) * 2 * half)
        for near_ref, out_ref, which in ((dk_near_ref, dk_ref, 0), (dv_near_ref, dv_ref, 1)):
            own = own_ref[block, which]
            back = back_ref[block, which].astype(F32)
            far = jnp.concatenate([jnp.where(mine, own, back), jnp.where(mine, back, own)], axis=0)
            summed = (near_ref[span] + far).astype(BF16)
            out_ref[span] = dot_first(order, summed).astype(BF16)


def take_rows(array, index):
    return array.at[index].get(mode="promise_in_bounds")


def whole_blocks(queries, keys, values, output_cotangent, block_lists, list_counts):
    grp_count = lax.axis_size("grp")
    uly_count = lax.axis_size("uly")
    tokens, heads, width = queries.shape
    kv_heads = keys.shape[1]
    per_group = block_lists.shape[0] // grp_count
    block_tok = tokens * uly_count // per_group
    mine_blocks = tokens // block_tok
    rows = block_tok * heads
    cols = block_tok * kv_heads
    half = cols // 2
    sizes = dict(heads=heads, kv_heads=kv_heads, score_scale=width ** (-0.5))
    swap = [(0, 1), (1, 0)]

    sib_at, source_at, give_at, seen_at = plan_spans(grp_count, mine_blocks)

    q2 = queries.reshape(tokens * heads, width)
    g2 = output_cotangent.reshape(tokens * heads, width)
    k2 = keys.reshape(tokens * kv_heads, width)
    v2 = values.reshape(tokens * kv_heads, width)

    part_shape = jax.ShapeDtypeStruct((mine_blocks, 2, half, width), BF16)
    slot_shape = pltpu.HBM((grp_count, 2, half, width), BF16)
    stat_shape = jax.ShapeDtypeStruct((mine_blocks, 8, rows), F32)
    row_shape = jax.ShapeDtypeStruct(q2.shape, BF16)
    near_shape = jax.ShapeDtypeStruct(k2.shape, F32)
    small_shape = jax.ShapeDtypeStruct(k2.shape, BF16)
    sum_scratch = [pltpu.VMEM((mine_blocks, 2, half, width), F32)]
    slot_sems = [pltpu.SemaphoreType.DMA((grp_count,))]
    limit = pltpu.CompilerParams(vmem_limit_bytes=24 * 1024 * 1024)
    vmem = pl.BlockSpec(memory_space=pltpu.VMEM)
    smem = pl.BlockSpec(memory_space=pltpu.SMEM)
    anywhere = pl.BlockSpec(memory_space=pltpu.HBM)

    def call(kernel, name, scalars, operands, out_shape, scratch=(), into=None, out_spec=vmem):
        extra = () if into is None else (into,)
        return pl.pallas_call(
            kernel,
            in_specs=[smem] * len(scalars) + [vmem] * len(operands) + [anywhere] * len(extra),
            out_specs=jax.tree.map(lambda _: out_spec, out_shape),
            out_shape=out_shape,
            scratch_shapes=scratch,
            input_output_aliases={len(scalars) + len(operands): 0} if extra else {},
            compiler_params=limit,
            name=name,
        )(*scalars, *operands, *extra)

    def in_hbm(array):
        return pltpu.with_memory_space_constraint(array, pltpu.HBM)

    kept, given = pl.pallas_call(
        partial(pack_kernel, kv_heads=kv_heads),
        in_specs=[anywhere, anywhere],
        out_specs=[vmem, vmem],
        out_shape=[part_shape, part_shape],
        scratch_shapes=[
            pltpu.VMEM(k2.shape, BF16), pltpu.VMEM(k2.shape, BF16), pltpu.SemaphoreType.DMA((2,))
        ],
        compiler_params=limit,
        name="pack",
    )(in_hbm(k2), in_hbm(v2))
    plan = pl.pallas_call(
        partial(plan_kernel, grp_count=grp_count, blocks=mine_blocks),
        in_specs=[smem, smem],
        out_specs=smem,
        out_shape=pltpu.SMEM((seen_at + mine_blocks,), jnp.int32),
        compiler_params=limit,
        name="plan",
    )(in_hbm(block_lists.reshape(-1)), in_hbm(list_counts))
    gotten = lax.ppermute(given, "uly", swap)
    outgoing = call(
        partial(outgoing_kernel, first=0), "send_own", (plan,), (kept,),
        slot_shape, slot_sems, out_spec=anywhere,
    )
    outgoing = call(
        partial(outgoing_kernel, first=sib_at), "send_sibling", (plan,), (gotten,),
        slot_shape, slot_sems, into=outgoing, out_spec=anywhere,
    )
    outgoing, given = lax.optimization_barrier((outgoing, given))
    arrived = lax.all_to_all(outgoing, "grp", split_axis=0, concat_axis=0, tiled=True)
    stats = call(
        partial(near_kernel, **sizes), "near", (), (q2, g2, kept, given), stat_shape
    )
    arrived, stats = lax.optimization_barrier((arrived, stats))
    chunks = 2 if mine_blocks % 2 == 0 else 1
    chunk = mine_blocks // chunks
    chunk_shape = jax.ShapeDtypeStruct((chunk, 2, half, width), BF16)
    giving = call(
        partial(giving_kernel, give_at=give_at), "give", (plan,), (arrived,),
        [chunk_shape] * chunks,
    )
    others = [lax.ppermute(part, "uly", swap) for part in giving]
    stats = call(
        partial(mid_kernel, source_at=source_at, seen_at=seen_at, **sizes), "mid", (plan,),
        (q2, g2, stats, arrived), stat_shape,
    )
    grads, final = [], []
    for at, other in enumerate(others):
        if grads:
            other, grads[-1] = lax.optimization_barrier((other, grads[-1]))
        grad, stat = call(
            partial(far_kernel, seen_at=seen_at, first=at * chunk, **sizes), "far", (plan,),
            (q2, g2, stats, other),
            [chunk_shape, jax.ShapeDtypeStruct((chunk, 8, rows), F32)],
        )
        grads.append(grad)
        final.append(stat)
    from_sib = [lax.ppermute(part, "uly", swap) for part in grads]
    if chunks > 1:
        from_sib[0], final[-1] = lax.optimization_barrier((from_sib[0], final[-1]))
    returning = call(
        partial(mine_kernel, source_at=source_at, seen_at=seen_at, **sizes), "mine", (plan,),
        (q2, g2, arrived, *final), slot_shape,
        [pltpu.VMEM(part_shape.shape, BF16), pltpu.SemaphoreType.DMA((mine_blocks,))],
        out_spec=anywhere,
    )
    for at, part in enumerate(from_sib):
        returning = call(
            partial(returning_kernel, give_at=give_at + at * chunk), "return_sibling", (plan,),
            (part,), slot_shape, [pltpu.SemaphoreType.DMA((chunk,))], into=returning,
            out_spec=anywhere,
        )
    other = jnp.concatenate(others)
    returning, k2l = lax.optimization_barrier((returning, k2))
    landed = lax.all_to_all(returning, "grp", split_axis=0, concat_axis=0, tiled=True)

    def step_rows(i, *_):
        return (i, 0)

    def step_part(i, *_):
        return (i, 0, 0, 0)

    def from_source(i, plan_ref):
        return (plan_ref[source_at + i], 0, 0, 0)

    row_spec = pl.BlockSpec((rows, width), step_rows)
    col_spec = pl.BlockSpec((cols, width), step_rows)
    attended, dq, dk_near, dv_near = pl.pallas_call(
        partial(local_kernel, seen_at=seen_at, **sizes),
        grid_spec=pltpu.PrefetchScalarGridSpec(
            num_scalar_prefetch=1,
            grid=(mine_blocks,),
            in_specs=[
                row_spec, row_spec, col_spec, col_spec,
                pl.BlockSpec((1, 2, half, width), from_source),
                pl.BlockSpec((1, 2, half, width), step_part),
            ],
            out_specs=[row_spec, row_spec, col_spec, col_spec],
            scratch_shapes=[pltpu.VMEM((rows, 2 * cols), F32)],
        ),
        out_shape=[row_shape, row_shape, near_shape, near_shape],
        compiler_params=limit,
        name="local",
    )(plan, q2, g2, k2l, v2, arrived, other)
    landed, dk_near = lax.optimization_barrier((landed, dk_near))
    give = call(
        partial(landing_kernel, first=sib_at), "land_sibling", (plan,), (landed,), part_shape,
        sum_scratch,
    )
    back = lax.ppermute(give, "uly", swap)
    own = call(
        partial(landing_kernel, first=0), "land_own", (plan,), (landed,),
        jax.ShapeDtypeStruct(part_shape.shape, F32), sum_scratch,
    )
    dk, dv = call(
        partial(finish_kernel, kv_heads=kv_heads), "finish", (),
        (dk_near, dv_near, own, back), [small_shape, small_shape],
    )
    return (
        attended.reshape(queries.shape), dq.reshape(queries.shape),
        dk.reshape(keys.shape), dv.reshape(keys.shape),
    )


def on_device(queries, keys, values, output_cotangent, block_lists, list_counts):
    uly_count = lax.axis_size("uly")
    grp_count = lax.axis_size("grp")
    blocks_all, remote = block_lists.shape
    block_tok = queries.shape[0] * uly_count * grp_count // blocks_all
    held_whole = queries.shape[0] % block_tok == 0
    run = whole_blocks if held_whole and remote == 1 and uly_count == 2 else spread_blocks
    return run(queries, keys, values, output_cotangent, block_lists, list_counts)


def solution(mesh):
    placed = (
        P(("grp", "uly"), None, None),
        P(("grp", "uly"), None, None),
        P(("grp", "uly"), None, None),
        P(("grp", "uly"), None, None),
        P(),
        P(),
    )
    return jax.shard_map(
        on_device,
        mesh=mesh,
        in_specs=placed,
        out_specs=(
            P(("grp", "uly"), None, None),
            P(("grp", "uly"), None, None),
            P(("grp", "uly"), None, None),
            P(("grp", "uly"), None, None),
        ),
        check_vma=False,
    )
```

```python
from functools import partial

import jax
import jax.numpy as jnp
from jax import lax
from jax.experimental import pallas as pl
from jax.experimental.pallas import tpu as pltpu
from jax.sharding import PartitionSpec as P


def spread_blocks(queries, keys, values, output_cotangent, block_lists, list_counts):
    uly_count = lax.axis_size("uly")
    grp_count = lax.axis_size("grp")
    my_group = lax.axis_index("grp")
    tokens, head_count, head_width = queries.shape
    kv_heads = keys.shape[1]
    copies = max(1, uly_count // kv_heads)
    blocks_all, remote = block_lists.shape
    per_group = blocks_all // grp_count
    block_tok = tokens * uly_count // per_group
    group_tok = tokens * uly_count
    score_scale = head_width ** (-0.5)
    lists = block_lists.reshape(grp_count, per_group, remote)
    counted = (jnp.arange(remote)[None, :] < list_counts[:, None]).reshape(
        grp_count, per_group, remote
    )
    wanted = (lists // per_group == my_group) & counted
    send_place = jnp.sum(jnp.where(wanted, lists % per_group, 0), axis=(1, 2))
    sending = jnp.any(wanted, axis=(1, 2))
    mine_source = lax.dynamic_index_in_dim(lists, my_group, 0, keepdims=False) // per_group
    mine_counted = lax.dynamic_index_in_dim(counted, my_group, 0, keepdims=False)
    trip_count = jnp.max(jnp.sum(mine_counted.astype(jnp.int32), axis=1))

    def to_blocks(array_in):
        return array_in.reshape((per_group, block_tok) + array_in.shape[1:])

    keys_wide = jnp.repeat(keys, copies, axis=1)
    values_wide = jnp.repeat(values, copies, axis=1)
    query_heads, grad_heads, key_heads, value_heads = (
        lax.all_to_all(queries, "uly", split_axis=1, concat_axis=0, tiled=True),
        lax.all_to_all(output_cotangent, "uly", split_axis=1, concat_axis=0, tiled=True),
        lax.all_to_all(keys_wide, "uly", split_axis=1, concat_axis=0, tiled=True),
        lax.all_to_all(values_wide, "uly", split_axis=1, concat_axis=0, tiled=True),
    )
    stacked = jnp.stack([to_blocks(key_heads), to_blocks(value_heads)])
    outgoing = jnp.take(stacked, send_place, axis=1)
    arrived = lax.all_to_all(outgoing, "grp", split_axis=1, concat_axis=1, tiled=True)
    kv_local = key_heads.shape[1]
    heads_local = query_heads.shape[1]
    heads_per_group = heads_local // kv_local
    query_blk = query_heads.reshape(per_group, block_tok, kv_local, heads_per_group, head_width)
    grad_blk = grad_heads.reshape(per_group, block_tok, kv_local, heads_per_group, head_width)
    key_blk = to_blocks(key_heads)
    value_blk = to_blocks(value_heads)
    far_keys = arrived[0]
    far_values = arrived[1]
    causal = jnp.arange(block_tok)[:, None] >= jnp.arange(block_tok)[None, :]

    def logits(key_rows):
        return (
            jnp.einsum("pqkgd,pjkd->pkgqj", query_blk, key_rows, preferred_element_type=jnp.float32)
            * score_scale
        )

    def slot_rows(slot_index):
        source = lax.dynamic_index_in_dim(mine_source, slot_index, 1, keepdims=False)
        counted_slot = lax.dynamic_index_in_dim(mine_counted, slot_index, 1, keepdims=False)
        return (
            jnp.take(far_keys, source, axis=0),
            jnp.take(far_values, source, axis=0),
            counted_slot,
            source,
        )

    def masked(scores, counted_slot):
        return jnp.where(counted_slot[:, None, None, None, None], scores, -jnp.inf)

    near_scores = jnp.where(causal, logits(key_blk), -jnp.inf)
    highest = jnp.max(near_scores, axis=-1)
    denominator = jnp.sum(jnp.exp(near_scores - highest[..., None]), axis=-1)

    def max_sweep(slot_index, state_pair):
        highest, denominator = state_pair
        key_rows, value_rows, counted_slot, source = slot_rows(slot_index)
        scores = masked(logits(key_rows), counted_slot)
        new_highest = jnp.maximum(highest, jnp.max(scores, axis=-1))
        denominator = denominator * jnp.exp(highest - new_highest) + jnp.sum(
            jnp.exp(scores - new_highest[..., None]), axis=-1
        )
        return (new_highest, denominator)

    highest, denominator = lax.fori_loop(0, trip_count, max_sweep, (highest, denominator))
    log_total = highest + jnp.log(denominator)

    def softmax_weights(scores):
        return jnp.exp(scores - log_total[..., None])

    summed = jnp.einsum(
        "pkgqj,pjkd->pqkgd",
        softmax_weights(near_scores).astype(jnp.bfloat16),
        value_blk,
        preferred_element_type=jnp.float32,
    )

    def value_sweep(slot_index, summed):
        key_rows, value_rows, counted_slot, source = slot_rows(slot_index)
        weights = softmax_weights(masked(logits(key_rows), counted_slot)).astype(jnp.bfloat16)
        return summed + jnp.einsum(
            "pkgqj,pjkd->pqkgd", weights, value_rows, preferred_element_type=jnp.float32
        )

    summed = lax.fori_loop(0, trip_count, value_sweep, summed)
    attended_blk = summed.astype(jnp.bfloat16)
    row_delta = jnp.transpose(
        jnp.sum(grad_blk.astype(jnp.float32) * attended_blk.astype(jnp.float32), axis=-1),
        (0, 2, 3, 1),
    )

    def backward(scores, key_rows, value_rows):
        probs = softmax_weights(scores)
        weights = probs.astype(jnp.bfloat16)
        dprobs = jnp.einsum(
            "pqkgd,pjkd->pkgqj", grad_blk, value_rows, preferred_element_type=jnp.float32
        )
        dscores = (probs * (dprobs - row_delta[..., None])).astype(jnp.bfloat16)
        query_term = jnp.einsum(
            "pkgqj,pjkd->pqkgd", dscores, key_rows, preferred_element_type=jnp.float32
        )
        key_term = (
            jnp.einsum("pkgqj,pqkgd->pjkd", dscores, query_blk, preferred_element_type=jnp.float32)
            * score_scale
        )
        value_term = jnp.einsum(
            "pkgqj,pqkgd->pjkd", weights, grad_blk, preferred_element_type=jnp.float32
        )
        return (query_term, key_term, value_term)

    query_sum, key_near, value_near = backward(near_scores, key_blk, value_blk)
    far_grads = jnp.zeros((2, grp_count, block_tok, kv_local, head_width), jnp.float32)

    def grad_sweep(slot_index, state_pair):
        query_sum, far_grads = state_pair
        key_rows, value_rows, counted_slot, source = slot_rows(slot_index)
        query_term, key_term, value_term = backward(
            masked(logits(key_rows), counted_slot), key_rows, value_rows
        )
        routing = (
            (source[:, None] == jnp.arange(grp_count)[None, :]) & counted_slot[:, None]
        ).astype(jnp.float32)
        routed = jnp.einsum(
            "ps,xpjkd->xsjkd",
            routing,
            jnp.stack([key_term, value_term]),
            precision=lax.Precision.HIGHEST,
        )
        return (query_sum + query_term, far_grads + routed)

    query_sum, far_grads = lax.fori_loop(0, trip_count, grad_sweep, (query_sum, far_grads))
    owners = ((send_place[:, None] == jnp.arange(per_group)[None, :]) & sending[:, None]).astype(
        jnp.float32
    )
    returned = lax.all_to_all(far_grads, "grp", split_axis=1, concat_axis=1, tiled=True)
    landed = jnp.einsum("sp,xsjkd->xpjkd", owners, returned, precision=lax.Precision.HIGHEST)
    key_local = (key_near + landed[0]).reshape(group_tok, kv_local, head_width)
    value_local = (value_near + landed[1]).reshape(group_tok, kv_local, head_width)
    attended_rows = attended_blk.reshape(group_tok, heads_local, head_width)
    query_rows = (
        (query_sum * score_scale).astype(jnp.bfloat16).reshape(group_tok, heads_local, head_width)
    )
    attended, query_grad = (
        lax.all_to_all(attended_rows, "uly", split_axis=0, concat_axis=1, tiled=True),
        lax.all_to_all(query_rows, "uly", split_axis=0, concat_axis=1, tiled=True),
    )
    key_parts, value_parts = (
        lax.all_to_all(key_local, "uly", split_axis=0, concat_axis=1, tiled=True),
        lax.all_to_all(value_local, "uly", split_axis=0, concat_axis=1, tiled=True),
    )
    key_gradient = jnp.sum(key_parts.reshape(tokens, kv_heads, copies, head_width), axis=2).astype(
        jnp.bfloat16
    )
    value_gradient = jnp.sum(
        value_parts.reshape(tokens, kv_heads, copies, head_width), axis=2
    ).astype(jnp.bfloat16)
    return (attended, query_grad, key_gradient, value_gradient)


HIDDEN = -1e30
LAST = (((1,), (1,)), ((), ()))
FIRST = (((0,), (0,)), ((), ()))
F32 = jnp.float32
BF16 = jnp.bfloat16


def dot_last(left, right):
    return lax.dot_general(left, right, LAST, preferred_element_type=F32)


def dot_first(left, right):
    return lax.dot_general(left, right, FIRST, preferred_element_type=F32)


def head_major(cols, kv_heads):
    half = cols // 2
    place = half // kv_heads
    row = lax.broadcasted_iota(jnp.int32, (cols, cols), 0)
    col = lax.broadcasted_iota(jnp.int32, (cols, cols), 1)
    token = row // half * place + row % place
    return jnp.where(col == token * kv_heads + row % half // place, 1.0, 0.0).astype(BF16)


def reorder(one_hot, array):
    return jnp.dot(one_hot, array, preferred_element_type=F32).astype(BF16)


def own_head(scores, lane_head, kv_heads):
    place = scores.shape[0] // kv_heads
    kept = scores[:place]
    for head in range(1, kv_heads):
        kept = jnp.where(lane_head == head, scores[head * place:(head + 1) * place], kept)
    return kept


def all_heads(kept, lane_head, kv_heads):
    none = jnp.zeros_like(kept)
    return jnp.concatenate(
        [jnp.where(lane_head == head, kept, none) for head in range(kv_heads)], axis=0
    )


def lanes(rows, heads, kv_heads):
    lane = lax.broadcasted_iota(jnp.int32, (1, rows), 1)
    return lane // heads, lane % heads // (heads // kv_heads)


def plan_spans(grp_count, blocks):
    return grp_count, 2 * grp_count, 2 * grp_count + blocks, 2 * grp_count + 2 * blocks


def plan_kernel(lists_ref, counts_ref, plan_ref, *, grp_count, blocks):
    group, mine = lax.axis_index("grp"), lax.axis_index("uly")
    per_group = 2 * blocks
    low = group * per_group
    sib_at, source_at, give_at, seen_at = plan_spans(grp_count, blocks)
    for other in range(grp_count):
        place = jnp.int32(-1)
        for at in range(other * per_group, (other + 1) * per_group):
            here = lists_ref[at] - low
            wanted = (here >= 0) & (here < per_group) & (counts_ref[at] > 0)
            place = jnp.where(wanted, here, place)
        own = place - mine * blocks
        sib = place - (1 - mine) * blocks
        plan_ref[other] = jnp.where((own >= 0) & (own < blocks), own, -1)
        plan_ref[sib_at + other] = jnp.where((sib >= 0) & (sib < blocks), sib, -1)
    for block in range(blocks):
        at = low + mine * blocks + block
        plan_ref[source_at + block] = lax.div(lists_ref[at], per_group)
        plan_ref[seen_at + block] = counts_ref[at]
        at = low + (1 - mine) * blocks + block
        plan_ref[give_at + block] = lax.div(lists_ref[at], per_group)


def pack_kernel(k_hbm, v_hbm, kept_ref, given_ref, k_ref, v_ref, sems, *, kv_heads):
    blocks, _, half, _ = kept_ref.shape
    copies = [
        pltpu.make_async_copy(k_hbm, k_ref, sems.at[0]),
        pltpu.make_async_copy(v_hbm, v_ref, sems.at[1]),
    ]
    for copy in copies:
        copy.start()
    first = lax.axis_index("uly") == 0
    order = head_major(2 * half, kv_heads)
    for which, ref in enumerate((k_ref, v_ref)):
        copies[which].wait()
        for block in range(blocks):
            ordered = reorder(order, ref[block * 2 * half:(block + 1) * 2 * half])
            kept_ref[block, which] = jnp.where(first, ordered[:half], ordered[half:])
            given_ref[block, which] = jnp.where(first, ordered[half:], ordered[:half])


def outgoing_kernel(plan_ref, blocks_ref, *refs, first):
    out_ref, sems = refs[-2:]
    copies = []
    for group in range(out_ref.shape[0]):
        place = plan_ref[first + group]
        source = blocks_ref.at[jnp.maximum(place, 0)]
        copy = pltpu.make_async_copy(source, out_ref.at[group], sems.at[group])
        copies.append((place >= 0, copy))
    for wanted, copy in copies:
        pl.when(wanted)(copy.start)
    for wanted, copy in copies:
        pl.when(wanted)(copy.wait)


def giving_kernel(plan_ref, arrived_ref, *out_refs, give_at):
    block = 0
    for out_ref in out_refs:
        for at in range(out_ref.shape[0]):
            out_ref[at] = arrived_ref[plan_ref[give_at + block]]
            block += 1


def returning_kernel(plan_ref, *refs, give_at):
    part_refs, (out_ref, sems) = refs[:-3], refs[-2:]
    copies = []
    for part_ref in part_refs:
        for at in range(part_ref.shape[0]):
            block = len(copies)
            target = out_ref.at[plan_ref[give_at + block]]
            copies.append(pltpu.make_async_copy(part_ref.at[at], target, sems.at[block]))
            copies[-1].start()
    for copy in copies:
        copy.wait()


def near_kernel(
    q_ref, g_ref, kept_ref, given_ref, stat_ref, *, heads, kv_heads, score_scale
):
    blocks = stat_ref.shape[0]
    rows = q_ref.shape[0] // blocks
    place = kept_ref.shape[2] // kv_heads
    token, lane_head = lanes(rows, heads, kv_heads)
    key = lax.broadcasted_iota(jnp.int32, (2 * place, rows), 0)
    mine = lax.axis_index("uly")
    part = jnp.where(key < place, mine, 1 - mine)
    causal = key % place + part * place <= token
    for block in range(blocks):
        span = slice(block * rows, (block + 1) * rows)
        pieces = []
        for which, ref in enumerate((q_ref, g_ref)):
            both = jnp.concatenate([kept_ref[block, which], given_ref[block, which]], axis=0)
            full = dot_last(both, ref[span])
            half = full.shape[0] // 2
            pieces.append(
                jnp.concatenate(
                    [
                        own_head(full[:half], lane_head, kv_heads),
                        own_head(full[half:], lane_head, kv_heads),
                    ],
                    axis=0,
                )
            )
        scores = jnp.where(causal, pieces[0] * score_scale, HIDDEN)
        highest = jnp.max(scores, axis=0, keepdims=True)
        raised = jnp.exp(scores - highest)
        stat_ref[block, 0:1] = highest
        stat_ref[block, 1:2] = jnp.sum(raised, axis=0, keepdims=True)
        stat_ref[block, 2:3] = jnp.sum(raised * pieces[1], axis=0, keepdims=True)


def far_scores(part_ref, at, q, g, seen, lane_head, kv_heads, score_scale):
    hidden = jnp.where(seen > 0, 0.0, HIDDEN)
    scores = own_head(dot_last(part_ref[at, 0], q), lane_head, kv_heads) * score_scale + hidden
    return scores, own_head(dot_last(part_ref[at, 1], g), lane_head, kv_heads)


def merged(stat_ref, block, scores, dprobs):
    before = stat_ref[block, 0:1]
    highest = jnp.maximum(before, jnp.max(scores, axis=0, keepdims=True))
    raised = jnp.exp(scores - highest)
    shrink = jnp.exp(before - highest)
    total = shrink * stat_ref[block, 1:2] + jnp.sum(raised, axis=0, keepdims=True)
    delta = shrink * stat_ref[block, 2:3] + jnp.sum(raised * dprobs, axis=0, keepdims=True)
    return highest, raised, total, delta


def far_gradients(probs, dprobs, delta, q, g, lane_head, kv_heads, score_scale):
    dscores = (probs * (dprobs - delta)).astype(BF16)
    dk = jnp.dot(all_heads(dscores, lane_head, kv_heads), q, preferred_element_type=F32)
    dv = jnp.dot(all_heads(probs.astype(BF16), lane_head, kv_heads), g, preferred_element_type=F32)
    return (dk * score_scale).astype(BF16), dv.astype(BF16)


def mid_kernel(
    plan_ref, q_ref, g_ref, stat_ref, arrived_ref, out_ref,
    *, heads, kv_heads, score_scale, source_at, seen_at
):
    blocks = stat_ref.shape[0]
    rows = q_ref.shape[0] // blocks
    _, lane_head = lanes(rows, heads, kv_heads)
    for block in range(blocks):
        span = slice(block * rows, (block + 1) * rows)
        scores, dprobs = far_scores(
            arrived_ref, plan_ref[source_at + block], q_ref[span], g_ref[span],
            plan_ref[seen_at + block],            lane_head, kv_heads, score_scale,
        )
        highest, _, total, delta = merged(stat_ref, block, scores, dprobs)
        out_ref[block, 0:1] = highest
        out_ref[block, 1:2] = total
        out_ref[block, 2:3] = delta


def far_kernel(
    plan_ref, q_ref, g_ref, stat_ref, other_ref, grad_ref, out_ref,
    *, heads, kv_heads, score_scale, seen_at, first
):
    rows = q_ref.shape[0] // stat_ref.shape[0]
    _, lane_head = lanes(rows, heads, kv_heads)
    for at in range(other_ref.shape[0]):
        block = first + at
        span = slice(block * rows, (block + 1) * rows)
        q = q_ref[span]
        g = g_ref[span]
        scores, dprobs = far_scores(
            other_ref, at, q, g, plan_ref[seen_at + block], lane_head, kv_heads, score_scale
        )
        highest, raised, total, delta = merged(stat_ref, block, scores, dprobs)
        inverse = 1.0 / total
        delta = delta * inverse
        grad_ref[at, 0], grad_ref[at, 1] = far_gradients(
            raised * inverse, dprobs, delta, q, g, lane_head, kv_heads, score_scale
        )
        out_ref[at, 0:1] = highest
        out_ref[at, 1:2] = inverse
        out_ref[at, 2:3] = delta


def mine_kernel(
    plan_ref, q_ref, g_ref, arrived_ref, stat_ref, *refs,
    heads, kv_heads, score_scale, source_at, seen_at, rows, first
):
    out_ref, grad_ref, sems = refs[-3:]
    _, lane_head = lanes(rows, heads, kv_heads)
    copies = []
    for at in range(stat_ref.shape[0]):
        block = first + at
        span = slice(block * rows, (block + 1) * rows)
        q = q_ref[span]
        g = g_ref[span]
        source = plan_ref[source_at + block]
        scores, dprobs = far_scores(
            arrived_ref, source, q, g, plan_ref[seen_at + block], lane_head, kv_heads, score_scale
        )
        probs = jnp.exp(scores - stat_ref[at, 0:1]) * stat_ref[at, 1:2]
        grad_ref[at, 0], grad_ref[at, 1] = far_gradients(
            probs, dprobs, stat_ref[at, 2:3], q, g, lane_head, kv_heads, score_scale
        )
        copies.append(pltpu.make_async_copy(grad_ref.at[at], out_ref.at[source], sems.at[at]))
        copies[-1].start()
    for copy in copies:
        copy.wait()


def local_kernel(
    plan_ref, q_ref, g_ref, k_ref, v_ref, mine_ref, other_ref,
    att_ref, dq_ref, dk_ref, dv_ref, bias_ref, *, heads, kv_heads, score_scale, seen_at
):
    step = pl.program_id(0)
    rows = q_ref.shape[0]
    cols = k_ref.shape[0]

    @pl.when(step == 0)
    def _():
        half = cols // 2
        place = half // kv_heads
        row = lax.broadcasted_iota(jnp.int32, (rows, cols), 0)
        col = lax.broadcasted_iota(jnp.int32, (rows, cols), 1)
        same = row % heads // (heads // kv_heads) == col % half // place
        causal = col // half * place + col % place <= row // heads
        bias_ref[:, :cols] = jnp.where(same & causal, 0.0, HIDDEN)
        bias_ref[:, cols:] = jnp.where(same, 0.0, HIDDEN)

    far_bias = jnp.where(plan_ref[seen_at + step] > 0, 0.0, HIDDEN)
    order = head_major(cols, kv_heads)
    k_near = reorder(order, k_ref[...])
    v_near = reorder(order, v_ref[...])
    k_all = jnp.concatenate([k_near, mine_ref[0, 0], other_ref[0, 0]], axis=0)
    v_all = jnp.concatenate([v_near, mine_ref[0, 1], other_ref[0, 1]], axis=0)
    q = q_ref[...]
    g = g_ref[...]
    scores = dot_last(q, k_all) * score_scale + bias_ref[...]
    scores = jnp.concatenate([scores[:, :cols], scores[:, cols:] + far_bias], axis=1)
    highest = jnp.max(scores, axis=1, keepdims=True)
    raised = jnp.exp(scores - highest)
    total = jnp.sum(raised, axis=1, keepdims=True)
    probs = raised * (1.0 / total)
    weights = probs.astype(BF16)
    attended = jnp.dot(weights, v_all, preferred_element_type=F32).astype(BF16)
    att_ref[...] = attended
    delta = jnp.sum(g.astype(F32) * attended.astype(F32), axis=1, keepdims=True)
    dscores = (probs * (dot_last(g, v_all) - delta)).astype(BF16)
    dq = jnp.dot(dscores, k_all, preferred_element_type=F32) * score_scale
    dq_ref[...] = dq.astype(BF16)
    dk_ref[...] = dot_first(dscores[:, :cols], q) * score_scale
    dv_ref[...] = dot_first(weights[:, :cols], g)


def landing_kernel(plan_ref, landed_ref, out_ref, sum_ref, *, first):
    sum_ref[...] = jnp.zeros_like(sum_ref)
    for group in range(landed_ref.shape[0]):
        place = plan_ref[first + group]

        @pl.when(place >= 0)
        def _():
            sum_ref[place] = sum_ref[place] + landed_ref[group].astype(F32)

    out_ref[...] = sum_ref[...].astype(out_ref.dtype)


def finish_kernel(
    dk_near_ref, dv_near_ref, own_ref, back_ref, dk_ref, dv_ref, *, kv_heads
):
    blocks, _, half, _ = back_ref.shape
    mine = lax.axis_index("uly") == 0
    order = head_major(2 * half, kv_heads)
    for block in range(blocks):
        span = slice(block * 2 * half, (block + 1) * 2 * half)
        for near_ref, out_ref, which in ((dk_near_ref, dk_ref, 0), (dv_near_ref, dv_ref, 1)):
            own = own_ref[block, which]
            back = back_ref[block, which].astype(F32)
            far = jnp.concatenate([jnp.where(mine, own, back), jnp.where(mine, back, own)], axis=0)
            summed = (near_ref[span] + far).astype(BF16)
            out_ref[span] = dot_first(order, summed).astype(BF16)


def take_rows(array, index):
    return array.at[index].get(mode="promise_in_bounds")


def whole_blocks(queries, keys, values, output_cotangent, block_lists, list_counts):
    grp_count = lax.axis_size("grp")
    uly_count = lax.axis_size("uly")
    tokens, heads, width = queries.shape
    kv_heads = keys.shape[1]
    per_group = block_lists.shape[0] // grp_count
    block_tok = tokens * uly_count // per_group
    mine_blocks = tokens // block_tok
    rows = block_tok * heads
    cols = block_tok * kv_heads
    half = cols // 2
    sizes = dict(heads=heads, kv_heads=kv_heads, score_scale=width ** (-0.5))
    swap = [(0, 1), (1, 0)]

    sib_at, source_at, give_at, seen_at = plan_spans(grp_count, mine_blocks)

    q2 = queries.reshape(tokens * heads, width)
    g2 = output_cotangent.reshape(tokens * heads, width)
    k2 = keys.reshape(tokens * kv_heads, width)
    v2 = values.reshape(tokens * kv_heads, width)

    part_shape = jax.ShapeDtypeStruct((mine_blocks, 2, half, width), BF16)
    slot_shape = pltpu.HBM((grp_count, 2, half, width), BF16)
    stat_shape = jax.ShapeDtypeStruct((mine_blocks, 8, rows), F32)
    row_shape = jax.ShapeDtypeStruct(q2.shape, BF16)
    near_shape = jax.ShapeDtypeStruct(k2.shape, F32)
    small_shape = jax.ShapeDtypeStruct(k2.shape, BF16)
    sum_scratch = [pltpu.VMEM((mine_blocks, 2, half, width), F32)]
    slot_sems = [pltpu.SemaphoreType.DMA((grp_count,))]
    limit = pltpu.CompilerParams(vmem_limit_bytes=24 * 1024 * 1024)
    vmem = pl.BlockSpec(memory_space=pltpu.VMEM)
    smem = pl.BlockSpec(memory_space=pltpu.SMEM)
    anywhere = pl.BlockSpec(memory_space=pltpu.HBM)

    def call(kernel, name, scalars, operands, out_shape, scratch=(), into=None, out_spec=vmem):
        extra = () if into is None else (into,)
        return pl.pallas_call(
            kernel,
            in_specs=[smem] * len(scalars) + [vmem] * len(operands) + [anywhere] * len(extra),
            out_specs=jax.tree.map(lambda _: out_spec, out_shape),
            out_shape=out_shape,
            scratch_shapes=scratch,
            input_output_aliases={len(scalars) + len(operands): 0} if extra else {},
            compiler_params=limit,
            name=name,
        )(*scalars, *operands, *extra)

    def in_hbm(array):
        return pltpu.with_memory_space_constraint(array, pltpu.HBM)

    kept, given = pl.pallas_call(
        partial(pack_kernel, kv_heads=kv_heads),
        in_specs=[anywhere, anywhere],
        out_specs=[vmem, vmem],
        out_shape=[part_shape, part_shape],
        scratch_shapes=[
            pltpu.VMEM(k2.shape, BF16), pltpu.VMEM(k2.shape, BF16), pltpu.SemaphoreType.DMA((2,))
        ],
        compiler_params=limit,
        name="pack",
    )(in_hbm(k2), in_hbm(v2))
    plan = pl.pallas_call(
        partial(plan_kernel, grp_count=grp_count, blocks=mine_blocks),
        in_specs=[smem, smem],
        out_specs=smem,
        out_shape=pltpu.SMEM((seen_at + mine_blocks,), jnp.int32),
        compiler_params=limit,
        name="plan",
    )(in_hbm(block_lists.reshape(-1)), in_hbm(list_counts))
    gotten = lax.ppermute(given, "uly", swap)
    outgoing = call(
        partial(outgoing_kernel, first=0), "send_own", (plan,), (kept,),
        slot_shape, slot_sems, out_spec=anywhere,
    )
    outgoing = call(
        partial(outgoing_kernel, first=sib_at), "send_sibling", (plan,), (gotten,),
        slot_shape, slot_sems, into=outgoing, out_spec=anywhere,
    )
    outgoing, given = lax.optimization_barrier((outgoing, given))
    arrived = lax.all_to_all(outgoing, "grp", split_axis=0, concat_axis=0, tiled=True)
    stats = call(
        partial(near_kernel, **sizes), "near", (), (q2, g2, kept, given), stat_shape
    )
    arrived, stats = lax.optimization_barrier((arrived, stats))
    chunks = 2 if mine_blocks % 2 == 0 else 1
    chunk = mine_blocks // chunks
    chunk_shape = jax.ShapeDtypeStruct((chunk, 2, half, width), BF16)
    giving = call(
        partial(giving_kernel, give_at=give_at), "give", (plan,), (arrived,),
        [chunk_shape] * chunks,
    )
    others = [lax.ppermute(part, "uly", swap) for part in giving]
    stats = call(
        partial(mid_kernel, source_at=source_at, seen_at=seen_at, **sizes), "mid", (plan,),
        (q2, g2, stats, arrived), stat_shape,
    )
    grads, final = [], []
    for at, other in enumerate(others):
        if grads:
            other, grads[-1] = lax.optimization_barrier((other, grads[-1]))
        grad, stat = call(
            partial(far_kernel, seen_at=seen_at, first=at * chunk, **sizes), "far", (plan,),
            (q2, g2, stats, other),
            [chunk_shape, jax.ShapeDtypeStruct((chunk, 8, rows), F32)],
        )
        grads.append(grad)
        final.append(stat)
    from_sib = [lax.ppermute(part, "uly", swap) for part in grads]
    returning = None
    for at in reversed(range(chunks)):
        if returning is not None:
            from_sib[at], final[at] = lax.optimization_barrier((from_sib[at], final[at]))
        returning = call(
            partial(
                mine_kernel, source_at=source_at, seen_at=seen_at, rows=rows, first=at * chunk,
                **sizes,
            ),
            "mine", (plan,), (q2, g2, arrived, final[at]), slot_shape,
            [pltpu.VMEM(chunk_shape.shape, BF16), pltpu.SemaphoreType.DMA((chunk,))],
            into=returning, out_spec=anywhere,
        )
    returning = call(
        partial(returning_kernel, give_at=give_at), "return_sibling", (plan,), from_sib,
        slot_shape, [pltpu.SemaphoreType.DMA((mine_blocks,))], into=returning, out_spec=anywhere,
    )
    other = jnp.concatenate(others)
    returning, k2l = lax.optimization_barrier((returning, k2))
    landed = lax.all_to_all(returning, "grp", split_axis=0, concat_axis=0, tiled=True)

    def step_rows(i, *_):
        return (i, 0)

    def step_part(i, *_):
        return (i, 0, 0, 0)

    def from_source(i, plan_ref):
        return (plan_ref[source_at + i], 0, 0, 0)

    row_spec = pl.BlockSpec((rows, width), step_rows)
    col_spec = pl.BlockSpec((cols, width), step_rows)
    attended, dq, dk_near, dv_near = pl.pallas_call(
        partial(local_kernel, seen_at=seen_at, **sizes),
        grid_spec=pltpu.PrefetchScalarGridSpec(
            num_scalar_prefetch=1,
            grid=(mine_blocks,),
            in_specs=[
                row_spec, row_spec, col_spec, col_spec,
                pl.BlockSpec((1, 2, half, width), from_source),
                pl.BlockSpec((1, 2, half, width), step_part),
            ],
            out_specs=[row_spec, row_spec, col_spec, col_spec],
            scratch_shapes=[pltpu.VMEM((rows, 2 * cols), F32)],
        ),
        out_shape=[row_shape, row_shape, near_shape, near_shape],
        compiler_params=limit,
        name="local",
    )(plan, q2, g2, k2l, v2, arrived, other)
    landed, dk_near = lax.optimization_barrier((landed, dk_near))
    give = call(
        partial(landing_kernel, first=sib_at), "land_sibling", (plan,), (landed,), part_shape,
        sum_scratch,
    )
    back = lax.ppermute(give, "uly", swap)
    own = call(
        partial(landing_kernel, first=0), "land_own", (plan,), (landed,),
        jax.ShapeDtypeStruct(part_shape.shape, F32), sum_scratch,
    )
    dk, dv = call(
        partial(finish_kernel, kv_heads=kv_heads), "finish", (),
        (dk_near, dv_near, own, back), [small_shape, small_shape],
    )
    return (
        attended.reshape(queries.shape), dq.reshape(queries.shape),
        dk.reshape(keys.shape), dv.reshape(keys.shape),
    )


def on_device(queries, keys, values, output_cotangent, block_lists, list_counts):
    uly_count = lax.axis_size("uly")
    grp_count = lax.axis_size("grp")
    blocks_all, remote = block_lists.shape
    block_tok = queries.shape[0] * uly_count * grp_count // blocks_all
    held_whole = queries.shape[0] % block_tok == 0
    run = whole_blocks if held_whole and remote == 1 and uly_count == 2 else spread_blocks
    return run(queries, keys, values, output_cotangent, block_lists, list_counts)


def solution(mesh):
    placed = (
        P(("grp", "uly"), None, None),
        P(("grp", "uly"), None, None),
        P(("grp", "uly"), None, None),
        P(("grp", "uly"), None, None),
        P(),
        P(),
    )
    return jax.shard_map(
        on_device,
        mesh=mesh,
        in_specs=placed,
        out_specs=(
            P(("grp", "uly"), None, None),
            P(("grp", "uly"), None, None),
            P(("grp", "uly"), None, None),
            P(("grp", "uly"), None, None),
        ),
        check_vma=False,
    )
```

```python
from functools import partial

import jax
import jax.numpy as jnp
from jax import lax
from jax.experimental import pallas as pl
from jax.experimental.pallas import tpu as pltpu
from jax.sharding import PartitionSpec as P


def spread_blocks(queries, keys, values, output_cotangent, block_lists, list_counts):
    uly_count = lax.axis_size("uly")
    grp_count = lax.axis_size("grp")
    my_group = lax.axis_index("grp")
    tokens, head_count, head_width = queries.shape
    kv_heads = keys.shape[1]
    copies = max(1, uly_count // kv_heads)
    blocks_all, remote = block_lists.shape
    per_group = blocks_all // grp_count
    block_tok = tokens * uly_count // per_group
    group_tok = tokens * uly_count
    score_scale = head_width ** (-0.5)
    lists = block_lists.reshape(grp_count, per_group, remote)
    counted = (jnp.arange(remote)[None, :] < list_counts[:, None]).reshape(
        grp_count, per_group, remote
    )
    wanted = (lists // per_group == my_group) & counted
    send_place = jnp.sum(jnp.where(wanted, lists % per_group, 0), axis=(1, 2))
    sending = jnp.any(wanted, axis=(1, 2))
    mine_source = lax.dynamic_index_in_dim(lists, my_group, 0, keepdims=False) // per_group
    mine_counted = lax.dynamic_index_in_dim(counted, my_group, 0, keepdims=False)
    trip_count = jnp.max(jnp.sum(mine_counted.astype(jnp.int32), axis=1))

    def to_blocks(array_in):
        return array_in.reshape((per_group, block_tok) + array_in.shape[1:])

    keys_wide = jnp.repeat(keys, copies, axis=1)
    values_wide = jnp.repeat(values, copies, axis=1)
    query_heads, grad_heads, key_heads, value_heads = (
        lax.all_to_all(queries, "uly", split_axis=1, concat_axis=0, tiled=True),
        lax.all_to_all(output_cotangent, "uly", split_axis=1, concat_axis=0, tiled=True),
        lax.all_to_all(keys_wide, "uly", split_axis=1, concat_axis=0, tiled=True),
        lax.all_to_all(values_wide, "uly", split_axis=1, concat_axis=0, tiled=True),
    )
    stacked = jnp.stack([to_blocks(key_heads), to_blocks(value_heads)])
    outgoing = jnp.take(stacked, send_place, axis=1)
    arrived = lax.all_to_all(outgoing, "grp", split_axis=1, concat_axis=1, tiled=True)
    kv_local = key_heads.shape[1]
    heads_local = query_heads.shape[1]
    heads_per_group = heads_local // kv_local
    query_blk = query_heads.reshape(per_group, block_tok, kv_local, heads_per_group, head_width)
    grad_blk = grad_heads.reshape(per_group, block_tok, kv_local, heads_per_group, head_width)
    key_blk = to_blocks(key_heads)
    value_blk = to_blocks(value_heads)
    far_keys = arrived[0]
    far_values = arrived[1]
    causal = jnp.arange(block_tok)[:, None] >= jnp.arange(block_tok)[None, :]

    def logits(key_rows):
        return (
            jnp.einsum("pqkgd,pjkd->pkgqj", query_blk, key_rows, preferred_element_type=jnp.float32)
            * score_scale
        )

    def slot_rows(slot_index):
        source = lax.dynamic_index_in_dim(mine_source, slot_index, 1, keepdims=False)
        counted_slot = lax.dynamic_index_in_dim(mine_counted, slot_index, 1, keepdims=False)
        return (
            jnp.take(far_keys, source, axis=0),
            jnp.take(far_values, source, axis=0),
            counted_slot,
            source,
        )

    def masked(scores, counted_slot):
        return jnp.where(counted_slot[:, None, None, None, None], scores, -jnp.inf)

    near_scores = jnp.where(causal, logits(key_blk), -jnp.inf)
    highest = jnp.max(near_scores, axis=-1)
    denominator = jnp.sum(jnp.exp(near_scores - highest[..., None]), axis=-1)

    def max_sweep(slot_index, state_pair):
        highest, denominator = state_pair
        key_rows, value_rows, counted_slot, source = slot_rows(slot_index)
        scores = masked(logits(key_rows), counted_slot)
        new_highest = jnp.maximum(highest, jnp.max(scores, axis=-1))
        denominator = denominator * jnp.exp(highest - new_highest) + jnp.sum(
            jnp.exp(scores - new_highest[..., None]), axis=-1
        )
        return (new_highest, denominator)

    highest, denominator = lax.fori_loop(0, trip_count, max_sweep, (highest, denominator))
    log_total = highest + jnp.log(denominator)

    def softmax_weights(scores):
        return jnp.exp(scores - log_total[..., None])

    summed = jnp.einsum(
        "pkgqj,pjkd->pqkgd",
        softmax_weights(near_scores).astype(jnp.bfloat16),
        value_blk,
        preferred_element_type=jnp.float32,
    )

    def value_sweep(slot_index, summed):
        key_rows, value_rows, counted_slot, source = slot_rows(slot_index)
        weights = softmax_weights(masked(logits(key_rows), counted_slot)).astype(jnp.bfloat16)
        return summed + jnp.einsum(
            "pkgqj,pjkd->pqkgd", weights, value_rows, preferred_element_type=jnp.float32
        )

    summed = lax.fori_loop(0, trip_count, value_sweep, summed)
    attended_blk = summed.astype(jnp.bfloat16)
    row_delta = jnp.transpose(
        jnp.sum(grad_blk.astype(jnp.float32) * attended_blk.astype(jnp.float32), axis=-1),
        (0, 2, 3, 1),
    )

    def backward(scores, key_rows, value_rows):
        probs = softmax_weights(scores)
        weights = probs.astype(jnp.bfloat16)
        dprobs = jnp.einsum(
            "pqkgd,pjkd->pkgqj", grad_blk, value_rows, preferred_element_type=jnp.float32
        )
        dscores = (probs * (dprobs - row_delta[..., None])).astype(jnp.bfloat16)
        query_term = jnp.einsum(
            "pkgqj,pjkd->pqkgd", dscores, key_rows, preferred_element_type=jnp.float32
        )
        key_term = (
            jnp.einsum("pkgqj,pqkgd->pjkd", dscores, query_blk, preferred_element_type=jnp.float32)
            * score_scale
        )
        value_term = jnp.einsum(
            "pkgqj,pqkgd->pjkd", weights, grad_blk, preferred_element_type=jnp.float32
        )
        return (query_term, key_term, value_term)

    query_sum, key_near, value_near = backward(near_scores, key_blk, value_blk)
    far_grads = jnp.zeros((2, grp_count, block_tok, kv_local, head_width), jnp.float32)

    def grad_sweep(slot_index, state_pair):
        query_sum, far_grads = state_pair
        key_rows, value_rows, counted_slot, source = slot_rows(slot_index)
        query_term, key_term, value_term = backward(
            masked(logits(key_rows), counted_slot), key_rows, value_rows
        )
        routing = (
            (source[:, None] == jnp.arange(grp_count)[None, :]) & counted_slot[:, None]
        ).astype(jnp.float32)
        routed = jnp.einsum(
            "ps,xpjkd->xsjkd",
            routing,
            jnp.stack([key_term, value_term]),
            precision=lax.Precision.HIGHEST,
        )
        return (query_sum + query_term, far_grads + routed)

    query_sum, far_grads = lax.fori_loop(0, trip_count, grad_sweep, (query_sum, far_grads))
    owners = ((send_place[:, None] == jnp.arange(per_group)[None, :]) & sending[:, None]).astype(
        jnp.float32
    )
    returned = lax.all_to_all(far_grads, "grp", split_axis=1, concat_axis=1, tiled=True)
    landed = jnp.einsum("sp,xsjkd->xpjkd", owners, returned, precision=lax.Precision.HIGHEST)
    key_local = (key_near + landed[0]).reshape(group_tok, kv_local, head_width)
    value_local = (value_near + landed[1]).reshape(group_tok, kv_local, head_width)
    attended_rows = attended_blk.reshape(group_tok, heads_local, head_width)
    query_rows = (
        (query_sum * score_scale).astype(jnp.bfloat16).reshape(group_tok, heads_local, head_width)
    )
    attended, query_grad = (
        lax.all_to_all(attended_rows, "uly", split_axis=0, concat_axis=1, tiled=True),
        lax.all_to_all(query_rows, "uly", split_axis=0, concat_axis=1, tiled=True),
    )
    key_parts, value_parts = (
        lax.all_to_all(key_local, "uly", split_axis=0, concat_axis=1, tiled=True),
        lax.all_to_all(value_local, "uly", split_axis=0, concat_axis=1, tiled=True),
    )
    key_gradient = jnp.sum(key_parts.reshape(tokens, kv_heads, copies, head_width), axis=2).astype(
        jnp.bfloat16
    )
    value_gradient = jnp.sum(
        value_parts.reshape(tokens, kv_heads, copies, head_width), axis=2
    ).astype(jnp.bfloat16)
    return (attended, query_grad, key_gradient, value_gradient)


HIDDEN = -1e30
LAST = (((1,), (1,)), ((), ()))
FIRST = (((0,), (0,)), ((), ()))
F32 = jnp.float32
BF16 = jnp.bfloat16


def dot_last(left, right):
    return lax.dot_general(left, right, LAST, preferred_element_type=F32)


def dot_first(left, right):
    return lax.dot_general(left, right, FIRST, preferred_element_type=F32)


def head_major(cols, kv_heads):
    half = cols // 2
    place = half // kv_heads
    row = lax.broadcasted_iota(jnp.int32, (cols, cols), 0)
    col = lax.broadcasted_iota(jnp.int32, (cols, cols), 1)
    token = row // half * place + row % place
    return jnp.where(col == token * kv_heads + row % half // place, 1.0, 0.0).astype(BF16)


def reorder(one_hot, array):
    return jnp.dot(one_hot, array, preferred_element_type=F32).astype(BF16)


def own_head(scores, lane_head, kv_heads):
    place = scores.shape[0] // kv_heads
    kept = scores[:place]
    for head in range(1, kv_heads):
        kept = jnp.where(lane_head == head, scores[head * place:(head + 1) * place], kept)
    return kept


def all_heads(kept, lane_head, kv_heads):
    none = jnp.zeros_like(kept)
    return jnp.concatenate(
        [jnp.where(lane_head == head, kept, none) for head in range(kv_heads)], axis=0
    )


def lanes(rows, heads, kv_heads):
    lane = lax.broadcasted_iota(jnp.int32, (1, rows), 1)
    return lane // heads, lane % heads // (heads // kv_heads)


def plan_spans(grp_count, blocks):
    return grp_count, 2 * grp_count, 2 * grp_count + blocks, 2 * grp_count + 2 * blocks


def plan_kernel(lists_ref, counts_ref, plan_ref, *, grp_count, blocks):
    group, mine = lax.axis_index("grp"), lax.axis_index("uly")
    per_group = 2 * blocks
    low = group * per_group
    sib_at, source_at, give_at, seen_at = plan_spans(grp_count, blocks)
    for other in range(grp_count):
        place = jnp.int32(-1)
        for at in range(other * per_group, (other + 1) * per_group):
            here = lists_ref[at] - low
            wanted = (here >= 0) & (here < per_group) & (counts_ref[at] > 0)
            place = jnp.where(wanted, here, place)
        own = place - mine * blocks
        sib = place - (1 - mine) * blocks
        plan_ref[other] = jnp.where((own >= 0) & (own < blocks), own, -1)
        plan_ref[sib_at + other] = jnp.where((sib >= 0) & (sib < blocks), sib, -1)
    for block in range(blocks):
        at = low + mine * blocks + block
        plan_ref[source_at + block] = lax.div(lists_ref[at], per_group)
        plan_ref[seen_at + block] = counts_ref[at]
        at = low + (1 - mine) * blocks + block
        plan_ref[give_at + block] = lax.div(lists_ref[at], per_group)


def pack_kernel(k_hbm, v_hbm, kept_ref, given_ref, k_ref, v_ref, sems, *, kv_heads):
    blocks, _, half, _ = kept_ref.shape
    copies = [
        pltpu.make_async_copy(k_hbm, k_ref, sems.at[0]),
        pltpu.make_async_copy(v_hbm, v_ref, sems.at[1]),
    ]
    for copy in copies:
        copy.start()
    first = lax.axis_index("uly") == 0
    order = head_major(2 * half, kv_heads)
    for which, ref in enumerate((k_ref, v_ref)):
        copies[which].wait()
        for block in range(blocks):
            ordered = reorder(order, ref[block * 2 * half:(block + 1) * 2 * half])
            kept_ref[block, which] = jnp.where(first, ordered[:half], ordered[half:])
            given_ref[block, which] = jnp.where(first, ordered[half:], ordered[:half])


def outgoing_kernel(plan_ref, blocks_ref, *refs, first):
    out_ref, sems = refs[-2:]
    copies = []
    for group in range(out_ref.shape[0]):
        place = plan_ref[first + group]
        source = blocks_ref.at[jnp.maximum(place, 0)]
        copy = pltpu.make_async_copy(source, out_ref.at[group], sems.at[group])
        copies.append((place >= 0, copy))
    for wanted, copy in copies:
        pl.when(wanted)(copy.start)
    for wanted, copy in copies:
        pl.when(wanted)(copy.wait)


def giving_kernel(plan_ref, arrived_ref, *out_refs, give_at):
    block = 0
    for out_ref in out_refs:
        for at in range(out_ref.shape[0]):
            out_ref[at] = arrived_ref[plan_ref[give_at + block]]
            block += 1


def returning_kernel(plan_ref, *refs, source_at):
    part_refs, (out_ref, sems) = refs[:-2], refs[-2:]
    copies = []
    for part_ref in part_refs:
        for at in range(part_ref.shape[0]):
            block = len(copies)
            target = out_ref.at[plan_ref[source_at + block]]
            copies.append(pltpu.make_async_copy(part_ref.at[at], target, sems.at[block]))
            copies[-1].start()
    for copy in copies:
        copy.wait()


def near_kernel(
    q_ref, g_ref, kept_ref, given_ref, stat_ref, *, heads, kv_heads, score_scale
):
    blocks = stat_ref.shape[0]
    rows = q_ref.shape[0] // blocks
    place = kept_ref.shape[2] // kv_heads
    token, lane_head = lanes(rows, heads, kv_heads)
    key = lax.broadcasted_iota(jnp.int32, (2 * place, rows), 0)
    mine = lax.axis_index("uly")
    part = jnp.where(key < place, mine, 1 - mine)
    causal = key % place + part * place <= token
    for block in range(blocks):
        span = slice(block * rows, (block + 1) * rows)
        pieces = []
        for which, ref in enumerate((q_ref, g_ref)):
            both = jnp.concatenate([kept_ref[block, which], given_ref[block, which]], axis=0)
            full = dot_last(both, ref[span])
            half = full.shape[0] // 2
            pieces.append(
                jnp.concatenate(
                    [
                        own_head(full[:half], lane_head, kv_heads),
                        own_head(full[half:], lane_head, kv_heads),
                    ],
                    axis=0,
                )
            )
        scores = jnp.where(causal, pieces[0] * score_scale, HIDDEN)
        highest = jnp.max(scores, axis=0, keepdims=True)
        raised = jnp.exp(scores - highest)
        stat_ref[block, 0:1] = highest
        stat_ref[block, 1:2] = jnp.sum(raised, axis=0, keepdims=True)
        stat_ref[block, 2:3] = jnp.sum(raised * pieces[1], axis=0, keepdims=True)


def far_scores(part_ref, at, q, g, seen, lane_head, kv_heads, score_scale):
    hidden = jnp.where(seen > 0, 0.0, HIDDEN)
    scores = own_head(dot_last(part_ref[at, 0], q), lane_head, kv_heads) * score_scale + hidden
    return scores, own_head(dot_last(part_ref[at, 1], g), lane_head, kv_heads)


def merged(stat_ref, block, scores, dprobs):
    before = stat_ref[block, 0:1]
    highest = jnp.maximum(before, jnp.max(scores, axis=0, keepdims=True))
    raised = jnp.exp(scores - highest)
    shrink = jnp.exp(before - highest)
    total = shrink * stat_ref[block, 1:2] + jnp.sum(raised, axis=0, keepdims=True)
    delta = shrink * stat_ref[block, 2:3] + jnp.sum(raised * dprobs, axis=0, keepdims=True)
    return highest, raised, total, delta


def far_gradients(probs, dprobs, delta, q, g, lane_head, kv_heads, score_scale):
    dscores = (probs * (dprobs - delta)).astype(BF16)
    dk = jnp.dot(all_heads(dscores, lane_head, kv_heads), q, preferred_element_type=F32)
    dv = jnp.dot(all_heads(probs.astype(BF16), lane_head, kv_heads), g, preferred_element_type=F32)
    return (dk * score_scale).astype(BF16), dv.astype(BF16)


def mid_kernel(
    plan_ref, q_ref, g_ref, stat_ref, arrived_ref, out_ref,
    *, heads, kv_heads, score_scale, source_at, seen_at
):
    blocks = stat_ref.shape[0]
    rows = q_ref.shape[0] // blocks
    _, lane_head = lanes(rows, heads, kv_heads)
    for block in range(blocks):
        span = slice(block * rows, (block + 1) * rows)
        scores, dprobs = far_scores(
            arrived_ref, plan_ref[source_at + block], q_ref[span], g_ref[span],
            plan_ref[seen_at + block],            lane_head, kv_heads, score_scale,
        )
        highest, _, total, delta = merged(stat_ref, block, scores, dprobs)
        out_ref[block, 0:1] = highest
        out_ref[block, 1:2] = total
        out_ref[block, 2:3] = delta


def far_kernel(
    plan_ref, q_ref, g_ref, stat_ref, other_ref, grad_ref, out_ref,
    *, heads, kv_heads, score_scale, seen_at, first
):
    rows = q_ref.shape[0] // stat_ref.shape[0]
    _, lane_head = lanes(rows, heads, kv_heads)
    for at in range(other_ref.shape[0]):
        block = first + at
        span = slice(block * rows, (block + 1) * rows)
        q = q_ref[span]
        g = g_ref[span]
        scores, dprobs = far_scores(
            other_ref, at, q, g, plan_ref[seen_at + block], lane_head, kv_heads, score_scale
        )
        highest, raised, total, delta = merged(stat_ref, block, scores, dprobs)
        inverse = 1.0 / total
        delta = delta * inverse
        grad_ref[at, 0], grad_ref[at, 1] = far_gradients(
            raised * inverse, dprobs, delta, q, g, lane_head, kv_heads, score_scale
        )
        out_ref[at, 0:1] = highest
        out_ref[at, 1:2] = inverse
        out_ref[at, 2:3] = delta


def mine_kernel(
    plan_ref, q_ref, g_ref, arrived_ref, stat_ref, grad_ref,
    *, heads, kv_heads, score_scale, source_at, seen_at, rows, first
):
    _, lane_head = lanes(rows, heads, kv_heads)
    for at in range(stat_ref.shape[0]):
        block = first + at
        span = slice(block * rows, (block + 1) * rows)
        q = q_ref[span]
        g = g_ref[span]
        scores, dprobs = far_scores(
            arrived_ref, plan_ref[source_at + block], q, g, plan_ref[seen_at + block],
            lane_head, kv_heads, score_scale,
        )
        probs = jnp.exp(scores - stat_ref[at, 0:1]) * stat_ref[at, 1:2]
        grad_ref[at, 0], grad_ref[at, 1] = far_gradients(
            probs, dprobs, stat_ref[at, 2:3], q, g, lane_head, kv_heads, score_scale
        )


def local_kernel(
    plan_ref, q_ref, g_ref, k_ref, v_ref, mine_ref, other_ref,
    att_ref, dq_ref, dk_ref, dv_ref, bias_ref, *, heads, kv_heads, score_scale, seen_at
):
    step = pl.program_id(0)
    rows = q_ref.shape[0]
    cols = k_ref.shape[0]

    @pl.when(step == 0)
    def _():
        half = cols // 2
        place = half // kv_heads
        row = lax.broadcasted_iota(jnp.int32, (rows, cols), 0)
        col = lax.broadcasted_iota(jnp.int32, (rows, cols), 1)
        same = row % heads // (heads // kv_heads) == col % half // place
        causal = col // half * place + col % place <= row // heads
        bias_ref[:, :cols] = jnp.where(same & causal, 0.0, HIDDEN)
        bias_ref[:, cols:] = jnp.where(same, 0.0, HIDDEN)

    far_bias = jnp.where(plan_ref[seen_at + step] > 0, 0.0, HIDDEN)
    order = head_major(cols, kv_heads)
    k_near = reorder(order, k_ref[...])
    v_near = reorder(order, v_ref[...])
    k_all = jnp.concatenate([k_near, mine_ref[0, 0], other_ref[0, 0]], axis=0)
    v_all = jnp.concatenate([v_near, mine_ref[0, 1], other_ref[0, 1]], axis=0)
    q = q_ref[...]
    g = g_ref[...]
    scores = dot_last(q, k_all) * score_scale + bias_ref[...]
    scores = jnp.concatenate([scores[:, :cols], scores[:, cols:] + far_bias], axis=1)
    highest = jnp.max(scores, axis=1, keepdims=True)
    raised = jnp.exp(scores - highest)
    total = jnp.sum(raised, axis=1, keepdims=True)
    probs = raised * (1.0 / total)
    weights = probs.astype(BF16)
    attended = jnp.dot(weights, v_all, preferred_element_type=F32).astype(BF16)
    att_ref[...] = attended
    delta = jnp.sum(g.astype(F32) * attended.astype(F32), axis=1, keepdims=True)
    dscores = (probs * (dot_last(g, v_all) - delta)).astype(BF16)
    dq = jnp.dot(dscores, k_all, preferred_element_type=F32) * score_scale
    dq_ref[...] = dq.astype(BF16)
    dk_ref[...] = dot_first(dscores[:, :cols], q) * score_scale
    dv_ref[...] = dot_first(weights[:, :cols], g)


def landing_kernel(plan_ref, landed_ref, out_ref, sum_ref, *, first):
    sum_ref[...] = jnp.zeros_like(sum_ref)
    for group in range(landed_ref.shape[0]):
        place = plan_ref[first + group]

        @pl.when(place >= 0)
        def _():
            sum_ref[place] = sum_ref[place] + landed_ref[group].astype(F32)

    out_ref[...] = sum_ref[...].astype(out_ref.dtype)


def finish_kernel(
    dk_near_ref, dv_near_ref, own_ref, back_ref, dk_ref, dv_ref, *, kv_heads
):
    blocks, _, half, _ = back_ref.shape
    mine = lax.axis_index("uly") == 0
    order = head_major(2 * half, kv_heads)
    for block in range(blocks):
        span = slice(block * 2 * half, (block + 1) * 2 * half)
        for near_ref, out_ref, which in ((dk_near_ref, dk_ref, 0), (dv_near_ref, dv_ref, 1)):
            own = own_ref[block, which]
            back = back_ref[block, which].astype(F32)
            far = jnp.concatenate([jnp.where(mine, own, back), jnp.where(mine, back, own)], axis=0)
            summed = (near_ref[span] + far).astype(BF16)
            out_ref[span] = dot_first(order, summed).astype(BF16)


def take_rows(array, index):
    return array.at[index].get(mode="promise_in_bounds")


def whole_blocks(queries, keys, values, output_cotangent, block_lists, list_counts):
    grp_count = lax.axis_size("grp")
    uly_count = lax.axis_size("uly")
    tokens, heads, width = queries.shape
    kv_heads = keys.shape[1]
    per_group = block_lists.shape[0] // grp_count
    block_tok = tokens * uly_count // per_group
    mine_blocks = tokens // block_tok
    rows = block_tok * heads
    cols = block_tok * kv_heads
    half = cols // 2
    sizes = dict(heads=heads, kv_heads=kv_heads, score_scale=width ** (-0.5))
    swap = [(0, 1), (1, 0)]

    sib_at, source_at, give_at, seen_at = plan_spans(grp_count, mine_blocks)

    q2 = queries.reshape(tokens * heads, width)
    g2 = output_cotangent.reshape(tokens * heads, width)
    k2 = keys.reshape(tokens * kv_heads, width)
    v2 = values.reshape(tokens * kv_heads, width)

    part_shape = jax.ShapeDtypeStruct((mine_blocks, 2, half, width), BF16)
    slot_shape = pltpu.HBM((grp_count, 2, half, width), BF16)
    stat_shape = jax.ShapeDtypeStruct((mine_blocks, 8, rows), F32)
    row_shape = jax.ShapeDtypeStruct(q2.shape, BF16)
    near_shape = jax.ShapeDtypeStruct(k2.shape, F32)
    small_shape = jax.ShapeDtypeStruct(k2.shape, BF16)
    sum_scratch = [pltpu.VMEM((mine_blocks, 2, half, width), F32)]
    slot_sems = [pltpu.SemaphoreType.DMA((grp_count,))]
    limit = pltpu.CompilerParams(vmem_limit_bytes=24 * 1024 * 1024)
    vmem = pl.BlockSpec(memory_space=pltpu.VMEM)
    smem = pl.BlockSpec(memory_space=pltpu.SMEM)
    anywhere = pl.BlockSpec(memory_space=pltpu.HBM)

    def call(kernel, name, scalars, operands, out_shape, scratch=(), into=None, out_spec=vmem):
        extra = () if into is None else (into,)
        return pl.pallas_call(
            kernel,
            in_specs=[smem] * len(scalars) + [vmem] * len(operands) + [anywhere] * len(extra),
            out_specs=jax.tree.map(lambda _: out_spec, out_shape),
            out_shape=out_shape,
            scratch_shapes=scratch,
            input_output_aliases={len(scalars) + len(operands): 0} if extra else {},
            compiler_params=limit,
            name=name,
        )(*scalars, *operands, *extra)

    def in_hbm(array):
        return pltpu.with_memory_space_constraint(array, pltpu.HBM)

    kept, given = pl.pallas_call(
        partial(pack_kernel, kv_heads=kv_heads),
        in_specs=[anywhere, anywhere],
        out_specs=[vmem, vmem],
        out_shape=[part_shape, part_shape],
        scratch_shapes=[
            pltpu.VMEM(k2.shape, BF16), pltpu.VMEM(k2.shape, BF16), pltpu.SemaphoreType.DMA((2,))
        ],
        compiler_params=limit,
        name="pack",
    )(in_hbm(k2), in_hbm(v2))
    plan = pl.pallas_call(
        partial(plan_kernel, grp_count=grp_count, blocks=mine_blocks),
        in_specs=[smem, smem],
        out_specs=smem,
        out_shape=pltpu.SMEM((seen_at + mine_blocks,), jnp.int32),
        compiler_params=limit,
        name="plan",
    )(in_hbm(block_lists.reshape(-1)), in_hbm(list_counts))
    gotten = lax.ppermute(given, "uly", swap)
    outgoing = call(
        partial(outgoing_kernel, first=0), "send_own", (plan,), (kept,),
        slot_shape, slot_sems, out_spec=anywhere,
    )
    outgoing = call(
        partial(outgoing_kernel, first=sib_at), "send_sibling", (plan,), (gotten,),
        slot_shape, slot_sems, into=outgoing, out_spec=anywhere,
    )
    outgoing, given = lax.optimization_barrier((outgoing, given))
    arrived = lax.all_to_all(outgoing, "grp", split_axis=0, concat_axis=0, tiled=True)
    stats = call(
        partial(near_kernel, **sizes), "near", (), (q2, g2, kept, given), stat_shape
    )
    arrived, stats = lax.optimization_barrier((arrived, stats))
    chunks = 2 if mine_blocks % 2 == 0 else 1
    chunk = mine_blocks // chunks
    chunk_shape = jax.ShapeDtypeStruct((chunk, 2, half, width), BF16)
    giving = call(
        partial(giving_kernel, give_at=give_at), "give", (plan,), (arrived,),
        [chunk_shape] * chunks,
    )
    stats = call(
        partial(mid_kernel, source_at=source_at, seen_at=seen_at, **sizes), "mid", (plan,),
        (q2, g2, stats, arrived), stat_shape,
    )
    others = []
    for part in giving:
        if others:
            part, stats = lax.optimization_barrier((part, stats))
        others.append(lax.ppermute(part, "uly", swap))
    grads, final = [], []
    for at, other in enumerate(others):
        grad, stat = call(
            partial(far_kernel, seen_at=seen_at, first=at * chunk, **sizes), "far", (plan,),
            (q2, g2, stats, other),
            [chunk_shape, jax.ShapeDtypeStruct((chunk, 8, rows), F32)],
        )
        grads.append(grad)
        final.append(stat)
    from_sib = [lax.ppermute(part, "uly", swap) for part in grads]
    mine = [None] * chunks
    for at in reversed(range(chunks)):
        if at + 1 < chunks:
            from_sib[at], final[at] = lax.optimization_barrier((from_sib[at], final[at]))
        mine[at] = call(
            partial(
                mine_kernel, source_at=source_at, seen_at=seen_at, rows=rows, first=at * chunk,
                **sizes,
            ),
            "mine", (plan,), (q2, g2, arrived, final[at]), chunk_shape,
        )
    returning = call(
        partial(returning_kernel, source_at=source_at), "return", (plan,), mine + from_sib,
        slot_shape, [pltpu.SemaphoreType.DMA((per_group,))], out_spec=anywhere,
    )
    other = jnp.concatenate(others)
    returning, k2l = lax.optimization_barrier((returning, k2))
    landed = lax.all_to_all(returning, "grp", split_axis=0, concat_axis=0, tiled=True)

    def step_rows(i, *_):
        return (i, 0)

    def step_part(i, *_):
        return (i, 0, 0, 0)

    def from_source(i, plan_ref):
        return (plan_ref[source_at + i], 0, 0, 0)

    row_spec = pl.BlockSpec((rows, width), step_rows)
    col_spec = pl.BlockSpec((cols, width), step_rows)
    attended, dq, dk_near, dv_near = pl.pallas_call(
        partial(local_kernel, seen_at=seen_at, **sizes),
        grid_spec=pltpu.PrefetchScalarGridSpec(
            num_scalar_prefetch=1,
            grid=(mine_blocks,),
            in_specs=[
                row_spec, row_spec, col_spec, col_spec,
                pl.BlockSpec((1, 2, half, width), from_source),
                pl.BlockSpec((1, 2, half, width), step_part),
            ],
            out_specs=[row_spec, row_spec, col_spec, col_spec],
            scratch_shapes=[pltpu.VMEM((rows, 2 * cols), F32)],
        ),
        out_shape=[row_shape, row_shape, near_shape, near_shape],
        compiler_params=limit,
        name="local",
    )(plan, q2, g2, k2l, v2, arrived, other)
    landed, dk_near = lax.optimization_barrier((landed, dk_near))
    give = call(
        partial(landing_kernel, first=sib_at), "land_sibling", (plan,), (landed,), part_shape,
        sum_scratch,
    )
    back = lax.ppermute(give, "uly", swap)
    own = call(
        partial(landing_kernel, first=0), "land_own", (plan,), (landed,),
        jax.ShapeDtypeStruct(part_shape.shape, F32), sum_scratch,
    )
    dk, dv = call(
        partial(finish_kernel, kv_heads=kv_heads), "finish", (),
        (dk_near, dv_near, own, back), [small_shape, small_shape],
    )
    return (
        attended.reshape(queries.shape), dq.reshape(queries.shape),
        dk.reshape(keys.shape), dv.reshape(keys.shape),
    )


def on_device(queries, keys, values, output_cotangent, block_lists, list_counts):
    uly_count = lax.axis_size("uly")
    grp_count = lax.axis_size("grp")
    blocks_all, remote = block_lists.shape
    block_tok = queries.shape[0] * uly_count * grp_count // blocks_all
    held_whole = queries.shape[0] % block_tok == 0
    run = whole_blocks if held_whole and remote == 1 and uly_count == 2 else spread_blocks
    return run(queries, keys, values, output_cotangent, block_lists, list_counts)


def solution(mesh):
    placed = (
        P(("grp", "uly"), None, None),
        P(("grp", "uly"), None, None),
        P(("grp", "uly"), None, None),
        P(("grp", "uly"), None, None),
        P(),
        P(),
    )
    return jax.shard_map(
        on_device,
        mesh=mesh,
        in_specs=placed,
        out_specs=(
            P(("grp", "uly"), None, None),
            P(("grp", "uly"), None, None),
            P(("grp", "uly"), None, None),
            P(("grp", "uly"), None, None),
        ),
        check_vma=False,
    )
```

```python
from functools import partial

import jax
import jax.numpy as jnp
from jax import lax
from jax.experimental import pallas as pl
from jax.experimental.pallas import tpu as pltpu
from jax.sharding import PartitionSpec as P


def spread_blocks(queries, keys, values, output_cotangent, block_lists, list_counts):
    uly_count = lax.axis_size("uly")
    grp_count = lax.axis_size("grp")
    my_group = lax.axis_index("grp")
    tokens, head_count, head_width = queries.shape
    kv_heads = keys.shape[1]
    copies = max(1, uly_count // kv_heads)
    blocks_all, remote = block_lists.shape
    per_group = blocks_all // grp_count
    block_tok = tokens * uly_count // per_group
    group_tok = tokens * uly_count
    score_scale = head_width ** (-0.5)
    lists = block_lists.reshape(grp_count, per_group, remote)
    counted = (jnp.arange(remote)[None, :] < list_counts[:, None]).reshape(
        grp_count, per_group, remote
    )
    wanted = (lists // per_group == my_group) & counted
    send_place = jnp.sum(jnp.where(wanted, lists % per_group, 0), axis=(1, 2))
    sending = jnp.any(wanted, axis=(1, 2))
    mine_source = lax.dynamic_index_in_dim(lists, my_group, 0, keepdims=False) // per_group
    mine_counted = lax.dynamic_index_in_dim(counted, my_group, 0, keepdims=False)
    trip_count = jnp.max(jnp.sum(mine_counted.astype(jnp.int32), axis=1))

    def to_blocks(array_in):
        return array_in.reshape((per_group, block_tok) + array_in.shape[1:])

    keys_wide = jnp.repeat(keys, copies, axis=1)
    values_wide = jnp.repeat(values, copies, axis=1)
    query_heads, grad_heads, key_heads, value_heads = (
        lax.all_to_all(queries, "uly", split_axis=1, concat_axis=0, tiled=True),
        lax.all_to_all(output_cotangent, "uly", split_axis=1, concat_axis=0, tiled=True),
        lax.all_to_all(keys_wide, "uly", split_axis=1, concat_axis=0, tiled=True),
        lax.all_to_all(values_wide, "uly", split_axis=1, concat_axis=0, tiled=True),
    )
    stacked = jnp.stack([to_blocks(key_heads), to_blocks(value_heads)])
    outgoing = jnp.take(stacked, send_place, axis=1)
    arrived = lax.all_to_all(outgoing, "grp", split_axis=1, concat_axis=1, tiled=True)
    kv_local = key_heads.shape[1]
    heads_local = query_heads.shape[1]
    heads_per_group = heads_local // kv_local
    query_blk = query_heads.reshape(per_group, block_tok, kv_local, heads_per_group, head_width)
    grad_blk = grad_heads.reshape(per_group, block_tok, kv_local, heads_per_group, head_width)
    key_blk = to_blocks(key_heads)
    value_blk = to_blocks(value_heads)
    far_keys = arrived[0]
    far_values = arrived[1]
    causal = jnp.arange(block_tok)[:, None] >= jnp.arange(block_tok)[None, :]

    def logits(key_rows):
        return (
            jnp.einsum("pqkgd,pjkd->pkgqj", query_blk, key_rows, preferred_element_type=jnp.float32)
            * score_scale
        )

    def slot_rows(slot_index):
        source = lax.dynamic_index_in_dim(mine_source, slot_index, 1, keepdims=False)
        counted_slot = lax.dynamic_index_in_dim(mine_counted, slot_index, 1, keepdims=False)
        return (
            jnp.take(far_keys, source, axis=0),
            jnp.take(far_values, source, axis=0),
            counted_slot,
            source,
        )

    def masked(scores, counted_slot):
        return jnp.where(counted_slot[:, None, None, None, None], scores, -jnp.inf)

    near_scores = jnp.where(causal, logits(key_blk), -jnp.inf)
    highest = jnp.max(near_scores, axis=-1)
    denominator = jnp.sum(jnp.exp(near_scores - highest[..., None]), axis=-1)

    def max_sweep(slot_index, state_pair):
        highest, denominator = state_pair
        key_rows, value_rows, counted_slot, source = slot_rows(slot_index)
        scores = masked(logits(key_rows), counted_slot)
        new_highest = jnp.maximum(highest, jnp.max(scores, axis=-1))
        denominator = denominator * jnp.exp(highest - new_highest) + jnp.sum(
            jnp.exp(scores - new_highest[..., None]), axis=-1
        )
        return (new_highest, denominator)

    highest, denominator = lax.fori_loop(0, trip_count, max_sweep, (highest, denominator))
    log_total = highest + jnp.log(denominator)

    def softmax_weights(scores):
        return jnp.exp(scores - log_total[..., None])

    summed = jnp.einsum(
        "pkgqj,pjkd->pqkgd",
        softmax_weights(near_scores).astype(jnp.bfloat16),
        value_blk,
        preferred_element_type=jnp.float32,
    )

    def value_sweep(slot_index, summed):
        key_rows, value_rows, counted_slot, source = slot_rows(slot_index)
        weights = softmax_weights(masked(logits(key_rows), counted_slot)).astype(jnp.bfloat16)
        return summed + jnp.einsum(
            "pkgqj,pjkd->pqkgd", weights, value_rows, preferred_element_type=jnp.float32
        )

    summed = lax.fori_loop(0, trip_count, value_sweep, summed)
    attended_blk = summed.astype(jnp.bfloat16)
    row_delta = jnp.transpose(
        jnp.sum(grad_blk.astype(jnp.float32) * attended_blk.astype(jnp.float32), axis=-1),
        (0, 2, 3, 1),
    )

    def backward(scores, key_rows, value_rows):
        probs = softmax_weights(scores)
        weights = probs.astype(jnp.bfloat16)
        dprobs = jnp.einsum(
            "pqkgd,pjkd->pkgqj", grad_blk, value_rows, preferred_element_type=jnp.float32
        )
        dscores = (probs * (dprobs - row_delta[..., None])).astype(jnp.bfloat16)
        query_term = jnp.einsum(
            "pkgqj,pjkd->pqkgd", dscores, key_rows, preferred_element_type=jnp.float32
        )
        key_term = (
            jnp.einsum("pkgqj,pqkgd->pjkd", dscores, query_blk, preferred_element_type=jnp.float32)
            * score_scale
        )
        value_term = jnp.einsum(
            "pkgqj,pqkgd->pjkd", weights, grad_blk, preferred_element_type=jnp.float32
        )
        return (query_term, key_term, value_term)

    query_sum, key_near, value_near = backward(near_scores, key_blk, value_blk)
    far_grads = jnp.zeros((2, grp_count, block_tok, kv_local, head_width), jnp.float32)

    def grad_sweep(slot_index, state_pair):
        query_sum, far_grads = state_pair
        key_rows, value_rows, counted_slot, source = slot_rows(slot_index)
        query_term, key_term, value_term = backward(
            masked(logits(key_rows), counted_slot), key_rows, value_rows
        )
        routing = (
            (source[:, None] == jnp.arange(grp_count)[None, :]) & counted_slot[:, None]
        ).astype(jnp.float32)
        routed = jnp.einsum(
            "ps,xpjkd->xsjkd",
            routing,
            jnp.stack([key_term, value_term]),
            precision=lax.Precision.HIGHEST,
        )
        return (query_sum + query_term, far_grads + routed)

    query_sum, far_grads = lax.fori_loop(0, trip_count, grad_sweep, (query_sum, far_grads))
    owners = ((send_place[:, None] == jnp.arange(per_group)[None, :]) & sending[:, None]).astype(
        jnp.float32
    )
    returned = lax.all_to_all(far_grads, "grp", split_axis=1, concat_axis=1, tiled=True)
    landed = jnp.einsum("sp,xsjkd->xpjkd", owners, returned, precision=lax.Precision.HIGHEST)
    key_local = (key_near + landed[0]).reshape(group_tok, kv_local, head_width)
    value_local = (value_near + landed[1]).reshape(group_tok, kv_local, head_width)
    attended_rows = attended_blk.reshape(group_tok, heads_local, head_width)
    query_rows = (
        (query_sum * score_scale).astype(jnp.bfloat16).reshape(group_tok, heads_local, head_width)
    )
    attended, query_grad = (
        lax.all_to_all(attended_rows, "uly", split_axis=0, concat_axis=1, tiled=True),
        lax.all_to_all(query_rows, "uly", split_axis=0, concat_axis=1, tiled=True),
    )
    key_parts, value_parts = (
        lax.all_to_all(key_local, "uly", split_axis=0, concat_axis=1, tiled=True),
        lax.all_to_all(value_local, "uly", split_axis=0, concat_axis=1, tiled=True),
    )
    key_gradient = jnp.sum(key_parts.reshape(tokens, kv_heads, copies, head_width), axis=2).astype(
        jnp.bfloat16
    )
    value_gradient = jnp.sum(
        value_parts.reshape(tokens, kv_heads, copies, head_width), axis=2
    ).astype(jnp.bfloat16)
    return (attended, query_grad, key_gradient, value_gradient)


HIDDEN = -1e30
LAST = (((1,), (1,)), ((), ()))
FIRST = (((0,), (0,)), ((), ()))
F32 = jnp.float32
BF16 = jnp.bfloat16


def dot_last(left, right):
    return lax.dot_general(left, right, LAST, preferred_element_type=F32)


def dot_first(left, right):
    return lax.dot_general(left, right, FIRST, preferred_element_type=F32)


def head_major(cols, kv_heads):
    half = cols // 2
    place = half // kv_heads
    row = lax.broadcasted_iota(jnp.int32, (cols, cols), 0)
    col = lax.broadcasted_iota(jnp.int32, (cols, cols), 1)
    token = row // half * place + row % place
    return jnp.where(col == token * kv_heads + row % half // place, 1.0, 0.0).astype(BF16)


def reorder(one_hot, array):
    return jnp.dot(one_hot, array, preferred_element_type=F32).astype(BF16)


def own_head(scores, lane_head, kv_heads):
    place = scores.shape[0] // kv_heads
    kept = scores[:place]
    for head in range(1, kv_heads):
        kept = jnp.where(lane_head == head, scores[head * place:(head + 1) * place], kept)
    return kept


def all_heads(kept, lane_head, kv_heads):
    none = jnp.zeros_like(kept)
    return jnp.concatenate(
        [jnp.where(lane_head == head, kept, none) for head in range(kv_heads)], axis=0
    )


def lanes(rows, heads, kv_heads):
    lane = lax.broadcasted_iota(jnp.int32, (1, rows), 1)
    return lane // heads, lane % heads // (heads // kv_heads)


def plan_spans(grp_count, blocks):
    return grp_count, 2 * grp_count, 2 * grp_count + blocks, 2 * grp_count + 2 * blocks


def plan_kernel(lists_ref, counts_ref, plan_ref, *, grp_count, blocks):
    group, mine = lax.axis_index("grp"), lax.axis_index("uly")
    per_group = 2 * blocks
    low = group * per_group
    sib_at, source_at, give_at, seen_at = plan_spans(grp_count, blocks)
    for other in range(grp_count):
        place = jnp.int32(-1)
        for at in range(other * per_group, (other + 1) * per_group):
            here = lists_ref[at] - low
            wanted = (here >= 0) & (here < per_group) & (counts_ref[at] > 0)
            place = jnp.where(wanted, here, place)
        own = place - mine * blocks
        sib = place - (1 - mine) * blocks
        plan_ref[other] = jnp.where((own >= 0) & (own < blocks), own, -1)
        plan_ref[sib_at + other] = jnp.where((sib >= 0) & (sib < blocks), sib, -1)
    for block in range(blocks):
        at = low + mine * blocks + block
        plan_ref[source_at + block] = lax.div(lists_ref[at], per_group)
        plan_ref[seen_at + block] = counts_ref[at]
        at = low + (1 - mine) * blocks + block
        plan_ref[give_at + block] = lax.div(lists_ref[at], per_group)


def pack_kernel(k_hbm, v_hbm, kept_ref, given_ref, k_ref, v_ref, sems, *, kv_heads):
    blocks, _, half, _ = kept_ref.shape
    copies = [
        pltpu.make_async_copy(k_hbm, k_ref, sems.at[0]),
        pltpu.make_async_copy(v_hbm, v_ref, sems.at[1]),
    ]
    for copy in copies:
        copy.start()
    first = lax.axis_index("uly") == 0
    order = head_major(2 * half, kv_heads)
    for which, ref in enumerate((k_ref, v_ref)):
        copies[which].wait()
        for block in range(blocks):
            ordered = reorder(order, ref[block * 2 * half:(block + 1) * 2 * half])
            kept_ref[block, which] = jnp.where(first, ordered[:half], ordered[half:])
            given_ref[block, which] = jnp.where(first, ordered[half:], ordered[:half])


def send_own_kernel(plan_ref, blocks_ref, out_ref):
    for group in range(out_ref.shape[0]):
        out_ref[group] = blocks_ref[jnp.maximum(plan_ref[group], 0)]


def send_sibling_kernel(plan_ref, blocks_ref, _, out_ref, *, first):
    for group in range(out_ref.shape[0]):
        place = plan_ref[first + group]

        @pl.when(place >= 0)
        def _():
            out_ref[group] = blocks_ref[place]


def giving_kernel(plan_ref, arrived_ref, *out_refs, give_at):
    block = 0
    for out_ref in out_refs:
        for at in range(out_ref.shape[0]):
            out_ref[at] = arrived_ref[plan_ref[give_at + block]]
            block += 1


def returning_kernel(plan_ref, *refs, source_at):
    part_refs, (out_ref, sems) = refs[:-2], refs[-2:]
    copies = []
    for part_ref in part_refs:
        for at in range(part_ref.shape[0]):
            block = len(copies)
            target = out_ref.at[plan_ref[source_at + block]]
            copies.append(pltpu.make_async_copy(part_ref.at[at], target, sems.at[block]))
            copies[-1].start()
    for copy in copies:
        copy.wait()


def near_kernel(
    q_ref, g_ref, kept_ref, given_ref, stat_ref, *, heads, kv_heads, score_scale
):
    rows = q_ref.shape[0]
    place = kept_ref.shape[2] // kv_heads
    token, lane_head = lanes(rows, heads, kv_heads)
    key = lax.broadcasted_iota(jnp.int32, (2 * place, rows), 0)
    mine = lax.axis_index("uly")
    part = jnp.where(key < place, mine, 1 - mine)
    causal = key % place + part * place <= token
    pieces = []
    for which, ref in enumerate((q_ref, g_ref)):
        both = jnp.concatenate([kept_ref[0, which], given_ref[0, which]], axis=0)
        full = dot_last(both, ref[...])
        half = full.shape[0] // 2
        pieces.append(
            jnp.concatenate(
                [
                    own_head(full[:half], lane_head, kv_heads),
                    own_head(full[half:], lane_head, kv_heads),
                ],
                axis=0,
            )
        )
    scores = jnp.where(causal, pieces[0] * score_scale, HIDDEN)
    highest = jnp.max(scores, axis=0, keepdims=True)
    raised = jnp.exp(scores - highest)
    stat_ref[0, 0:1] = highest
    stat_ref[0, 1:2] = jnp.sum(raised, axis=0, keepdims=True)
    stat_ref[0, 2:3] = jnp.sum(raised * pieces[1], axis=0, keepdims=True)


def far_scores(part_ref, at, q, g, seen, lane_head, kv_heads, score_scale):
    hidden = jnp.where(seen > 0, 0.0, HIDDEN)
    scores = own_head(dot_last(part_ref[at, 0], q), lane_head, kv_heads) * score_scale + hidden
    return scores, own_head(dot_last(part_ref[at, 1], g), lane_head, kv_heads)


def merged(stat_ref, block, scores, dprobs):
    before = stat_ref[block, 0:1]
    highest = jnp.maximum(before, jnp.max(scores, axis=0, keepdims=True))
    raised = jnp.exp(scores - highest)
    shrink = jnp.exp(before - highest)
    total = shrink * stat_ref[block, 1:2] + jnp.sum(raised, axis=0, keepdims=True)
    delta = shrink * stat_ref[block, 2:3] + jnp.sum(raised * dprobs, axis=0, keepdims=True)
    return highest, raised, total, delta


def far_gradients(probs, dprobs, delta, q, g, lane_head, kv_heads, score_scale):
    dscores = (probs * (dprobs - delta)).astype(BF16)
    dk = jnp.dot(all_heads(dscores, lane_head, kv_heads), q, preferred_element_type=F32)
    dv = jnp.dot(all_heads(probs.astype(BF16), lane_head, kv_heads), g, preferred_element_type=F32)
    return (dk * score_scale).astype(BF16), dv.astype(BF16)


def mid_kernel(
    plan_ref, q_ref, g_ref, stat_ref, arrived_ref, out_ref,
    *, heads, kv_heads, score_scale, source_at, seen_at
):
    blocks = stat_ref.shape[0]
    rows = q_ref.shape[0] // blocks
    _, lane_head = lanes(rows, heads, kv_heads)
    for block in range(blocks):
        span = slice(block * rows, (block + 1) * rows)
        scores, dprobs = far_scores(
            arrived_ref, plan_ref[source_at + block], q_ref[span], g_ref[span],
            plan_ref[seen_at + block],            lane_head, kv_heads, score_scale,
        )
        highest, _, total, delta = merged(stat_ref, block, scores, dprobs)
        out_ref[block, 0:1] = highest
        out_ref[block, 1:2] = total
        out_ref[block, 2:3] = delta


def far_kernel(
    plan_ref, q_ref, g_ref, stat_ref, other_ref, grad_ref, out_ref,
    *, heads, kv_heads, score_scale, seen_at, first
):
    rows = q_ref.shape[0] // stat_ref.shape[0]
    _, lane_head = lanes(rows, heads, kv_heads)
    for at in range(other_ref.shape[0]):
        block = first + at
        span = slice(block * rows, (block + 1) * rows)
        q = q_ref[span]
        g = g_ref[span]
        scores, dprobs = far_scores(
            other_ref, at, q, g, plan_ref[seen_at + block], lane_head, kv_heads, score_scale
        )
        highest, raised, total, delta = merged(stat_ref, block, scores, dprobs)
        inverse = 1.0 / total
        delta = delta * inverse
        grad_ref[at, 0], grad_ref[at, 1] = far_gradients(
            raised * inverse, dprobs, delta, q, g, lane_head, kv_heads, score_scale
        )
        out_ref[at, 0:1] = highest
        out_ref[at, 1:2] = inverse
        out_ref[at, 2:3] = delta


def mine_kernel(
    plan_ref, q_ref, g_ref, arrived_ref, stat_ref, grad_ref,
    *, heads, kv_heads, score_scale, source_at, seen_at, rows, first
):
    _, lane_head = lanes(rows, heads, kv_heads)
    for at in range(stat_ref.shape[0]):
        block = first + at
        span = slice(block * rows, (block + 1) * rows)
        q = q_ref[span]
        g = g_ref[span]
        scores, dprobs = far_scores(
            arrived_ref, plan_ref[source_at + block], q, g, plan_ref[seen_at + block],
            lane_head, kv_heads, score_scale,
        )
        probs = jnp.exp(scores - stat_ref[at, 0:1]) * stat_ref[at, 1:2]
        grad_ref[at, 0], grad_ref[at, 1] = far_gradients(
            probs, dprobs, stat_ref[at, 2:3], q, g, lane_head, kv_heads, score_scale
        )


def local_kernel(
    plan_ref, q_ref, g_ref, k_ref, v_ref, mine_ref, other_ref,
    att_ref, dq_ref, dk_ref, dv_ref, bias_ref, *, heads, kv_heads, score_scale, seen_at
):
    step = pl.program_id(0)
    rows = q_ref.shape[0]
    cols = k_ref.shape[0]

    @pl.when(step == 0)
    def _():
        half = cols // 2
        place = half // kv_heads
        row = lax.broadcasted_iota(jnp.int32, (rows, cols), 0)
        col = lax.broadcasted_iota(jnp.int32, (rows, cols), 1)
        same = row % heads // (heads // kv_heads) == col % half // place
        causal = col // half * place + col % place <= row // heads
        bias_ref[:, :cols] = jnp.where(same & causal, 0.0, HIDDEN)
        bias_ref[:, cols:] = jnp.where(same, 0.0, HIDDEN)

    far_bias = jnp.where(plan_ref[seen_at + step] > 0, 0.0, HIDDEN)
    order = head_major(cols, kv_heads)
    k_near = reorder(order, k_ref[...])
    v_near = reorder(order, v_ref[...])
    k_all = jnp.concatenate([k_near, mine_ref[0, 0], other_ref[0, 0]], axis=0)
    v_all = jnp.concatenate([v_near, mine_ref[0, 1], other_ref[0, 1]], axis=0)
    q = q_ref[...]
    g = g_ref[...]
    scores = dot_last(q, k_all) * score_scale + bias_ref[...]
    scores = jnp.concatenate([scores[:, :cols], scores[:, cols:] + far_bias], axis=1)
    highest = jnp.max(scores, axis=1, keepdims=True)
    raised = jnp.exp(scores - highest)
    total = jnp.sum(raised, axis=1, keepdims=True)
    probs = raised * (1.0 / total)
    weights = probs.astype(BF16)
    attended = jnp.dot(weights, v_all, preferred_element_type=F32).astype(BF16)
    att_ref[...] = attended
    delta = jnp.sum(g.astype(F32) * attended.astype(F32), axis=1, keepdims=True)
    dscores = (probs * (dot_last(g, v_all) - delta)).astype(BF16)
    dq = jnp.dot(dscores, k_all, preferred_element_type=F32) * score_scale
    dq_ref[...] = dq.astype(BF16)
    dk_ref[...] = dot_first(dscores[:, :cols], q) * score_scale
    dv_ref[...] = dot_first(weights[:, :cols], g)


def landing_kernel(plan_ref, landed_ref, out_ref, sum_ref, *, first):
    sum_ref[...] = jnp.zeros_like(sum_ref)
    for group in range(landed_ref.shape[0]):
        place = plan_ref[first + group]

        @pl.when(place >= 0)
        def _():
            sum_ref[place] = sum_ref[place] + landed_ref[group].astype(F32)

    out_ref[...] = sum_ref[...].astype(out_ref.dtype)


def finish_kernel(
    dk_near_ref, dv_near_ref, own_ref, back_ref, dk_ref, dv_ref, *, kv_heads
):
    blocks, _, half, _ = back_ref.shape
    mine = lax.axis_index("uly") == 0
    order = head_major(2 * half, kv_heads)
    for block in range(blocks):
        span = slice(block * 2 * half, (block + 1) * 2 * half)
        for near_ref, out_ref, which in ((dk_near_ref, dk_ref, 0), (dv_near_ref, dv_ref, 1)):
            own = own_ref[block, which]
            back = back_ref[block, which].astype(F32)
            far = jnp.concatenate([jnp.where(mine, own, back), jnp.where(mine, back, own)], axis=0)
            summed = (near_ref[span] + far).astype(BF16)
            out_ref[span] = dot_first(order, summed).astype(BF16)


def take_rows(array, index):
    return array.at[index].get(mode="promise_in_bounds")


def whole_blocks(queries, keys, values, output_cotangent, block_lists, list_counts):
    grp_count = lax.axis_size("grp")
    uly_count = lax.axis_size("uly")
    tokens, heads, width = queries.shape
    kv_heads = keys.shape[1]
    per_group = block_lists.shape[0] // grp_count
    block_tok = tokens * uly_count // per_group
    mine_blocks = tokens // block_tok
    rows = block_tok * heads
    cols = block_tok * kv_heads
    half = cols // 2
    sizes = dict(heads=heads, kv_heads=kv_heads, score_scale=width ** (-0.5))
    swap = [(0, 1), (1, 0)]

    sib_at, source_at, give_at, seen_at = plan_spans(grp_count, mine_blocks)

    q2 = queries.reshape(tokens * heads, width)
    g2 = output_cotangent.reshape(tokens * heads, width)
    k2 = keys.reshape(tokens * kv_heads, width)
    v2 = values.reshape(tokens * kv_heads, width)

    part_shape = jax.ShapeDtypeStruct((mine_blocks, 2, half, width), BF16)
    slots = (grp_count, 2, half, width)
    stat_shape = jax.ShapeDtypeStruct((mine_blocks, 8, rows), F32)
    row_shape = jax.ShapeDtypeStruct(q2.shape, BF16)
    near_shape = jax.ShapeDtypeStruct(k2.shape, F32)
    small_shape = jax.ShapeDtypeStruct(k2.shape, BF16)
    sum_scratch = [pltpu.VMEM((mine_blocks, 2, half, width), F32)]
    limit = pltpu.CompilerParams(vmem_limit_bytes=24 * 1024 * 1024)
    vmem = pl.BlockSpec(memory_space=pltpu.VMEM)
    smem = pl.BlockSpec(memory_space=pltpu.SMEM)
    anywhere = pl.BlockSpec(memory_space=pltpu.HBM)

    def call(kernel, name, scalars, operands, out_shape, scratch=(), into=None, out_spec=vmem):
        extra = () if into is None else (into,)
        return pl.pallas_call(
            kernel,
            in_specs=[smem] * len(scalars) + [vmem] * (len(operands) + len(extra)),
            out_specs=jax.tree.map(lambda _: out_spec, out_shape),
            out_shape=out_shape,
            scratch_shapes=scratch,
            input_output_aliases={len(scalars) + len(operands): 0} if extra else {},
            compiler_params=limit,
            name=name,
        )(*scalars, *operands, *extra)

    def step_rows(i, *_):
        return (i, 0)

    def step_part(i, *_):
        return (i, 0, 0, 0)

    def in_hbm(array):
        return pltpu.with_memory_space_constraint(array, pltpu.HBM)

    kept, given = pl.pallas_call(
        partial(pack_kernel, kv_heads=kv_heads),
        in_specs=[anywhere, anywhere],
        out_specs=[vmem, vmem],
        out_shape=[part_shape, part_shape],
        scratch_shapes=[
            pltpu.VMEM(k2.shape, BF16), pltpu.VMEM(k2.shape, BF16), pltpu.SemaphoreType.DMA((2,))
        ],
        compiler_params=limit,
        name="pack",
    )(in_hbm(k2), in_hbm(v2))
    plan = pl.pallas_call(
        partial(plan_kernel, grp_count=grp_count, blocks=mine_blocks),
        in_specs=[smem, smem],
        out_specs=smem,
        out_shape=pltpu.SMEM((seen_at + mine_blocks,), jnp.int32),
        compiler_params=limit,
        name="plan",
    )(in_hbm(block_lists.reshape(-1)), in_hbm(list_counts))
    gotten = lax.ppermute(given, "uly", swap)
    row_spec = pl.BlockSpec((rows, width), step_rows)
    part_spec = pl.BlockSpec((1, 2, half, width), step_part)
    stats = pl.pallas_call(
        partial(near_kernel, **sizes),
        grid=(mine_blocks,),
        in_specs=[row_spec, row_spec, part_spec, part_spec],
        out_specs=pl.BlockSpec((1, 8, rows), lambda i: (i, 0, 0)),
        out_shape=stat_shape,
        compiler_params=limit,
        name="near",
    )(in_hbm(q2), in_hbm(g2), kept, given)
    outgoing = call(
        send_own_kernel, "send_own", (plan,), (kept,),
        jax.ShapeDtypeStruct(slots, BF16),
    )
    gotten, stats = lax.optimization_barrier((gotten, stats))
    outgoing = call(
        partial(send_sibling_kernel, first=sib_at), "send_sibling", (plan,), (gotten,),
        jax.ShapeDtypeStruct(slots, BF16), into=outgoing,
    )
    arrived = lax.all_to_all(outgoing, "grp", split_axis=0, concat_axis=0, tiled=True)
    chunks = 2 if mine_blocks % 2 == 0 else 1
    chunk = mine_blocks // chunks
    chunk_shape = jax.ShapeDtypeStruct((chunk, 2, half, width), BF16)
    giving = call(
        partial(giving_kernel, give_at=give_at), "give", (plan,), (arrived,),
        [chunk_shape] * chunks,
    )
    stats = call(
        partial(mid_kernel, source_at=source_at, seen_at=seen_at, **sizes), "mid", (plan,),
        (q2, g2, stats, arrived), stat_shape,
    )
    others = []
    for part in giving:
        if others:
            part, stats = lax.optimization_barrier((part, stats))
        others.append(lax.ppermute(part, "uly", swap))
    grads, final = [], []
    for at, other in enumerate(others):
        grad, stat = call(
            partial(far_kernel, seen_at=seen_at, first=at * chunk, **sizes), "far", (plan,),
            (q2, g2, stats, other),
            [chunk_shape, jax.ShapeDtypeStruct((chunk, 8, rows), F32)],
        )
        grads.append(grad)
        final.append(stat)
    from_sib = [lax.ppermute(part, "uly", swap) for part in grads]
    mine = [None] * chunks
    for at in reversed(range(chunks)):
        if at + 1 < chunks:
            from_sib[at], final[at] = lax.optimization_barrier((from_sib[at], final[at]))
        mine[at] = call(
            partial(
                mine_kernel, source_at=source_at, seen_at=seen_at, rows=rows, first=at * chunk,
                **sizes,
            ),
            "mine", (plan,), (q2, g2, arrived, final[at]), chunk_shape,
        )
    returning = call(
        partial(returning_kernel, source_at=source_at), "return", (plan,), mine + from_sib,
        pltpu.HBM(slots, BF16), [pltpu.SemaphoreType.DMA((per_group,))], out_spec=anywhere,
    )
    other = jnp.concatenate(others)
    returning, k2l = lax.optimization_barrier((returning, k2))
    landed = lax.all_to_all(returning, "grp", split_axis=0, concat_axis=0, tiled=True)

    def from_source(i, plan_ref):
        return (plan_ref[source_at + i], 0, 0, 0)

    col_spec = pl.BlockSpec((cols, width), step_rows)
    attended, dq, dk_near, dv_near = pl.pallas_call(
        partial(local_kernel, seen_at=seen_at, **sizes),
        grid_spec=pltpu.PrefetchScalarGridSpec(
            num_scalar_prefetch=1,
            grid=(mine_blocks,),
            in_specs=[
                row_spec, row_spec, col_spec, col_spec,
                pl.BlockSpec((1, 2, half, width), from_source),
                part_spec,
            ],
            out_specs=[row_spec, row_spec, col_spec, col_spec],
            scratch_shapes=[pltpu.VMEM((rows, 2 * cols), F32)],
        ),
        out_shape=[row_shape, row_shape, near_shape, near_shape],
        compiler_params=limit,
        name="local",
    )(plan, q2, g2, k2l, v2, arrived, other)
    landed, dk_near = lax.optimization_barrier((landed, dk_near))
    give = call(
        partial(landing_kernel, first=sib_at), "land_sibling", (plan,), (landed,), part_shape,
        sum_scratch,
    )
    back = lax.ppermute(give, "uly", swap)
    own = call(
        partial(landing_kernel, first=0), "land_own", (plan,), (landed,),
        jax.ShapeDtypeStruct(part_shape.shape, F32), sum_scratch,
    )
    dk, dv = call(
        partial(finish_kernel, kv_heads=kv_heads), "finish", (),
        (dk_near, dv_near, own, back), [small_shape, small_shape],
    )
    return (
        attended.reshape(queries.shape), dq.reshape(queries.shape),
        dk.reshape(keys.shape), dv.reshape(keys.shape),
    )


def on_device(queries, keys, values, output_cotangent, block_lists, list_counts):
    uly_count = lax.axis_size("uly")
    grp_count = lax.axis_size("grp")
    blocks_all, remote = block_lists.shape
    block_tok = queries.shape[0] * uly_count * grp_count // blocks_all
    held_whole = queries.shape[0] % block_tok == 0
    run = whole_blocks if held_whole and remote == 1 and uly_count == 2 else spread_blocks
    return run(queries, keys, values, output_cotangent, block_lists, list_counts)


def solution(mesh):
    placed = (
        P(("grp", "uly"), None, None),
        P(("grp", "uly"), None, None),
        P(("grp", "uly"), None, None),
        P(("grp", "uly"), None, None),
        P(),
        P(),
    )
    return jax.shard_map(
        on_device,
        mesh=mesh,
        in_specs=placed,
        out_specs=(
            P(("grp", "uly"), None, None),
            P(("grp", "uly"), None, None),
            P(("grp", "uly"), None, None),
            P(("grp", "uly"), None, None),
        ),
        check_vma=False,
    )
```

```python
from functools import partial

import jax
import jax.numpy as jnp
from jax import lax
from jax.experimental import pallas as pl
from jax.experimental.pallas import tpu as pltpu
from jax.sharding import PartitionSpec as P


def spread_blocks(queries, keys, values, output_cotangent, block_lists, list_counts):
    uly_count = lax.axis_size("uly")
    grp_count = lax.axis_size("grp")
    my_group = lax.axis_index("grp")
    tokens, head_count, head_width = queries.shape
    kv_heads = keys.shape[1]
    copies = max(1, uly_count // kv_heads)
    blocks_all, remote = block_lists.shape
    per_group = blocks_all // grp_count
    block_tok = tokens * uly_count // per_group
    group_tok = tokens * uly_count
    score_scale = head_width ** (-0.5)
    lists = block_lists.reshape(grp_count, per_group, remote)
    counted = (jnp.arange(remote)[None, :] < list_counts[:, None]).reshape(
        grp_count, per_group, remote
    )
    wanted = (lists // per_group == my_group) & counted
    send_place = jnp.sum(jnp.where(wanted, lists % per_group, 0), axis=(1, 2))
    sending = jnp.any(wanted, axis=(1, 2))
    mine_source = lax.dynamic_index_in_dim(lists, my_group, 0, keepdims=False) // per_group
    mine_counted = lax.dynamic_index_in_dim(counted, my_group, 0, keepdims=False)
    trip_count = jnp.max(jnp.sum(mine_counted.astype(jnp.int32), axis=1))

    def to_blocks(array_in):
        return array_in.reshape((per_group, block_tok) + array_in.shape[1:])

    keys_wide = jnp.repeat(keys, copies, axis=1)
    values_wide = jnp.repeat(values, copies, axis=1)
    query_heads, grad_heads, key_heads, value_heads = (
        lax.all_to_all(queries, "uly", split_axis=1, concat_axis=0, tiled=True),
        lax.all_to_all(output_cotangent, "uly", split_axis=1, concat_axis=0, tiled=True),
        lax.all_to_all(keys_wide, "uly", split_axis=1, concat_axis=0, tiled=True),
        lax.all_to_all(values_wide, "uly", split_axis=1, concat_axis=0, tiled=True),
    )
    stacked = jnp.stack([to_blocks(key_heads), to_blocks(value_heads)])
    outgoing = jnp.take(stacked, send_place, axis=1)
    arrived = lax.all_to_all(outgoing, "grp", split_axis=1, concat_axis=1, tiled=True)
    kv_local = key_heads.shape[1]
    heads_local = query_heads.shape[1]
    heads_per_group = heads_local // kv_local
    query_blk = query_heads.reshape(per_group, block_tok, kv_local, heads_per_group, head_width)
    grad_blk = grad_heads.reshape(per_group, block_tok, kv_local, heads_per_group, head_width)
    key_blk = to_blocks(key_heads)
    value_blk = to_blocks(value_heads)
    far_keys = arrived[0]
    far_values = arrived[1]
    causal = jnp.arange(block_tok)[:, None] >= jnp.arange(block_tok)[None, :]

    def logits(key_rows):
        return (
            jnp.einsum("pqkgd,pjkd->pkgqj", query_blk, key_rows, preferred_element_type=jnp.float32)
            * score_scale
        )

    def slot_rows(slot_index):
        source = lax.dynamic_index_in_dim(mine_source, slot_index, 1, keepdims=False)
        counted_slot = lax.dynamic_index_in_dim(mine_counted, slot_index, 1, keepdims=False)
        return (
            jnp.take(far_keys, source, axis=0),
            jnp.take(far_values, source, axis=0),
            counted_slot,
            source,
        )

    def masked(scores, counted_slot):
        return jnp.where(counted_slot[:, None, None, None, None], scores, -jnp.inf)

    near_scores = jnp.where(causal, logits(key_blk), -jnp.inf)
    highest = jnp.max(near_scores, axis=-1)
    denominator = jnp.sum(jnp.exp(near_scores - highest[..., None]), axis=-1)

    def max_sweep(slot_index, state_pair):
        highest, denominator = state_pair
        key_rows, value_rows, counted_slot, source = slot_rows(slot_index)
        scores = masked(logits(key_rows), counted_slot)
        new_highest = jnp.maximum(highest, jnp.max(scores, axis=-1))
        denominator = denominator * jnp.exp(highest - new_highest) + jnp.sum(
            jnp.exp(scores - new_highest[..., None]), axis=-1
        )
        return (new_highest, denominator)

    highest, denominator = lax.fori_loop(0, trip_count, max_sweep, (highest, denominator))
    log_total = highest + jnp.log(denominator)

    def softmax_weights(scores):
        return jnp.exp(scores - log_total[..., None])

    summed = jnp.einsum(
        "pkgqj,pjkd->pqkgd",
        softmax_weights(near_scores).astype(jnp.bfloat16),
        value_blk,
        preferred_element_type=jnp.float32,
    )

    def value_sweep(slot_index, summed):
        key_rows, value_rows, counted_slot, source = slot_rows(slot_index)
        weights = softmax_weights(masked(logits(key_rows), counted_slot)).astype(jnp.bfloat16)
        return summed + jnp.einsum(
            "pkgqj,pjkd->pqkgd", weights, value_rows, preferred_element_type=jnp.float32
        )

    summed = lax.fori_loop(0, trip_count, value_sweep, summed)
    attended_blk = summed.astype(jnp.bfloat16)
    row_delta = jnp.transpose(
        jnp.sum(grad_blk.astype(jnp.float32) * attended_blk.astype(jnp.float32), axis=-1),
        (0, 2, 3, 1),
    )

    def backward(scores, key_rows, value_rows):
        probs = softmax_weights(scores)
        weights = probs.astype(jnp.bfloat16)
        dprobs = jnp.einsum(
            "pqkgd,pjkd->pkgqj", grad_blk, value_rows, preferred_element_type=jnp.float32
        )
        dscores = (probs * (dprobs - row_delta[..., None])).astype(jnp.bfloat16)
        query_term = jnp.einsum(
            "pkgqj,pjkd->pqkgd", dscores, key_rows, preferred_element_type=jnp.float32
        )
        key_term = (
            jnp.einsum("pkgqj,pqkgd->pjkd", dscores, query_blk, preferred_element_type=jnp.float32)
            * score_scale
        )
        value_term = jnp.einsum(
            "pkgqj,pqkgd->pjkd", weights, grad_blk, preferred_element_type=jnp.float32
        )
        return (query_term, key_term, value_term)

    query_sum, key_near, value_near = backward(near_scores, key_blk, value_blk)
    far_grads = jnp.zeros((2, grp_count, block_tok, kv_local, head_width), jnp.float32)

    def grad_sweep(slot_index, state_pair):
        query_sum, far_grads = state_pair
        key_rows, value_rows, counted_slot, source = slot_rows(slot_index)
        query_term, key_term, value_term = backward(
            masked(logits(key_rows), counted_slot), key_rows, value_rows
        )
        routing = (
            (source[:, None] == jnp.arange(grp_count)[None, :]) & counted_slot[:, None]
        ).astype(jnp.float32)
        routed = jnp.einsum(
            "ps,xpjkd->xsjkd",
            routing,
            jnp.stack([key_term, value_term]),
            precision=lax.Precision.HIGHEST,
        )
        return (query_sum + query_term, far_grads + routed)

    query_sum, far_grads = lax.fori_loop(0, trip_count, grad_sweep, (query_sum, far_grads))
    owners = ((send_place[:, None] == jnp.arange(per_group)[None, :]) & sending[:, None]).astype(
        jnp.float32
    )
    returned = lax.all_to_all(far_grads, "grp", split_axis=1, concat_axis=1, tiled=True)
    landed = jnp.einsum("sp,xsjkd->xpjkd", owners, returned, precision=lax.Precision.HIGHEST)
    key_local = (key_near + landed[0]).reshape(group_tok, kv_local, head_width)
    value_local = (value_near + landed[1]).reshape(group_tok, kv_local, head_width)
    attended_rows = attended_blk.reshape(group_tok, heads_local, head_width)
    query_rows = (
        (query_sum * score_scale).astype(jnp.bfloat16).reshape(group_tok, heads_local, head_width)
    )
    attended, query_grad = (
        lax.all_to_all(attended_rows, "uly", split_axis=0, concat_axis=1, tiled=True),
        lax.all_to_all(query_rows, "uly", split_axis=0, concat_axis=1, tiled=True),
    )
    key_parts, value_parts = (
        lax.all_to_all(key_local, "uly", split_axis=0, concat_axis=1, tiled=True),
        lax.all_to_all(value_local, "uly", split_axis=0, concat_axis=1, tiled=True),
    )
    key_gradient = jnp.sum(key_parts.reshape(tokens, kv_heads, copies, head_width), axis=2).astype(
        jnp.bfloat16
    )
    value_gradient = jnp.sum(
        value_parts.reshape(tokens, kv_heads, copies, head_width), axis=2
    ).astype(jnp.bfloat16)
    return (attended, query_grad, key_gradient, value_gradient)


HIDDEN = -1e30
LAST = (((1,), (1,)), ((), ()))
FIRST = (((0,), (0,)), ((), ()))
F32 = jnp.float32
BF16 = jnp.bfloat16


def dot_last(left, right):
    return lax.dot_general(left, right, LAST, preferred_element_type=F32)


def dot_first(left, right):
    return lax.dot_general(left, right, FIRST, preferred_element_type=F32)


def head_major(cols, kv_heads):
    half = cols // 2
    place = half // kv_heads
    row = lax.broadcasted_iota(jnp.int32, (cols, cols), 0)
    col = lax.broadcasted_iota(jnp.int32, (cols, cols), 1)
    token = row // half * place + row % place
    return jnp.where(col == token * kv_heads + row % half // place, 1.0, 0.0).astype(BF16)


def half_order(cols, kv_heads, which):
    half = cols // 2
    place = half // kv_heads
    row = lax.broadcasted_iota(jnp.int32, (half, cols), 0)
    col = lax.broadcasted_iota(jnp.int32, (half, cols), 1)
    token = which * place + row % place
    return jnp.where(col == token * kv_heads + row // place, 1.0, 0.0).astype(BF16)


def reorder(one_hot, array):
    return jnp.dot(one_hot, array, preferred_element_type=F32).astype(BF16)


def own_head(scores, lane_head, kv_heads):
    place = scores.shape[0] // kv_heads
    kept = scores[:place]
    for head in range(1, kv_heads):
        kept = jnp.where(lane_head == head, scores[head * place:(head + 1) * place], kept)
    return kept


def all_heads(kept, lane_head, kv_heads):
    none = jnp.zeros_like(kept)
    return jnp.concatenate(
        [jnp.where(lane_head == head, kept, none) for head in range(kv_heads)], axis=0
    )


def lanes(rows, heads, kv_heads):
    lane = lax.broadcasted_iota(jnp.int32, (1, rows), 1)
    return lane // heads, lane % heads // (heads // kv_heads)


def plan_spans(grp_count, blocks):
    return grp_count, 2 * grp_count, 2 * grp_count + blocks, 2 * grp_count + 2 * blocks


def plan_kernel(lists_ref, counts_ref, plan_ref, *, grp_count, blocks):
    group, mine = lax.axis_index("grp"), lax.axis_index("uly")
    per_group = 2 * blocks
    low = group * per_group
    sib_at, source_at, give_at, seen_at = plan_spans(grp_count, blocks)
    for other in range(grp_count):
        place = jnp.int32(-1)
        for at in range(other * per_group, (other + 1) * per_group):
            here = lists_ref[at] - low
            wanted = (here >= 0) & (here < per_group) & (counts_ref[at] > 0)
            place = jnp.where(wanted, here, place)
        own = place - mine * blocks
        sib = place - (1 - mine) * blocks
        plan_ref[other] = jnp.where((own >= 0) & (own < blocks), own, -1)
        plan_ref[sib_at + other] = jnp.where((sib >= 0) & (sib < blocks), sib, -1)
    for block in range(blocks):
        at = low + mine * blocks + block
        plan_ref[source_at + block] = lax.div(lists_ref[at], per_group)
        plan_ref[seen_at + block] = counts_ref[at]
        at = low + (1 - mine) * blocks + block
        plan_ref[give_at + block] = lax.div(lists_ref[at], per_group)


def pack_kernel(k_hbm, v_hbm, k_ref, v_ref, given_ref, sems, *, kv_heads):
    blocks, _, half, _ = given_ref.shape
    copies = [
        pltpu.make_async_copy(k_hbm, k_ref, sems.at[0]),
        pltpu.make_async_copy(v_hbm, v_ref, sems.at[1]),
    ]
    for copy in copies:
        copy.start()
    order = half_order(2 * half, kv_heads, 1 - lax.axis_index("uly"))
    for which, ref in enumerate((k_ref, v_ref)):
        copies[which].wait()
        for block in range(blocks):
            given_ref[block, which] = reorder(order, ref[block * 2 * half:(block + 1) * 2 * half])


def send_own_kernel(plan_ref, blocks_ref, out_ref):
    for group in range(out_ref.shape[0]):
        out_ref[group] = blocks_ref[jnp.maximum(plan_ref[group], 0)]


def send_sibling_kernel(plan_ref, blocks_ref, _, out_ref, *, first):
    for group in range(out_ref.shape[0]):
        place = plan_ref[first + group]

        @pl.when(place >= 0)
        def _():
            out_ref[group] = blocks_ref[place]


def giving_kernel(plan_ref, arrived_ref, *out_refs, give_at):
    block = 0
    for out_ref in out_refs:
        for at in range(out_ref.shape[0]):
            out_ref[at] = arrived_ref[plan_ref[give_at + block]]
            block += 1


def returning_kernel(plan_ref, *refs, source_at):
    part_refs, (out_ref, sems) = refs[:-2], refs[-2:]
    copies = []
    for part_ref in part_refs:
        for at in range(part_ref.shape[0]):
            block = len(copies)
            target = out_ref.at[plan_ref[source_at + block]]
            copies.append(pltpu.make_async_copy(part_ref.at[at], target, sems.at[block]))
            copies[-1].start()
    for copy in copies:
        copy.wait()


def near_kernel(
    q_hbm, g_hbm, k_ref, v_ref, given_ref, stat_ref, kept_ref, q_ref, g_ref, sems,
    *, heads, kv_heads, score_scale
):
    blocks = stat_ref.shape[0]
    rows = q_ref.shape[0] // blocks
    half = given_ref.shape[2]
    place = half // kv_heads
    copies = []
    for block in range(blocks):
        span = pl.ds(block * rows, rows)
        for which, (source, target) in enumerate(((q_hbm, q_ref), (g_hbm, g_ref))):
            sem = sems.at[which, block]
            copies.append(pltpu.make_async_copy(source.at[span], target.at[span], sem))
            copies[-1].start()
    mine = lax.axis_index("uly")
    order = half_order(2 * half, kv_heads, mine)
    for block in range(blocks):
        narrow = slice(block * 2 * half, (block + 1) * 2 * half)
        kept_ref[block, 0] = reorder(order, k_ref[narrow])
        kept_ref[block, 1] = reorder(order, v_ref[narrow])
    token, lane_head = lanes(rows, heads, kv_heads)
    key = lax.broadcasted_iota(jnp.int32, (2 * place, rows), 0)
    part = jnp.where(key < place, mine, 1 - mine)
    causal = key % place + part * place <= token
    for block in range(blocks):
        span = slice(block * rows, (block + 1) * rows)
        pieces = []
        for which, ref in enumerate((q_ref, g_ref)):
            copies[2 * block + which].wait()
            both = jnp.concatenate([kept_ref[block, which], given_ref[block, which]], axis=0)
            full = dot_last(both, ref[span])
            pieces.append(
                jnp.concatenate(
                    [
                        own_head(full[:half], lane_head, kv_heads),
                        own_head(full[half:], lane_head, kv_heads),
                    ],
                    axis=0,
                )
            )
        scores = jnp.where(causal, pieces[0] * score_scale, HIDDEN)
        highest = jnp.max(scores, axis=0, keepdims=True)
        raised = jnp.exp(scores - highest)
        stat_ref[block, 0:1] = highest
        stat_ref[block, 1:2] = jnp.sum(raised, axis=0, keepdims=True)
        stat_ref[block, 2:3] = jnp.sum(raised * pieces[1], axis=0, keepdims=True)


def far_scores(part_ref, at, q, g, seen, lane_head, kv_heads, score_scale):
    hidden = jnp.where(seen > 0, 0.0, HIDDEN)
    scores = own_head(dot_last(part_ref[at, 0], q), lane_head, kv_heads) * score_scale + hidden
    return scores, own_head(dot_last(part_ref[at, 1], g), lane_head, kv_heads)


def merged(stat_ref, block, scores, dprobs):
    before = stat_ref[block, 0:1]
    highest = jnp.maximum(before, jnp.max(scores, axis=0, keepdims=True))
    raised = jnp.exp(scores - highest)
    shrink = jnp.exp(before - highest)
    total = shrink * stat_ref[block, 1:2] + jnp.sum(raised, axis=0, keepdims=True)
    delta = shrink * stat_ref[block, 2:3] + jnp.sum(raised * dprobs, axis=0, keepdims=True)
    return highest, raised, total, delta


def far_gradients(probs, dprobs, delta, q, g, lane_head, kv_heads, score_scale):
    dscores = (probs * (dprobs - delta)).astype(BF16)
    dk = jnp.dot(all_heads(dscores, lane_head, kv_heads), q, preferred_element_type=F32)
    dv = jnp.dot(all_heads(probs.astype(BF16), lane_head, kv_heads), g, preferred_element_type=F32)
    return (dk * score_scale).astype(BF16), dv.astype(BF16)


def mid_kernel(
    plan_ref, q_ref, g_ref, stat_ref, arrived_ref, out_ref,
    *, heads, kv_heads, score_scale, source_at, seen_at
):
    blocks = stat_ref.shape[0]
    rows = q_ref.shape[0] // blocks
    _, lane_head = lanes(rows, heads, kv_heads)
    for block in range(blocks):
        span = slice(block * rows, (block + 1) * rows)
        scores, dprobs = far_scores(
            arrived_ref, plan_ref[source_at + block], q_ref[span], g_ref[span],
            plan_ref[seen_at + block],            lane_head, kv_heads, score_scale,
        )
        highest, _, total, delta = merged(stat_ref, block, scores, dprobs)
        out_ref[block, 0:1] = highest
        out_ref[block, 1:2] = total
        out_ref[block, 2:3] = delta


def far_kernel(
    plan_ref, q_ref, g_ref, stat_ref, other_ref, grad_ref, out_ref,
    *, heads, kv_heads, score_scale, seen_at, first
):
    rows = q_ref.shape[0] // stat_ref.shape[0]
    _, lane_head = lanes(rows, heads, kv_heads)
    for at in range(other_ref.shape[0]):
        block = first + at
        span = slice(block * rows, (block + 1) * rows)
        q = q_ref[span]
        g = g_ref[span]
        scores, dprobs = far_scores(
            other_ref, at, q, g, plan_ref[seen_at + block], lane_head, kv_heads, score_scale
        )
        highest, raised, total, delta = merged(stat_ref, block, scores, dprobs)
        inverse = 1.0 / total
        delta = delta * inverse
        grad_ref[at, 0], grad_ref[at, 1] = far_gradients(
            raised * inverse, dprobs, delta, q, g, lane_head, kv_heads, score_scale
        )
        out_ref[at, 0:1] = highest
        out_ref[at, 1:2] = inverse
        out_ref[at, 2:3] = delta


def mine_kernel(
    plan_ref, q_ref, g_ref, arrived_ref, stat_ref, grad_ref,
    *, heads, kv_heads, score_scale, source_at, seen_at, rows, first
):
    _, lane_head = lanes(rows, heads, kv_heads)
    for at in range(stat_ref.shape[0]):
        block = first + at
        span = slice(block * rows, (block + 1) * rows)
        q = q_ref[span]
        g = g_ref[span]
        scores, dprobs = far_scores(
            arrived_ref, plan_ref[source_at + block], q, g, plan_ref[seen_at + block],
            lane_head, kv_heads, score_scale,
        )
        probs = jnp.exp(scores - stat_ref[at, 0:1]) * stat_ref[at, 1:2]
        grad_ref[at, 0], grad_ref[at, 1] = far_gradients(
            probs, dprobs, stat_ref[at, 2:3], q, g, lane_head, kv_heads, score_scale
        )


def local_kernel(
    plan_ref, q_ref, g_ref, k_ref, v_ref, mine_ref, other_ref,
    att_ref, dq_ref, dk_ref, dv_ref, bias_ref, *, heads, kv_heads, score_scale, seen_at
):
    step = pl.program_id(0)
    rows = q_ref.shape[0]
    cols = k_ref.shape[0]

    @pl.when(step == 0)
    def _():
        half = cols // 2
        place = half // kv_heads
        row = lax.broadcasted_iota(jnp.int32, (rows, cols), 0)
        col = lax.broadcasted_iota(jnp.int32, (rows, cols), 1)
        same = row % heads // (heads // kv_heads) == col % half // place
        causal = col // half * place + col % place <= row // heads
        bias_ref[:, :cols] = jnp.where(same & causal, 0.0, HIDDEN)
        bias_ref[:, cols:] = jnp.where(same, 0.0, HIDDEN)

    far_bias = jnp.where(plan_ref[seen_at + step] > 0, 0.0, HIDDEN)
    order = head_major(cols, kv_heads)
    k_near = reorder(order, k_ref[...])
    v_near = reorder(order, v_ref[...])
    k_all = jnp.concatenate([k_near, mine_ref[0, 0], other_ref[0, 0]], axis=0)
    v_all = jnp.concatenate([v_near, mine_ref[0, 1], other_ref[0, 1]], axis=0)
    q = q_ref[...]
    g = g_ref[...]
    scores = dot_last(q, k_all) * score_scale + bias_ref[...]
    scores = jnp.concatenate([scores[:, :cols], scores[:, cols:] + far_bias], axis=1)
    highest = jnp.max(scores, axis=1, keepdims=True)
    raised = jnp.exp(scores - highest)
    total = jnp.sum(raised, axis=1, keepdims=True)
    probs = raised * (1.0 / total)
    weights = probs.astype(BF16)
    attended = jnp.dot(weights, v_all, preferred_element_type=F32).astype(BF16)
    att_ref[...] = attended
    delta = jnp.sum(g.astype(F32) * attended.astype(F32), axis=1, keepdims=True)
    dscores = (probs * (dot_last(g, v_all) - delta)).astype(BF16)
    dq = jnp.dot(dscores, k_all, preferred_element_type=F32) * score_scale
    dq_ref[...] = dq.astype(BF16)
    dk_ref[...] = dot_first(dscores[:, :cols], q) * score_scale
    dv_ref[...] = dot_first(weights[:, :cols], g)


def landing_kernel(plan_ref, landed_ref, out_ref, sum_ref, *, first):
    sum_ref[...] = jnp.zeros_like(sum_ref)
    for group in range(landed_ref.shape[0]):
        place = plan_ref[first + group]

        @pl.when(place >= 0)
        def _():
            sum_ref[place] = sum_ref[place] + landed_ref[group].astype(F32)

    out_ref[...] = sum_ref[...].astype(out_ref.dtype)


def finish_kernel(
    dk_near_ref, dv_near_ref, own_ref, back_ref, dk_ref, dv_ref, *, kv_heads
):
    blocks, _, half, _ = back_ref.shape
    mine = lax.axis_index("uly") == 0
    order = head_major(2 * half, kv_heads)
    for block in range(blocks):
        span = slice(block * 2 * half, (block + 1) * 2 * half)
        for near_ref, out_ref, which in ((dk_near_ref, dk_ref, 0), (dv_near_ref, dv_ref, 1)):
            own = own_ref[block, which]
            back = back_ref[block, which].astype(F32)
            far = jnp.concatenate([jnp.where(mine, own, back), jnp.where(mine, back, own)], axis=0)
            summed = (near_ref[span] + far).astype(BF16)
            out_ref[span] = dot_first(order, summed).astype(BF16)


def take_rows(array, index):
    return array.at[index].get(mode="promise_in_bounds")


def whole_blocks(queries, keys, values, output_cotangent, block_lists, list_counts):
    grp_count = lax.axis_size("grp")
    uly_count = lax.axis_size("uly")
    tokens, heads, width = queries.shape
    kv_heads = keys.shape[1]
    per_group = block_lists.shape[0] // grp_count
    block_tok = tokens * uly_count // per_group
    mine_blocks = tokens // block_tok
    rows = block_tok * heads
    cols = block_tok * kv_heads
    half = cols // 2
    sizes = dict(heads=heads, kv_heads=kv_heads, score_scale=width ** (-0.5))
    swap = [(0, 1), (1, 0)]

    sib_at, source_at, give_at, seen_at = plan_spans(grp_count, mine_blocks)

    q2 = queries.reshape(tokens * heads, width)
    g2 = output_cotangent.reshape(tokens * heads, width)
    k2 = keys.reshape(tokens * kv_heads, width)
    v2 = values.reshape(tokens * kv_heads, width)

    part_shape = jax.ShapeDtypeStruct((mine_blocks, 2, half, width), BF16)
    slots = (grp_count, 2, half, width)
    stat_shape = jax.ShapeDtypeStruct((mine_blocks, 8, rows), F32)
    row_shape = jax.ShapeDtypeStruct(q2.shape, BF16)
    near_shape = jax.ShapeDtypeStruct(k2.shape, F32)
    small_shape = jax.ShapeDtypeStruct(k2.shape, BF16)
    sum_scratch = [pltpu.VMEM((mine_blocks, 2, half, width), F32)]
    limit = pltpu.CompilerParams(vmem_limit_bytes=24 * 1024 * 1024)
    vmem = pl.BlockSpec(memory_space=pltpu.VMEM)
    smem = pl.BlockSpec(memory_space=pltpu.SMEM)
    anywhere = pl.BlockSpec(memory_space=pltpu.HBM)

    def call(kernel, name, scalars, operands, out_shape, scratch=(), into=None, out_spec=vmem):
        extra = () if into is None else (into,)
        return pl.pallas_call(
            kernel,
            in_specs=[smem] * len(scalars) + [vmem] * (len(operands) + len(extra)),
            out_specs=jax.tree.map(lambda _: out_spec, out_shape),
            out_shape=out_shape,
            scratch_shapes=scratch,
            input_output_aliases={len(scalars) + len(operands): 0} if extra else {},
            compiler_params=limit,
            name=name,
        )(*scalars, *operands, *extra)

    def step_rows(i, *_):
        return (i, 0)

    def step_part(i, *_):
        return (i, 0, 0, 0)

    def in_hbm(array):
        return pltpu.with_memory_space_constraint(array, pltpu.HBM)

    k_here, v_here, given = pl.pallas_call(
        partial(pack_kernel, kv_heads=kv_heads),
        in_specs=[anywhere, anywhere],
        out_specs=[vmem, vmem, vmem],
        out_shape=[small_shape, small_shape, part_shape],
        scratch_shapes=[pltpu.SemaphoreType.DMA((2,))],
        compiler_params=limit,
        name="pack",
    )(in_hbm(k2), in_hbm(v2))
    plan = pl.pallas_call(
        partial(plan_kernel, grp_count=grp_count, blocks=mine_blocks),
        in_specs=[smem, smem],
        out_specs=smem,
        out_shape=pltpu.SMEM((seen_at + mine_blocks,), jnp.int32),
        compiler_params=limit,
        name="plan",
    )(in_hbm(block_lists.reshape(-1)), in_hbm(list_counts))
    gotten = lax.ppermute(given, "uly", swap)
    row_spec = pl.BlockSpec((rows, width), step_rows)
    part_spec = pl.BlockSpec((1, 2, half, width), step_part)
    stats, kept = pl.pallas_call(
        partial(near_kernel, **sizes),
        in_specs=[anywhere, anywhere, vmem, vmem, vmem],
        out_specs=[vmem, vmem],
        out_shape=[stat_shape, part_shape],
        scratch_shapes=[
            pltpu.VMEM(q2.shape, BF16), pltpu.VMEM(q2.shape, BF16),
            pltpu.SemaphoreType.DMA((2, mine_blocks)),
        ],
        compiler_params=limit,
        name="near",
    )(in_hbm(q2), in_hbm(g2), k_here, v_here, given)
    outgoing = call(
        send_own_kernel, "send_own", (plan,), (kept,),
        jax.ShapeDtypeStruct(slots, BF16),
    )
    gotten, stats = lax.optimization_barrier((gotten, stats))
    outgoing = call(
        partial(send_sibling_kernel, first=sib_at), "send_sibling", (plan,), (gotten,),
        jax.ShapeDtypeStruct(slots, BF16), into=outgoing,
    )
    arrived = lax.all_to_all(outgoing, "grp", split_axis=0, concat_axis=0, tiled=True)
    chunks = 2 if mine_blocks % 2 == 0 else 1
    chunk = mine_blocks // chunks
    chunk_shape = jax.ShapeDtypeStruct((chunk, 2, half, width), BF16)
    giving = call(
        partial(giving_kernel, give_at=give_at), "give", (plan,), (arrived,),
        [chunk_shape] * chunks,
    )
    stats = call(
        partial(mid_kernel, source_at=source_at, seen_at=seen_at, **sizes), "mid", (plan,),
        (q2, g2, stats, arrived), stat_shape,
    )
    others = []
    for part in giving:
        if others:
            part, stats = lax.optimization_barrier((part, stats))
        others.append(lax.ppermute(part, "uly", swap))
    grads, final = [], []
    for at, other in enumerate(others):
        grad, stat = call(
            partial(far_kernel, seen_at=seen_at, first=at * chunk, **sizes), "far", (plan,),
            (q2, g2, stats, other),
            [chunk_shape, jax.ShapeDtypeStruct((chunk, 8, rows), F32)],
        )
        grads.append(grad)
        final.append(stat)
    from_sib = [lax.ppermute(part, "uly", swap) for part in grads]
    mine = [None] * chunks
    for at in reversed(range(chunks)):
        if at + 1 < chunks:
            from_sib[at], final[at] = lax.optimization_barrier((from_sib[at], final[at]))
        mine[at] = call(
            partial(
                mine_kernel, source_at=source_at, seen_at=seen_at, rows=rows, first=at * chunk,
                **sizes,
            ),
            "mine", (plan,), (q2, g2, arrived, final[at]), chunk_shape,
        )
    returning = call(
        partial(returning_kernel, source_at=source_at), "return", (plan,), mine + from_sib,
        pltpu.HBM(slots, BF16), [pltpu.SemaphoreType.DMA((per_group,))], out_spec=anywhere,
    )
    other = jnp.concatenate(others)
    returning, k2l = lax.optimization_barrier((returning, k2))
    landed = lax.all_to_all(returning, "grp", split_axis=0, concat_axis=0, tiled=True)

    def from_source(i, plan_ref):
        return (plan_ref[source_at + i], 0, 0, 0)

    col_spec = pl.BlockSpec((cols, width), step_rows)
    attended, dq, dk_near, dv_near = pl.pallas_call(
        partial(local_kernel, seen_at=seen_at, **sizes),
        grid_spec=pltpu.PrefetchScalarGridSpec(
            num_scalar_prefetch=1,
            grid=(mine_blocks,),
            in_specs=[
                row_spec, row_spec, col_spec, col_spec,
                pl.BlockSpec((1, 2, half, width), from_source),
                part_spec,
            ],
            out_specs=[row_spec, row_spec, col_spec, col_spec],
            scratch_shapes=[pltpu.VMEM((rows, 2 * cols), F32)],
        ),
        out_shape=[row_shape, row_shape, near_shape, near_shape],
        compiler_params=limit,
        name="local",
    )(plan, q2, g2, k2l, v2, arrived, other)
    landed, dk_near = lax.optimization_barrier((landed, dk_near))
    give = call(
        partial(landing_kernel, first=sib_at), "land_sibling", (plan,), (landed,), part_shape,
        sum_scratch,
    )
    back = lax.ppermute(give, "uly", swap)
    own = call(
        partial(landing_kernel, first=0), "land_own", (plan,), (landed,),
        jax.ShapeDtypeStruct(part_shape.shape, F32), sum_scratch,
    )
    dk, dv = call(
        partial(finish_kernel, kv_heads=kv_heads), "finish", (),
        (dk_near, dv_near, own, back), [small_shape, small_shape],
    )
    return (
        attended.reshape(queries.shape), dq.reshape(queries.shape),
        dk.reshape(keys.shape), dv.reshape(keys.shape),
    )


def on_device(queries, keys, values, output_cotangent, block_lists, list_counts):
    uly_count = lax.axis_size("uly")
    grp_count = lax.axis_size("grp")
    blocks_all, remote = block_lists.shape
    block_tok = queries.shape[0] * uly_count * grp_count // blocks_all
    held_whole = queries.shape[0] % block_tok == 0
    run = whole_blocks if held_whole and remote == 1 and uly_count == 2 else spread_blocks
    return run(queries, keys, values, output_cotangent, block_lists, list_counts)


def solution(mesh):
    placed = (
        P(("grp", "uly"), None, None),
        P(("grp", "uly"), None, None),
        P(("grp", "uly"), None, None),
        P(("grp", "uly"), None, None),
        P(),
        P(),
    )
    return jax.shard_map(
        on_device,
        mesh=mesh,
        in_specs=placed,
        out_specs=(
            P(("grp", "uly"), None, None),
            P(("grp", "uly"), None, None),
            P(("grp", "uly"), None, None),
            P(("grp", "uly"), None, None),
        ),
        check_vma=False,
    )
```

```python
from functools import partial

import jax
import jax.numpy as jnp
from jax import lax
from jax.experimental import pallas as pl
from jax.experimental.pallas import tpu as pltpu
from jax.sharding import PartitionSpec as P


def spread_blocks(queries, keys, values, output_cotangent, block_lists, list_counts):
    uly_count = lax.axis_size("uly")
    grp_count = lax.axis_size("grp")
    my_group = lax.axis_index("grp")
    tokens, head_count, head_width = queries.shape
    kv_heads = keys.shape[1]
    copies = max(1, uly_count // kv_heads)
    blocks_all, remote = block_lists.shape
    per_group = blocks_all // grp_count
    block_tok = tokens * uly_count // per_group
    group_tok = tokens * uly_count
    score_scale = head_width ** (-0.5)
    lists = block_lists.reshape(grp_count, per_group, remote)
    counted = (jnp.arange(remote)[None, :] < list_counts[:, None]).reshape(
        grp_count, per_group, remote
    )
    wanted = (lists // per_group == my_group) & counted
    send_place = jnp.sum(jnp.where(wanted, lists % per_group, 0), axis=(1, 2))
    sending = jnp.any(wanted, axis=(1, 2))
    mine_source = lax.dynamic_index_in_dim(lists, my_group, 0, keepdims=False) // per_group
    mine_counted = lax.dynamic_index_in_dim(counted, my_group, 0, keepdims=False)
    trip_count = jnp.max(jnp.sum(mine_counted.astype(jnp.int32), axis=1))

    def to_blocks(array_in):
        return array_in.reshape((per_group, block_tok) + array_in.shape[1:])

    keys_wide = jnp.repeat(keys, copies, axis=1)
    values_wide = jnp.repeat(values, copies, axis=1)
    query_heads, grad_heads, key_heads, value_heads = (
        lax.all_to_all(queries, "uly", split_axis=1, concat_axis=0, tiled=True),
        lax.all_to_all(output_cotangent, "uly", split_axis=1, concat_axis=0, tiled=True),
        lax.all_to_all(keys_wide, "uly", split_axis=1, concat_axis=0, tiled=True),
        lax.all_to_all(values_wide, "uly", split_axis=1, concat_axis=0, tiled=True),
    )
    stacked = jnp.stack([to_blocks(key_heads), to_blocks(value_heads)])
    outgoing = jnp.take(stacked, send_place, axis=1)
    arrived = lax.all_to_all(outgoing, "grp", split_axis=1, concat_axis=1, tiled=True)
    kv_local = key_heads.shape[1]
    heads_local = query_heads.shape[1]
    heads_per_group = heads_local // kv_local
    query_blk = query_heads.reshape(per_group, block_tok, kv_local, heads_per_group, head_width)
    grad_blk = grad_heads.reshape(per_group, block_tok, kv_local, heads_per_group, head_width)
    key_blk = to_blocks(key_heads)
    value_blk = to_blocks(value_heads)
    far_keys = arrived[0]
    far_values = arrived[1]
    causal = jnp.arange(block_tok)[:, None] >= jnp.arange(block_tok)[None, :]

    def logits(key_rows):
        return (
            jnp.einsum("pqkgd,pjkd->pkgqj", query_blk, key_rows, preferred_element_type=jnp.float32)
            * score_scale
        )

    def slot_rows(slot_index):
        source = lax.dynamic_index_in_dim(mine_source, slot_index, 1, keepdims=False)
        counted_slot = lax.dynamic_index_in_dim(mine_counted, slot_index, 1, keepdims=False)
        return (
            jnp.take(far_keys, source, axis=0),
            jnp.take(far_values, source, axis=0),
            counted_slot,
            source,
        )

    def masked(scores, counted_slot):
        return jnp.where(counted_slot[:, None, None, None, None], scores, -jnp.inf)

    near_scores = jnp.where(causal, logits(key_blk), -jnp.inf)
    highest = jnp.max(near_scores, axis=-1)
    denominator = jnp.sum(jnp.exp(near_scores - highest[..., None]), axis=-1)

    def max_sweep(slot_index, state_pair):
        highest, denominator = state_pair
        key_rows, value_rows, counted_slot, source = slot_rows(slot_index)
        scores = masked(logits(key_rows), counted_slot)
        new_highest = jnp.maximum(highest, jnp.max(scores, axis=-1))
        denominator = denominator * jnp.exp(highest - new_highest) + jnp.sum(
            jnp.exp(scores - new_highest[..., None]), axis=-1
        )
        return (new_highest, denominator)

    highest, denominator = lax.fori_loop(0, trip_count, max_sweep, (highest, denominator))
    log_total = highest + jnp.log(denominator)

    def softmax_weights(scores):
        return jnp.exp(scores - log_total[..., None])

    summed = jnp.einsum(
        "pkgqj,pjkd->pqkgd",
        softmax_weights(near_scores).astype(jnp.bfloat16),
        value_blk,
        preferred_element_type=jnp.float32,
    )

    def value_sweep(slot_index, summed):
        key_rows, value_rows, counted_slot, source = slot_rows(slot_index)
        weights = softmax_weights(masked(logits(key_rows), counted_slot)).astype(jnp.bfloat16)
        return summed + jnp.einsum(
            "pkgqj,pjkd->pqkgd", weights, value_rows, preferred_element_type=jnp.float32
        )

    summed = lax.fori_loop(0, trip_count, value_sweep, summed)
    attended_blk = summed.astype(jnp.bfloat16)
    row_delta = jnp.transpose(
        jnp.sum(grad_blk.astype(jnp.float32) * attended_blk.astype(jnp.float32), axis=-1),
        (0, 2, 3, 1),
    )

    def backward(scores, key_rows, value_rows):
        probs = softmax_weights(scores)
        weights = probs.astype(jnp.bfloat16)
        dprobs = jnp.einsum(
            "pqkgd,pjkd->pkgqj", grad_blk, value_rows, preferred_element_type=jnp.float32
        )
        dscores = (probs * (dprobs - row_delta[..., None])).astype(jnp.bfloat16)
        query_term = jnp.einsum(
            "pkgqj,pjkd->pqkgd", dscores, key_rows, preferred_element_type=jnp.float32
        )
        key_term = (
            jnp.einsum("pkgqj,pqkgd->pjkd", dscores, query_blk, preferred_element_type=jnp.float32)
            * score_scale
        )
        value_term = jnp.einsum(
            "pkgqj,pqkgd->pjkd", weights, grad_blk, preferred_element_type=jnp.float32
        )
        return (query_term, key_term, value_term)

    query_sum, key_near, value_near = backward(near_scores, key_blk, value_blk)
    far_grads = jnp.zeros((2, grp_count, block_tok, kv_local, head_width), jnp.float32)

    def grad_sweep(slot_index, state_pair):
        query_sum, far_grads = state_pair
        key_rows, value_rows, counted_slot, source = slot_rows(slot_index)
        query_term, key_term, value_term = backward(
            masked(logits(key_rows), counted_slot), key_rows, value_rows
        )
        routing = (
            (source[:, None] == jnp.arange(grp_count)[None, :]) & counted_slot[:, None]
        ).astype(jnp.float32)
        routed = jnp.einsum(
            "ps,xpjkd->xsjkd",
            routing,
            jnp.stack([key_term, value_term]),
            precision=lax.Precision.HIGHEST,
        )
        return (query_sum + query_term, far_grads + routed)

    query_sum, far_grads = lax.fori_loop(0, trip_count, grad_sweep, (query_sum, far_grads))
    owners = ((send_place[:, None] == jnp.arange(per_group)[None, :]) & sending[:, None]).astype(
        jnp.float32
    )
    returned = lax.all_to_all(far_grads, "grp", split_axis=1, concat_axis=1, tiled=True)
    landed = jnp.einsum("sp,xsjkd->xpjkd", owners, returned, precision=lax.Precision.HIGHEST)
    key_local = (key_near + landed[0]).reshape(group_tok, kv_local, head_width)
    value_local = (value_near + landed[1]).reshape(group_tok, kv_local, head_width)
    attended_rows = attended_blk.reshape(group_tok, heads_local, head_width)
    query_rows = (
        (query_sum * score_scale).astype(jnp.bfloat16).reshape(group_tok, heads_local, head_width)
    )
    attended, query_grad = (
        lax.all_to_all(attended_rows, "uly", split_axis=0, concat_axis=1, tiled=True),
        lax.all_to_all(query_rows, "uly", split_axis=0, concat_axis=1, tiled=True),
    )
    key_parts, value_parts = (
        lax.all_to_all(key_local, "uly", split_axis=0, concat_axis=1, tiled=True),
        lax.all_to_all(value_local, "uly", split_axis=0, concat_axis=1, tiled=True),
    )
    key_gradient = jnp.sum(key_parts.reshape(tokens, kv_heads, copies, head_width), axis=2).astype(
        jnp.bfloat16
    )
    value_gradient = jnp.sum(
        value_parts.reshape(tokens, kv_heads, copies, head_width), axis=2
    ).astype(jnp.bfloat16)
    return (attended, query_grad, key_gradient, value_gradient)


HIDDEN = -1e30
LAST = (((1,), (1,)), ((), ()))
FIRST = (((0,), (0,)), ((), ()))
F32 = jnp.float32
BF16 = jnp.bfloat16


def dot_last(left, right):
    return lax.dot_general(left, right, LAST, preferred_element_type=F32)


def dot_first(left, right):
    return lax.dot_general(left, right, FIRST, preferred_element_type=F32)


def head_major(cols, kv_heads):
    half = cols // 2
    place = half // kv_heads
    row = lax.broadcasted_iota(jnp.int32, (cols, cols), 0)
    col = lax.broadcasted_iota(jnp.int32, (cols, cols), 1)
    token = row // half * place + row % place
    return jnp.where(col == token * kv_heads + row % half // place, 1.0, 0.0).astype(BF16)


def half_order(cols, kv_heads, which):
    half = cols // 2
    place = half // kv_heads
    row = lax.broadcasted_iota(jnp.int32, (half, cols), 0)
    col = lax.broadcasted_iota(jnp.int32, (half, cols), 1)
    token = which * place + row % place
    return jnp.where(col == token * kv_heads + row // place, 1.0, 0.0).astype(BF16)


def reorder(one_hot, array):
    return jnp.dot(one_hot, array, preferred_element_type=F32).astype(BF16)


def own_head(scores, lane_head, kv_heads):
    place = scores.shape[0] // kv_heads
    kept = scores[:place]
    for head in range(1, kv_heads):
        kept = jnp.where(lane_head == head, scores[head * place:(head + 1) * place], kept)
    return kept


def all_heads(kept, lane_head, kv_heads):
    none = jnp.zeros_like(kept)
    return jnp.concatenate(
        [jnp.where(lane_head == head, kept, none) for head in range(kv_heads)], axis=0
    )


def lanes(rows, heads, kv_heads):
    lane = lax.broadcasted_iota(jnp.int32, (1, rows), 1)
    return lane // heads, lane % heads // (heads // kv_heads)


def plan_spans(grp_count, blocks):
    return grp_count, 2 * grp_count, 2 * grp_count + blocks, 2 * grp_count + 2 * blocks


def plan_kernel(lists_ref, counts_ref, plan_ref, *, grp_count, blocks):
    group, mine = lax.axis_index("grp"), lax.axis_index("uly")
    per_group = 2 * blocks
    low = group * per_group
    sib_at, source_at, give_at, seen_at = plan_spans(grp_count, blocks)
    for other in range(grp_count):
        place = jnp.int32(-1)
        for at in range(other * per_group, (other + 1) * per_group):
            here = lists_ref[at] - low
            wanted = (here >= 0) & (here < per_group) & (counts_ref[at] > 0)
            place = jnp.where(wanted, here, place)
        own = place - mine * blocks
        sib = place - (1 - mine) * blocks
        plan_ref[other] = jnp.where((own >= 0) & (own < blocks), own, -1)
        plan_ref[sib_at + other] = jnp.where((sib >= 0) & (sib < blocks), sib, -1)
    for block in range(blocks):
        at = low + mine * blocks + block
        plan_ref[source_at + block] = lax.div(lists_ref[at], per_group)
        plan_ref[seen_at + block] = counts_ref[at]
        at = low + (1 - mine) * blocks + block
        plan_ref[give_at + block] = lax.div(lists_ref[at], per_group)


def pack_kernel(k_hbm, v_hbm, k_ref, v_ref, given_ref, sems, *, kv_heads):
    blocks, _, half, _ = given_ref.shape
    copies = [
        pltpu.make_async_copy(k_hbm, k_ref, sems.at[0]),
        pltpu.make_async_copy(v_hbm, v_ref, sems.at[1]),
    ]
    for copy in copies:
        copy.start()
    order = half_order(2 * half, kv_heads, 1 - lax.axis_index("uly"))
    for which, ref in enumerate((k_ref, v_ref)):
        copies[which].wait()
        for block in range(blocks):
            given_ref[block, which] = reorder(order, ref[block * 2 * half:(block + 1) * 2 * half])


def send_own_kernel(plan_ref, k_ref, v_ref, kept_ref, out_ref, *, kv_heads):
    blocks, _, half, _ = kept_ref.shape
    order = half_order(2 * half, kv_heads, lax.axis_index("uly"))
    for block in range(blocks):
        span = slice(block * 2 * half, (block + 1) * 2 * half)
        kept_ref[block, 0] = reorder(order, k_ref[span])
        kept_ref[block, 1] = reorder(order, v_ref[span])
    for group in range(out_ref.shape[0]):
        out_ref[group] = kept_ref[jnp.maximum(plan_ref[group], 0)]


def send_sibling_kernel(plan_ref, blocks_ref, _, out_ref, *, first):
    for group in range(out_ref.shape[0]):
        place = plan_ref[first + group]

        @pl.when(place >= 0)
        def _():
            out_ref[group] = blocks_ref[place]


def giving_kernel(plan_ref, arrived_ref, *out_refs, give_at):
    block = 0
    for out_ref in out_refs:
        for at in range(out_ref.shape[0]):
            out_ref[at] = arrived_ref[plan_ref[give_at + block]]
            block += 1


def returning_kernel(plan_ref, *refs, source_at):
    part_refs, (out_ref, sems) = refs[:-2], refs[-2:]
    copies = []
    for part_ref in part_refs:
        for at in range(part_ref.shape[0]):
            block = len(copies)
            target = out_ref.at[plan_ref[source_at + block]]
            copies.append(pltpu.make_async_copy(part_ref.at[at], target, sems.at[block]))
            copies[-1].start()
    for copy in copies:
        copy.wait()


def near_kernel(
    q_ref, g_ref, kept_ref, given_ref, stat_ref, *, heads, kv_heads, score_scale
):
    blocks = stat_ref.shape[0]
    rows = q_ref.shape[0] // blocks
    half = given_ref.shape[2]
    place = half // kv_heads
    mine = lax.axis_index("uly")
    token, lane_head = lanes(rows, heads, kv_heads)
    key = lax.broadcasted_iota(jnp.int32, (2 * place, rows), 0)
    part = jnp.where(key < place, mine, 1 - mine)
    causal = key % place + part * place <= token
    for block in range(blocks):
        span = slice(block * rows, (block + 1) * rows)
        pieces = []
        for which, ref in enumerate((q_ref, g_ref)):
            both = jnp.concatenate([kept_ref[block, which], given_ref[block, which]], axis=0)
            full = dot_last(both, ref[span])
            pieces.append(
                jnp.concatenate(
                    [
                        own_head(full[:half], lane_head, kv_heads),
                        own_head(full[half:], lane_head, kv_heads),
                    ],
                    axis=0,
                )
            )
        scores = jnp.where(causal, pieces[0] * score_scale, HIDDEN)
        highest = jnp.max(scores, axis=0, keepdims=True)
        raised = jnp.exp(scores - highest)
        stat_ref[block, 0:1] = highest
        stat_ref[block, 1:2] = jnp.sum(raised, axis=0, keepdims=True)
        stat_ref[block, 2:3] = jnp.sum(raised * pieces[1], axis=0, keepdims=True)


def far_scores(part_ref, at, q, g, seen, lane_head, kv_heads, score_scale):
    hidden = jnp.where(seen > 0, 0.0, HIDDEN)
    scores = own_head(dot_last(part_ref[at, 0], q), lane_head, kv_heads) * score_scale + hidden
    return scores, own_head(dot_last(part_ref[at, 1], g), lane_head, kv_heads)


def merged(stat_ref, block, scores, dprobs):
    before = stat_ref[block, 0:1]
    highest = jnp.maximum(before, jnp.max(scores, axis=0, keepdims=True))
    raised = jnp.exp(scores - highest)
    shrink = jnp.exp(before - highest)
    total = shrink * stat_ref[block, 1:2] + jnp.sum(raised, axis=0, keepdims=True)
    delta = shrink * stat_ref[block, 2:3] + jnp.sum(raised * dprobs, axis=0, keepdims=True)
    return highest, raised, total, delta


def far_gradients(probs, dprobs, delta, q, g, lane_head, kv_heads, score_scale):
    dscores = (probs * (dprobs - delta)).astype(BF16)
    dk = jnp.dot(all_heads(dscores, lane_head, kv_heads), q, preferred_element_type=F32)
    dv = jnp.dot(all_heads(probs.astype(BF16), lane_head, kv_heads), g, preferred_element_type=F32)
    return (dk * score_scale).astype(BF16), dv.astype(BF16)


def mid_kernel(
    plan_ref, q_ref, g_ref, stat_ref, arrived_ref, out_ref,
    *, heads, kv_heads, score_scale, source_at, seen_at
):
    blocks = stat_ref.shape[0]
    rows = q_ref.shape[0] // blocks
    _, lane_head = lanes(rows, heads, kv_heads)
    for block in range(blocks):
        span = slice(block * rows, (block + 1) * rows)
        scores, dprobs = far_scores(
            arrived_ref, plan_ref[source_at + block], q_ref[span], g_ref[span],
            plan_ref[seen_at + block],            lane_head, kv_heads, score_scale,
        )
        highest, _, total, delta = merged(stat_ref, block, scores, dprobs)
        out_ref[block, 0:1] = highest
        out_ref[block, 1:2] = total
        out_ref[block, 2:3] = delta


def far_kernel(
    plan_ref, q_ref, g_ref, stat_ref, other_ref, grad_ref, out_ref,
    *, heads, kv_heads, score_scale, seen_at, first
):
    rows = q_ref.shape[0] // stat_ref.shape[0]
    _, lane_head = lanes(rows, heads, kv_heads)
    for at in range(other_ref.shape[0]):
        block = first + at
        span = slice(block * rows, (block + 1) * rows)
        q = q_ref[span]
        g = g_ref[span]
        scores, dprobs = far_scores(
            other_ref, at, q, g, plan_ref[seen_at + block], lane_head, kv_heads, score_scale
        )
        highest, raised, total, delta = merged(stat_ref, block, scores, dprobs)
        inverse = 1.0 / total
        delta = delta * inverse
        grad_ref[at, 0], grad_ref[at, 1] = far_gradients(
            raised * inverse, dprobs, delta, q, g, lane_head, kv_heads, score_scale
        )
        out_ref[at, 0:1] = highest
        out_ref[at, 1:2] = inverse
        out_ref[at, 2:3] = delta


def mine_kernel(
    plan_ref, q_ref, g_ref, arrived_ref, stat_ref, grad_ref,
    *, heads, kv_heads, score_scale, source_at, seen_at, rows, first
):
    _, lane_head = lanes(rows, heads, kv_heads)
    for at in range(stat_ref.shape[0]):
        block = first + at
        span = slice(block * rows, (block + 1) * rows)
        q = q_ref[span]
        g = g_ref[span]
        scores, dprobs = far_scores(
            arrived_ref, plan_ref[source_at + block], q, g, plan_ref[seen_at + block],
            lane_head, kv_heads, score_scale,
        )
        probs = jnp.exp(scores - stat_ref[at, 0:1]) * stat_ref[at, 1:2]
        grad_ref[at, 0], grad_ref[at, 1] = far_gradients(
            probs, dprobs, stat_ref[at, 2:3], q, g, lane_head, kv_heads, score_scale
        )


def local_kernel(
    plan_ref, q_ref, g_ref, k_ref, v_ref, mine_ref, other_ref,
    att_ref, dq_ref, dk_ref, dv_ref, bias_ref, *, heads, kv_heads, score_scale, seen_at
):
    step = pl.program_id(0)
    rows = q_ref.shape[0]
    cols = k_ref.shape[0]

    @pl.when(step == 0)
    def _():
        half = cols // 2
        place = half // kv_heads
        row = lax.broadcasted_iota(jnp.int32, (rows, cols), 0)
        col = lax.broadcasted_iota(jnp.int32, (rows, cols), 1)
        same = row % heads // (heads // kv_heads) == col % half // place
        causal = col // half * place + col % place <= row // heads
        bias_ref[:, :cols] = jnp.where(same & causal, 0.0, HIDDEN)
        bias_ref[:, cols:] = jnp.where(same, 0.0, HIDDEN)

    far_bias = jnp.where(plan_ref[seen_at + step] > 0, 0.0, HIDDEN)
    order = head_major(cols, kv_heads)
    k_near = reorder(order, k_ref[...])
    v_near = reorder(order, v_ref[...])
    k_all = jnp.concatenate([k_near, mine_ref[0, 0], other_ref[0, 0]], axis=0)
    v_all = jnp.concatenate([v_near, mine_ref[0, 1], other_ref[0, 1]], axis=0)
    q = q_ref[...]
    g = g_ref[...]
    scores = dot_last(q, k_all) * score_scale + bias_ref[...]
    scores = jnp.concatenate([scores[:, :cols], scores[:, cols:] + far_bias], axis=1)
    highest = jnp.max(scores, axis=1, keepdims=True)
    raised = jnp.exp(scores - highest)
    total = jnp.sum(raised, axis=1, keepdims=True)
    probs = raised * (1.0 / total)
    weights = probs.astype(BF16)
    attended = jnp.dot(weights, v_all, preferred_element_type=F32).astype(BF16)
    att_ref[...] = attended
    delta = jnp.sum(g.astype(F32) * attended.astype(F32), axis=1, keepdims=True)
    dscores = (probs * (dot_last(g, v_all) - delta)).astype(BF16)
    dq = jnp.dot(dscores, k_all, preferred_element_type=F32) * score_scale
    dq_ref[...] = dq.astype(BF16)
    dk_ref[...] = dot_first(dscores[:, :cols], q) * score_scale
    dv_ref[...] = dot_first(weights[:, :cols], g)


def landing_kernel(plan_ref, landed_ref, out_ref, sum_ref, *, first):
    sum_ref[...] = jnp.zeros_like(sum_ref)
    for group in range(landed_ref.shape[0]):
        place = plan_ref[first + group]

        @pl.when(place >= 0)
        def _():
            sum_ref[place] = sum_ref[place] + landed_ref[group].astype(F32)

    out_ref[...] = sum_ref[...].astype(out_ref.dtype)


def finish_kernel(
    dk_near_ref, dv_near_ref, own_ref, back_ref, dk_ref, dv_ref, *, kv_heads
):
    blocks, _, half, _ = back_ref.shape
    mine = lax.axis_index("uly") == 0
    order = head_major(2 * half, kv_heads)
    for block in range(blocks):
        span = slice(block * 2 * half, (block + 1) * 2 * half)
        for near_ref, out_ref, which in ((dk_near_ref, dk_ref, 0), (dv_near_ref, dv_ref, 1)):
            own = own_ref[block, which]
            back = back_ref[block, which].astype(F32)
            far = jnp.concatenate([jnp.where(mine, own, back), jnp.where(mine, back, own)], axis=0)
            summed = (near_ref[span] + far).astype(BF16)
            out_ref[span] = dot_first(order, summed).astype(BF16)


def take_rows(array, index):
    return array.at[index].get(mode="promise_in_bounds")


def whole_blocks(queries, keys, values, output_cotangent, block_lists, list_counts):
    grp_count = lax.axis_size("grp")
    uly_count = lax.axis_size("uly")
    tokens, heads, width = queries.shape
    kv_heads = keys.shape[1]
    per_group = block_lists.shape[0] // grp_count
    block_tok = tokens * uly_count // per_group
    mine_blocks = tokens // block_tok
    rows = block_tok * heads
    cols = block_tok * kv_heads
    half = cols // 2
    sizes = dict(heads=heads, kv_heads=kv_heads, score_scale=width ** (-0.5))
    swap = [(0, 1), (1, 0)]

    sib_at, source_at, give_at, seen_at = plan_spans(grp_count, mine_blocks)

    q2 = queries.reshape(tokens * heads, width)
    g2 = output_cotangent.reshape(tokens * heads, width)
    k2 = keys.reshape(tokens * kv_heads, width)
    v2 = values.reshape(tokens * kv_heads, width)

    part_shape = jax.ShapeDtypeStruct((mine_blocks, 2, half, width), BF16)
    slots = (grp_count, 2, half, width)
    stat_shape = jax.ShapeDtypeStruct((mine_blocks, 8, rows), F32)
    row_shape = jax.ShapeDtypeStruct(q2.shape, BF16)
    near_shape = jax.ShapeDtypeStruct(k2.shape, F32)
    small_shape = jax.ShapeDtypeStruct(k2.shape, BF16)
    sum_scratch = [pltpu.VMEM((mine_blocks, 2, half, width), F32)]
    limit = pltpu.CompilerParams(vmem_limit_bytes=24 * 1024 * 1024)
    vmem = pl.BlockSpec(memory_space=pltpu.VMEM)
    smem = pl.BlockSpec(memory_space=pltpu.SMEM)
    anywhere = pl.BlockSpec(memory_space=pltpu.HBM)

    def call(kernel, name, scalars, operands, out_shape, scratch=(), into=None, out_spec=vmem):
        extra = () if into is None else (into,)
        return pl.pallas_call(
            kernel,
            in_specs=[smem] * len(scalars) + [vmem] * (len(operands) + len(extra)),
            out_specs=jax.tree.map(lambda _: out_spec, out_shape),
            out_shape=out_shape,
            scratch_shapes=scratch,
            input_output_aliases={len(scalars) + len(operands): 0} if extra else {},
            compiler_params=limit,
            name=name,
        )(*scalars, *operands, *extra)

    def step_rows(i, *_):
        return (i, 0)

    def step_part(i, *_):
        return (i, 0, 0, 0)

    def in_hbm(array):
        return pltpu.with_memory_space_constraint(array, pltpu.HBM)

    k_here, v_here, given = pl.pallas_call(
        partial(pack_kernel, kv_heads=kv_heads),
        in_specs=[anywhere, anywhere],
        out_specs=[vmem, vmem, vmem],
        out_shape=[small_shape, small_shape, part_shape],
        scratch_shapes=[pltpu.SemaphoreType.DMA((2,))],
        compiler_params=limit,
        name="pack",
    )(in_hbm(k2), in_hbm(v2))
    plan = pl.pallas_call(
        partial(plan_kernel, grp_count=grp_count, blocks=mine_blocks),
        in_specs=[smem, smem],
        out_specs=smem,
        out_shape=pltpu.SMEM((seen_at + mine_blocks,), jnp.int32),
        compiler_params=limit,
        name="plan",
    )(in_hbm(block_lists.reshape(-1)), in_hbm(list_counts))
    gotten = lax.ppermute(given, "uly", swap)
    row_spec = pl.BlockSpec((rows, width), step_rows)
    part_spec = pl.BlockSpec((1, 2, half, width), step_part)
    kept, outgoing = call(
        partial(send_own_kernel, kv_heads=kv_heads), "send_own", (plan,), (k_here, v_here),
        [part_shape, jax.ShapeDtypeStruct(slots, BF16)],
    )
    outgoing = call(
        partial(send_sibling_kernel, first=sib_at), "send_sibling", (plan,), (gotten,),
        jax.ShapeDtypeStruct(slots, BF16), into=outgoing,
    )
    arrived = lax.all_to_all(outgoing, "grp", split_axis=0, concat_axis=0, tiled=True)
    kept, arrived = lax.optimization_barrier((kept, arrived))
    chunks = 2 if mine_blocks % 2 == 0 else 1
    chunk = mine_blocks // chunks
    chunk_shape = jax.ShapeDtypeStruct((chunk, 2, half, width), BF16)
    giving = call(
        partial(giving_kernel, give_at=give_at), "give", (plan,), (arrived,),
        [chunk_shape] * chunks,
    )
    stats = call(partial(near_kernel, **sizes), "near", (), (q2, g2, kept, given), stat_shape)
    stats = call(
        partial(mid_kernel, source_at=source_at, seen_at=seen_at, **sizes), "mid", (plan,),
        (q2, g2, stats, arrived), stat_shape,
    )
    others = []
    for part in giving:
        if others:
            part, stats = lax.optimization_barrier((part, stats))
        others.append(lax.ppermute(part, "uly", swap))
    grads, final = [], []
    for at, other in enumerate(others):
        grad, stat = call(
            partial(far_kernel, seen_at=seen_at, first=at * chunk, **sizes), "far", (plan,),
            (q2, g2, stats, other),
            [chunk_shape, jax.ShapeDtypeStruct((chunk, 8, rows), F32)],
        )
        grads.append(grad)
        final.append(stat)
    from_sib = [lax.ppermute(part, "uly", swap) for part in grads]
    mine = [None] * chunks
    for at in reversed(range(chunks)):
        if at + 1 < chunks:
            from_sib[at], final[at] = lax.optimization_barrier((from_sib[at], final[at]))
        mine[at] = call(
            partial(
                mine_kernel, source_at=source_at, seen_at=seen_at, rows=rows, first=at * chunk,
                **sizes,
            ),
            "mine", (plan,), (q2, g2, arrived, final[at]), chunk_shape,
        )
    returning = call(
        partial(returning_kernel, source_at=source_at), "return", (plan,), mine + from_sib,
        pltpu.HBM(slots, BF16), [pltpu.SemaphoreType.DMA((per_group,))], out_spec=anywhere,
    )
    other = jnp.concatenate(others)
    returning, k2l = lax.optimization_barrier((returning, k2))
    landed = lax.all_to_all(returning, "grp", split_axis=0, concat_axis=0, tiled=True)

    def from_source(i, plan_ref):
        return (plan_ref[source_at + i], 0, 0, 0)

    col_spec = pl.BlockSpec((cols, width), step_rows)
    attended, dq, dk_near, dv_near = pl.pallas_call(
        partial(local_kernel, seen_at=seen_at, **sizes),
        grid_spec=pltpu.PrefetchScalarGridSpec(
            num_scalar_prefetch=1,
            grid=(mine_blocks,),
            in_specs=[
                row_spec, row_spec, col_spec, col_spec,
                pl.BlockSpec((1, 2, half, width), from_source),
                part_spec,
            ],
            out_specs=[row_spec, row_spec, col_spec, col_spec],
            scratch_shapes=[pltpu.VMEM((rows, 2 * cols), F32)],
        ),
        out_shape=[row_shape, row_shape, near_shape, near_shape],
        compiler_params=limit,
        name="local",
    )(plan, q2, g2, k2l, v2, arrived, other)
    landed, dk_near = lax.optimization_barrier((landed, dk_near))
    give = call(
        partial(landing_kernel, first=sib_at), "land_sibling", (plan,), (landed,), part_shape,
        sum_scratch,
    )
    back = lax.ppermute(give, "uly", swap)
    own = call(
        partial(landing_kernel, first=0), "land_own", (plan,), (landed,),
        jax.ShapeDtypeStruct(part_shape.shape, F32), sum_scratch,
    )
    dk, dv = call(
        partial(finish_kernel, kv_heads=kv_heads), "finish", (),
        (dk_near, dv_near, own, back), [small_shape, small_shape],
    )
    return (
        attended.reshape(queries.shape), dq.reshape(queries.shape),
        dk.reshape(keys.shape), dv.reshape(keys.shape),
    )


def on_device(queries, keys, values, output_cotangent, block_lists, list_counts):
    uly_count = lax.axis_size("uly")
    grp_count = lax.axis_size("grp")
    blocks_all, remote = block_lists.shape
    block_tok = queries.shape[0] * uly_count * grp_count // blocks_all
    held_whole = queries.shape[0] % block_tok == 0
    run = whole_blocks if held_whole and remote == 1 and uly_count == 2 else spread_blocks
    return run(queries, keys, values, output_cotangent, block_lists, list_counts)


def solution(mesh):
    placed = (
        P(("grp", "uly"), None, None),
        P(("grp", "uly"), None, None),
        P(("grp", "uly"), None, None),
        P(("grp", "uly"), None, None),
        P(),
        P(),
    )
    return jax.shard_map(
        on_device,
        mesh=mesh,
        in_specs=placed,
        out_specs=(
            P(("grp", "uly"), None, None),
            P(("grp", "uly"), None, None),
            P(("grp", "uly"), None, None),
            P(("grp", "uly"), None, None),
        ),
        check_vma=False,
    )
```

```python
from functools import partial

import jax
import jax.numpy as jnp
from jax import lax
from jax.experimental import pallas as pl
from jax.experimental.pallas import tpu as pltpu
from jax.sharding import PartitionSpec as P


def spread_blocks(queries, keys, values, output_cotangent, block_lists, list_counts):
    uly_count = lax.axis_size("uly")
    grp_count = lax.axis_size("grp")
    my_group = lax.axis_index("grp")
    tokens, head_count, head_width = queries.shape
    kv_heads = keys.shape[1]
    copies = max(1, uly_count // kv_heads)
    blocks_all, remote = block_lists.shape
    per_group = blocks_all // grp_count
    block_tok = tokens * uly_count // per_group
    group_tok = tokens * uly_count
    score_scale = head_width ** (-0.5)
    lists = block_lists.reshape(grp_count, per_group, remote)
    counted = (jnp.arange(remote)[None, :] < list_counts[:, None]).reshape(
        grp_count, per_group, remote
    )
    wanted = (lists // per_group == my_group) & counted
    send_place = jnp.sum(jnp.where(wanted, lists % per_group, 0), axis=(1, 2))
    sending = jnp.any(wanted, axis=(1, 2))
    mine_source = lax.dynamic_index_in_dim(lists, my_group, 0, keepdims=False) // per_group
    mine_counted = lax.dynamic_index_in_dim(counted, my_group, 0, keepdims=False)
    trip_count = jnp.max(jnp.sum(mine_counted.astype(jnp.int32), axis=1))

    def to_blocks(array_in):
        return array_in.reshape((per_group, block_tok) + array_in.shape[1:])

    keys_wide = jnp.repeat(keys, copies, axis=1)
    values_wide = jnp.repeat(values, copies, axis=1)
    query_heads, grad_heads, key_heads, value_heads = (
        lax.all_to_all(queries, "uly", split_axis=1, concat_axis=0, tiled=True),
        lax.all_to_all(output_cotangent, "uly", split_axis=1, concat_axis=0, tiled=True),
        lax.all_to_all(keys_wide, "uly", split_axis=1, concat_axis=0, tiled=True),
        lax.all_to_all(values_wide, "uly", split_axis=1, concat_axis=0, tiled=True),
    )
    stacked = jnp.stack([to_blocks(key_heads), to_blocks(value_heads)])
    outgoing = jnp.take(stacked, send_place, axis=1)
    arrived = lax.all_to_all(outgoing, "grp", split_axis=1, concat_axis=1, tiled=True)
    kv_local = key_heads.shape[1]
    heads_local = query_heads.shape[1]
    heads_per_group = heads_local // kv_local
    query_blk = query_heads.reshape(per_group, block_tok, kv_local, heads_per_group, head_width)
    grad_blk = grad_heads.reshape(per_group, block_tok, kv_local, heads_per_group, head_width)
    key_blk = to_blocks(key_heads)
    value_blk = to_blocks(value_heads)
    far_keys = arrived[0]
    far_values = arrived[1]
    causal = jnp.arange(block_tok)[:, None] >= jnp.arange(block_tok)[None, :]

    def logits(key_rows):
        return (
            jnp.einsum("pqkgd,pjkd->pkgqj", query_blk, key_rows, preferred_element_type=jnp.float32)
            * score_scale
        )

    def slot_rows(slot_index):
        source = lax.dynamic_index_in_dim(mine_source, slot_index, 1, keepdims=False)
        counted_slot = lax.dynamic_index_in_dim(mine_counted, slot_index, 1, keepdims=False)
        return (
            jnp.take(far_keys, source, axis=0),
            jnp.take(far_values, source, axis=0),
            counted_slot,
            source,
        )

    def masked(scores, counted_slot):
        return jnp.where(counted_slot[:, None, None, None, None], scores, -jnp.inf)

    near_scores = jnp.where(causal, logits(key_blk), -jnp.inf)
    highest = jnp.max(near_scores, axis=-1)
    denominator = jnp.sum(jnp.exp(near_scores - highest[..., None]), axis=-1)

    def max_sweep(slot_index, state_pair):
        highest, denominator = state_pair
        key_rows, value_rows, counted_slot, source = slot_rows(slot_index)
        scores = masked(logits(key_rows), counted_slot)
        new_highest = jnp.maximum(highest, jnp.max(scores, axis=-1))
        denominator = denominator * jnp.exp(highest - new_highest) + jnp.sum(
            jnp.exp(scores - new_highest[..., None]), axis=-1
        )
        return (new_highest, denominator)

    highest, denominator = lax.fori_loop(0, trip_count, max_sweep, (highest, denominator))
    log_total = highest + jnp.log(denominator)

    def softmax_weights(scores):
        return jnp.exp(scores - log_total[..., None])

    summed = jnp.einsum(
        "pkgqj,pjkd->pqkgd",
        softmax_weights(near_scores).astype(jnp.bfloat16),
        value_blk,
        preferred_element_type=jnp.float32,
    )

    def value_sweep(slot_index, summed):
        key_rows, value_rows, counted_slot, source = slot_rows(slot_index)
        weights = softmax_weights(masked(logits(key_rows), counted_slot)).astype(jnp.bfloat16)
        return summed + jnp.einsum(
            "pkgqj,pjkd->pqkgd", weights, value_rows, preferred_element_type=jnp.float32
        )

    summed = lax.fori_loop(0, trip_count, value_sweep, summed)
    attended_blk = summed.astype(jnp.bfloat16)
    row_delta = jnp.transpose(
        jnp.sum(grad_blk.astype(jnp.float32) * attended_blk.astype(jnp.float32), axis=-1),
        (0, 2, 3, 1),
    )

    def backward(scores, key_rows, value_rows):
        probs = softmax_weights(scores)
        weights = probs.astype(jnp.bfloat16)
        dprobs = jnp.einsum(
            "pqkgd,pjkd->pkgqj", grad_blk, value_rows, preferred_element_type=jnp.float32
        )
        dscores = (probs * (dprobs - row_delta[..., None])).astype(jnp.bfloat16)
        query_term = jnp.einsum(
            "pkgqj,pjkd->pqkgd", dscores, key_rows, preferred_element_type=jnp.float32
        )
        key_term = (
            jnp.einsum("pkgqj,pqkgd->pjkd", dscores, query_blk, preferred_element_type=jnp.float32)
            * score_scale
        )
        value_term = jnp.einsum(
            "pkgqj,pqkgd->pjkd", weights, grad_blk, preferred_element_type=jnp.float32
        )
        return (query_term, key_term, value_term)

    query_sum, key_near, value_near = backward(near_scores, key_blk, value_blk)
    far_grads = jnp.zeros((2, grp_count, block_tok, kv_local, head_width), jnp.float32)

    def grad_sweep(slot_index, state_pair):
        query_sum, far_grads = state_pair
        key_rows, value_rows, counted_slot, source = slot_rows(slot_index)
        query_term, key_term, value_term = backward(
            masked(logits(key_rows), counted_slot), key_rows, value_rows
        )
        routing = (
            (source[:, None] == jnp.arange(grp_count)[None, :]) & counted_slot[:, None]
        ).astype(jnp.float32)
        routed = jnp.einsum(
            "ps,xpjkd->xsjkd",
            routing,
            jnp.stack([key_term, value_term]),
            precision=lax.Precision.HIGHEST,
        )
        return (query_sum + query_term, far_grads + routed)

    query_sum, far_grads = lax.fori_loop(0, trip_count, grad_sweep, (query_sum, far_grads))
    owners = ((send_place[:, None] == jnp.arange(per_group)[None, :]) & sending[:, None]).astype(
        jnp.float32
    )
    returned = lax.all_to_all(far_grads, "grp", split_axis=1, concat_axis=1, tiled=True)
    landed = jnp.einsum("sp,xsjkd->xpjkd", owners, returned, precision=lax.Precision.HIGHEST)
    key_local = (key_near + landed[0]).reshape(group_tok, kv_local, head_width)
    value_local = (value_near + landed[1]).reshape(group_tok, kv_local, head_width)
    attended_rows = attended_blk.reshape(group_tok, heads_local, head_width)
    query_rows = (
        (query_sum * score_scale).astype(jnp.bfloat16).reshape(group_tok, heads_local, head_width)
    )
    attended, query_grad = (
        lax.all_to_all(attended_rows, "uly", split_axis=0, concat_axis=1, tiled=True),
        lax.all_to_all(query_rows, "uly", split_axis=0, concat_axis=1, tiled=True),
    )
    key_parts, value_parts = (
        lax.all_to_all(key_local, "uly", split_axis=0, concat_axis=1, tiled=True),
        lax.all_to_all(value_local, "uly", split_axis=0, concat_axis=1, tiled=True),
    )
    key_gradient = jnp.sum(key_parts.reshape(tokens, kv_heads, copies, head_width), axis=2).astype(
        jnp.bfloat16
    )
    value_gradient = jnp.sum(
        value_parts.reshape(tokens, kv_heads, copies, head_width), axis=2
    ).astype(jnp.bfloat16)
    return (attended, query_grad, key_gradient, value_gradient)


HIDDEN = -1e30
LAST = (((1,), (1,)), ((), ()))
FIRST = (((0,), (0,)), ((), ()))
F32 = jnp.float32
BF16 = jnp.bfloat16


def dot_last(left, right):
    return lax.dot_general(left, right, LAST, preferred_element_type=F32)


def dot_first(left, right):
    return lax.dot_general(left, right, FIRST, preferred_element_type=F32)


def head_major(cols, kv_heads):
    half = cols // 2
    place = half // kv_heads
    row = lax.broadcasted_iota(jnp.int32, (cols, cols), 0)
    col = lax.broadcasted_iota(jnp.int32, (cols, cols), 1)
    token = row // half * place + row % place
    return jnp.where(col == token * kv_heads + row % half // place, 1.0, 0.0).astype(BF16)


def half_order(cols, kv_heads, which):
    half = cols // 2
    place = half // kv_heads
    row = lax.broadcasted_iota(jnp.int32, (half, cols), 0)
    col = lax.broadcasted_iota(jnp.int32, (half, cols), 1)
    token = which * place + row % place
    return jnp.where(col == token * kv_heads + row // place, 1.0, 0.0).astype(BF16)


def reorder(one_hot, array):
    return jnp.dot(one_hot, array, preferred_element_type=F32).astype(BF16)


def own_head(scores, lane_head, kv_heads):
    place = scores.shape[0] // kv_heads
    kept = scores[:place]
    for head in range(1, kv_heads):
        kept = jnp.where(lane_head == head, scores[head * place:(head + 1) * place], kept)
    return kept


def all_heads(kept, lane_head, kv_heads):
    none = jnp.zeros_like(kept)
    return jnp.concatenate(
        [jnp.where(lane_head == head, kept, none) for head in range(kv_heads)], axis=0
    )


def lanes(rows, heads, kv_heads):
    lane = lax.broadcasted_iota(jnp.int32, (1, rows), 1)
    return lane // heads, lane % heads // (heads // kv_heads)


def plan_spans(grp_count, blocks):
    return grp_count, 2 * grp_count, 2 * grp_count + blocks, 2 * grp_count + 2 * blocks


def plan_kernel(lists_ref, counts_ref, plan_ref, *, grp_count, blocks):
    group, mine = lax.axis_index("grp"), lax.axis_index("uly")
    per_group = 2 * blocks
    low = group * per_group
    sib_at, source_at, give_at, seen_at = plan_spans(grp_count, blocks)
    for other in range(grp_count):
        place = jnp.int32(-1)
        for at in range(other * per_group, (other + 1) * per_group):
            here = lists_ref[at] - low
            wanted = (here >= 0) & (here < per_group) & (counts_ref[at] > 0)
            place = jnp.where(wanted, here, place)
        own = place - mine * blocks
        sib = place - (1 - mine) * blocks
        plan_ref[other] = jnp.where((own >= 0) & (own < blocks), own, -1)
        plan_ref[sib_at + other] = jnp.where((sib >= 0) & (sib < blocks), sib, -1)
    for block in range(blocks):
        at = low + mine * blocks + block
        plan_ref[source_at + block] = lax.div(lists_ref[at], per_group)
        plan_ref[seen_at + block] = counts_ref[at]
        at = low + (1 - mine) * blocks + block
        plan_ref[give_at + block] = lax.div(lists_ref[at], per_group)


def pack_kernel(k_hbm, v_hbm, k_ref, v_ref, given_ref, sems, *, kv_heads):
    blocks, _, half, _ = given_ref.shape
    copies = [
        pltpu.make_async_copy(k_hbm, k_ref, sems.at[0]),
        pltpu.make_async_copy(v_hbm, v_ref, sems.at[1]),
    ]
    for copy in copies:
        copy.start()
    order = half_order(2 * half, kv_heads, 1 - lax.axis_index("uly"))
    for which, ref in enumerate((k_ref, v_ref)):
        copies[which].wait()
        for block in range(blocks):
            given_ref[block, which] = reorder(order, ref[block * 2 * half:(block + 1) * 2 * half])


def send_own_kernel(plan_ref, k_ref, v_ref, kept_ref, out_ref, *, kv_heads):
    blocks, _, half, _ = kept_ref.shape
    order = half_order(2 * half, kv_heads, lax.axis_index("uly"))
    for block in range(blocks):
        span = slice(block * 2 * half, (block + 1) * 2 * half)
        kept_ref[block, 0] = reorder(order, k_ref[span])
        kept_ref[block, 1] = reorder(order, v_ref[span])
    for group in range(out_ref.shape[0]):
        out_ref[group] = kept_ref[jnp.maximum(plan_ref[group], 0)]


def send_sibling_kernel(plan_ref, blocks_ref, _, out_ref, *, first):
    for group in range(out_ref.shape[0]):
        place = plan_ref[first + group]

        @pl.when(place >= 0)
        def _():
            out_ref[group] = blocks_ref[place]


def giving_kernel(plan_ref, arrived_ref, *out_refs, give_at):
    block = 0
    for out_ref in out_refs:
        for at in range(out_ref.shape[0]):
            out_ref[at] = arrived_ref[plan_ref[give_at + block]]
            block += 1


def returning_kernel(plan_ref, *refs, source_at):
    part_refs, (out_ref, sems) = refs[:-2], refs[-2:]
    copies = []
    for part_ref in part_refs:
        for at in range(part_ref.shape[0]):
            block = len(copies)
            target = out_ref.at[plan_ref[source_at + block]]
            copies.append(pltpu.make_async_copy(part_ref.at[at], target, sems.at[block]))
            copies[-1].start()
    for copy in copies:
        copy.wait()


def near_kernel(
    q_ref, g_ref, kept_ref, given_ref, stat_ref, *, heads, kv_heads, score_scale
):
    blocks = stat_ref.shape[0]
    rows = q_ref.shape[0] // blocks
    half = given_ref.shape[2]
    place = half // kv_heads
    mine = lax.axis_index("uly")
    token, lane_head = lanes(rows, heads, kv_heads)
    key = lax.broadcasted_iota(jnp.int32, (2 * place, rows), 0)
    part = jnp.where(key < place, mine, 1 - mine)
    causal = key % place + part * place <= token
    for block in range(blocks):
        span = slice(block * rows, (block + 1) * rows)
        pieces = []
        for which, ref in enumerate((q_ref, g_ref)):
            both = jnp.concatenate([kept_ref[block, which], given_ref[block, which]], axis=0)
            full = dot_last(both, ref[span])
            pieces.append(
                jnp.concatenate(
                    [
                        own_head(full[:half], lane_head, kv_heads),
                        own_head(full[half:], lane_head, kv_heads),
                    ],
                    axis=0,
                )
            )
        scores = jnp.where(causal, pieces[0] * score_scale, HIDDEN)
        highest = jnp.max(scores, axis=0, keepdims=True)
        raised = jnp.exp(scores - highest)
        stat_ref[block, 0:1] = highest
        stat_ref[block, 1:2] = jnp.sum(raised, axis=0, keepdims=True)
        stat_ref[block, 2:3] = jnp.sum(raised * pieces[1], axis=0, keepdims=True)


def far_scores(part_ref, at, q, g, seen, lane_head, kv_heads, score_scale):
    hidden = jnp.where(seen > 0, 0.0, HIDDEN)
    scores = own_head(dot_last(part_ref[at, 0], q), lane_head, kv_heads) * score_scale + hidden
    return scores, own_head(dot_last(part_ref[at, 1], g), lane_head, kv_heads)


def merged(stat_ref, block, scores, dprobs):
    before = stat_ref[block, 0:1]
    highest = jnp.maximum(before, jnp.max(scores, axis=0, keepdims=True))
    raised = jnp.exp(scores - highest)
    shrink = jnp.exp(before - highest)
    total = shrink * stat_ref[block, 1:2] + jnp.sum(raised, axis=0, keepdims=True)
    delta = shrink * stat_ref[block, 2:3] + jnp.sum(raised * dprobs, axis=0, keepdims=True)
    return highest, raised, total, delta


def far_gradients(probs, dprobs, delta, q, g, lane_head, kv_heads, score_scale):
    dscores = (probs * (dprobs - delta)).astype(BF16)
    dk = jnp.dot(all_heads(dscores, lane_head, kv_heads), q, preferred_element_type=F32)
    dv = jnp.dot(all_heads(probs.astype(BF16), lane_head, kv_heads), g, preferred_element_type=F32)
    return (dk * score_scale).astype(BF16), dv.astype(BF16)


def mid_kernel(
    plan_ref, q_ref, g_ref, stat_ref, arrived_ref, out_ref,
    *, heads, kv_heads, score_scale, source_at, seen_at
):
    blocks = stat_ref.shape[0]
    rows = q_ref.shape[0] // blocks
    _, lane_head = lanes(rows, heads, kv_heads)
    for block in range(blocks):
        span = slice(block * rows, (block + 1) * rows)
        scores, dprobs = far_scores(
            arrived_ref, plan_ref[source_at + block], q_ref[span], g_ref[span],
            plan_ref[seen_at + block],            lane_head, kv_heads, score_scale,
        )
        highest, _, total, delta = merged(stat_ref, block, scores, dprobs)
        out_ref[block, 0:1] = highest
        out_ref[block, 1:2] = total
        out_ref[block, 2:3] = delta


def far_kernel(
    plan_ref, q_ref, g_ref, stat_ref, other_ref, grad_ref, out_ref,
    *, heads, kv_heads, score_scale, seen_at, first
):
    rows = q_ref.shape[0] // stat_ref.shape[0]
    _, lane_head = lanes(rows, heads, kv_heads)
    for at in range(other_ref.shape[0]):
        block = first + at
        span = slice(block * rows, (block + 1) * rows)
        q = q_ref[span]
        g = g_ref[span]
        scores, dprobs = far_scores(
            other_ref, at, q, g, plan_ref[seen_at + block], lane_head, kv_heads, score_scale
        )
        highest, raised, total, delta = merged(stat_ref, block, scores, dprobs)
        inverse = 1.0 / total
        delta = delta * inverse
        grad_ref[at, 0], grad_ref[at, 1] = far_gradients(
            raised * inverse, dprobs, delta, q, g, lane_head, kv_heads, score_scale
        )
        out_ref[at, 0:1] = highest
        out_ref[at, 1:2] = inverse
        out_ref[at, 2:3] = delta


def mine_kernel(
    plan_ref, q_ref, g_ref, arrived_ref, stat_ref, grad_ref,
    *, heads, kv_heads, score_scale, source_at, seen_at, rows, first
):
    _, lane_head = lanes(rows, heads, kv_heads)
    for at in range(stat_ref.shape[0]):
        block = first + at
        span = slice(block * rows, (block + 1) * rows)
        q = q_ref[span]
        g = g_ref[span]
        scores, dprobs = far_scores(
            arrived_ref, plan_ref[source_at + block], q, g, plan_ref[seen_at + block],
            lane_head, kv_heads, score_scale,
        )
        probs = jnp.exp(scores - stat_ref[at, 0:1]) * stat_ref[at, 1:2]
        grad_ref[at, 0], grad_ref[at, 1] = far_gradients(
            probs, dprobs, stat_ref[at, 2:3], q, g, lane_head, kv_heads, score_scale
        )


def local_kernel(
    plan_ref, q_ref, g_ref, k_ref, v_ref, mine_ref, other_ref,
    att_ref, dq_ref, dk_ref, dv_ref, bias_ref, *, heads, kv_heads, score_scale, seen_at
):
    step = pl.program_id(0)
    rows = q_ref.shape[0]
    cols = k_ref.shape[0]

    @pl.when(step == 0)
    def _():
        half = cols // 2
        place = half // kv_heads
        row = lax.broadcasted_iota(jnp.int32, (rows, cols), 0)
        col = lax.broadcasted_iota(jnp.int32, (rows, cols), 1)
        same = row % heads // (heads // kv_heads) == col % half // place
        causal = col // half * place + col % place <= row // heads
        bias_ref[:, :cols] = jnp.where(same & causal, 0.0, HIDDEN)
        bias_ref[:, cols:] = jnp.where(same, 0.0, HIDDEN)

    far_bias = jnp.where(plan_ref[seen_at + step] > 0, 0.0, HIDDEN)
    order = head_major(cols, kv_heads)
    k_near = reorder(order, k_ref[...])
    v_near = reorder(order, v_ref[...])
    k_all = jnp.concatenate([k_near, mine_ref[0, 0], other_ref[0, 0]], axis=0)
    v_all = jnp.concatenate([v_near, mine_ref[0, 1], other_ref[0, 1]], axis=0)
    q = q_ref[...]
    g = g_ref[...]
    scores = dot_last(q, k_all) * score_scale + bias_ref[...]
    scores = jnp.concatenate([scores[:, :cols], scores[:, cols:] + far_bias], axis=1)
    highest = jnp.max(scores, axis=1, keepdims=True)
    raised = jnp.exp(scores - highest)
    total = jnp.sum(raised, axis=1, keepdims=True)
    probs = raised * (1.0 / total)
    weights = probs.astype(BF16)
    attended = jnp.dot(weights, v_all, preferred_element_type=F32).astype(BF16)
    att_ref[...] = attended
    delta = jnp.sum(g.astype(F32) * attended.astype(F32), axis=1, keepdims=True)
    dscores = (probs * (dot_last(g, v_all) - delta)).astype(BF16)
    dq = jnp.dot(dscores, k_all, preferred_element_type=F32) * score_scale
    dq_ref[...] = dq.astype(BF16)
    dk_ref[...] = dot_first(dscores[:, :cols], q) * score_scale
    dv_ref[...] = dot_first(weights[:, :cols], g)


def landing_kernel(plan_ref, landed_ref, out_ref, sum_ref, *, first):
    sum_ref[...] = jnp.zeros_like(sum_ref)
    for group in range(landed_ref.shape[0]):
        place = plan_ref[first + group]

        @pl.when(place >= 0)
        def _():
            sum_ref[place] = sum_ref[place] + landed_ref[group].astype(F32)

    out_ref[...] = sum_ref[...].astype(out_ref.dtype)


def finish_kernel(
    dk_near_ref, dv_near_ref, own_ref, back_ref, dk_ref, dv_ref, *, kv_heads
):
    blocks, _, half, _ = back_ref.shape
    mine = lax.axis_index("uly") == 0
    order = head_major(2 * half, kv_heads)
    for block in range(blocks):
        span = slice(block * 2 * half, (block + 1) * 2 * half)
        for near_ref, out_ref, which in ((dk_near_ref, dk_ref, 0), (dv_near_ref, dv_ref, 1)):
            own = own_ref[block, which]
            back = back_ref[block, which].astype(F32)
            far = jnp.concatenate([jnp.where(mine, own, back), jnp.where(mine, back, own)], axis=0)
            summed = (near_ref[span] + far).astype(BF16)
            out_ref[span] = dot_first(order, summed).astype(BF16)


def take_rows(array, index):
    return array.at[index].get(mode="promise_in_bounds")


def whole_blocks(queries, keys, values, output_cotangent, block_lists, list_counts):
    grp_count = lax.axis_size("grp")
    uly_count = lax.axis_size("uly")
    tokens, heads, width = queries.shape
    kv_heads = keys.shape[1]
    per_group = block_lists.shape[0] // grp_count
    block_tok = tokens * uly_count // per_group
    mine_blocks = tokens // block_tok
    rows = block_tok * heads
    cols = block_tok * kv_heads
    half = cols // 2
    sizes = dict(heads=heads, kv_heads=kv_heads, score_scale=width ** (-0.5))
    swap = [(0, 1), (1, 0)]

    sib_at, source_at, give_at, seen_at = plan_spans(grp_count, mine_blocks)

    q2 = queries.reshape(tokens * heads, width)
    g2 = output_cotangent.reshape(tokens * heads, width)
    k2 = keys.reshape(tokens * kv_heads, width)
    v2 = values.reshape(tokens * kv_heads, width)

    part_shape = jax.ShapeDtypeStruct((mine_blocks, 2, half, width), BF16)
    slots = (grp_count, 2, half, width)
    stat_shape = jax.ShapeDtypeStruct((mine_blocks, 8, rows), F32)
    row_shape = jax.ShapeDtypeStruct(q2.shape, BF16)
    near_shape = jax.ShapeDtypeStruct(k2.shape, F32)
    small_shape = jax.ShapeDtypeStruct(k2.shape, BF16)
    sum_scratch = [pltpu.VMEM((mine_blocks, 2, half, width), F32)]
    limit = pltpu.CompilerParams(vmem_limit_bytes=24 * 1024 * 1024)
    vmem = pl.BlockSpec(memory_space=pltpu.VMEM)
    smem = pl.BlockSpec(memory_space=pltpu.SMEM)
    anywhere = pl.BlockSpec(memory_space=pltpu.HBM)

    def call(kernel, name, scalars, operands, out_shape, scratch=(), into=None, out_spec=vmem):
        extra = () if into is None else (into,)
        return pl.pallas_call(
            kernel,
            in_specs=[smem] * len(scalars) + [vmem] * (len(operands) + len(extra)),
            out_specs=jax.tree.map(lambda _: out_spec, out_shape),
            out_shape=out_shape,
            scratch_shapes=scratch,
            input_output_aliases={len(scalars) + len(operands): 0} if extra else {},
            compiler_params=limit,
            name=name,
        )(*scalars, *operands, *extra)

    def step_rows(i, *_):
        return (i, 0)

    def step_part(i, *_):
        return (i, 0, 0, 0)

    def in_hbm(array):
        return pltpu.with_memory_space_constraint(array, pltpu.HBM)

    k_here, v_here, given = pl.pallas_call(
        partial(pack_kernel, kv_heads=kv_heads),
        in_specs=[anywhere, anywhere],
        out_specs=[vmem, vmem, vmem],
        out_shape=[small_shape, small_shape, part_shape],
        scratch_shapes=[pltpu.SemaphoreType.DMA((2,))],
        compiler_params=limit,
        name="pack",
    )(in_hbm(k2), in_hbm(v2))
    plan = pl.pallas_call(
        partial(plan_kernel, grp_count=grp_count, blocks=mine_blocks),
        in_specs=[smem, smem],
        out_specs=smem,
        out_shape=pltpu.SMEM((seen_at + mine_blocks,), jnp.int32),
        compiler_params=limit,
        name="plan",
    )(in_hbm(block_lists.reshape(-1)), in_hbm(list_counts))
    gotten = lax.ppermute(given, "uly", swap)
    row_spec = pl.BlockSpec((rows, width), step_rows)
    part_spec = pl.BlockSpec((1, 2, half, width), step_part)
    kept, outgoing = call(
        partial(send_own_kernel, kv_heads=kv_heads), "send_own", (plan,), (k_here, v_here),
        [part_shape, jax.ShapeDtypeStruct(slots, BF16)],
    )
    outgoing = call(
        partial(send_sibling_kernel, first=sib_at), "send_sibling", (plan,), (gotten,),
        jax.ShapeDtypeStruct(slots, BF16), into=outgoing,
    )
    arrived = lax.all_to_all(outgoing, "grp", split_axis=0, concat_axis=0, tiled=True)
    kept, arrived = lax.optimization_barrier((kept, arrived))
    chunks = 2 if mine_blocks % 2 == 0 else 1
    chunk = mine_blocks // chunks
    chunk_shape = jax.ShapeDtypeStruct((chunk, 2, half, width), BF16)
    giving = call(
        partial(giving_kernel, give_at=give_at), "give", (plan,), (arrived,),
        [chunk_shape] * chunks,
    )
    stats = call(partial(near_kernel, **sizes), "near", (), (q2, g2, kept, given), stat_shape)
    others = []
    for part in giving:
        if others:
            part, stats = lax.optimization_barrier((part, stats))
        others.append(lax.ppermute(part, "uly", swap))
    stats = call(
        partial(mid_kernel, source_at=source_at, seen_at=seen_at, **sizes), "mid", (plan,),
        (q2, g2, stats, arrived), stat_shape,
    )
    grads, final = [], []
    for at, other in enumerate(others):
        grad, stat = call(
            partial(far_kernel, seen_at=seen_at, first=at * chunk, **sizes), "far", (plan,),
            (q2, g2, stats, other),
            [chunk_shape, jax.ShapeDtypeStruct((chunk, 8, rows), F32)],
        )
        grads.append(grad)
        final.append(stat)
    from_sib = [lax.ppermute(part, "uly", swap) for part in grads]
    mine = [None] * chunks
    for at in reversed(range(chunks)):
        if at + 1 < chunks:
            from_sib[at], final[at] = lax.optimization_barrier((from_sib[at], final[at]))
        mine[at] = call(
            partial(
                mine_kernel, source_at=source_at, seen_at=seen_at, rows=rows, first=at * chunk,
                **sizes,
            ),
            "mine", (plan,), (q2, g2, arrived, final[at]), chunk_shape,
        )
    returning = call(
        partial(returning_kernel, source_at=source_at), "return", (plan,), mine + from_sib,
        pltpu.HBM(slots, BF16), [pltpu.SemaphoreType.DMA((per_group,))], out_spec=anywhere,
    )
    other = jnp.concatenate(others)
    returning, k2l = lax.optimization_barrier((returning, k2))
    landed = lax.all_to_all(returning, "grp", split_axis=0, concat_axis=0, tiled=True)

    def from_source(i, plan_ref):
        return (plan_ref[source_at + i], 0, 0, 0)

    col_spec = pl.BlockSpec((cols, width), step_rows)
    attended, dq, dk_near, dv_near = pl.pallas_call(
        partial(local_kernel, seen_at=seen_at, **sizes),
        grid_spec=pltpu.PrefetchScalarGridSpec(
            num_scalar_prefetch=1,
            grid=(mine_blocks,),
            in_specs=[
                row_spec, row_spec, col_spec, col_spec,
                pl.BlockSpec((1, 2, half, width), from_source),
                part_spec,
            ],
            out_specs=[row_spec, row_spec, col_spec, col_spec],
            scratch_shapes=[pltpu.VMEM((rows, 2 * cols), F32)],
        ),
        out_shape=[row_shape, row_shape, near_shape, near_shape],
        compiler_params=limit,
        name="local",
    )(plan, q2, g2, k2l, v2, arrived, other)
    landed, dk_near = lax.optimization_barrier((landed, dk_near))
    give = call(
        partial(landing_kernel, first=sib_at), "land_sibling", (plan,), (landed,), part_shape,
        sum_scratch,
    )
    back = lax.ppermute(give, "uly", swap)
    own = call(
        partial(landing_kernel, first=0), "land_own", (plan,), (landed,),
        jax.ShapeDtypeStruct(part_shape.shape, F32), sum_scratch,
    )
    dk, dv = call(
        partial(finish_kernel, kv_heads=kv_heads), "finish", (),
        (dk_near, dv_near, own, back), [small_shape, small_shape],
    )
    return (
        attended.reshape(queries.shape), dq.reshape(queries.shape),
        dk.reshape(keys.shape), dv.reshape(keys.shape),
    )


def on_device(queries, keys, values, output_cotangent, block_lists, list_counts):
    uly_count = lax.axis_size("uly")
    grp_count = lax.axis_size("grp")
    blocks_all, remote = block_lists.shape
    block_tok = queries.shape[0] * uly_count * grp_count // blocks_all
    held_whole = queries.shape[0] % block_tok == 0
    run = whole_blocks if held_whole and remote == 1 and uly_count == 2 else spread_blocks
    return run(queries, keys, values, output_cotangent, block_lists, list_counts)


def solution(mesh):
    placed = (
        P(("grp", "uly"), None, None),
        P(("grp", "uly"), None, None),
        P(("grp", "uly"), None, None),
        P(("grp", "uly"), None, None),
        P(),
        P(),
    )
    return jax.shard_map(
        on_device,
        mesh=mesh,
        in_specs=placed,
        out_specs=(
            P(("grp", "uly"), None, None),
            P(("grp", "uly"), None, None),
            P(("grp", "uly"), None, None),
            P(("grp", "uly"), None, None),
        ),
        check_vma=False,
    )
```

```python
from functools import partial

import jax
import jax.numpy as jnp
from jax import lax
from jax.experimental import pallas as pl
from jax.experimental.pallas import tpu as pltpu
from jax.sharding import PartitionSpec as P


def spread_blocks(queries, keys, values, output_cotangent, block_lists, list_counts):
    uly_count = lax.axis_size("uly")
    grp_count = lax.axis_size("grp")
    my_group = lax.axis_index("grp")
    tokens, head_count, head_width = queries.shape
    kv_heads = keys.shape[1]
    copies = max(1, uly_count // kv_heads)
    blocks_all, remote = block_lists.shape
    per_group = blocks_all // grp_count
    block_tok = tokens * uly_count // per_group
    group_tok = tokens * uly_count
    score_scale = head_width ** (-0.5)
    lists = block_lists.reshape(grp_count, per_group, remote)
    counted = (jnp.arange(remote)[None, :] < list_counts[:, None]).reshape(
        grp_count, per_group, remote
    )
    wanted = (lists // per_group == my_group) & counted
    send_place = jnp.sum(jnp.where(wanted, lists % per_group, 0), axis=(1, 2))
    sending = jnp.any(wanted, axis=(1, 2))
    mine_source = lax.dynamic_index_in_dim(lists, my_group, 0, keepdims=False) // per_group
    mine_counted = lax.dynamic_index_in_dim(counted, my_group, 0, keepdims=False)
    trip_count = jnp.max(jnp.sum(mine_counted.astype(jnp.int32), axis=1))

    def to_blocks(array_in):
        return array_in.reshape((per_group, block_tok) + array_in.shape[1:])

    keys_wide = jnp.repeat(keys, copies, axis=1)
    values_wide = jnp.repeat(values, copies, axis=1)
    query_heads, grad_heads, key_heads, value_heads = (
        lax.all_to_all(queries, "uly", split_axis=1, concat_axis=0, tiled=True),
        lax.all_to_all(output_cotangent, "uly", split_axis=1, concat_axis=0, tiled=True),
        lax.all_to_all(keys_wide, "uly", split_axis=1, concat_axis=0, tiled=True),
        lax.all_to_all(values_wide, "uly", split_axis=1, concat_axis=0, tiled=True),
    )
    stacked = jnp.stack([to_blocks(key_heads), to_blocks(value_heads)])
    outgoing = jnp.take(stacked, send_place, axis=1)
    arrived = lax.all_to_all(outgoing, "grp", split_axis=1, concat_axis=1, tiled=True)
    kv_local = key_heads.shape[1]
    heads_local = query_heads.shape[1]
    heads_per_group = heads_local // kv_local
    query_blk = query_heads.reshape(per_group, block_tok, kv_local, heads_per_group, head_width)
    grad_blk = grad_heads.reshape(per_group, block_tok, kv_local, heads_per_group, head_width)
    key_blk = to_blocks(key_heads)
    value_blk = to_blocks(value_heads)
    far_keys = arrived[0]
    far_values = arrived[1]
    causal = jnp.arange(block_tok)[:, None] >= jnp.arange(block_tok)[None, :]

    def logits(key_rows):
        return (
            jnp.einsum("pqkgd,pjkd->pkgqj", query_blk, key_rows, preferred_element_type=jnp.float32)
            * score_scale
        )

    def slot_rows(slot_index):
        source = lax.dynamic_index_in_dim(mine_source, slot_index, 1, keepdims=False)
        counted_slot = lax.dynamic_index_in_dim(mine_counted, slot_index, 1, keepdims=False)
        return (
            jnp.take(far_keys, source, axis=0),
            jnp.take(far_values, source, axis=0),
            counted_slot,
            source,
        )

    def masked(scores, counted_slot):
        return jnp.where(counted_slot[:, None, None, None, None], scores, -jnp.inf)

    near_scores = jnp.where(causal, logits(key_blk), -jnp.inf)
    highest = jnp.max(near_scores, axis=-1)
    denominator = jnp.sum(jnp.exp(near_scores - highest[..., None]), axis=-1)

    def max_sweep(slot_index, state_pair):
        highest, denominator = state_pair
        key_rows, value_rows, counted_slot, source = slot_rows(slot_index)
        scores = masked(logits(key_rows), counted_slot)
        new_highest = jnp.maximum(highest, jnp.max(scores, axis=-1))
        denominator = denominator * jnp.exp(highest - new_highest) + jnp.sum(
            jnp.exp(scores - new_highest[..., None]), axis=-1
        )
        return (new_highest, denominator)

    highest, denominator = lax.fori_loop(0, trip_count, max_sweep, (highest, denominator))
    log_total = highest + jnp.log(denominator)

    def softmax_weights(scores):
        return jnp.exp(scores - log_total[..., None])

    summed = jnp.einsum(
        "pkgqj,pjkd->pqkgd",
        softmax_weights(near_scores).astype(jnp.bfloat16),
        value_blk,
        preferred_element_type=jnp.float32,
    )

    def value_sweep(slot_index, summed):
        key_rows, value_rows, counted_slot, source = slot_rows(slot_index)
        weights = softmax_weights(masked(logits(key_rows), counted_slot)).astype(jnp.bfloat16)
        return summed + jnp.einsum(
            "pkgqj,pjkd->pqkgd", weights, value_rows, preferred_element_type=jnp.float32
        )

    summed = lax.fori_loop(0, trip_count, value_sweep, summed)
    attended_blk = summed.astype(jnp.bfloat16)
    row_delta = jnp.transpose(
        jnp.sum(grad_blk.astype(jnp.float32) * attended_blk.astype(jnp.float32), axis=-1),
        (0, 2, 3, 1),
    )

    def backward(scores, key_rows, value_rows):
        probs = softmax_weights(scores)
        weights = probs.astype(jnp.bfloat16)
        dprobs = jnp.einsum(
            "pqkgd,pjkd->pkgqj", grad_blk, value_rows, preferred_element_type=jnp.float32
        )
        dscores = (probs * (dprobs - row_delta[..., None])).astype(jnp.bfloat16)
        query_term = jnp.einsum(
            "pkgqj,pjkd->pqkgd", dscores, key_rows, preferred_element_type=jnp.float32
        )
        key_term = (
            jnp.einsum("pkgqj,pqkgd->pjkd", dscores, query_blk, preferred_element_type=jnp.float32)
            * score_scale
        )
        value_term = jnp.einsum(
            "pkgqj,pqkgd->pjkd", weights, grad_blk, preferred_element_type=jnp.float32
        )
        return (query_term, key_term, value_term)

    query_sum, key_near, value_near = backward(near_scores, key_blk, value_blk)
    far_grads = jnp.zeros((2, grp_count, block_tok, kv_local, head_width), jnp.float32)

    def grad_sweep(slot_index, state_pair):
        query_sum, far_grads = state_pair
        key_rows, value_rows, counted_slot, source = slot_rows(slot_index)
        query_term, key_term, value_term = backward(
            masked(logits(key_rows), counted_slot), key_rows, value_rows
        )
        routing = (
            (source[:, None] == jnp.arange(grp_count)[None, :]) & counted_slot[:, None]
        ).astype(jnp.float32)
        routed = jnp.einsum(
            "ps,xpjkd->xsjkd",
            routing,
            jnp.stack([key_term, value_term]),
            precision=lax.Precision.HIGHEST,
        )
        return (query_sum + query_term, far_grads + routed)

    query_sum, far_grads = lax.fori_loop(0, trip_count, grad_sweep, (query_sum, far_grads))
    owners = ((send_place[:, None] == jnp.arange(per_group)[None, :]) & sending[:, None]).astype(
        jnp.float32
    )
    returned = lax.all_to_all(far_grads, "grp", split_axis=1, concat_axis=1, tiled=True)
    landed = jnp.einsum("sp,xsjkd->xpjkd", owners, returned, precision=lax.Precision.HIGHEST)
    key_local = (key_near + landed[0]).reshape(group_tok, kv_local, head_width)
    value_local = (value_near + landed[1]).reshape(group_tok, kv_local, head_width)
    attended_rows = attended_blk.reshape(group_tok, heads_local, head_width)
    query_rows = (
        (query_sum * score_scale).astype(jnp.bfloat16).reshape(group_tok, heads_local, head_width)
    )
    attended, query_grad = (
        lax.all_to_all(attended_rows, "uly", split_axis=0, concat_axis=1, tiled=True),
        lax.all_to_all(query_rows, "uly", split_axis=0, concat_axis=1, tiled=True),
    )
    key_parts, value_parts = (
        lax.all_to_all(key_local, "uly", split_axis=0, concat_axis=1, tiled=True),
        lax.all_to_all(value_local, "uly", split_axis=0, concat_axis=1, tiled=True),
    )
    key_gradient = jnp.sum(key_parts.reshape(tokens, kv_heads, copies, head_width), axis=2).astype(
        jnp.bfloat16
    )
    value_gradient = jnp.sum(
        value_parts.reshape(tokens, kv_heads, copies, head_width), axis=2
    ).astype(jnp.bfloat16)
    return (attended, query_grad, key_gradient, value_gradient)


HIDDEN = -1e30
LAST = (((1,), (1,)), ((), ()))
FIRST = (((0,), (0,)), ((), ()))
F32 = jnp.float32
BF16 = jnp.bfloat16


def dot_last(left, right):
    return lax.dot_general(left, right, LAST, preferred_element_type=F32)


def dot_first(left, right):
    return lax.dot_general(left, right, FIRST, preferred_element_type=F32)


def head_major(cols, kv_heads):
    half = cols // 2
    place = half // kv_heads
    row = lax.broadcasted_iota(jnp.int32, (cols, cols), 0)
    col = lax.broadcasted_iota(jnp.int32, (cols, cols), 1)
    token = row // half * place + row % place
    return jnp.where(col == token * kv_heads + row % half // place, 1.0, 0.0).astype(BF16)


def half_order(cols, kv_heads, which):
    half = cols // 2
    place = half // kv_heads
    row = lax.broadcasted_iota(jnp.int32, (half, cols), 0)
    col = lax.broadcasted_iota(jnp.int32, (half, cols), 1)
    token = which * place + row % place
    return jnp.where(col == token * kv_heads + row // place, 1.0, 0.0).astype(BF16)


def reorder(one_hot, array):
    return jnp.dot(one_hot, array, preferred_element_type=F32).astype(BF16)


def own_head(scores, lane_head, kv_heads):
    place = scores.shape[0] // kv_heads
    kept = scores[:place]
    for head in range(1, kv_heads):
        kept = jnp.where(lane_head == head, scores[head * place:(head + 1) * place], kept)
    return kept


def all_heads(kept, lane_head, kv_heads):
    none = jnp.zeros_like(kept)
    return jnp.concatenate(
        [jnp.where(lane_head == head, kept, none) for head in range(kv_heads)], axis=0
    )


def lanes(rows, heads, kv_heads):
    lane = lax.broadcasted_iota(jnp.int32, (1, rows), 1)
    return lane // heads, lane % heads // (heads // kv_heads)


def plan_spans(grp_count, blocks):
    return grp_count, 2 * grp_count, 2 * grp_count + blocks, 2 * grp_count + 2 * blocks


def fill_plan(lists_ref, counts_ref, plan_ref, grp_count, blocks):
    group, mine = lax.axis_index("grp"), lax.axis_index("uly")
    per_group = 2 * blocks
    low = group * per_group
    sib_at, source_at, give_at, seen_at = plan_spans(grp_count, blocks)
    for other in range(grp_count):
        place = jnp.int32(-1)
        for at in range(other * per_group, (other + 1) * per_group):
            here = lists_ref[at] - low
            wanted = (here >= 0) & (here < per_group) & (counts_ref[at] > 0)
            place = jnp.where(wanted, here, place)
        own = place - mine * blocks
        sib = place - (1 - mine) * blocks
        plan_ref[other] = jnp.where((own >= 0) & (own < blocks), own, -1)
        plan_ref[sib_at + other] = jnp.where((sib >= 0) & (sib < blocks), sib, -1)
    for block in range(blocks):
        at = low + mine * blocks + block
        plan_ref[source_at + block] = lax.div(lists_ref[at], per_group)
        plan_ref[seen_at + block] = counts_ref[at]
        at = low + (1 - mine) * blocks + block
        plan_ref[give_at + block] = lax.div(lists_ref[at], per_group)


def pack_kernel(k_hbm, v_hbm, k_ref, v_ref, given_ref, sems, *, kv_heads):
    blocks, _, half, _ = given_ref.shape
    copies = [
        pltpu.make_async_copy(k_hbm, k_ref, sems.at[0]),
        pltpu.make_async_copy(v_hbm, v_ref, sems.at[1]),
    ]
    for copy in copies:
        copy.start()
    order = half_order(2 * half, kv_heads, 1 - lax.axis_index("uly"))
    for which, ref in enumerate((k_ref, v_ref)):
        copies[which].wait()
        for block in range(blocks):
            given_ref[block, which] = reorder(order, ref[block * 2 * half:(block + 1) * 2 * half])


def send_own_kernel(plan_ref, blocks_ref, out_ref):
    for group in range(out_ref.shape[0]):
        out_ref[group] = blocks_ref[jnp.maximum(plan_ref[group], 0)]


def send_sibling_kernel(plan_ref, blocks_ref, _, out_ref, *, first):
    for group in range(out_ref.shape[0]):
        place = plan_ref[first + group]

        @pl.when(place >= 0)
        def _():
            out_ref[group] = blocks_ref[place]


def giving_kernel(plan_ref, arrived_ref, *out_refs, give_at):
    block = 0
    for out_ref in out_refs:
        for at in range(out_ref.shape[0]):
            out_ref[at] = arrived_ref[plan_ref[give_at + block]]
            block += 1


def returning_kernel(plan_ref, *refs, source_at):
    part_refs, (out_ref, sems) = refs[:-2], refs[-2:]
    copies = []
    for part_ref in part_refs:
        for at in range(part_ref.shape[0]):
            block = len(copies)
            target = out_ref.at[plan_ref[source_at + block]]
            copies.append(pltpu.make_async_copy(part_ref.at[at], target, sems.at[block]))
            copies[-1].start()
    for copy in copies:
        copy.wait()


def near_kernel(
    lists_ref, counts_ref, q_hbm, g_hbm, k_ref, v_ref, given_ref,
    plan_ref, stat_ref, kept_ref, q_ref, g_ref, sems, *, heads, kv_heads, score_scale, grp_count
):
    blocks = stat_ref.shape[0]
    rows = q_ref.shape[0] // blocks
    half = given_ref.shape[2]
    place = half // kv_heads
    copies = []
    for block in range(blocks):
        span = pl.ds(block * rows, rows)
        for which, (source, target) in enumerate(((q_hbm, q_ref), (g_hbm, g_ref))):
            sem = sems.at[which, block]
            copies.append(pltpu.make_async_copy(source.at[span], target.at[span], sem))
            copies[-1].start()
    fill_plan(lists_ref, counts_ref, plan_ref, grp_count, blocks)
    mine = lax.axis_index("uly")
    order = half_order(2 * half, kv_heads, mine)
    for block in range(blocks):
        narrow = slice(block * 2 * half, (block + 1) * 2 * half)
        kept_ref[block, 0] = reorder(order, k_ref[narrow])
        kept_ref[block, 1] = reorder(order, v_ref[narrow])
    token, lane_head = lanes(rows, heads, kv_heads)
    key = lax.broadcasted_iota(jnp.int32, (2 * place, rows), 0)
    part = jnp.where(key < place, mine, 1 - mine)
    causal = key % place + part * place <= token
    for block in range(blocks):
        span = slice(block * rows, (block + 1) * rows)
        pieces = []
        for which, ref in enumerate((q_ref, g_ref)):
            copies[2 * block + which].wait()
            both = jnp.concatenate([kept_ref[block, which], given_ref[block, which]], axis=0)
            full = dot_last(both, ref[span])
            pieces.append(
                jnp.concatenate(
                    [
                        own_head(full[:half], lane_head, kv_heads),
                        own_head(full[half:], lane_head, kv_heads),
                    ],
                    axis=0,
                )
            )
        scores = jnp.where(causal, pieces[0] * score_scale, HIDDEN)
        highest = jnp.max(scores, axis=0, keepdims=True)
        raised = jnp.exp(scores - highest)
        stat_ref[block, 0:1] = highest
        stat_ref[block, 1:2] = jnp.sum(raised, axis=0, keepdims=True)
        stat_ref[block, 2:3] = jnp.sum(raised * pieces[1], axis=0, keepdims=True)


def far_scores(part_ref, at, q, g, seen, lane_head, kv_heads, score_scale):
    hidden = jnp.where(seen > 0, 0.0, HIDDEN)
    scores = own_head(dot_last(part_ref[at, 0], q), lane_head, kv_heads) * score_scale + hidden
    return scores, own_head(dot_last(part_ref[at, 1], g), lane_head, kv_heads)


def merged(stat_ref, block, scores, dprobs):
    before = stat_ref[block, 0:1]
    highest = jnp.maximum(before, jnp.max(scores, axis=0, keepdims=True))
    raised = jnp.exp(scores - highest)
    shrink = jnp.exp(before - highest)
    total = shrink * stat_ref[block, 1:2] + jnp.sum(raised, axis=0, keepdims=True)
    delta = shrink * stat_ref[block, 2:3] + jnp.sum(raised * dprobs, axis=0, keepdims=True)
    return highest, raised, total, delta


def far_gradients(probs, dprobs, delta, q, g, lane_head, kv_heads, score_scale):
    dscores = (probs * (dprobs - delta)).astype(BF16)
    dk = jnp.dot(all_heads(dscores, lane_head, kv_heads), q, preferred_element_type=F32)
    dv = jnp.dot(all_heads(probs.astype(BF16), lane_head, kv_heads), g, preferred_element_type=F32)
    return (dk * score_scale).astype(BF16), dv.astype(BF16)


def mid_kernel(
    plan_ref, q_ref, g_ref, stat_ref, arrived_ref, out_ref,
    *, heads, kv_heads, score_scale, source_at, seen_at
):
    blocks = stat_ref.shape[0]
    rows = q_ref.shape[0] // blocks
    _, lane_head = lanes(rows, heads, kv_heads)
    for block in range(blocks):
        span = slice(block * rows, (block + 1) * rows)
        scores, dprobs = far_scores(
            arrived_ref, plan_ref[source_at + block], q_ref[span], g_ref[span],
            plan_ref[seen_at + block],            lane_head, kv_heads, score_scale,
        )
        highest, _, total, delta = merged(stat_ref, block, scores, dprobs)
        out_ref[block, 0:1] = highest
        out_ref[block, 1:2] = total
        out_ref[block, 2:3] = delta


def far_kernel(
    plan_ref, q_ref, g_ref, stat_ref, other_ref, grad_ref, out_ref,
    *, heads, kv_heads, score_scale, seen_at, first
):
    rows = q_ref.shape[0] // stat_ref.shape[0]
    _, lane_head = lanes(rows, heads, kv_heads)
    for at in range(other_ref.shape[0]):
        block = first + at
        span = slice(block * rows, (block + 1) * rows)
        q = q_ref[span]
        g = g_ref[span]
        scores, dprobs = far_scores(
            other_ref, at, q, g, plan_ref[seen_at + block], lane_head, kv_heads, score_scale
        )
        highest, raised, total, delta = merged(stat_ref, block, scores, dprobs)
        inverse = 1.0 / total
        delta = delta * inverse
        grad_ref[at, 0], grad_ref[at, 1] = far_gradients(
            raised * inverse, dprobs, delta, q, g, lane_head, kv_heads, score_scale
        )
        out_ref[at, 0:1] = highest
        out_ref[at, 1:2] = inverse
        out_ref[at, 2:3] = delta


def mine_kernel(
    plan_ref, q_ref, g_ref, arrived_ref, stat_ref, grad_ref,
    *, heads, kv_heads, score_scale, source_at, seen_at, rows, first
):
    _, lane_head = lanes(rows, heads, kv_heads)
    for at in range(stat_ref.shape[0]):
        block = first + at
        span = slice(block * rows, (block + 1) * rows)
        q = q_ref[span]
        g = g_ref[span]
        scores, dprobs = far_scores(
            arrived_ref, plan_ref[source_at + block], q, g, plan_ref[seen_at + block],
            lane_head, kv_heads, score_scale,
        )
        probs = jnp.exp(scores - stat_ref[at, 0:1]) * stat_ref[at, 1:2]
        grad_ref[at, 0], grad_ref[at, 1] = far_gradients(
            probs, dprobs, stat_ref[at, 2:3], q, g, lane_head, kv_heads, score_scale
        )


def local_kernel(
    plan_ref, q_ref, g_ref, k_ref, v_ref, mine_ref, other_ref,
    att_ref, dq_ref, dk_ref, dv_ref, bias_ref, *, heads, kv_heads, score_scale, seen_at
):
    step = pl.program_id(0)
    rows = q_ref.shape[0]
    cols = k_ref.shape[0]

    @pl.when(step == 0)
    def _():
        half = cols // 2
        place = half // kv_heads
        row = lax.broadcasted_iota(jnp.int32, (rows, cols), 0)
        col = lax.broadcasted_iota(jnp.int32, (rows, cols), 1)
        same = row % heads // (heads // kv_heads) == col % half // place
        causal = col // half * place + col % place <= row // heads
        bias_ref[:, :cols] = jnp.where(same & causal, 0.0, HIDDEN)
        bias_ref[:, cols:] = jnp.where(same, 0.0, HIDDEN)

    far_bias = jnp.where(plan_ref[seen_at + step] > 0, 0.0, HIDDEN)
    order = head_major(cols, kv_heads)
    k_near = reorder(order, k_ref[...])
    v_near = reorder(order, v_ref[...])
    k_all = jnp.concatenate([k_near, mine_ref[0, 0], other_ref[0, 0]], axis=0)
    v_all = jnp.concatenate([v_near, mine_ref[0, 1], other_ref[0, 1]], axis=0)
    q = q_ref[...]
    g = g_ref[...]
    scores = dot_last(q, k_all) * score_scale + bias_ref[...]
    scores = jnp.concatenate([scores[:, :cols], scores[:, cols:] + far_bias], axis=1)
    highest = jnp.max(scores, axis=1, keepdims=True)
    raised = jnp.exp(scores - highest)
    total = jnp.sum(raised, axis=1, keepdims=True)
    probs = raised * (1.0 / total)
    weights = probs.astype(BF16)
    attended = jnp.dot(weights, v_all, preferred_element_type=F32).astype(BF16)
    att_ref[...] = attended
    delta = jnp.sum(g.astype(F32) * attended.astype(F32), axis=1, keepdims=True)
    dscores = (probs * (dot_last(g, v_all) - delta)).astype(BF16)
    dq = jnp.dot(dscores, k_all, preferred_element_type=F32) * score_scale
    dq_ref[...] = dq.astype(BF16)
    dk_ref[...] = dot_first(dscores[:, :cols], q) * score_scale
    dv_ref[...] = dot_first(weights[:, :cols], g)


def landing_kernel(plan_ref, landed_ref, out_ref, sum_ref, *, first):
    sum_ref[...] = jnp.zeros_like(sum_ref)
    for group in range(landed_ref.shape[0]):
        place = plan_ref[first + group]

        @pl.when(place >= 0)
        def _():
            sum_ref[place] = sum_ref[place] + landed_ref[group].astype(F32)

    out_ref[...] = sum_ref[...].astype(out_ref.dtype)


def finish_kernel(
    dk_near_ref, dv_near_ref, own_ref, back_ref, dk_ref, dv_ref, *, kv_heads
):
    blocks, _, half, _ = back_ref.shape
    mine = lax.axis_index("uly") == 0
    order = head_major(2 * half, kv_heads)
    for block in range(blocks):
        span = slice(block * 2 * half, (block + 1) * 2 * half)
        for near_ref, out_ref, which in ((dk_near_ref, dk_ref, 0), (dv_near_ref, dv_ref, 1)):
            own = own_ref[block, which]
            back = back_ref[block, which].astype(F32)
            far = jnp.concatenate([jnp.where(mine, own, back), jnp.where(mine, back, own)], axis=0)
            summed = (near_ref[span] + far).astype(BF16)
            out_ref[span] = dot_first(order, summed).astype(BF16)


def take_rows(array, index):
    return array.at[index].get(mode="promise_in_bounds")


def whole_blocks(queries, keys, values, output_cotangent, block_lists, list_counts):
    grp_count = lax.axis_size("grp")
    uly_count = lax.axis_size("uly")
    tokens, heads, width = queries.shape
    kv_heads = keys.shape[1]
    per_group = block_lists.shape[0] // grp_count
    block_tok = tokens * uly_count // per_group
    mine_blocks = tokens // block_tok
    rows = block_tok * heads
    cols = block_tok * kv_heads
    half = cols // 2
    sizes = dict(heads=heads, kv_heads=kv_heads, score_scale=width ** (-0.5))
    swap = [(0, 1), (1, 0)]

    sib_at, source_at, give_at, seen_at = plan_spans(grp_count, mine_blocks)

    q2 = queries.reshape(tokens * heads, width)
    g2 = output_cotangent.reshape(tokens * heads, width)
    k2 = keys.reshape(tokens * kv_heads, width)
    v2 = values.reshape(tokens * kv_heads, width)

    part_shape = jax.ShapeDtypeStruct((mine_blocks, 2, half, width), BF16)
    slots = (grp_count, 2, half, width)
    stat_shape = jax.ShapeDtypeStruct((mine_blocks, 8, rows), F32)
    row_shape = jax.ShapeDtypeStruct(q2.shape, BF16)
    near_shape = jax.ShapeDtypeStruct(k2.shape, F32)
    small_shape = jax.ShapeDtypeStruct(k2.shape, BF16)
    sum_scratch = [pltpu.VMEM((mine_blocks, 2, half, width), F32)]
    limit = pltpu.CompilerParams(vmem_limit_bytes=24 * 1024 * 1024)
    vmem = pl.BlockSpec(memory_space=pltpu.VMEM)
    smem = pl.BlockSpec(memory_space=pltpu.SMEM)
    anywhere = pl.BlockSpec(memory_space=pltpu.HBM)

    def call(kernel, name, scalars, operands, out_shape, scratch=(), into=None, out_spec=vmem):
        extra = () if into is None else (into,)
        return pl.pallas_call(
            kernel,
            in_specs=[smem] * len(scalars) + [vmem] * (len(operands) + len(extra)),
            out_specs=jax.tree.map(lambda _: out_spec, out_shape),
            out_shape=out_shape,
            scratch_shapes=scratch,
            input_output_aliases={len(scalars) + len(operands): 0} if extra else {},
            compiler_params=limit,
            name=name,
        )(*scalars, *operands, *extra)

    def step_rows(i, *_):
        return (i, 0)

    def step_part(i, *_):
        return (i, 0, 0, 0)

    def in_hbm(array):
        return pltpu.with_memory_space_constraint(array, pltpu.HBM)

    k_here, v_here, given = pl.pallas_call(
        partial(pack_kernel, kv_heads=kv_heads),
        in_specs=[anywhere, anywhere],
        out_specs=[vmem, vmem, vmem],
        out_shape=[small_shape, small_shape, part_shape],
        scratch_shapes=[pltpu.SemaphoreType.DMA((2,))],
        compiler_params=limit,
        name="pack",
    )(in_hbm(k2), in_hbm(v2))
    gotten = lax.ppermute(given, "uly", swap)
    row_spec = pl.BlockSpec((rows, width), step_rows)
    part_spec = pl.BlockSpec((1, 2, half, width), step_part)
    plan, stats, kept, q2, g2 = pl.pallas_call(
        partial(near_kernel, grp_count=grp_count, **sizes),
        in_specs=[smem, smem, anywhere, anywhere, vmem, vmem, vmem],
        out_specs=[smem, vmem, vmem, vmem, vmem],
        out_shape=[
            pltpu.SMEM((seen_at + mine_blocks,), jnp.int32), stat_shape, part_shape,
            pltpu.VMEM(q2.shape, BF16), pltpu.VMEM(q2.shape, BF16),
        ],
        scratch_shapes=[pltpu.SemaphoreType.DMA((2, mine_blocks))],
        compiler_params=limit,
        name="near",
    )(
        in_hbm(block_lists.reshape(-1)), in_hbm(list_counts), in_hbm(q2), in_hbm(g2),
        k_here, v_here, given,
    )
    outgoing = call(
        send_own_kernel, "send_own", (plan,), (kept,),
        jax.ShapeDtypeStruct(slots, BF16),
    )
    gotten, stats = lax.optimization_barrier((gotten, stats))
    outgoing = call(
        partial(send_sibling_kernel, first=sib_at), "send_sibling", (plan,), (gotten,),
        jax.ShapeDtypeStruct(slots, BF16), into=outgoing,
    )
    arrived = lax.all_to_all(outgoing, "grp", split_axis=0, concat_axis=0, tiled=True)
    chunks = 2 if mine_blocks % 2 == 0 else 1
    chunk = mine_blocks // chunks
    chunk_shape = jax.ShapeDtypeStruct((chunk, 2, half, width), BF16)
    giving = call(
        partial(giving_kernel, give_at=give_at), "give", (plan,), (arrived,),
        [chunk_shape] * chunks,
    )
    stats = call(
        partial(mid_kernel, source_at=source_at, seen_at=seen_at, **sizes), "mid", (plan,),
        (q2, g2, stats, arrived), stat_shape,
    )
    others = []
    for part in giving:
        if others:
            part, stats = lax.optimization_barrier((part, stats))
        others.append(lax.ppermute(part, "uly", swap))
    grads, final = [], []
    for at, other in enumerate(others):
        grad, stat = call(
            partial(far_kernel, seen_at=seen_at, first=at * chunk, **sizes), "far", (plan,),
            (q2, g2, stats, other),
            [chunk_shape, jax.ShapeDtypeStruct((chunk, 8, rows), F32)],
        )
        grads.append(grad)
        final.append(stat)
    from_sib = [lax.ppermute(part, "uly", swap) for part in grads]
    mine = [None] * chunks
    for at in reversed(range(chunks)):
        if at + 1 < chunks:
            from_sib[at], final[at] = lax.optimization_barrier((from_sib[at], final[at]))
        mine[at] = call(
            partial(
                mine_kernel, source_at=source_at, seen_at=seen_at, rows=rows, first=at * chunk,
                **sizes,
            ),
            "mine", (plan,), (q2, g2, arrived, final[at]), chunk_shape,
        )
    returning = call(
        partial(returning_kernel, source_at=source_at), "return", (plan,), mine + from_sib,
        pltpu.HBM(slots, BF16), [pltpu.SemaphoreType.DMA((per_group,))], out_spec=anywhere,
    )
    other = jnp.concatenate(others)
    returning, k2l = lax.optimization_barrier((returning, k2))
    landed = lax.all_to_all(returning, "grp", split_axis=0, concat_axis=0, tiled=True)

    def from_source(i, plan_ref):
        return (plan_ref[source_at + i], 0, 0, 0)

    col_spec = pl.BlockSpec((cols, width), step_rows)
    attended, dq, dk_near, dv_near = pl.pallas_call(
        partial(local_kernel, seen_at=seen_at, **sizes),
        grid_spec=pltpu.PrefetchScalarGridSpec(
            num_scalar_prefetch=1,
            grid=(mine_blocks,),
            in_specs=[
                row_spec, row_spec, col_spec, col_spec,
                pl.BlockSpec((1, 2, half, width), from_source),
                part_spec,
            ],
            out_specs=[row_spec, row_spec, col_spec, col_spec],
            scratch_shapes=[pltpu.VMEM((rows, 2 * cols), F32)],
        ),
        out_shape=[row_shape, row_shape, near_shape, near_shape],
        compiler_params=limit,
        name="local",
    )(plan, q2, g2, k2l, v2, arrived, other)
    landed, dk_near = lax.optimization_barrier((landed, dk_near))
    give = call(
        partial(landing_kernel, first=sib_at), "land_sibling", (plan,), (landed,), part_shape,
        sum_scratch,
    )
    back = lax.ppermute(give, "uly", swap)
    own = call(
        partial(landing_kernel, first=0), "land_own", (plan,), (landed,),
        jax.ShapeDtypeStruct(part_shape.shape, F32), sum_scratch,
    )
    dk, dv = call(
        partial(finish_kernel, kv_heads=kv_heads), "finish", (),
        (dk_near, dv_near, own, back), [small_shape, small_shape],
    )
    return (
        attended.reshape(queries.shape), dq.reshape(queries.shape),
        dk.reshape(keys.shape), dv.reshape(keys.shape),
    )


def on_device(queries, keys, values, output_cotangent, block_lists, list_counts):
    uly_count = lax.axis_size("uly")
    grp_count = lax.axis_size("grp")
    blocks_all, remote = block_lists.shape
    block_tok = queries.shape[0] * uly_count * grp_count // blocks_all
    held_whole = queries.shape[0] % block_tok == 0
    run = whole_blocks if held_whole and remote == 1 and uly_count == 2 else spread_blocks
    return run(queries, keys, values, output_cotangent, block_lists, list_counts)


def solution(mesh):
    placed = (
        P(("grp", "uly"), None, None),
        P(("grp", "uly"), None, None),
        P(("grp", "uly"), None, None),
        P(("grp", "uly"), None, None),
        P(),
        P(),
    )
    return jax.shard_map(
        on_device,
        mesh=mesh,
        in_specs=placed,
        out_specs=(
            P(("grp", "uly"), None, None),
            P(("grp", "uly"), None, None),
            P(("grp", "uly"), None, None),
            P(("grp", "uly"), None, None),
        ),
        check_vma=False,
    )
```

```python
from functools import partial

import jax
import jax.numpy as jnp
from jax import lax
from jax.experimental import pallas as pl
from jax.experimental.pallas import tpu as pltpu
from jax.sharding import PartitionSpec as P


def spread_blocks(queries, keys, values, output_cotangent, block_lists, list_counts):
    uly_count = lax.axis_size("uly")
    grp_count = lax.axis_size("grp")
    my_group = lax.axis_index("grp")
    tokens, head_count, head_width = queries.shape
    kv_heads = keys.shape[1]
    copies = max(1, uly_count // kv_heads)
    blocks_all, remote = block_lists.shape
    per_group = blocks_all // grp_count
    block_tok = tokens * uly_count // per_group
    group_tok = tokens * uly_count
    score_scale = head_width ** (-0.5)
    lists = block_lists.reshape(grp_count, per_group, remote)
    counted = (jnp.arange(remote)[None, :] < list_counts[:, None]).reshape(
        grp_count, per_group, remote
    )
    wanted = (lists // per_group == my_group) & counted
    send_place = jnp.sum(jnp.where(wanted, lists % per_group, 0), axis=(1, 2))
    sending = jnp.any(wanted, axis=(1, 2))
    mine_source = lax.dynamic_index_in_dim(lists, my_group, 0, keepdims=False) // per_group
    mine_counted = lax.dynamic_index_in_dim(counted, my_group, 0, keepdims=False)
    trip_count = jnp.max(jnp.sum(mine_counted.astype(jnp.int32), axis=1))

    def to_blocks(array_in):
        return array_in.reshape((per_group, block_tok) + array_in.shape[1:])

    keys_wide = jnp.repeat(keys, copies, axis=1)
    values_wide = jnp.repeat(values, copies, axis=1)
    query_heads, grad_heads, key_heads, value_heads = (
        lax.all_to_all(queries, "uly", split_axis=1, concat_axis=0, tiled=True),
        lax.all_to_all(output_cotangent, "uly", split_axis=1, concat_axis=0, tiled=True),
        lax.all_to_all(keys_wide, "uly", split_axis=1, concat_axis=0, tiled=True),
        lax.all_to_all(values_wide, "uly", split_axis=1, concat_axis=0, tiled=True),
    )
    stacked = jnp.stack([to_blocks(key_heads), to_blocks(value_heads)])
    outgoing = jnp.take(stacked, send_place, axis=1)
    arrived = lax.all_to_all(outgoing, "grp", split_axis=1, concat_axis=1, tiled=True)
    kv_local = key_heads.shape[1]
    heads_local = query_heads.shape[1]
    heads_per_group = heads_local // kv_local
    query_blk = query_heads.reshape(per_group, block_tok, kv_local, heads_per_group, head_width)
    grad_blk = grad_heads.reshape(per_group, block_tok, kv_local, heads_per_group, head_width)
    key_blk = to_blocks(key_heads)
    value_blk = to_blocks(value_heads)
    far_keys = arrived[0]
    far_values = arrived[1]
    causal = jnp.arange(block_tok)[:, None] >= jnp.arange(block_tok)[None, :]

    def logits(key_rows):
        return (
            jnp.einsum("pqkgd,pjkd->pkgqj", query_blk, key_rows, preferred_element_type=jnp.float32)
            * score_scale
        )

    def slot_rows(slot_index):
        source = lax.dynamic_index_in_dim(mine_source, slot_index, 1, keepdims=False)
        counted_slot = lax.dynamic_index_in_dim(mine_counted, slot_index, 1, keepdims=False)
        return (
            jnp.take(far_keys, source, axis=0),
            jnp.take(far_values, source, axis=0),
            counted_slot,
            source,
        )

    def masked(scores, counted_slot):
        return jnp.where(counted_slot[:, None, None, None, None], scores, -jnp.inf)

    near_scores = jnp.where(causal, logits(key_blk), -jnp.inf)
    highest = jnp.max(near_scores, axis=-1)
    denominator = jnp.sum(jnp.exp(near_scores - highest[..., None]), axis=-1)

    def max_sweep(slot_index, state_pair):
        highest, denominator = state_pair
        key_rows, value_rows, counted_slot, source = slot_rows(slot_index)
        scores = masked(logits(key_rows), counted_slot)
        new_highest = jnp.maximum(highest, jnp.max(scores, axis=-1))
        denominator = denominator * jnp.exp(highest - new_highest) + jnp.sum(
            jnp.exp(scores - new_highest[..., None]), axis=-1
        )
        return (new_highest, denominator)

    highest, denominator = lax.fori_loop(0, trip_count, max_sweep, (highest, denominator))
    log_total = highest + jnp.log(denominator)

    def softmax_weights(scores):
        return jnp.exp(scores - log_total[..., None])

    summed = jnp.einsum(
        "pkgqj,pjkd->pqkgd",
        softmax_weights(near_scores).astype(jnp.bfloat16),
        value_blk,
        preferred_element_type=jnp.float32,
    )

    def value_sweep(slot_index, summed):
        key_rows, value_rows, counted_slot, source = slot_rows(slot_index)
        weights = softmax_weights(masked(logits(key_rows), counted_slot)).astype(jnp.bfloat16)
        return summed + jnp.einsum(
            "pkgqj,pjkd->pqkgd", weights, value_rows, preferred_element_type=jnp.float32
        )

    summed = lax.fori_loop(0, trip_count, value_sweep, summed)
    attended_blk = summed.astype(jnp.bfloat16)
    row_delta = jnp.transpose(
        jnp.sum(grad_blk.astype(jnp.float32) * attended_blk.astype(jnp.float32), axis=-1),
        (0, 2, 3, 1),
    )

    def backward(scores, key_rows, value_rows):
        probs = softmax_weights(scores)
        weights = probs.astype(jnp.bfloat16)
        dprobs = jnp.einsum(
            "pqkgd,pjkd->pkgqj", grad_blk, value_rows, preferred_element_type=jnp.float32
        )
        dscores = (probs * (dprobs - row_delta[..., None])).astype(jnp.bfloat16)
        query_term = jnp.einsum(
            "pkgqj,pjkd->pqkgd", dscores, key_rows, preferred_element_type=jnp.float32
        )
        key_term = (
            jnp.einsum("pkgqj,pqkgd->pjkd", dscores, query_blk, preferred_element_type=jnp.float32)
            * score_scale
        )
        value_term = jnp.einsum(
            "pkgqj,pqkgd->pjkd", weights, grad_blk, preferred_element_type=jnp.float32
        )
        return (query_term, key_term, value_term)

    query_sum, key_near, value_near = backward(near_scores, key_blk, value_blk)
    far_grads = jnp.zeros((2, grp_count, block_tok, kv_local, head_width), jnp.float32)

    def grad_sweep(slot_index, state_pair):
        query_sum, far_grads = state_pair
        key_rows, value_rows, counted_slot, source = slot_rows(slot_index)
        query_term, key_term, value_term = backward(
            masked(logits(key_rows), counted_slot), key_rows, value_rows
        )
        routing = (
            (source[:, None] == jnp.arange(grp_count)[None, :]) & counted_slot[:, None]
        ).astype(jnp.float32)
        routed = jnp.einsum(
            "ps,xpjkd->xsjkd",
            routing,
            jnp.stack([key_term, value_term]),
            precision=lax.Precision.HIGHEST,
        )
        return (query_sum + query_term, far_grads + routed)

    query_sum, far_grads = lax.fori_loop(0, trip_count, grad_sweep, (query_sum, far_grads))
    owners = ((send_place[:, None] == jnp.arange(per_group)[None, :]) & sending[:, None]).astype(
        jnp.float32
    )
    returned = lax.all_to_all(far_grads, "grp", split_axis=1, concat_axis=1, tiled=True)
    landed = jnp.einsum("sp,xsjkd->xpjkd", owners, returned, precision=lax.Precision.HIGHEST)
    key_local = (key_near + landed[0]).reshape(group_tok, kv_local, head_width)
    value_local = (value_near + landed[1]).reshape(group_tok, kv_local, head_width)
    attended_rows = attended_blk.reshape(group_tok, heads_local, head_width)
    query_rows = (
        (query_sum * score_scale).astype(jnp.bfloat16).reshape(group_tok, heads_local, head_width)
    )
    attended, query_grad = (
        lax.all_to_all(attended_rows, "uly", split_axis=0, concat_axis=1, tiled=True),
        lax.all_to_all(query_rows, "uly", split_axis=0, concat_axis=1, tiled=True),
    )
    key_parts, value_parts = (
        lax.all_to_all(key_local, "uly", split_axis=0, concat_axis=1, tiled=True),
        lax.all_to_all(value_local, "uly", split_axis=0, concat_axis=1, tiled=True),
    )
    key_gradient = jnp.sum(key_parts.reshape(tokens, kv_heads, copies, head_width), axis=2).astype(
        jnp.bfloat16
    )
    value_gradient = jnp.sum(
        value_parts.reshape(tokens, kv_heads, copies, head_width), axis=2
    ).astype(jnp.bfloat16)
    return (attended, query_grad, key_gradient, value_gradient)


HIDDEN = -1e30
LAST = (((1,), (1,)), ((), ()))
FIRST = (((0,), (0,)), ((), ()))
F32 = jnp.float32
BF16 = jnp.bfloat16


def dot_last(left, right):
    return lax.dot_general(left, right, LAST, preferred_element_type=F32)


def dot_first(left, right):
    return lax.dot_general(left, right, FIRST, preferred_element_type=F32)


def head_major(cols, kv_heads):
    half = cols // 2
    place = half // kv_heads
    row = lax.broadcasted_iota(jnp.int32, (cols, cols), 0)
    col = lax.broadcasted_iota(jnp.int32, (cols, cols), 1)
    token = row // half * place + row % place
    return jnp.where(col == token * kv_heads + row % half // place, 1.0, 0.0).astype(BF16)


def half_order(cols, kv_heads, which):
    half = cols // 2
    place = half // kv_heads
    row = lax.broadcasted_iota(jnp.int32, (half, cols), 0)
    col = lax.broadcasted_iota(jnp.int32, (half, cols), 1)
    token = which * place + row % place
    return jnp.where(col == token * kv_heads + row // place, 1.0, 0.0).astype(BF16)


def reorder(one_hot, array):
    return jnp.dot(one_hot, array, preferred_element_type=F32).astype(BF16)


def own_head(scores, lane_head, kv_heads):
    place = scores.shape[0] // kv_heads
    kept = scores[:place]
    for head in range(1, kv_heads):
        kept = jnp.where(lane_head == head, scores[head * place:(head + 1) * place], kept)
    return kept


def all_heads(kept, lane_head, kv_heads):
    none = jnp.zeros_like(kept)
    return jnp.concatenate(
        [jnp.where(lane_head == head, kept, none) for head in range(kv_heads)], axis=0
    )


def lanes(rows, heads, kv_heads):
    lane = lax.broadcasted_iota(jnp.int32, (1, rows), 1)
    return lane // heads, lane % heads // (heads // kv_heads)


def plan_spans(grp_count, blocks):
    return grp_count, 2 * grp_count, 2 * grp_count + blocks, 2 * grp_count + 2 * blocks


def plan_kernel(lists_ref, counts_ref, plan_ref, *, grp_count, blocks):
    group, mine = lax.axis_index("grp"), lax.axis_index("uly")
    per_group = 2 * blocks
    low = group * per_group
    sib_at, source_at, give_at, seen_at = plan_spans(grp_count, blocks)
    for other in range(grp_count):
        place = jnp.int32(-1)
        for at in range(other * per_group, (other + 1) * per_group):
            here = lists_ref[at] - low
            wanted = (here >= 0) & (here < per_group) & (counts_ref[at] > 0)
            place = jnp.where(wanted, here, place)
        own = place - mine * blocks
        sib = place - (1 - mine) * blocks
        plan_ref[other] = jnp.where((own >= 0) & (own < blocks), own, -1)
        plan_ref[sib_at + other] = jnp.where((sib >= 0) & (sib < blocks), sib, -1)
    for block in range(blocks):
        at = low + mine * blocks + block
        plan_ref[source_at + block] = lax.div(lists_ref[at], per_group)
        plan_ref[seen_at + block] = counts_ref[at]
        at = low + (1 - mine) * blocks + block
        plan_ref[give_at + block] = lax.div(lists_ref[at], per_group)


def pack_kernel(k_hbm, v_hbm, k_ref, v_ref, given_ref, sems, *, kv_heads):
    blocks, _, half, _ = given_ref.shape
    copies = [
        pltpu.make_async_copy(k_hbm, k_ref, sems.at[0]),
        pltpu.make_async_copy(v_hbm, v_ref, sems.at[1]),
    ]
    for copy in copies:
        copy.start()
    order = half_order(2 * half, kv_heads, 1 - lax.axis_index("uly"))
    for which, ref in enumerate((k_ref, v_ref)):
        copies[which].wait()
        for block in range(blocks):
            given_ref[block, which] = reorder(order, ref[block * 2 * half:(block + 1) * 2 * half])


def send_own_kernel(plan_ref, k_ref, v_ref, kept_ref, out_ref, *, kv_heads):
    blocks, _, half, _ = kept_ref.shape
    order = half_order(2 * half, kv_heads, lax.axis_index("uly"))
    for block in range(blocks):
        span = slice(block * 2 * half, (block + 1) * 2 * half)
        kept_ref[block, 0] = reorder(order, k_ref[span])
        kept_ref[block, 1] = reorder(order, v_ref[span])
    for group in range(out_ref.shape[0]):
        out_ref[group] = kept_ref[jnp.maximum(plan_ref[group], 0)]


def send_sibling_kernel(plan_ref, blocks_ref, _, out_ref, *, first):
    for group in range(out_ref.shape[0]):
        place = plan_ref[first + group]

        @pl.when(place >= 0)
        def _():
            out_ref[group] = blocks_ref[place]


def giving_kernel(plan_ref, arrived_ref, *out_refs, give_at):
    block = 0
    for out_ref in out_refs:
        for at in range(out_ref.shape[0]):
            out_ref[at] = arrived_ref[plan_ref[give_at + block]]
            block += 1


def returning_kernel(plan_ref, *refs, source_at):
    part_refs, (out_ref, sems) = refs[:-2], refs[-2:]
    copies = []
    for part_ref in part_refs:
        for at in range(part_ref.shape[0]):
            block = len(copies)
            target = out_ref.at[plan_ref[source_at + block]]
            copies.append(pltpu.make_async_copy(part_ref.at[at], target, sems.at[block]))
            copies[-1].start()
    for copy in copies:
        copy.wait()


def near_kernel(
    q_ref, g_ref, kept_ref, given_ref, stat_ref, *, heads, kv_heads, score_scale
):
    blocks = stat_ref.shape[0]
    rows = q_ref.shape[0] // blocks
    half = given_ref.shape[2]
    place = half // kv_heads
    mine = lax.axis_index("uly")
    token, lane_head = lanes(rows, heads, kv_heads)
    key = lax.broadcasted_iota(jnp.int32, (2 * place, rows), 0)
    part = jnp.where(key < place, mine, 1 - mine)
    causal = key % place + part * place <= token
    for block in range(blocks):
        span = slice(block * rows, (block + 1) * rows)
        pieces = []
        for which, ref in enumerate((q_ref, g_ref)):
            both = jnp.concatenate([kept_ref[block, which], given_ref[block, which]], axis=0)
            full = dot_last(both, ref[span])
            pieces.append(
                jnp.concatenate(
                    [
                        own_head(full[:half], lane_head, kv_heads),
                        own_head(full[half:], lane_head, kv_heads),
                    ],
                    axis=0,
                )
            )
        scores = jnp.where(causal, pieces[0] * score_scale, HIDDEN)
        highest = jnp.max(scores, axis=0, keepdims=True)
        raised = jnp.exp(scores - highest)
        stat_ref[block, 0:1] = highest
        stat_ref[block, 1:2] = jnp.sum(raised, axis=0, keepdims=True)
        stat_ref[block, 2:3] = jnp.sum(raised * pieces[1], axis=0, keepdims=True)


def far_scores(part_ref, at, q, g, seen, lane_head, kv_heads, score_scale):
    hidden = jnp.where(seen > 0, 0.0, HIDDEN)
    scores = own_head(dot_last(part_ref[at, 0], q), lane_head, kv_heads) * score_scale + hidden
    return scores, own_head(dot_last(part_ref[at, 1], g), lane_head, kv_heads)


def merged(stat_ref, block, scores, dprobs):
    before = stat_ref[block, 0:1]
    highest = jnp.maximum(before, jnp.max(scores, axis=0, keepdims=True))
    raised = jnp.exp(scores - highest)
    shrink = jnp.exp(before - highest)
    total = shrink * stat_ref[block, 1:2] + jnp.sum(raised, axis=0, keepdims=True)
    delta = shrink * stat_ref[block, 2:3] + jnp.sum(raised * dprobs, axis=0, keepdims=True)
    return highest, raised, total, delta


def far_gradients(probs, dprobs, delta, q, g, lane_head, kv_heads, score_scale):
    dscores = (probs * (dprobs - delta)).astype(BF16)
    dk = jnp.dot(all_heads(dscores, lane_head, kv_heads), q, preferred_element_type=F32)
    dv = jnp.dot(all_heads(probs.astype(BF16), lane_head, kv_heads), g, preferred_element_type=F32)
    return (dk * score_scale).astype(BF16), dv.astype(BF16)


def mid_kernel(
    plan_ref, q_ref, g_ref, stat_ref, arrived_ref, out_ref,
    *, heads, kv_heads, score_scale, source_at, seen_at
):
    blocks = stat_ref.shape[0]
    rows = q_ref.shape[0] // blocks
    _, lane_head = lanes(rows, heads, kv_heads)
    for block in range(blocks):
        span = slice(block * rows, (block + 1) * rows)
        scores, dprobs = far_scores(
            arrived_ref, plan_ref[source_at + block], q_ref[span], g_ref[span],
            plan_ref[seen_at + block],            lane_head, kv_heads, score_scale,
        )
        highest, _, total, delta = merged(stat_ref, block, scores, dprobs)
        out_ref[block, 0:1] = highest
        out_ref[block, 1:2] = total
        out_ref[block, 2:3] = delta


def far_kernel(
    plan_ref, q_ref, g_ref, stat_ref, other_ref, grad_ref, out_ref,
    *, heads, kv_heads, score_scale, seen_at, first
):
    rows = q_ref.shape[0] // stat_ref.shape[0]
    _, lane_head = lanes(rows, heads, kv_heads)
    for at in range(other_ref.shape[0]):
        block = first + at
        span = slice(block * rows, (block + 1) * rows)
        q = q_ref[span]
        g = g_ref[span]
        scores, dprobs = far_scores(
            other_ref, at, q, g, plan_ref[seen_at + block], lane_head, kv_heads, score_scale
        )
        highest, raised, total, delta = merged(stat_ref, block, scores, dprobs)
        inverse = 1.0 / total
        delta = delta * inverse
        grad_ref[at, 0], grad_ref[at, 1] = far_gradients(
            raised * inverse, dprobs, delta, q, g, lane_head, kv_heads, score_scale
        )
        out_ref[at, 0:1] = highest
        out_ref[at, 1:2] = inverse
        out_ref[at, 2:3] = delta


def mine_kernel(
    plan_ref, q_ref, g_ref, arrived_ref, stat_ref, grad_ref,
    *, heads, kv_heads, score_scale, source_at, seen_at, rows, first
):
    _, lane_head = lanes(rows, heads, kv_heads)
    for at in range(stat_ref.shape[0]):
        block = first + at
        span = slice(block * rows, (block + 1) * rows)
        q = q_ref[span]
        g = g_ref[span]
        scores, dprobs = far_scores(
            arrived_ref, plan_ref[source_at + block], q, g, plan_ref[seen_at + block],
            lane_head, kv_heads, score_scale,
        )
        probs = jnp.exp(scores - stat_ref[at, 0:1]) * stat_ref[at, 1:2]
        grad_ref[at, 0], grad_ref[at, 1] = far_gradients(
            probs, dprobs, stat_ref[at, 2:3], q, g, lane_head, kv_heads, score_scale
        )


def local_kernel(
    plan_ref, q_ref, g_ref, k_ref, v_ref, mine_ref, other_ref,
    att_ref, dq_ref, dk_ref, dv_ref, bias_ref, *, heads, kv_heads, score_scale, seen_at
):
    step = pl.program_id(0)
    rows = q_ref.shape[0]
    cols = k_ref.shape[0]

    @pl.when(step == 0)
    def _():
        half = cols // 2
        place = half // kv_heads
        row = lax.broadcasted_iota(jnp.int32, (rows, cols), 0)
        col = lax.broadcasted_iota(jnp.int32, (rows, cols), 1)
        same = row % heads // (heads // kv_heads) == col % half // place
        causal = col // half * place + col % place <= row // heads
        bias_ref[:, :cols] = jnp.where(same & causal, 0.0, HIDDEN)
        bias_ref[:, cols:] = jnp.where(same, 0.0, HIDDEN)

    far_bias = jnp.where(plan_ref[seen_at + step] > 0, 0.0, HIDDEN)
    order = head_major(cols, kv_heads)
    k_near = reorder(order, k_ref[...])
    v_near = reorder(order, v_ref[...])
    k_all = jnp.concatenate([k_near, mine_ref[0, 0], other_ref[0, 0]], axis=0)
    v_all = jnp.concatenate([v_near, mine_ref[0, 1], other_ref[0, 1]], axis=0)
    q = q_ref[...]
    g = g_ref[...]
    scores = dot_last(q, k_all) * score_scale + bias_ref[...]
    scores = jnp.concatenate([scores[:, :cols], scores[:, cols:] + far_bias], axis=1)
    highest = jnp.max(scores, axis=1, keepdims=True)
    raised = jnp.exp(scores - highest)
    total = jnp.sum(raised, axis=1, keepdims=True)
    probs = raised * (1.0 / total)
    weights = probs.astype(BF16)
    attended = jnp.dot(weights, v_all, preferred_element_type=F32).astype(BF16)
    att_ref[...] = attended
    delta = jnp.sum(g.astype(F32) * attended.astype(F32), axis=1, keepdims=True)
    dscores = (probs * (dot_last(g, v_all) - delta)).astype(BF16)
    dq = jnp.dot(dscores, k_all, preferred_element_type=F32) * score_scale
    dq_ref[...] = dq.astype(BF16)
    dk_ref[...] = dot_first(dscores[:, :cols], q) * score_scale
    dv_ref[...] = dot_first(weights[:, :cols], g)


def landing_kernel(plan_ref, landed_ref, out_ref, sum_ref, *, first):
    sum_ref[...] = jnp.zeros_like(sum_ref)
    for group in range(landed_ref.shape[0]):
        place = plan_ref[first + group]

        @pl.when(place >= 0)
        def _():
            sum_ref[place] = sum_ref[place] + landed_ref[group].astype(F32)

    out_ref[...] = sum_ref[...].astype(out_ref.dtype)


def finish_kernel(
    dk_near_ref, dv_near_ref, own_ref, back_ref, dk_ref, dv_ref, *, kv_heads
):
    blocks, _, half, _ = back_ref.shape
    mine = lax.axis_index("uly") == 0
    order = head_major(2 * half, kv_heads)
    for block in range(blocks):
        span = slice(block * 2 * half, (block + 1) * 2 * half)
        for near_ref, out_ref, which in ((dk_near_ref, dk_ref, 0), (dv_near_ref, dv_ref, 1)):
            own = own_ref[block, which]
            back = back_ref[block, which].astype(F32)
            far = jnp.concatenate([jnp.where(mine, own, back), jnp.where(mine, back, own)], axis=0)
            summed = (near_ref[span] + far).astype(BF16)
            out_ref[span] = dot_first(order, summed).astype(BF16)


def take_rows(array, index):
    return array.at[index].get(mode="promise_in_bounds")


def whole_blocks(queries, keys, values, output_cotangent, block_lists, list_counts):
    grp_count = lax.axis_size("grp")
    uly_count = lax.axis_size("uly")
    tokens, heads, width = queries.shape
    kv_heads = keys.shape[1]
    per_group = block_lists.shape[0] // grp_count
    block_tok = tokens * uly_count // per_group
    mine_blocks = tokens // block_tok
    rows = block_tok * heads
    cols = block_tok * kv_heads
    half = cols // 2
    sizes = dict(heads=heads, kv_heads=kv_heads, score_scale=width ** (-0.5))
    swap = [(0, 1), (1, 0)]

    sib_at, source_at, give_at, seen_at = plan_spans(grp_count, mine_blocks)

    q2 = queries.reshape(tokens * heads, width)
    g2 = output_cotangent.reshape(tokens * heads, width)
    k2 = keys.reshape(tokens * kv_heads, width)
    v2 = values.reshape(tokens * kv_heads, width)

    part_shape = jax.ShapeDtypeStruct((mine_blocks, 2, half, width), BF16)
    slots = (grp_count, 2, half, width)
    stat_shape = jax.ShapeDtypeStruct((mine_blocks, 8, rows), F32)
    row_shape = jax.ShapeDtypeStruct(q2.shape, BF16)
    near_shape = jax.ShapeDtypeStruct(k2.shape, F32)
    small_shape = jax.ShapeDtypeStruct(k2.shape, BF16)
    sum_scratch = [pltpu.VMEM((mine_blocks, 2, half, width), F32)]
    limit = pltpu.CompilerParams(vmem_limit_bytes=24 * 1024 * 1024)
    vmem = pl.BlockSpec(memory_space=pltpu.VMEM)
    smem = pl.BlockSpec(memory_space=pltpu.SMEM)
    anywhere = pl.BlockSpec(memory_space=pltpu.HBM)

    def call(kernel, name, scalars, operands, out_shape, scratch=(), into=None, out_spec=vmem):
        extra = () if into is None else (into,)
        return pl.pallas_call(
            kernel,
            in_specs=[smem] * len(scalars) + [vmem] * (len(operands) + len(extra)),
            out_specs=jax.tree.map(lambda _: out_spec, out_shape),
            out_shape=out_shape,
            scratch_shapes=scratch,
            input_output_aliases={len(scalars) + len(operands): 0} if extra else {},
            compiler_params=limit,
            name=name,
        )(*scalars, *operands, *extra)

    def step_rows(i, *_):
        return (i, 0)

    def step_part(i, *_):
        return (i, 0, 0, 0)

    def in_hbm(array):
        return pltpu.with_memory_space_constraint(array, pltpu.HBM)

    k_here, v_here, given = pl.pallas_call(
        partial(pack_kernel, kv_heads=kv_heads),
        in_specs=[anywhere, anywhere],
        out_specs=[vmem, vmem, vmem],
        out_shape=[small_shape, small_shape, part_shape],
        scratch_shapes=[pltpu.SemaphoreType.DMA((2,))],
        compiler_params=limit,
        name="pack",
    )(in_hbm(k2), in_hbm(v2))
    plan = pl.pallas_call(
        partial(plan_kernel, grp_count=grp_count, blocks=mine_blocks),
        in_specs=[smem, smem],
        out_specs=smem,
        out_shape=pltpu.SMEM((seen_at + mine_blocks,), jnp.int32),
        compiler_params=limit,
        name="plan",
    )(in_hbm(block_lists.reshape(-1)), in_hbm(list_counts))
    gotten = lax.ppermute(given, "uly", swap)
    row_spec = pl.BlockSpec((rows, width), step_rows)
    part_spec = pl.BlockSpec((1, 2, half, width), step_part)
    kept, outgoing = call(
        partial(send_own_kernel, kv_heads=kv_heads), "send_own", (plan,), (k_here, v_here),
        [part_shape, jax.ShapeDtypeStruct(slots, BF16)],
    )
    outgoing = call(
        partial(send_sibling_kernel, first=sib_at), "send_sibling", (plan,), (gotten,),
        jax.ShapeDtypeStruct(slots, BF16), into=outgoing,
    )
    arrived = lax.all_to_all(outgoing, "grp", split_axis=0, concat_axis=0, tiled=True)
    kept, arrived = lax.optimization_barrier((kept, arrived))
    chunks = 1
    chunk = mine_blocks // chunks
    chunk_shape = jax.ShapeDtypeStruct((chunk, 2, half, width), BF16)
    giving = call(
        partial(giving_kernel, give_at=give_at), "give", (plan,), (arrived,),
        [chunk_shape] * chunks,
    )
    stats = call(partial(near_kernel, **sizes), "near", (), (q2, g2, kept, given), stat_shape)
    others = []
    for part in giving:
        if others:
            part, stats = lax.optimization_barrier((part, stats))
        others.append(lax.ppermute(part, "uly", swap))
    stats = call(
        partial(mid_kernel, source_at=source_at, seen_at=seen_at, **sizes), "mid", (plan,),
        (q2, g2, stats, arrived), stat_shape,
    )
    grads, final = [], []
    for at, other in enumerate(others):
        grad, stat = call(
            partial(far_kernel, seen_at=seen_at, first=at * chunk, **sizes), "far", (plan,),
            (q2, g2, stats, other),
            [chunk_shape, jax.ShapeDtypeStruct((chunk, 8, rows), F32)],
        )
        grads.append(grad)
        final.append(stat)
    from_sib = [lax.ppermute(part, "uly", swap) for part in grads]
    mine = [None] * chunks
    for at in reversed(range(chunks)):
        if at + 1 < chunks:
            from_sib[at], final[at] = lax.optimization_barrier((from_sib[at], final[at]))
        mine[at] = call(
            partial(
                mine_kernel, source_at=source_at, seen_at=seen_at, rows=rows, first=at * chunk,
                **sizes,
            ),
            "mine", (plan,), (q2, g2, arrived, final[at]), chunk_shape,
        )
    returning = call(
        partial(returning_kernel, source_at=source_at), "return", (plan,), mine + from_sib,
        pltpu.HBM(slots, BF16), [pltpu.SemaphoreType.DMA((per_group,))], out_spec=anywhere,
    )
    other = jnp.concatenate(others)
    returning, k2l = lax.optimization_barrier((returning, k2))
    landed = lax.all_to_all(returning, "grp", split_axis=0, concat_axis=0, tiled=True)

    def from_source(i, plan_ref):
        return (plan_ref[source_at + i], 0, 0, 0)

    col_spec = pl.BlockSpec((cols, width), step_rows)
    attended, dq, dk_near, dv_near = pl.pallas_call(
        partial(local_kernel, seen_at=seen_at, **sizes),
        grid_spec=pltpu.PrefetchScalarGridSpec(
            num_scalar_prefetch=1,
            grid=(mine_blocks,),
            in_specs=[
                row_spec, row_spec, col_spec, col_spec,
                pl.BlockSpec((1, 2, half, width), from_source),
                part_spec,
            ],
            out_specs=[row_spec, row_spec, col_spec, col_spec],
            scratch_shapes=[pltpu.VMEM((rows, 2 * cols), F32)],
        ),
        out_shape=[row_shape, row_shape, near_shape, near_shape],
        compiler_params=limit,
        name="local",
    )(plan, q2, g2, k2l, v2, arrived, other)
    landed, dk_near = lax.optimization_barrier((landed, dk_near))
    give = call(
        partial(landing_kernel, first=sib_at), "land_sibling", (plan,), (landed,), part_shape,
        sum_scratch,
    )
    back = lax.ppermute(give, "uly", swap)
    own = call(
        partial(landing_kernel, first=0), "land_own", (plan,), (landed,),
        jax.ShapeDtypeStruct(part_shape.shape, F32), sum_scratch,
    )
    dk, dv = call(
        partial(finish_kernel, kv_heads=kv_heads), "finish", (),
        (dk_near, dv_near, own, back), [small_shape, small_shape],
    )
    return (
        attended.reshape(queries.shape), dq.reshape(queries.shape),
        dk.reshape(keys.shape), dv.reshape(keys.shape),
    )


def on_device(queries, keys, values, output_cotangent, block_lists, list_counts):
    uly_count = lax.axis_size("uly")
    grp_count = lax.axis_size("grp")
    blocks_all, remote = block_lists.shape
    block_tok = queries.shape[0] * uly_count * grp_count // blocks_all
    held_whole = queries.shape[0] % block_tok == 0
    run = whole_blocks if held_whole and remote == 1 and uly_count == 2 else spread_blocks
    return run(queries, keys, values, output_cotangent, block_lists, list_counts)


def solution(mesh):
    placed = (
        P(("grp", "uly"), None, None),
        P(("grp", "uly"), None, None),
        P(("grp", "uly"), None, None),
        P(("grp", "uly"), None, None),
        P(),
        P(),
    )
    return jax.shard_map(
        on_device,
        mesh=mesh,
        in_specs=placed,
        out_specs=(
            P(("grp", "uly"), None, None),
            P(("grp", "uly"), None, None),
            P(("grp", "uly"), None, None),
            P(("grp", "uly"), None, None),
        ),
        check_vma=False,
    )
```

```python
from functools import partial

import jax
import jax.numpy as jnp
from jax import lax
from jax.experimental import pallas as pl
from jax.experimental.pallas import tpu as pltpu
from jax.sharding import PartitionSpec as P


def spread_blocks(queries, keys, values, output_cotangent, block_lists, list_counts):
    uly_count = lax.axis_size("uly")
    grp_count = lax.axis_size("grp")
    my_group = lax.axis_index("grp")
    tokens, head_count, head_width = queries.shape
    kv_heads = keys.shape[1]
    copies = max(1, uly_count // kv_heads)
    blocks_all, remote = block_lists.shape
    per_group = blocks_all // grp_count
    block_tok = tokens * uly_count // per_group
    group_tok = tokens * uly_count
    score_scale = head_width ** (-0.5)
    lists = block_lists.reshape(grp_count, per_group, remote)
    counted = (jnp.arange(remote)[None, :] < list_counts[:, None]).reshape(
        grp_count, per_group, remote
    )
    wanted = (lists // per_group == my_group) & counted
    send_place = jnp.sum(jnp.where(wanted, lists % per_group, 0), axis=(1, 2))
    sending = jnp.any(wanted, axis=(1, 2))
    mine_source = lax.dynamic_index_in_dim(lists, my_group, 0, keepdims=False) // per_group
    mine_counted = lax.dynamic_index_in_dim(counted, my_group, 0, keepdims=False)
    trip_count = jnp.max(jnp.sum(mine_counted.astype(jnp.int32), axis=1))

    def to_blocks(array_in):
        return array_in.reshape((per_group, block_tok) + array_in.shape[1:])

    keys_wide = jnp.repeat(keys, copies, axis=1)
    values_wide = jnp.repeat(values, copies, axis=1)
    query_heads, grad_heads, key_heads, value_heads = (
        lax.all_to_all(queries, "uly", split_axis=1, concat_axis=0, tiled=True),
        lax.all_to_all(output_cotangent, "uly", split_axis=1, concat_axis=0, tiled=True),
        lax.all_to_all(keys_wide, "uly", split_axis=1, concat_axis=0, tiled=True),
        lax.all_to_all(values_wide, "uly", split_axis=1, concat_axis=0, tiled=True),
    )
    stacked = jnp.stack([to_blocks(key_heads), to_blocks(value_heads)])
    outgoing = jnp.take(stacked, send_place, axis=1)
    arrived = lax.all_to_all(outgoing, "grp", split_axis=1, concat_axis=1, tiled=True)
    kv_local = key_heads.shape[1]
    heads_local = query_heads.shape[1]
    heads_per_group = heads_local // kv_local
    query_blk = query_heads.reshape(per_group, block_tok, kv_local, heads_per_group, head_width)
    grad_blk = grad_heads.reshape(per_group, block_tok, kv_local, heads_per_group, head_width)
    key_blk = to_blocks(key_heads)
    value_blk = to_blocks(value_heads)
    far_keys = arrived[0]
    far_values = arrived[1]
    causal = jnp.arange(block_tok)[:, None] >= jnp.arange(block_tok)[None, :]

    def logits(key_rows):
        return (
            jnp.einsum("pqkgd,pjkd->pkgqj", query_blk, key_rows, preferred_element_type=jnp.float32)
            * score_scale
        )

    def slot_rows(slot_index):
        source = lax.dynamic_index_in_dim(mine_source, slot_index, 1, keepdims=False)
        counted_slot = lax.dynamic_index_in_dim(mine_counted, slot_index, 1, keepdims=False)
        return (
            jnp.take(far_keys, source, axis=0),
            jnp.take(far_values, source, axis=0),
            counted_slot,
            source,
        )

    def masked(scores, counted_slot):
        return jnp.where(counted_slot[:, None, None, None, None], scores, -jnp.inf)

    near_scores = jnp.where(causal, logits(key_blk), -jnp.inf)
    highest = jnp.max(near_scores, axis=-1)
    denominator = jnp.sum(jnp.exp(near_scores - highest[..., None]), axis=-1)

    def max_sweep(slot_index, state_pair):
        highest, denominator = state_pair
        key_rows, value_rows, counted_slot, source = slot_rows(slot_index)
        scores = masked(logits(key_rows), counted_slot)
        new_highest = jnp.maximum(highest, jnp.max(scores, axis=-1))
        denominator = denominator * jnp.exp(highest - new_highest) + jnp.sum(
            jnp.exp(scores - new_highest[..., None]), axis=-1
        )
        return (new_highest, denominator)

    highest, denominator = lax.fori_loop(0, trip_count, max_sweep, (highest, denominator))
    log_total = highest + jnp.log(denominator)

    def softmax_weights(scores):
        return jnp.exp(scores - log_total[..., None])

    summed = jnp.einsum(
        "pkgqj,pjkd->pqkgd",
        softmax_weights(near_scores).astype(jnp.bfloat16),
        value_blk,
        preferred_element_type=jnp.float32,
    )

    def value_sweep(slot_index, summed):
        key_rows, value_rows, counted_slot, source = slot_rows(slot_index)
        weights = softmax_weights(masked(logits(key_rows), counted_slot)).astype(jnp.bfloat16)
        return summed + jnp.einsum(
            "pkgqj,pjkd->pqkgd", weights, value_rows, preferred_element_type=jnp.float32
        )

    summed = lax.fori_loop(0, trip_count, value_sweep, summed)
    attended_blk = summed.astype(jnp.bfloat16)
    row_delta = jnp.transpose(
        jnp.sum(grad_blk.astype(jnp.float32) * attended_blk.astype(jnp.float32), axis=-1),
        (0, 2, 3, 1),
    )

    def backward(scores, key_rows, value_rows):
        probs = softmax_weights(scores)
        weights = probs.astype(jnp.bfloat16)
        dprobs = jnp.einsum(
            "pqkgd,pjkd->pkgqj", grad_blk, value_rows, preferred_element_type=jnp.float32
        )
        dscores = (probs * (dprobs - row_delta[..., None])).astype(jnp.bfloat16)
        query_term = jnp.einsum(
            "pkgqj,pjkd->pqkgd", dscores, key_rows, preferred_element_type=jnp.float32
        )
        key_term = (
            jnp.einsum("pkgqj,pqkgd->pjkd", dscores, query_blk, preferred_element_type=jnp.float32)
            * score_scale
        )
        value_term = jnp.einsum(
            "pkgqj,pqkgd->pjkd", weights, grad_blk, preferred_element_type=jnp.float32
        )
        return (query_term, key_term, value_term)

    query_sum, key_near, value_near = backward(near_scores, key_blk, value_blk)
    far_grads = jnp.zeros((2, grp_count, block_tok, kv_local, head_width), jnp.float32)

    def grad_sweep(slot_index, state_pair):
        query_sum, far_grads = state_pair
        key_rows, value_rows, counted_slot, source = slot_rows(slot_index)
        query_term, key_term, value_term = backward(
            masked(logits(key_rows), counted_slot), key_rows, value_rows
        )
        routing = (
            (source[:, None] == jnp.arange(grp_count)[None, :]) & counted_slot[:, None]
        ).astype(jnp.float32)
        routed = jnp.einsum(
            "ps,xpjkd->xsjkd",
            routing,
            jnp.stack([key_term, value_term]),
            precision=lax.Precision.HIGHEST,
        )
        return (query_sum + query_term, far_grads + routed)

    query_sum, far_grads = lax.fori_loop(0, trip_count, grad_sweep, (query_sum, far_grads))
    owners = ((send_place[:, None] == jnp.arange(per_group)[None, :]) & sending[:, None]).astype(
        jnp.float32
    )
    returned = lax.all_to_all(far_grads, "grp", split_axis=1, concat_axis=1, tiled=True)
    landed = jnp.einsum("sp,xsjkd->xpjkd", owners, returned, precision=lax.Precision.HIGHEST)
    key_local = (key_near + landed[0]).reshape(group_tok, kv_local, head_width)
    value_local = (value_near + landed[1]).reshape(group_tok, kv_local, head_width)
    attended_rows = attended_blk.reshape(group_tok, heads_local, head_width)
    query_rows = (
        (query_sum * score_scale).astype(jnp.bfloat16).reshape(group_tok, heads_local, head_width)
    )
    attended, query_grad = (
        lax.all_to_all(attended_rows, "uly", split_axis=0, concat_axis=1, tiled=True),
        lax.all_to_all(query_rows, "uly", split_axis=0, concat_axis=1, tiled=True),
    )
    key_parts, value_parts = (
        lax.all_to_all(key_local, "uly", split_axis=0, concat_axis=1, tiled=True),
        lax.all_to_all(value_local, "uly", split_axis=0, concat_axis=1, tiled=True),
    )
    key_gradient = jnp.sum(key_parts.reshape(tokens, kv_heads, copies, head_width), axis=2).astype(
        jnp.bfloat16
    )
    value_gradient = jnp.sum(
        value_parts.reshape(tokens, kv_heads, copies, head_width), axis=2
    ).astype(jnp.bfloat16)
    return (attended, query_grad, key_gradient, value_gradient)


HIDDEN = -1e30
LAST = (((1,), (1,)), ((), ()))
FIRST = (((0,), (0,)), ((), ()))
F32 = jnp.float32
BF16 = jnp.bfloat16


def dot_last(left, right):
    return lax.dot_general(left, right, LAST, preferred_element_type=F32)


def dot_first(left, right):
    return lax.dot_general(left, right, FIRST, preferred_element_type=F32)


def head_major(cols, kv_heads):
    half = cols // 2
    place = half // kv_heads
    row = lax.broadcasted_iota(jnp.int32, (cols, cols), 0)
    col = lax.broadcasted_iota(jnp.int32, (cols, cols), 1)
    token = row // half * place + row % place
    return jnp.where(col == token * kv_heads + row % half // place, 1.0, 0.0).astype(BF16)


def token_major(half, kv_heads):
    place = half // kv_heads
    row = lax.broadcasted_iota(jnp.int32, (half, half), 0)
    col = lax.broadcasted_iota(jnp.int32, (half, half), 1)
    return jnp.where(col == row % kv_heads * place + row // kv_heads, 1.0, 0.0).astype(BF16)


def reorder(one_hot, array):
    return jnp.dot(one_hot, array, preferred_element_type=F32).astype(BF16)


def own_head(scores, lane_head, kv_heads):
    place = scores.shape[0] // kv_heads
    kept = scores[:place]
    for head in range(1, kv_heads):
        kept = jnp.where(lane_head == head, scores[head * place:(head + 1) * place], kept)
    return kept


def all_heads(kept, lane_head, kv_heads):
    none = jnp.zeros_like(kept)
    return jnp.concatenate(
        [jnp.where(lane_head == head, kept, none) for head in range(kv_heads)], axis=0
    )


def lanes(rows, heads, kv_heads):
    lane = lax.broadcasted_iota(jnp.int32, (1, rows), 1)
    return lane // heads, lane % heads // (heads // kv_heads)


def plan_spans(grp_count, blocks):
    return grp_count, 2 * grp_count, 2 * grp_count + blocks, 2 * grp_count + 2 * blocks


def plan_kernel(lists_ref, counts_ref, plan_ref, *, grp_count, blocks):
    group, mine = lax.axis_index("grp"), lax.axis_index("uly")
    per_group = 2 * blocks
    low = group * per_group
    sib_at, source_at, give_at, seen_at = plan_spans(grp_count, blocks)
    for other in range(grp_count):
        place = jnp.int32(-1)
        for at in range(other * per_group, (other + 1) * per_group):
            here = lists_ref[at] - low
            wanted = (here >= 0) & (here < per_group) & (counts_ref[at] > 0)
            place = jnp.where(wanted, here, place)
        own = place - mine * blocks
        sib = place - (1 - mine) * blocks
        plan_ref[other] = jnp.where((own >= 0) & (own < blocks), own, -1)
        plan_ref[sib_at + other] = jnp.where((sib >= 0) & (sib < blocks), sib, -1)
    for block in range(blocks):
        at = low + mine * blocks + block
        plan_ref[source_at + block] = lax.div(lists_ref[at], per_group)
        plan_ref[seen_at + block] = counts_ref[at]
        at = low + (1 - mine) * blocks + block
        plan_ref[give_at + block] = lax.div(lists_ref[at], per_group)


def pack_kernel(k_hbm, v_hbm, kept_ref, given_ref, k_ref, v_ref, sems, *, kv_heads):
    blocks, _, half, _ = kept_ref.shape
    arrays = ((k_hbm, k_ref), (v_hbm, v_ref))
    copies = []
    for block in range(blocks):
        span = pl.ds(block * 2 * half, 2 * half)
        for which, (source, target) in enumerate(arrays):
            sem = sems.at[which, block]
            copies.append(pltpu.make_async_copy(source.at[span], target.at[span], sem))
            copies[-1].start()
    first = lax.axis_index("uly") == 0
    order = head_major(2 * half, kv_heads)
    for block in range(blocks):
        for which, (_, ref) in enumerate(arrays):
            copies[2 * block + which].wait()
            ordered = reorder(order, ref[block * 2 * half:(block + 1) * 2 * half])
            kept_ref[block, which] = jnp.where(first, ordered[:half], ordered[half:])
            given_ref[block, which] = jnp.where(first, ordered[half:], ordered[:half])


def send_own_kernel(plan_ref, blocks_ref, out_ref):
    for group in range(out_ref.shape[0]):
        out_ref[group] = blocks_ref[jnp.maximum(plan_ref[group], 0)]


def send_sibling_kernel(plan_ref, blocks_ref, _, out_ref, *, first):
    for group in range(out_ref.shape[0]):
        place = plan_ref[first + group]

        @pl.when(place >= 0)
        def _():
            out_ref[group] = blocks_ref[place]


def giving_kernel(plan_ref, arrived_ref, *out_refs, give_at):
    block = 0
    for out_ref in out_refs:
        for at in range(out_ref.shape[0]):
            out_ref[at] = arrived_ref[plan_ref[give_at + block]]
            block += 1


def returning_kernel(plan_ref, *refs, source_at):
    part_refs, (out_ref, sems) = refs[:-2], refs[-2:]
    copies = []
    for part_ref in part_refs:
        for at in range(part_ref.shape[0]):
            block = len(copies)
            target = out_ref.at[plan_ref[source_at + block]]
            copies.append(pltpu.make_async_copy(part_ref.at[at], target, sems.at[block]))
            copies[-1].start()
    for copy in copies:
        copy.wait()


def near_kernel(
    q_ref, g_ref, kept_ref, given_ref, stat_ref, *, heads, kv_heads, score_scale
):
    rows = q_ref.shape[0]
    place = kept_ref.shape[2] // kv_heads
    token, lane_head = lanes(rows, heads, kv_heads)
    key = lax.broadcasted_iota(jnp.int32, (2 * place, rows), 0)
    mine = lax.axis_index("uly")
    part = jnp.where(key < place, mine, 1 - mine)
    causal = key % place + part * place <= token
    pieces = []
    for which, ref in enumerate((q_ref, g_ref)):
        both = jnp.concatenate([kept_ref[0, which], given_ref[0, which]], axis=0)
        full = dot_last(both, ref[...])
        half = full.shape[0] // 2
        pieces.append(
            jnp.concatenate(
                [
                    own_head(full[:half], lane_head, kv_heads),
                    own_head(full[half:], lane_head, kv_heads),
                ],
                axis=0,
            )
        )
    scores = jnp.where(causal, pieces[0] * score_scale, HIDDEN)
    highest = jnp.max(scores, axis=0, keepdims=True)
    raised = jnp.exp(scores - highest)
    stat_ref[0, 0:1] = highest
    stat_ref[0, 1:2] = jnp.sum(raised, axis=0, keepdims=True)
    stat_ref[0, 2:3] = jnp.sum(raised * pieces[1], axis=0, keepdims=True)


def far_scores(part_ref, at, q, g, seen, lane_head, kv_heads, score_scale):
    hidden = jnp.where(seen > 0, 0.0, HIDDEN)
    scores = own_head(dot_last(part_ref[at, 0], q), lane_head, kv_heads) * score_scale + hidden
    return scores, own_head(dot_last(part_ref[at, 1], g), lane_head, kv_heads)


def merged(stat_ref, block, scores, dprobs):
    before = stat_ref[block, 0:1]
    highest = jnp.maximum(before, jnp.max(scores, axis=0, keepdims=True))
    raised = jnp.exp(scores - highest)
    shrink = jnp.exp(before - highest)
    total = shrink * stat_ref[block, 1:2] + jnp.sum(raised, axis=0, keepdims=True)
    delta = shrink * stat_ref[block, 2:3] + jnp.sum(raised * dprobs, axis=0, keepdims=True)
    return highest, raised, total, delta


def far_gradients(probs, dprobs, delta, q, g, lane_head, kv_heads, score_scale):
    dscores = (probs * (dprobs - delta)).astype(BF16)
    dk = jnp.dot(all_heads(dscores, lane_head, kv_heads), q, preferred_element_type=F32)
    dv = jnp.dot(all_heads(probs.astype(BF16), lane_head, kv_heads), g, preferred_element_type=F32)
    return (dk * score_scale).astype(BF16), dv.astype(BF16)


def mid_kernel(
    plan_ref, q_ref, g_ref, stat_ref, arrived_ref, out_ref,
    *, heads, kv_heads, score_scale, source_at, seen_at
):
    blocks = stat_ref.shape[0]
    rows = q_ref.shape[0] // blocks
    _, lane_head = lanes(rows, heads, kv_heads)
    for block in range(blocks):
        span = slice(block * rows, (block + 1) * rows)
        scores, dprobs = far_scores(
            arrived_ref, plan_ref[source_at + block], q_ref[span], g_ref[span],
            plan_ref[seen_at + block],            lane_head, kv_heads, score_scale,
        )
        highest, _, total, delta = merged(stat_ref, block, scores, dprobs)
        out_ref[block, 0:1] = highest
        out_ref[block, 1:2] = total
        out_ref[block, 2:3] = delta


def far_kernel(
    plan_ref, q_ref, g_ref, stat_ref, other_ref, grad_ref, out_ref,
    *, heads, kv_heads, score_scale, seen_at, first
):
    rows = q_ref.shape[0] // stat_ref.shape[0]
    _, lane_head = lanes(rows, heads, kv_heads)
    for at in range(other_ref.shape[0]):
        block = first + at
        span = slice(block * rows, (block + 1) * rows)
        q = q_ref[span]
        g = g_ref[span]
        scores, dprobs = far_scores(
            other_ref, at, q, g, plan_ref[seen_at + block], lane_head, kv_heads, score_scale
        )
        highest, raised, total, delta = merged(stat_ref, block, scores, dprobs)
        inverse = 1.0 / total
        delta = delta * inverse
        grad_ref[at, 0], grad_ref[at, 1] = far_gradients(
            raised * inverse, dprobs, delta, q, g, lane_head, kv_heads, score_scale
        )
        out_ref[at, 0:1] = highest
        out_ref[at, 1:2] = inverse
        out_ref[at, 2:3] = delta


def mine_kernel(
    plan_ref, q_ref, g_ref, arrived_ref, stat_ref, grad_ref,
    *, heads, kv_heads, score_scale, source_at, seen_at, rows, first
):
    _, lane_head = lanes(rows, heads, kv_heads)
    for at in range(stat_ref.shape[0]):
        block = first + at
        span = slice(block * rows, (block + 1) * rows)
        q = q_ref[span]
        g = g_ref[span]
        scores, dprobs = far_scores(
            arrived_ref, plan_ref[source_at + block], q, g, plan_ref[seen_at + block],
            lane_head, kv_heads, score_scale,
        )
        probs = jnp.exp(scores - stat_ref[at, 0:1]) * stat_ref[at, 1:2]
        grad_ref[at, 0], grad_ref[at, 1] = far_gradients(
            probs, dprobs, stat_ref[at, 2:3], q, g, lane_head, kv_heads, score_scale
        )


def local_kernel(
    plan_ref, q_ref, g_ref, k_ref, v_ref, mine_ref, other_ref,
    att_ref, dq_ref, dk_ref, dv_ref, bias_ref, *, heads, kv_heads, score_scale, seen_at
):
    step = pl.program_id(0)
    rows = q_ref.shape[0]
    cols = k_ref.shape[0]

    @pl.when(step == 0)
    def _():
        half = cols // 2
        place = half // kv_heads
        row = lax.broadcasted_iota(jnp.int32, (rows, cols), 0)
        col = lax.broadcasted_iota(jnp.int32, (rows, cols), 1)
        same = row % heads // (heads // kv_heads) == col % half // place
        causal = col // half * place + col % place <= row // heads
        bias_ref[:, :cols] = jnp.where(same & causal, 0.0, HIDDEN)
        bias_ref[:, cols:] = jnp.where(same, 0.0, HIDDEN)

    far_bias = jnp.where(plan_ref[seen_at + step] > 0, 0.0, HIDDEN)
    order = head_major(cols, kv_heads)
    k_near = reorder(order, k_ref[...])
    v_near = reorder(order, v_ref[...])
    k_all = jnp.concatenate([k_near, mine_ref[0, 0], other_ref[0, 0]], axis=0)
    v_all = jnp.concatenate([v_near, mine_ref[0, 1], other_ref[0, 1]], axis=0)
    q = q_ref[...]
    g = g_ref[...]
    scores = dot_last(q, k_all) * score_scale + bias_ref[...]
    scores = jnp.concatenate([scores[:, :cols], scores[:, cols:] + far_bias], axis=1)
    highest = jnp.max(scores, axis=1, keepdims=True)
    raised = jnp.exp(scores - highest)
    total = jnp.sum(raised, axis=1, keepdims=True)
    probs = raised * (1.0 / total)
    weights = probs.astype(BF16)
    attended = jnp.dot(weights, v_all, preferred_element_type=F32).astype(BF16)
    att_ref[...] = attended
    delta = jnp.sum(g.astype(F32) * attended.astype(F32), axis=1, keepdims=True)
    dscores = (probs * (dot_last(g, v_all) - delta)).astype(BF16)
    dq = jnp.dot(dscores, k_all, preferred_element_type=F32) * score_scale
    dq_ref[...] = dq.astype(BF16)
    dk_ref[...] = dot_first(dscores[:, :cols], q) * score_scale
    dv_ref[...] = dot_first(weights[:, :cols], g)


def landing_kernel(plan_ref, landed_ref, out_ref, sum_ref, *, first):
    sum_ref[...] = jnp.zeros_like(sum_ref)
    for group in range(landed_ref.shape[0]):
        place = plan_ref[first + group]

        @pl.when(place >= 0)
        def _():
            sum_ref[place] = sum_ref[place] + landed_ref[group].astype(F32)

    out_ref[...] = sum_ref[...].astype(out_ref.dtype)


def own_half_kernel(
    plan_ref, landed_ref, dk_near_ref, dv_near_ref, out_ref, sum_ref, *, kv_heads
):
    sum_ref[...] = jnp.zeros_like(sum_ref)
    for group in range(landed_ref.shape[0]):
        place = plan_ref[group]

        @pl.when(place >= 0)
        def _():
            sum_ref[place] = sum_ref[place] + landed_ref[group].astype(F32)

    blocks, _, half, _ = out_ref.shape
    order = token_major(half, kv_heads)
    mine = lax.axis_index("uly")
    for block in range(blocks):
        span = pl.ds(pl.multiple_of((2 * block + mine) * half, half), half)
        for which, near_ref in enumerate((dk_near_ref, dv_near_ref)):
            summed = (near_ref[span] + sum_ref[block, which]).astype(BF16)
            out_ref[block, which] = reorder(order, summed)


def finish_kernel(
    dk_near_ref, dv_near_ref, own_ref, back_ref, dk_ref, dv_ref, *, kv_heads
):
    blocks, _, half, _ = back_ref.shape
    order = token_major(half, kv_heads)
    mine = lax.axis_index("uly")
    for which, (near_ref, out_ref) in enumerate(((dk_near_ref, dk_ref), (dv_near_ref, dv_ref))):
        for block in range(blocks):
            here = pl.ds(pl.multiple_of((2 * block + mine) * half, half), half)
            there = pl.ds(pl.multiple_of((2 * block + 1 - mine) * half, half), half)
            summed = (near_ref[there] + back_ref[block, which].astype(F32)).astype(BF16)
            out_ref[here] = own_ref[block, which]
            out_ref[there] = reorder(order, summed)


def take_rows(array, index):
    return array.at[index].get(mode="promise_in_bounds")


def whole_blocks(queries, keys, values, output_cotangent, block_lists, list_counts):
    grp_count = lax.axis_size("grp")
    uly_count = lax.axis_size("uly")
    tokens, heads, width = queries.shape
    kv_heads = keys.shape[1]
    per_group = block_lists.shape[0] // grp_count
    block_tok = tokens * uly_count // per_group
    mine_blocks = tokens // block_tok
    rows = block_tok * heads
    cols = block_tok * kv_heads
    half = cols // 2
    sizes = dict(heads=heads, kv_heads=kv_heads, score_scale=width ** (-0.5))
    swap = [(0, 1), (1, 0)]

    sib_at, source_at, give_at, seen_at = plan_spans(grp_count, mine_blocks)

    q2 = queries.reshape(tokens * heads, width)
    g2 = output_cotangent.reshape(tokens * heads, width)
    k2 = keys.reshape(tokens * kv_heads, width)
    v2 = values.reshape(tokens * kv_heads, width)

    part_shape = jax.ShapeDtypeStruct((mine_blocks, 2, half, width), BF16)
    slots = (grp_count, 2, half, width)
    stat_shape = jax.ShapeDtypeStruct((mine_blocks, 8, rows), F32)
    row_shape = jax.ShapeDtypeStruct(q2.shape, BF16)
    near_shape = jax.ShapeDtypeStruct(k2.shape, F32)
    small_shape = jax.ShapeDtypeStruct(k2.shape, BF16)
    sum_scratch = [pltpu.VMEM((mine_blocks, 2, half, width), F32)]
    limit = pltpu.CompilerParams(vmem_limit_bytes=24 * 1024 * 1024)
    vmem = pl.BlockSpec(memory_space=pltpu.VMEM)
    smem = pl.BlockSpec(memory_space=pltpu.SMEM)
    anywhere = pl.BlockSpec(memory_space=pltpu.HBM)

    def call(kernel, name, scalars, operands, out_shape, scratch=(), into=None, out_spec=vmem):
        extra = () if into is None else (into,)
        return pl.pallas_call(
            kernel,
            in_specs=[smem] * len(scalars) + [vmem] * (len(operands) + len(extra)),
            out_specs=jax.tree.map(lambda _: out_spec, out_shape),
            out_shape=out_shape,
            scratch_shapes=scratch,
            input_output_aliases={len(scalars) + len(operands): 0} if extra else {},
            compiler_params=limit,
            name=name,
        )(*scalars, *operands, *extra)

    def step_rows(i, *_):
        return (i, 0)

    def step_part(i, *_):
        return (i, 0, 0, 0)

    def in_hbm(array):
        return pltpu.with_memory_space_constraint(array, pltpu.HBM)

    kept, given = pl.pallas_call(
        partial(pack_kernel, kv_heads=kv_heads),
        in_specs=[anywhere, anywhere],
        out_specs=[vmem, vmem],
        out_shape=[part_shape, part_shape],
        scratch_shapes=[
            pltpu.VMEM(k2.shape, BF16), pltpu.VMEM(k2.shape, BF16),
            pltpu.SemaphoreType.DMA((2, mine_blocks)),
        ],
        compiler_params=limit,
        name="pack",
    )(in_hbm(k2), in_hbm(v2))
    plan = pl.pallas_call(
        partial(plan_kernel, grp_count=grp_count, blocks=mine_blocks),
        in_specs=[smem, smem],
        out_specs=smem,
        out_shape=pltpu.SMEM((seen_at + mine_blocks,), jnp.int32),
        compiler_params=limit,
        name="plan",
    )(in_hbm(block_lists.reshape(-1)), in_hbm(list_counts))
    gotten = lax.ppermute(given, "uly", swap)
    row_spec = pl.BlockSpec((rows, width), step_rows)
    part_spec = pl.BlockSpec((1, 2, half, width), step_part)
    stats = pl.pallas_call(
        partial(near_kernel, **sizes),
        grid=(mine_blocks,),
        in_specs=[row_spec, row_spec, part_spec, part_spec],
        out_specs=pl.BlockSpec((1, 8, rows), lambda i: (i, 0, 0)),
        out_shape=stat_shape,
        compiler_params=limit,
        name="near",
    )(in_hbm(q2), in_hbm(g2), kept, given)
    outgoing = call(
        send_own_kernel, "send_own", (plan,), (kept,),
        jax.ShapeDtypeStruct(slots, BF16),
    )
    gotten, stats = lax.optimization_barrier((gotten, stats))
    outgoing = call(
        partial(send_sibling_kernel, first=sib_at), "send_sibling", (plan,), (gotten,),
        jax.ShapeDtypeStruct(slots, BF16), into=outgoing,
    )
    arrived = lax.all_to_all(outgoing, "grp", split_axis=0, concat_axis=0, tiled=True)
    chunks = 2 if mine_blocks % 2 == 0 else 1
    chunk = mine_blocks // chunks
    chunk_shape = jax.ShapeDtypeStruct((chunk, 2, half, width), BF16)
    giving = call(
        partial(giving_kernel, give_at=give_at), "give", (plan,), (arrived,),
        [chunk_shape] * chunks,
    )
    stats = call(
        partial(mid_kernel, source_at=source_at, seen_at=seen_at, **sizes), "mid", (plan,),
        (q2, g2, stats, arrived), stat_shape,
    )
    others = []
    for part in giving:
        if others:
            part, stats = lax.optimization_barrier((part, stats))
        others.append(lax.ppermute(part, "uly", swap))
    grads, final = [], []
    for at, other in enumerate(others):
        grad, stat = call(
            partial(far_kernel, seen_at=seen_at, first=at * chunk, **sizes), "far", (plan,),
            (q2, g2, stats, other),
            [chunk_shape, jax.ShapeDtypeStruct((chunk, 8, rows), F32)],
        )
        grads.append(grad)
        final.append(stat)
    from_sib = [lax.ppermute(part, "uly", swap) for part in grads]
    mine = [None] * chunks
    for at in reversed(range(chunks)):
        if at + 1 < chunks:
            from_sib[at], final[at] = lax.optimization_barrier((from_sib[at], final[at]))
        mine[at] = call(
            partial(
                mine_kernel, source_at=source_at, seen_at=seen_at, rows=rows, first=at * chunk,
                **sizes,
            ),
            "mine", (plan,), (q2, g2, arrived, final[at]), chunk_shape,
        )
    returning = call(
        partial(returning_kernel, source_at=source_at), "return", (plan,), mine + from_sib,
        pltpu.HBM(slots, BF16), [pltpu.SemaphoreType.DMA((per_group,))], out_spec=anywhere,
    )
    other = jnp.concatenate(others)
    returning, k2l = lax.optimization_barrier((returning, k2))
    landed = lax.all_to_all(returning, "grp", split_axis=0, concat_axis=0, tiled=True)

    def from_source(i, plan_ref):
        return (plan_ref[source_at + i], 0, 0, 0)

    col_spec = pl.BlockSpec((cols, width), step_rows)
    attended, dq, dk_near, dv_near = pl.pallas_call(
        partial(local_kernel, seen_at=seen_at, **sizes),
        grid_spec=pltpu.PrefetchScalarGridSpec(
            num_scalar_prefetch=1,
            grid=(mine_blocks,),
            in_specs=[
                row_spec, row_spec, col_spec, col_spec,
                pl.BlockSpec((1, 2, half, width), from_source),
                part_spec,
            ],
            out_specs=[row_spec, row_spec, col_spec, col_spec],
            scratch_shapes=[pltpu.VMEM((rows, 2 * cols), F32)],
        ),
        out_shape=[row_shape, row_shape, near_shape, near_shape],
        compiler_params=limit,
        name="local",
    )(plan, q2, g2, k2l, v2, arrived, other)
    landed, dk_near = lax.optimization_barrier((landed, dk_near))
    give = call(
        partial(landing_kernel, first=sib_at), "land_sibling", (plan,), (landed,), part_shape,
        sum_scratch,
    )
    back = lax.ppermute(give, "uly", swap)
    own = call(
        partial(own_half_kernel, kv_heads=kv_heads), "land_own", (plan,),
        (landed, dk_near, dv_near), part_shape, sum_scratch,
    )
    dk, dv = call(
        partial(finish_kernel, kv_heads=kv_heads), "finish", (),
        (dk_near, dv_near, own, back), [small_shape, small_shape],
    )
    return (
        attended.reshape(queries.shape), dq.reshape(queries.shape),
        dk.reshape(keys.shape), dv.reshape(keys.shape),
    )


def on_device(queries, keys, values, output_cotangent, block_lists, list_counts):
    uly_count = lax.axis_size("uly")
    grp_count = lax.axis_size("grp")
    blocks_all, remote = block_lists.shape
    block_tok = queries.shape[0] * uly_count * grp_count // blocks_all
    held_whole = queries.shape[0] % block_tok == 0
    run = whole_blocks if held_whole and remote == 1 and uly_count == 2 else spread_blocks
    return run(queries, keys, values, output_cotangent, block_lists, list_counts)


def solution(mesh):
    placed = (
        P(("grp", "uly"), None, None),
        P(("grp", "uly"), None, None),
        P(("grp", "uly"), None, None),
        P(("grp", "uly"), None, None),
        P(),
        P(),
    )
    return jax.shard_map(
        on_device,
        mesh=mesh,
        in_specs=placed,
        out_specs=(
            P(("grp", "uly"), None, None),
            P(("grp", "uly"), None, None),
            P(("grp", "uly"), None, None),
            P(("grp", "uly"), None, None),
        ),
        check_vma=False,
    )
```

```python
from functools import partial

import jax
import jax.numpy as jnp
from jax import lax
from jax.experimental import pallas as pl
from jax.experimental.pallas import tpu as pltpu
from jax.sharding import PartitionSpec as P


def spread_blocks(queries, keys, values, output_cotangent, block_lists, list_counts):
    uly_count = lax.axis_size("uly")
    grp_count = lax.axis_size("grp")
    my_group = lax.axis_index("grp")
    tokens, head_count, head_width = queries.shape
    kv_heads = keys.shape[1]
    copies = max(1, uly_count // kv_heads)
    blocks_all, remote = block_lists.shape
    per_group = blocks_all // grp_count
    block_tok = tokens * uly_count // per_group
    group_tok = tokens * uly_count
    score_scale = head_width ** (-0.5)
    lists = block_lists.reshape(grp_count, per_group, remote)
    counted = (jnp.arange(remote)[None, :] < list_counts[:, None]).reshape(
        grp_count, per_group, remote
    )
    wanted = (lists // per_group == my_group) & counted
    send_place = jnp.sum(jnp.where(wanted, lists % per_group, 0), axis=(1, 2))
    sending = jnp.any(wanted, axis=(1, 2))
    mine_source = lax.dynamic_index_in_dim(lists, my_group, 0, keepdims=False) // per_group
    mine_counted = lax.dynamic_index_in_dim(counted, my_group, 0, keepdims=False)
    trip_count = jnp.max(jnp.sum(mine_counted.astype(jnp.int32), axis=1))

    def to_blocks(array_in):
        return array_in.reshape((per_group, block_tok) + array_in.shape[1:])

    keys_wide = jnp.repeat(keys, copies, axis=1)
    values_wide = jnp.repeat(values, copies, axis=1)
    query_heads, grad_heads, key_heads, value_heads = (
        lax.all_to_all(queries, "uly", split_axis=1, concat_axis=0, tiled=True),
        lax.all_to_all(output_cotangent, "uly", split_axis=1, concat_axis=0, tiled=True),
        lax.all_to_all(keys_wide, "uly", split_axis=1, concat_axis=0, tiled=True),
        lax.all_to_all(values_wide, "uly", split_axis=1, concat_axis=0, tiled=True),
    )
    stacked = jnp.stack([to_blocks(key_heads), to_blocks(value_heads)])
    outgoing = jnp.take(stacked, send_place, axis=1)
    arrived = lax.all_to_all(outgoing, "grp", split_axis=1, concat_axis=1, tiled=True)
    kv_local = key_heads.shape[1]
    heads_local = query_heads.shape[1]
    heads_per_group = heads_local // kv_local
    query_blk = query_heads.reshape(per_group, block_tok, kv_local, heads_per_group, head_width)
    grad_blk = grad_heads.reshape(per_group, block_tok, kv_local, heads_per_group, head_width)
    key_blk = to_blocks(key_heads)
    value_blk = to_blocks(value_heads)
    far_keys = arrived[0]
    far_values = arrived[1]
    causal = jnp.arange(block_tok)[:, None] >= jnp.arange(block_tok)[None, :]

    def logits(key_rows):
        return (
            jnp.einsum("pqkgd,pjkd->pkgqj", query_blk, key_rows, preferred_element_type=jnp.float32)
            * score_scale
        )

    def slot_rows(slot_index):
        source = lax.dynamic_index_in_dim(mine_source, slot_index, 1, keepdims=False)
        counted_slot = lax.dynamic_index_in_dim(mine_counted, slot_index, 1, keepdims=False)
        return (
            jnp.take(far_keys, source, axis=0),
            jnp.take(far_values, source, axis=0),
            counted_slot,
            source,
        )

    def masked(scores, counted_slot):
        return jnp.where(counted_slot[:, None, None, None, None], scores, -jnp.inf)

    near_scores = jnp.where(causal, logits(key_blk), -jnp.inf)
    highest = jnp.max(near_scores, axis=-1)
    denominator = jnp.sum(jnp.exp(near_scores - highest[..., None]), axis=-1)

    def max_sweep(slot_index, state_pair):
        highest, denominator = state_pair
        key_rows, value_rows, counted_slot, source = slot_rows(slot_index)
        scores = masked(logits(key_rows), counted_slot)
        new_highest = jnp.maximum(highest, jnp.max(scores, axis=-1))
        denominator = denominator * jnp.exp(highest - new_highest) + jnp.sum(
            jnp.exp(scores - new_highest[..., None]), axis=-1
        )
        return (new_highest, denominator)

    highest, denominator = lax.fori_loop(0, trip_count, max_sweep, (highest, denominator))
    log_total = highest + jnp.log(denominator)

    def softmax_weights(scores):
        return jnp.exp(scores - log_total[..., None])

    summed = jnp.einsum(
        "pkgqj,pjkd->pqkgd",
        softmax_weights(near_scores).astype(jnp.bfloat16),
        value_blk,
        preferred_element_type=jnp.float32,
    )

    def value_sweep(slot_index, summed):
        key_rows, value_rows, counted_slot, source = slot_rows(slot_index)
        weights = softmax_weights(masked(logits(key_rows), counted_slot)).astype(jnp.bfloat16)
        return summed + jnp.einsum(
            "pkgqj,pjkd->pqkgd", weights, value_rows, preferred_element_type=jnp.float32
        )

    summed = lax.fori_loop(0, trip_count, value_sweep, summed)
    attended_blk = summed.astype(jnp.bfloat16)
    row_delta = jnp.transpose(
        jnp.sum(grad_blk.astype(jnp.float32) * attended_blk.astype(jnp.float32), axis=-1),
        (0, 2, 3, 1),
    )

    def backward(scores, key_rows, value_rows):
        probs = softmax_weights(scores)
        weights = probs.astype(jnp.bfloat16)
        dprobs = jnp.einsum(
            "pqkgd,pjkd->pkgqj", grad_blk, value_rows, preferred_element_type=jnp.float32
        )
        dscores = (probs * (dprobs - row_delta[..., None])).astype(jnp.bfloat16)
        query_term = jnp.einsum(
            "pkgqj,pjkd->pqkgd", dscores, key_rows, preferred_element_type=jnp.float32
        )
        key_term = (
            jnp.einsum("pkgqj,pqkgd->pjkd", dscores, query_blk, preferred_element_type=jnp.float32)
            * score_scale
        )
        value_term = jnp.einsum(
            "pkgqj,pqkgd->pjkd", weights, grad_blk, preferred_element_type=jnp.float32
        )
        return (query_term, key_term, value_term)

    query_sum, key_near, value_near = backward(near_scores, key_blk, value_blk)
    far_grads = jnp.zeros((2, grp_count, block_tok, kv_local, head_width), jnp.float32)

    def grad_sweep(slot_index, state_pair):
        query_sum, far_grads = state_pair
        key_rows, value_rows, counted_slot, source = slot_rows(slot_index)
        query_term, key_term, value_term = backward(
            masked(logits(key_rows), counted_slot), key_rows, value_rows
        )
        routing = (
            (source[:, None] == jnp.arange(grp_count)[None, :]) & counted_slot[:, None]
        ).astype(jnp.float32)
        routed = jnp.einsum(
            "ps,xpjkd->xsjkd",
            routing,
            jnp.stack([key_term, value_term]),
            precision=lax.Precision.HIGHEST,
        )
        return (query_sum + query_term, far_grads + routed)

    query_sum, far_grads = lax.fori_loop(0, trip_count, grad_sweep, (query_sum, far_grads))
    owners = ((send_place[:, None] == jnp.arange(per_group)[None, :]) & sending[:, None]).astype(
        jnp.float32
    )
    returned = lax.all_to_all(far_grads, "grp", split_axis=1, concat_axis=1, tiled=True)
    landed = jnp.einsum("sp,xsjkd->xpjkd", owners, returned, precision=lax.Precision.HIGHEST)
    key_local = (key_near + landed[0]).reshape(group_tok, kv_local, head_width)
    value_local = (value_near + landed[1]).reshape(group_tok, kv_local, head_width)
    attended_rows = attended_blk.reshape(group_tok, heads_local, head_width)
    query_rows = (
        (query_sum * score_scale).astype(jnp.bfloat16).reshape(group_tok, heads_local, head_width)
    )
    attended, query_grad = (
        lax.all_to_all(attended_rows, "uly", split_axis=0, concat_axis=1, tiled=True),
        lax.all_to_all(query_rows, "uly", split_axis=0, concat_axis=1, tiled=True),
    )
    key_parts, value_parts = (
        lax.all_to_all(key_local, "uly", split_axis=0, concat_axis=1, tiled=True),
        lax.all_to_all(value_local, "uly", split_axis=0, concat_axis=1, tiled=True),
    )
    key_gradient = jnp.sum(key_parts.reshape(tokens, kv_heads, copies, head_width), axis=2).astype(
        jnp.bfloat16
    )
    value_gradient = jnp.sum(
        value_parts.reshape(tokens, kv_heads, copies, head_width), axis=2
    ).astype(jnp.bfloat16)
    return (attended, query_grad, key_gradient, value_gradient)


HIDDEN = -1e30
LAST = (((1,), (1,)), ((), ()))
FIRST = (((0,), (0,)), ((), ()))
F32 = jnp.float32
BF16 = jnp.bfloat16


def dot_last(left, right):
    return lax.dot_general(left, right, LAST, preferred_element_type=F32)


def dot_first(left, right):
    return lax.dot_general(left, right, FIRST, preferred_element_type=F32)


def head_major(cols, kv_heads):
    half = cols // 2
    place = half // kv_heads
    row = lax.broadcasted_iota(jnp.int32, (cols, cols), 0)
    col = lax.broadcasted_iota(jnp.int32, (cols, cols), 1)
    token = row // half * place + row % place
    return jnp.where(col == token * kv_heads + row % half // place, 1.0, 0.0).astype(BF16)


def half_order(cols, kv_heads, which):
    half = cols // 2
    place = half // kv_heads
    row = lax.broadcasted_iota(jnp.int32, (half, cols), 0)
    col = lax.broadcasted_iota(jnp.int32, (half, cols), 1)
    token = which * place + row % place
    return jnp.where(col == token * kv_heads + row // place, 1.0, 0.0).astype(BF16)


def token_major(half, kv_heads):
    place = half // kv_heads
    row = lax.broadcasted_iota(jnp.int32, (half, half), 0)
    col = lax.broadcasted_iota(jnp.int32, (half, half), 1)
    return jnp.where(col == row % kv_heads * place + row // kv_heads, 1.0, 0.0).astype(BF16)


def reorder(one_hot, array):
    return jnp.dot(one_hot, array, preferred_element_type=F32).astype(BF16)


def own_head(scores, lane_head, kv_heads):
    place = scores.shape[0] // kv_heads
    kept = scores[:place]
    for head in range(1, kv_heads):
        kept = jnp.where(lane_head == head, scores[head * place:(head + 1) * place], kept)
    return kept


def all_heads(kept, lane_head, kv_heads):
    none = jnp.zeros_like(kept)
    return jnp.concatenate(
        [jnp.where(lane_head == head, kept, none) for head in range(kv_heads)], axis=0
    )


def lanes(rows, heads, kv_heads):
    lane = lax.broadcasted_iota(jnp.int32, (1, rows), 1)
    return lane // heads, lane % heads // (heads // kv_heads)


def plan_spans(grp_count, blocks):
    return grp_count, 2 * grp_count, 2 * grp_count + blocks, 2 * grp_count + 2 * blocks


def fill_plan(lists_ref, counts_ref, plan_ref, grp_count, blocks):
    group, mine = lax.axis_index("grp"), lax.axis_index("uly")
    per_group = 2 * blocks
    low = group * per_group
    sib_at, source_at, give_at, seen_at = plan_spans(grp_count, blocks)
    for other in range(grp_count):
        place = jnp.int32(-1)
        for at in range(other * per_group, (other + 1) * per_group):
            here = lists_ref[at] - low
            wanted = (here >= 0) & (here < per_group) & (counts_ref[at] > 0)
            place = jnp.where(wanted, here, place)
        own = place - mine * blocks
        sib = place - (1 - mine) * blocks
        plan_ref[other] = jnp.where((own >= 0) & (own < blocks), own, -1)
        plan_ref[sib_at + other] = jnp.where((sib >= 0) & (sib < blocks), sib, -1)
    for block in range(blocks):
        at = low + mine * blocks + block
        plan_ref[source_at + block] = lax.div(lists_ref[at], per_group)
        plan_ref[seen_at + block] = counts_ref[at]
        at = low + (1 - mine) * blocks + block
        plan_ref[give_at + block] = lax.div(lists_ref[at], per_group)


def pack_kernel(k_hbm, v_hbm, k_ref, v_ref, given_ref, sems, *, kv_heads):
    blocks, _, half, _ = given_ref.shape
    copies = [
        pltpu.make_async_copy(k_hbm, k_ref, sems.at[0]),
        pltpu.make_async_copy(v_hbm, v_ref, sems.at[1]),
    ]
    for copy in copies:
        copy.start()
    order = half_order(2 * half, kv_heads, 1 - lax.axis_index("uly"))
    for which, ref in enumerate((k_ref, v_ref)):
        copies[which].wait()
        for block in range(blocks):
            given_ref[block, which] = reorder(order, ref[block * 2 * half:(block + 1) * 2 * half])


def send_own_kernel(plan_ref, blocks_ref, out_ref):
    for group in range(out_ref.shape[0]):
        out_ref[group] = blocks_ref[jnp.maximum(plan_ref[group], 0)]


def send_sibling_kernel(plan_ref, blocks_ref, _, out_ref, *, first):
    for group in range(out_ref.shape[0]):
        place = plan_ref[first + group]

        @pl.when(place >= 0)
        def _():
            out_ref[group] = blocks_ref[place]


def giving_kernel(plan_ref, arrived_ref, *out_refs, give_at):
    block = 0
    for out_ref in out_refs:
        for at in range(out_ref.shape[0]):
            out_ref[at] = arrived_ref[plan_ref[give_at + block]]
            block += 1


def returning_kernel(plan_ref, *refs, source_at):
    part_refs, (out_ref, sems) = refs[:-2], refs[-2:]
    copies = []
    for part_ref in part_refs:
        for at in range(part_ref.shape[0]):
            block = len(copies)
            target = out_ref.at[plan_ref[source_at + block]]
            copies.append(pltpu.make_async_copy(part_ref.at[at], target, sems.at[block]))
            copies[-1].start()
    for copy in copies:
        copy.wait()


def near_kernel(
    lists_ref, counts_ref, q_hbm, g_hbm, k_ref, v_ref, given_ref,
    plan_ref, stat_ref, kept_ref, q_ref, g_ref, sems, *, heads, kv_heads, score_scale, grp_count
):
    blocks = stat_ref.shape[0]
    rows = q_ref.shape[0] // blocks
    half = given_ref.shape[2]
    place = half // kv_heads
    copies = [
        pltpu.make_async_copy(q_hbm, q_ref, sems.at[0]),
        pltpu.make_async_copy(g_hbm, g_ref, sems.at[1]),
    ]
    for copy in copies:
        copy.start()
    fill_plan(lists_ref, counts_ref, plan_ref, grp_count, blocks)
    mine = lax.axis_index("uly")
    order = half_order(2 * half, kv_heads, mine)
    for block in range(blocks):
        narrow = slice(block * 2 * half, (block + 1) * 2 * half)
        kept_ref[block, 0] = reorder(order, k_ref[narrow])
        kept_ref[block, 1] = reorder(order, v_ref[narrow])
    token, lane_head = lanes(rows, heads, kv_heads)
    key = lax.broadcasted_iota(jnp.int32, (2 * place, rows), 0)
    part = jnp.where(key < place, mine, 1 - mine)
    causal = key % place + part * place <= token
    for block in range(blocks):
        span = slice(block * rows, (block + 1) * rows)
        pieces = []
        for which, ref in enumerate((q_ref, g_ref)):
            if block == 0:
                copies[which].wait()
            both = jnp.concatenate([kept_ref[block, which], given_ref[block, which]], axis=0)
            full = dot_last(both, ref[span])
            pieces.append(
                jnp.concatenate(
                    [
                        own_head(full[:half], lane_head, kv_heads),
                        own_head(full[half:], lane_head, kv_heads),
                    ],
                    axis=0,
                )
            )
        scores = jnp.where(causal, pieces[0] * score_scale, HIDDEN)
        highest = jnp.max(scores, axis=0, keepdims=True)
        raised = jnp.exp(scores - highest)
        stat_ref[block, 0:1] = highest
        stat_ref[block, 1:2] = jnp.sum(raised, axis=0, keepdims=True)
        stat_ref[block, 2:3] = jnp.sum(raised * pieces[1], axis=0, keepdims=True)


def far_scores(part_ref, at, q, g, seen, lane_head, kv_heads, score_scale):
    hidden = jnp.where(seen > 0, 0.0, HIDDEN)
    scores = own_head(dot_last(part_ref[at, 0], q), lane_head, kv_heads) * score_scale + hidden
    return scores, own_head(dot_last(part_ref[at, 1], g), lane_head, kv_heads)


def merged(stat_ref, block, scores, dprobs):
    before = stat_ref[block, 0:1]
    highest = jnp.maximum(before, jnp.max(scores, axis=0, keepdims=True))
    raised = jnp.exp(scores - highest)
    shrink = jnp.exp(before - highest)
    total = shrink * stat_ref[block, 1:2] + jnp.sum(raised, axis=0, keepdims=True)
    delta = shrink * stat_ref[block, 2:3] + jnp.sum(raised * dprobs, axis=0, keepdims=True)
    return highest, raised, total, delta


def far_gradients(probs, dprobs, delta, q, g, lane_head, kv_heads, score_scale):
    dscores = (probs * (dprobs - delta)).astype(BF16)
    dk = jnp.dot(all_heads(dscores, lane_head, kv_heads), q, preferred_element_type=F32)
    dv = jnp.dot(all_heads(probs.astype(BF16), lane_head, kv_heads), g, preferred_element_type=F32)
    return (dk * score_scale).astype(BF16), dv.astype(BF16)


def mid_kernel(
    plan_ref, q_ref, g_ref, stat_ref, arrived_ref, out_ref,
    *, heads, kv_heads, score_scale, source_at, seen_at
):
    blocks = stat_ref.shape[0]
    rows = q_ref.shape[0] // blocks
    _, lane_head = lanes(rows, heads, kv_heads)
    for block in range(blocks):
        span = slice(block * rows, (block + 1) * rows)
        scores, dprobs = far_scores(
            arrived_ref, plan_ref[source_at + block], q_ref[span], g_ref[span],
            plan_ref[seen_at + block],            lane_head, kv_heads, score_scale,
        )
        highest, _, total, delta = merged(stat_ref, block, scores, dprobs)
        out_ref[block, 0:1] = highest
        out_ref[block, 1:2] = total
        out_ref[block, 2:3] = delta


def far_kernel(
    plan_ref, q_ref, g_ref, stat_ref, other_ref, grad_ref, out_ref,
    *, heads, kv_heads, score_scale, seen_at, first
):
    rows = q_ref.shape[0] // stat_ref.shape[0]
    _, lane_head = lanes(rows, heads, kv_heads)
    for at in range(other_ref.shape[0]):
        block = first + at
        span = slice(block * rows, (block + 1) * rows)
        q = q_ref[span]
        g = g_ref[span]
        scores, dprobs = far_scores(
            other_ref, at, q, g, plan_ref[seen_at + block], lane_head, kv_heads, score_scale
        )
        highest, raised, total, delta = merged(stat_ref, block, scores, dprobs)
        inverse = 1.0 / total
        delta = delta * inverse
        grad_ref[at, 0], grad_ref[at, 1] = far_gradients(
            raised * inverse, dprobs, delta, q, g, lane_head, kv_heads, score_scale
        )
        out_ref[at, 0:1] = highest
        out_ref[at, 1:2] = inverse
        out_ref[at, 2:3] = delta


def mine_kernel(
    plan_ref, q_ref, g_ref, arrived_ref, stat_ref, grad_ref,
    *, heads, kv_heads, score_scale, source_at, seen_at, rows, first
):
    _, lane_head = lanes(rows, heads, kv_heads)
    for at in range(stat_ref.shape[0]):
        block = first + at
        span = slice(block * rows, (block + 1) * rows)
        q = q_ref[span]
        g = g_ref[span]
        scores, dprobs = far_scores(
            arrived_ref, plan_ref[source_at + block], q, g, plan_ref[seen_at + block],
            lane_head, kv_heads, score_scale,
        )
        probs = jnp.exp(scores - stat_ref[at, 0:1]) * stat_ref[at, 1:2]
        grad_ref[at, 0], grad_ref[at, 1] = far_gradients(
            probs, dprobs, stat_ref[at, 2:3], q, g, lane_head, kv_heads, score_scale
        )


def local_kernel(
    plan_ref, q_ref, g_ref, k_ref, v_ref, mine_ref, other_ref,
    att_ref, dq_ref, dk_ref, dv_ref, bias_ref, *, heads, kv_heads, score_scale, seen_at
):
    step = pl.program_id(0)
    rows = q_ref.shape[0]
    cols = k_ref.shape[0]

    @pl.when(step == 0)
    def _():
        half = cols // 2
        place = half // kv_heads
        row = lax.broadcasted_iota(jnp.int32, (rows, cols), 0)
        col = lax.broadcasted_iota(jnp.int32, (rows, cols), 1)
        same = row % heads // (heads // kv_heads) == col % half // place
        causal = col // half * place + col % place <= row // heads
        bias_ref[:, :cols] = jnp.where(same & causal, 0.0, HIDDEN)
        bias_ref[:, cols:] = jnp.where(same, 0.0, HIDDEN)

    far_bias = jnp.where(plan_ref[seen_at + step] > 0, 0.0, HIDDEN)
    order = head_major(cols, kv_heads)
    k_near = reorder(order, k_ref[...])
    v_near = reorder(order, v_ref[...])
    k_all = jnp.concatenate([k_near, mine_ref[0, 0], other_ref[0, 0]], axis=0)
    v_all = jnp.concatenate([v_near, mine_ref[0, 1], other_ref[0, 1]], axis=0)
    q = q_ref[...]
    g = g_ref[...]
    scores = dot_last(q, k_all) * score_scale + bias_ref[...]
    scores = jnp.concatenate([scores[:, :cols], scores[:, cols:] + far_bias], axis=1)
    highest = jnp.max(scores, axis=1, keepdims=True)
    raised = jnp.exp(scores - highest)
    total = jnp.sum(raised, axis=1, keepdims=True)
    probs = raised * (1.0 / total)
    weights = probs.astype(BF16)
    attended = jnp.dot(weights, v_all, preferred_element_type=F32).astype(BF16)
    att_ref[...] = attended
    delta = jnp.sum(g.astype(F32) * attended.astype(F32), axis=1, keepdims=True)
    dscores = (probs * (dot_last(g, v_all) - delta)).astype(BF16)
    dq = jnp.dot(dscores, k_all, preferred_element_type=F32) * score_scale
    dq_ref[...] = dq.astype(BF16)
    dk_ref[...] = dot_first(dscores[:, :cols], q) * score_scale
    dv_ref[...] = dot_first(weights[:, :cols], g)


def landing_kernel(plan_ref, landed_ref, out_ref, sum_ref, *, first):
    sum_ref[...] = jnp.zeros_like(sum_ref)
    for group in range(landed_ref.shape[0]):
        place = plan_ref[first + group]

        @pl.when(place >= 0)
        def _():
            sum_ref[place] = sum_ref[place] + landed_ref[group].astype(F32)

    out_ref[...] = sum_ref[...].astype(out_ref.dtype)


def own_half_kernel(
    plan_ref, landed_ref, dk_near_ref, dv_near_ref, out_ref, sum_ref, *, kv_heads
):
    sum_ref[...] = jnp.zeros_like(sum_ref)
    for group in range(landed_ref.shape[0]):
        place = plan_ref[group]

        @pl.when(place >= 0)
        def _():
            sum_ref[place] = sum_ref[place] + landed_ref[group].astype(F32)

    blocks, _, half, _ = out_ref.shape
    order = token_major(half, kv_heads)
    mine = lax.axis_index("uly")
    for block in range(blocks):
        span = pl.ds(pl.multiple_of((2 * block + mine) * half, half), half)
        for which, near_ref in enumerate((dk_near_ref, dv_near_ref)):
            summed = (near_ref[span] + sum_ref[block, which]).astype(BF16)
            out_ref[block, which] = reorder(order, summed)


def finish_kernel(
    dk_near_ref, dv_near_ref, own_ref, back_ref, dk_ref, dv_ref, *, kv_heads
):
    blocks, _, half, _ = back_ref.shape
    order = token_major(half, kv_heads)
    mine = lax.axis_index("uly")
    for which, (near_ref, out_ref) in enumerate(((dk_near_ref, dk_ref), (dv_near_ref, dv_ref))):
        for block in range(blocks):
            here = pl.ds(pl.multiple_of((2 * block + mine) * half, half), half)
            there = pl.ds(pl.multiple_of((2 * block + 1 - mine) * half, half), half)
            summed = (near_ref[there] + back_ref[block, which].astype(F32)).astype(BF16)
            out_ref[here] = own_ref[block, which]
            out_ref[there] = reorder(order, summed)


def take_rows(array, index):
    return array.at[index].get(mode="promise_in_bounds")


def whole_blocks(queries, keys, values, output_cotangent, block_lists, list_counts):
    grp_count = lax.axis_size("grp")
    uly_count = lax.axis_size("uly")
    tokens, heads, width = queries.shape
    kv_heads = keys.shape[1]
    per_group = block_lists.shape[0] // grp_count
    block_tok = tokens * uly_count // per_group
    mine_blocks = tokens // block_tok
    rows = block_tok * heads
    cols = block_tok * kv_heads
    half = cols // 2
    sizes = dict(heads=heads, kv_heads=kv_heads, score_scale=width ** (-0.5))
    swap = [(0, 1), (1, 0)]

    sib_at, source_at, give_at, seen_at = plan_spans(grp_count, mine_blocks)

    q2 = queries.reshape(tokens * heads, width)
    g2 = output_cotangent.reshape(tokens * heads, width)
    k2 = keys.reshape(tokens * kv_heads, width)
    v2 = values.reshape(tokens * kv_heads, width)

    part_shape = jax.ShapeDtypeStruct((mine_blocks, 2, half, width), BF16)
    slots = (grp_count, 2, half, width)
    stat_shape = jax.ShapeDtypeStruct((mine_blocks, 8, rows), F32)
    row_shape = jax.ShapeDtypeStruct(q2.shape, BF16)
    near_shape = jax.ShapeDtypeStruct(k2.shape, F32)
    small_shape = jax.ShapeDtypeStruct(k2.shape, BF16)
    sum_scratch = [pltpu.VMEM((mine_blocks, 2, half, width), F32)]
    limit = pltpu.CompilerParams(vmem_limit_bytes=24 * 1024 * 1024)
    vmem = pl.BlockSpec(memory_space=pltpu.VMEM)
    smem = pl.BlockSpec(memory_space=pltpu.SMEM)
    anywhere = pl.BlockSpec(memory_space=pltpu.HBM)

    def call(kernel, name, scalars, operands, out_shape, scratch=(), into=None, out_spec=vmem):
        extra = () if into is None else (into,)
        return pl.pallas_call(
            kernel,
            in_specs=[smem] * len(scalars) + [vmem] * (len(operands) + len(extra)),
            out_specs=jax.tree.map(lambda _: out_spec, out_shape),
            out_shape=out_shape,
            scratch_shapes=scratch,
            input_output_aliases={len(scalars) + len(operands): 0} if extra else {},
            compiler_params=limit,
            name=name,
        )(*scalars, *operands, *extra)

    def step_rows(i, *_):
        return (i, 0)

    def step_part(i, *_):
        return (i, 0, 0, 0)

    def in_hbm(array):
        return pltpu.with_memory_space_constraint(array, pltpu.HBM)

    k_here, v_here, given = pl.pallas_call(
        partial(pack_kernel, kv_heads=kv_heads),
        in_specs=[anywhere, anywhere],
        out_specs=[vmem, vmem, vmem],
        out_shape=[small_shape, small_shape, part_shape],
        scratch_shapes=[pltpu.SemaphoreType.DMA((2,))],
        compiler_params=limit,
        name="pack",
    )(in_hbm(k2), in_hbm(v2))
    gotten = lax.ppermute(given, "uly", swap)
    row_spec = pl.BlockSpec((rows, width), step_rows)
    part_spec = pl.BlockSpec((1, 2, half, width), step_part)
    plan, stats, kept, q2, g2 = pl.pallas_call(
        partial(near_kernel, grp_count=grp_count, **sizes),
        in_specs=[smem, smem, anywhere, anywhere, vmem, vmem, vmem],
        out_specs=[smem, vmem, vmem, vmem, vmem],
        out_shape=[
            pltpu.SMEM((seen_at + mine_blocks,), jnp.int32), stat_shape, part_shape,
            pltpu.VMEM(q2.shape, BF16), pltpu.VMEM(q2.shape, BF16),
        ],
        scratch_shapes=[pltpu.SemaphoreType.DMA((2,))],
        compiler_params=limit,
        name="near",
    )(
        in_hbm(block_lists.reshape(-1)), in_hbm(list_counts), in_hbm(q2), in_hbm(g2),
        k_here, v_here, given,
    )
    outgoing = call(
        send_own_kernel, "send_own", (plan,), (kept,),
        jax.ShapeDtypeStruct(slots, BF16),
    )
    gotten, stats = lax.optimization_barrier((gotten, stats))
    outgoing = call(
        partial(send_sibling_kernel, first=sib_at), "send_sibling", (plan,), (gotten,),
        jax.ShapeDtypeStruct(slots, BF16), into=outgoing,
    )
    arrived = lax.all_to_all(outgoing, "grp", split_axis=0, concat_axis=0, tiled=True)
    chunks = 2 if mine_blocks % 2 == 0 else 1
    chunk = mine_blocks // chunks
    chunk_shape = jax.ShapeDtypeStruct((chunk, 2, half, width), BF16)
    giving = call(
        partial(giving_kernel, give_at=give_at), "give", (plan,), (arrived,),
        [chunk_shape] * chunks,
    )
    stats = call(
        partial(mid_kernel, source_at=source_at, seen_at=seen_at, **sizes), "mid", (plan,),
        (q2, g2, stats, arrived), stat_shape,
    )
    others = []
    for part in giving:
        if others:
            part, stats = lax.optimization_barrier((part, stats))
        others.append(lax.ppermute(part, "uly", swap))
    grads, final = [], []
    for at, other in enumerate(others):
        grad, stat = call(
            partial(far_kernel, seen_at=seen_at, first=at * chunk, **sizes), "far", (plan,),
            (q2, g2, stats, other),
            [chunk_shape, jax.ShapeDtypeStruct((chunk, 8, rows), F32)],
        )
        grads.append(grad)
        final.append(stat)
    from_sib = [lax.ppermute(part, "uly", swap) for part in grads]
    mine = [None] * chunks
    for at in reversed(range(chunks)):
        if at + 1 < chunks:
            from_sib[at], final[at] = lax.optimization_barrier((from_sib[at], final[at]))
        mine[at] = call(
            partial(
                mine_kernel, source_at=source_at, seen_at=seen_at, rows=rows, first=at * chunk,
                **sizes,
            ),
            "mine", (plan,), (q2, g2, arrived, final[at]), chunk_shape,
        )
    returning = call(
        partial(returning_kernel, source_at=source_at), "return", (plan,), mine + from_sib,
        pltpu.HBM(slots, BF16), [pltpu.SemaphoreType.DMA((per_group,))], out_spec=anywhere,
    )
    other = jnp.concatenate(others)
    returning, k2l = lax.optimization_barrier((returning, k2))
    landed = lax.all_to_all(returning, "grp", split_axis=0, concat_axis=0, tiled=True)

    def from_source(i, plan_ref):
        return (plan_ref[source_at + i], 0, 0, 0)

    col_spec = pl.BlockSpec((cols, width), step_rows)
    attended, dq, dk_near, dv_near = pl.pallas_call(
        partial(local_kernel, seen_at=seen_at, **sizes),
        grid_spec=pltpu.PrefetchScalarGridSpec(
            num_scalar_prefetch=1,
            grid=(mine_blocks,),
            in_specs=[
                row_spec, row_spec, col_spec, col_spec,
                pl.BlockSpec((1, 2, half, width), from_source),
                part_spec,
            ],
            out_specs=[row_spec, row_spec, col_spec, col_spec],
            scratch_shapes=[pltpu.VMEM((rows, 2 * cols), F32)],
        ),
        out_shape=[row_shape, row_shape, near_shape, near_shape],
        compiler_params=limit,
        name="local",
    )(plan, q2, g2, k2l, v2, arrived, other)
    landed, dk_near = lax.optimization_barrier((landed, dk_near))
    give = call(
        partial(landing_kernel, first=sib_at), "land_sibling", (plan,), (landed,), part_shape,
        sum_scratch,
    )
    back = lax.ppermute(give, "uly", swap)
    own = call(
        partial(own_half_kernel, kv_heads=kv_heads), "land_own", (plan,),
        (landed, dk_near, dv_near), part_shape, sum_scratch,
    )
    dk, dv = call(
        partial(finish_kernel, kv_heads=kv_heads), "finish", (),
        (dk_near, dv_near, own, back), [small_shape, small_shape],
    )
    return (
        attended.reshape(queries.shape), dq.reshape(queries.shape),
        dk.reshape(keys.shape), dv.reshape(keys.shape),
    )


def on_device(queries, keys, values, output_cotangent, block_lists, list_counts):
    uly_count = lax.axis_size("uly")
    grp_count = lax.axis_size("grp")
    blocks_all, remote = block_lists.shape
    block_tok = queries.shape[0] * uly_count * grp_count // blocks_all
    held_whole = queries.shape[0] % block_tok == 0
    run = whole_blocks if held_whole and remote == 1 and uly_count == 2 else spread_blocks
    return run(queries, keys, values, output_cotangent, block_lists, list_counts)


def solution(mesh):
    placed = (
        P(("grp", "uly"), None, None),
        P(("grp", "uly"), None, None),
        P(("grp", "uly"), None, None),
        P(("grp", "uly"), None, None),
        P(),
        P(),
    )
    return jax.shard_map(
        on_device,
        mesh=mesh,
        in_specs=placed,
        out_specs=(
            P(("grp", "uly"), None, None),
            P(("grp", "uly"), None, None),
            P(("grp", "uly"), None, None),
            P(("grp", "uly"), None, None),
        ),
        check_vma=False,
    )
```

```python
from functools import partial

import jax
import jax.numpy as jnp
from jax import lax
from jax.experimental import pallas as pl
from jax.experimental.pallas import tpu as pltpu
from jax.sharding import PartitionSpec as P


def spread_blocks(queries, keys, values, output_cotangent, block_lists, list_counts):
    uly_count = lax.axis_size("uly")
    grp_count = lax.axis_size("grp")
    my_group = lax.axis_index("grp")
    tokens, head_count, head_width = queries.shape
    kv_heads = keys.shape[1]
    copies = max(1, uly_count // kv_heads)
    blocks_all, remote = block_lists.shape
    per_group = blocks_all // grp_count
    block_tok = tokens * uly_count // per_group
    group_tok = tokens * uly_count
    score_scale = head_width ** (-0.5)
    lists = block_lists.reshape(grp_count, per_group, remote)
    counted = (jnp.arange(remote)[None, :] < list_counts[:, None]).reshape(
        grp_count, per_group, remote
    )
    wanted = (lists // per_group == my_group) & counted
    send_place = jnp.sum(jnp.where(wanted, lists % per_group, 0), axis=(1, 2))
    sending = jnp.any(wanted, axis=(1, 2))
    mine_source = lax.dynamic_index_in_dim(lists, my_group, 0, keepdims=False) // per_group
    mine_counted = lax.dynamic_index_in_dim(counted, my_group, 0, keepdims=False)
    trip_count = jnp.max(jnp.sum(mine_counted.astype(jnp.int32), axis=1))

    def to_blocks(array_in):
        return array_in.reshape((per_group, block_tok) + array_in.shape[1:])

    keys_wide = jnp.repeat(keys, copies, axis=1)
    values_wide = jnp.repeat(values, copies, axis=1)
    query_heads, grad_heads, key_heads, value_heads = (
        lax.all_to_all(queries, "uly", split_axis=1, concat_axis=0, tiled=True),
        lax.all_to_all(output_cotangent, "uly", split_axis=1, concat_axis=0, tiled=True),
        lax.all_to_all(keys_wide, "uly", split_axis=1, concat_axis=0, tiled=True),
        lax.all_to_all(values_wide, "uly", split_axis=1, concat_axis=0, tiled=True),
    )
    stacked = jnp.stack([to_blocks(key_heads), to_blocks(value_heads)])
    outgoing = jnp.take(stacked, send_place, axis=1)
    arrived = lax.all_to_all(outgoing, "grp", split_axis=1, concat_axis=1, tiled=True)
    kv_local = key_heads.shape[1]
    heads_local = query_heads.shape[1]
    heads_per_group = heads_local // kv_local
    query_blk = query_heads.reshape(per_group, block_tok, kv_local, heads_per_group, head_width)
    grad_blk = grad_heads.reshape(per_group, block_tok, kv_local, heads_per_group, head_width)
    key_blk = to_blocks(key_heads)
    value_blk = to_blocks(value_heads)
    far_keys = arrived[0]
    far_values = arrived[1]
    causal = jnp.arange(block_tok)[:, None] >= jnp.arange(block_tok)[None, :]

    def logits(key_rows):
        return (
            jnp.einsum("pqkgd,pjkd->pkgqj", query_blk, key_rows, preferred_element_type=jnp.float32)
            * score_scale
        )

    def slot_rows(slot_index):
        source = lax.dynamic_index_in_dim(mine_source, slot_index, 1, keepdims=False)
        counted_slot = lax.dynamic_index_in_dim(mine_counted, slot_index, 1, keepdims=False)
        return (
            jnp.take(far_keys, source, axis=0),
            jnp.take(far_values, source, axis=0),
            counted_slot,
            source,
        )

    def masked(scores, counted_slot):
        return jnp.where(counted_slot[:, None, None, None, None], scores, -jnp.inf)

    near_scores = jnp.where(causal, logits(key_blk), -jnp.inf)
    highest = jnp.max(near_scores, axis=-1)
    denominator = jnp.sum(jnp.exp(near_scores - highest[..., None]), axis=-1)

    def max_sweep(slot_index, state_pair):
        highest, denominator = state_pair
        key_rows, value_rows, counted_slot, source = slot_rows(slot_index)
        scores = masked(logits(key_rows), counted_slot)
        new_highest = jnp.maximum(highest, jnp.max(scores, axis=-1))
        denominator = denominator * jnp.exp(highest - new_highest) + jnp.sum(
            jnp.exp(scores - new_highest[..., None]), axis=-1
        )
        return (new_highest, denominator)

    highest, denominator = lax.fori_loop(0, trip_count, max_sweep, (highest, denominator))
    log_total = highest + jnp.log(denominator)

    def softmax_weights(scores):
        return jnp.exp(scores - log_total[..., None])

    summed = jnp.einsum(
        "pkgqj,pjkd->pqkgd",
        softmax_weights(near_scores).astype(jnp.bfloat16),
        value_blk,
        preferred_element_type=jnp.float32,
    )

    def value_sweep(slot_index, summed):
        key_rows, value_rows, counted_slot, source = slot_rows(slot_index)
        weights = softmax_weights(masked(logits(key_rows), counted_slot)).astype(jnp.bfloat16)
        return summed + jnp.einsum(
            "pkgqj,pjkd->pqkgd", weights, value_rows, preferred_element_type=jnp.float32
        )

    summed = lax.fori_loop(0, trip_count, value_sweep, summed)
    attended_blk = summed.astype(jnp.bfloat16)
    row_delta = jnp.transpose(
        jnp.sum(grad_blk.astype(jnp.float32) * attended_blk.astype(jnp.float32), axis=-1),
        (0, 2, 3, 1),
    )

    def backward(scores, key_rows, value_rows):
        probs = softmax_weights(scores)
        weights = probs.astype(jnp.bfloat16)
        dprobs = jnp.einsum(
            "pqkgd,pjkd->pkgqj", grad_blk, value_rows, preferred_element_type=jnp.float32
        )
        dscores = (probs * (dprobs - row_delta[..., None])).astype(jnp.bfloat16)
        query_term = jnp.einsum(
            "pkgqj,pjkd->pqkgd", dscores, key_rows, preferred_element_type=jnp.float32
        )
        key_term = (
            jnp.einsum("pkgqj,pqkgd->pjkd", dscores, query_blk, preferred_element_type=jnp.float32)
            * score_scale
        )
        value_term = jnp.einsum(
            "pkgqj,pqkgd->pjkd", weights, grad_blk, preferred_element_type=jnp.float32
        )
        return (query_term, key_term, value_term)

    query_sum, key_near, value_near = backward(near_scores, key_blk, value_blk)
    far_grads = jnp.zeros((2, grp_count, block_tok, kv_local, head_width), jnp.float32)

    def grad_sweep(slot_index, state_pair):
        query_sum, far_grads = state_pair
        key_rows, value_rows, counted_slot, source = slot_rows(slot_index)
        query_term, key_term, value_term = backward(
            masked(logits(key_rows), counted_slot), key_rows, value_rows
        )
        routing = (
            (source[:, None] == jnp.arange(grp_count)[None, :]) & counted_slot[:, None]
        ).astype(jnp.float32)
        routed = jnp.einsum(
            "ps,xpjkd->xsjkd",
            routing,
            jnp.stack([key_term, value_term]),
            precision=lax.Precision.HIGHEST,
        )
        return (query_sum + query_term, far_grads + routed)

    query_sum, far_grads = lax.fori_loop(0, trip_count, grad_sweep, (query_sum, far_grads))
    owners = ((send_place[:, None] == jnp.arange(per_group)[None, :]) & sending[:, None]).astype(
        jnp.float32
    )
    returned = lax.all_to_all(far_grads, "grp", split_axis=1, concat_axis=1, tiled=True)
    landed = jnp.einsum("sp,xsjkd->xpjkd", owners, returned, precision=lax.Precision.HIGHEST)
    key_local = (key_near + landed[0]).reshape(group_tok, kv_local, head_width)
    value_local = (value_near + landed[1]).reshape(group_tok, kv_local, head_width)
    attended_rows = attended_blk.reshape(group_tok, heads_local, head_width)
    query_rows = (
        (query_sum * score_scale).astype(jnp.bfloat16).reshape(group_tok, heads_local, head_width)
    )
    attended, query_grad = (
        lax.all_to_all(attended_rows, "uly", split_axis=0, concat_axis=1, tiled=True),
        lax.all_to_all(query_rows, "uly", split_axis=0, concat_axis=1, tiled=True),
    )
    key_parts, value_parts = (
        lax.all_to_all(key_local, "uly", split_axis=0, concat_axis=1, tiled=True),
        lax.all_to_all(value_local, "uly", split_axis=0, concat_axis=1, tiled=True),
    )
    key_gradient = jnp.sum(key_parts.reshape(tokens, kv_heads, copies, head_width), axis=2).astype(
        jnp.bfloat16
    )
    value_gradient = jnp.sum(
        value_parts.reshape(tokens, kv_heads, copies, head_width), axis=2
    ).astype(jnp.bfloat16)
    return (attended, query_grad, key_gradient, value_gradient)


HIDDEN = -1e30
LAST = (((1,), (1,)), ((), ()))
FIRST = (((0,), (0,)), ((), ()))
F32 = jnp.float32
BF16 = jnp.bfloat16


def dot_last(left, right):
    return lax.dot_general(left, right, LAST, preferred_element_type=F32)


def dot_first(left, right):
    return lax.dot_general(left, right, FIRST, preferred_element_type=F32)


def head_major(cols, kv_heads):
    half = cols // 2
    place = half // kv_heads
    row = lax.broadcasted_iota(jnp.int32, (cols, cols), 0)
    col = lax.broadcasted_iota(jnp.int32, (cols, cols), 1)
    token = row // half * place + row % place
    return jnp.where(col == token * kv_heads + row % half // place, 1.0, 0.0).astype(BF16)


def token_major(half, kv_heads):
    place = half // kv_heads
    row = lax.broadcasted_iota(jnp.int32, (half, half), 0)
    col = lax.broadcasted_iota(jnp.int32, (half, half), 1)
    return jnp.where(col == row % kv_heads * place + row // kv_heads, 1.0, 0.0).astype(BF16)


def reorder(one_hot, array):
    return jnp.dot(one_hot, array, preferred_element_type=F32).astype(BF16)


def own_head(scores, lane_head, kv_heads):
    place = scores.shape[0] // kv_heads
    kept = scores[:place]
    for head in range(1, kv_heads):
        kept = jnp.where(lane_head == head, scores[head * place:(head + 1) * place], kept)
    return kept


def all_heads(kept, lane_head, kv_heads):
    none = jnp.zeros_like(kept)
    return jnp.concatenate(
        [jnp.where(lane_head == head, kept, none) for head in range(kv_heads)], axis=0
    )


def lanes(rows, heads, kv_heads):
    lane = lax.broadcasted_iota(jnp.int32, (1, rows), 1)
    return lane // heads, lane % heads // (heads // kv_heads)


def plan_spans(grp_count, blocks):
    return grp_count, 2 * grp_count, 2 * grp_count + blocks, 2 * grp_count + 2 * blocks


def plan_kernel(lists_ref, counts_ref, plan_ref, *, grp_count, blocks):
    group, mine = lax.axis_index("grp"), lax.axis_index("uly")
    per_group = 2 * blocks
    low = group * per_group
    sib_at, source_at, give_at, seen_at = plan_spans(grp_count, blocks)
    for other in range(grp_count):
        place = jnp.int32(-1)
        for at in range(other * per_group, (other + 1) * per_group):
            here = lists_ref[at] - low
            wanted = (here >= 0) & (here < per_group) & (counts_ref[at] > 0)
            place = jnp.where(wanted, here, place)
        own = place - mine * blocks
        sib = place - (1 - mine) * blocks
        plan_ref[other] = jnp.where((own >= 0) & (own < blocks), own, -1)
        plan_ref[sib_at + other] = jnp.where((sib >= 0) & (sib < blocks), sib, -1)
    for block in range(blocks):
        at = low + mine * blocks + block
        plan_ref[source_at + block] = lax.div(lists_ref[at], per_group)
        plan_ref[seen_at + block] = counts_ref[at]
        at = low + (1 - mine) * blocks + block
        plan_ref[give_at + block] = lax.div(lists_ref[at], per_group)


def pack_kernel(k_hbm, v_hbm, kept_ref, given_ref, k_ref, v_ref, sems, *, kv_heads):
    blocks, _, half, _ = kept_ref.shape
    copies = [
        pltpu.make_async_copy(k_hbm, k_ref, sems.at[0]),
        pltpu.make_async_copy(v_hbm, v_ref, sems.at[1]),
    ]
    for copy in copies:
        copy.start()
    first = lax.axis_index("uly") == 0
    order = head_major(2 * half, kv_heads)
    for which, ref in enumerate((k_ref, v_ref)):
        copies[which].wait()
        for block in range(blocks):
            ordered = reorder(order, ref[block * 2 * half:(block + 1) * 2 * half])
            kept_ref[block, which] = jnp.where(first, ordered[:half], ordered[half:])
            given_ref[block, which] = jnp.where(first, ordered[half:], ordered[:half])


def send_own_kernel(plan_ref, blocks_ref, out_ref):
    for group in range(out_ref.shape[0]):
        out_ref[group] = blocks_ref[jnp.maximum(plan_ref[group], 0)]


def send_sibling_kernel(plan_ref, blocks_ref, _, out_ref, *, first):
    for group in range(out_ref.shape[0]):
        place = plan_ref[first + group]

        @pl.when(place >= 0)
        def _():
            out_ref[group] = blocks_ref[place]


def giving_kernel(plan_ref, arrived_ref, *out_refs, give_at):
    block = 0
    for out_ref in out_refs:
        for at in range(out_ref.shape[0]):
            out_ref[at] = arrived_ref[plan_ref[give_at + block]]
            block += 1


def returning_kernel(plan_ref, *refs, source_at):
    part_refs, (out_ref, sems) = refs[:-2], refs[-2:]
    copies = []
    for part_ref in part_refs:
        for at in range(part_ref.shape[0]):
            block = len(copies)
            target = out_ref.at[plan_ref[source_at + block]]
            copies.append(pltpu.make_async_copy(part_ref.at[at], target, sems.at[block]))
            copies[-1].start()
    for copy in copies:
        copy.wait()


def near_kernel(
    q_ref, g_ref, kept_ref, given_ref, stat_ref, *, heads, kv_heads, score_scale
):
    rows = q_ref.shape[0]
    place = kept_ref.shape[2] // kv_heads
    token, lane_head = lanes(rows, heads, kv_heads)
    key = lax.broadcasted_iota(jnp.int32, (2 * place, rows), 0)
    mine = lax.axis_index("uly")
    part = jnp.where(key < place, mine, 1 - mine)
    causal = key % place + part * place <= token
    pieces = []
    for which, ref in enumerate((q_ref, g_ref)):
        both = jnp.concatenate([kept_ref[0, which], given_ref[0, which]], axis=0)
        full = dot_last(both, ref[...])
        half = full.shape[0] // 2
        pieces.append(
            jnp.concatenate(
                [
                    own_head(full[:half], lane_head, kv_heads),
                    own_head(full[half:], lane_head, kv_heads),
                ],
                axis=0,
            )
        )
    scores = jnp.where(causal, pieces[0] * score_scale, HIDDEN)
    highest = jnp.max(scores, axis=0, keepdims=True)
    raised = jnp.exp(scores - highest)
    stat_ref[0, 0:1] = highest
    stat_ref[0, 1:2] = jnp.sum(raised, axis=0, keepdims=True)
    stat_ref[0, 2:3] = jnp.sum(raised * pieces[1], axis=0, keepdims=True)


def far_scores(part_ref, at, q, g, seen, lane_head, kv_heads, score_scale):
    hidden = jnp.where(seen > 0, 0.0, HIDDEN)
    scores = own_head(dot_last(part_ref[at, 0], q), lane_head, kv_heads) * score_scale + hidden
    return scores, own_head(dot_last(part_ref[at, 1], g), lane_head, kv_heads)


def merged(stat_ref, block, scores, dprobs):
    before = stat_ref[block, 0:1]
    highest = jnp.maximum(before, jnp.max(scores, axis=0, keepdims=True))
    raised = jnp.exp(scores - highest)
    shrink = jnp.exp(before - highest)
    total = shrink * stat_ref[block, 1:2] + jnp.sum(raised, axis=0, keepdims=True)
    delta = shrink * stat_ref[block, 2:3] + jnp.sum(raised * dprobs, axis=0, keepdims=True)
    return highest, raised, total, delta


def far_gradients(probs, dprobs, delta, q, g, lane_head, kv_heads, score_scale):
    dscores = (probs * (dprobs - delta)).astype(BF16)
    dk = jnp.dot(all_heads(dscores, lane_head, kv_heads), q, preferred_element_type=F32)
    dv = jnp.dot(all_heads(probs.astype(BF16), lane_head, kv_heads), g, preferred_element_type=F32)
    return (dk * score_scale).astype(BF16), dv.astype(BF16)


def mid_kernel(
    plan_ref, q_ref, g_ref, stat_ref, arrived_ref, out_ref,
    *, heads, kv_heads, score_scale, source_at, seen_at
):
    blocks = stat_ref.shape[0]
    rows = q_ref.shape[0] // blocks
    _, lane_head = lanes(rows, heads, kv_heads)
    for block in range(blocks):
        span = slice(block * rows, (block + 1) * rows)
        scores, dprobs = far_scores(
            arrived_ref, plan_ref[source_at + block], q_ref[span], g_ref[span],
            plan_ref[seen_at + block],            lane_head, kv_heads, score_scale,
        )
        highest, _, total, delta = merged(stat_ref, block, scores, dprobs)
        out_ref[block, 0:1] = highest
        out_ref[block, 1:2] = total
        out_ref[block, 2:3] = delta


def far_kernel(
    plan_ref, q_ref, g_ref, stat_ref, other_ref, grad_ref, out_ref,
    *, heads, kv_heads, score_scale, seen_at, first
):
    rows = q_ref.shape[0] // stat_ref.shape[0]
    _, lane_head = lanes(rows, heads, kv_heads)
    for at in range(other_ref.shape[0]):
        block = first + at
        span = slice(block * rows, (block + 1) * rows)
        q = q_ref[span]
        g = g_ref[span]
        scores, dprobs = far_scores(
            other_ref, at, q, g, plan_ref[seen_at + block], lane_head, kv_heads, score_scale
        )
        highest, raised, total, delta = merged(stat_ref, block, scores, dprobs)
        inverse = 1.0 / total
        delta = delta * inverse
        grad_ref[at, 0], grad_ref[at, 1] = far_gradients(
            raised * inverse, dprobs, delta, q, g, lane_head, kv_heads, score_scale
        )
        out_ref[at, 0:1] = highest
        out_ref[at, 1:2] = inverse
        out_ref[at, 2:3] = delta


def mine_kernel(
    plan_ref, q_ref, g_ref, arrived_ref, stat_ref, grad_ref,
    *, heads, kv_heads, score_scale, source_at, seen_at, rows, first
):
    _, lane_head = lanes(rows, heads, kv_heads)
    for at in range(stat_ref.shape[0]):
        block = first + at
        span = slice(block * rows, (block + 1) * rows)
        q = q_ref[span]
        g = g_ref[span]
        scores, dprobs = far_scores(
            arrived_ref, plan_ref[source_at + block], q, g, plan_ref[seen_at + block],
            lane_head, kv_heads, score_scale,
        )
        probs = jnp.exp(scores - stat_ref[at, 0:1]) * stat_ref[at, 1:2]
        grad_ref[at, 0], grad_ref[at, 1] = far_gradients(
            probs, dprobs, stat_ref[at, 2:3], q, g, lane_head, kv_heads, score_scale
        )


def local_kernel(
    plan_ref, q_ref, g_ref, k_ref, v_ref, mine_ref, other_ref,
    att_ref, dq_ref, dk_ref, dv_ref, bias_ref, *, heads, kv_heads, score_scale, seen_at
):
    step = pl.program_id(0)
    rows = q_ref.shape[0]
    cols = k_ref.shape[0]

    @pl.when(step == 0)
    def _():
        half = cols // 2
        place = half // kv_heads
        row = lax.broadcasted_iota(jnp.int32, (rows, cols), 0)
        col = lax.broadcasted_iota(jnp.int32, (rows, cols), 1)
        same = row % heads // (heads // kv_heads) == col % half // place
        causal = col // half * place + col % place <= row // heads
        bias_ref[:, :cols] = jnp.where(same & causal, 0.0, HIDDEN)
        bias_ref[:, cols:] = jnp.where(same, 0.0, HIDDEN)

    far_bias = jnp.where(plan_ref[seen_at + step] > 0, 0.0, HIDDEN)
    order = head_major(cols, kv_heads)
    k_near = reorder(order, k_ref[...])
    v_near = reorder(order, v_ref[...])
    k_all = jnp.concatenate([k_near, mine_ref[0, 0], other_ref[0, 0]], axis=0)
    v_all = jnp.concatenate([v_near, mine_ref[0, 1], other_ref[0, 1]], axis=0)
    q = q_ref[...]
    g = g_ref[...]
    scores = dot_last(q, k_all) * score_scale + bias_ref[...]
    scores = jnp.concatenate([scores[:, :cols], scores[:, cols:] + far_bias], axis=1)
    highest = jnp.max(scores, axis=1, keepdims=True)
    raised = jnp.exp(scores - highest)
    total = jnp.sum(raised, axis=1, keepdims=True)
    probs = raised * (1.0 / total)
    weights = probs.astype(BF16)
    attended = jnp.dot(weights, v_all, preferred_element_type=F32).astype(BF16)
    att_ref[...] = attended
    delta = jnp.sum(g.astype(F32) * attended.astype(F32), axis=1, keepdims=True)
    dscores = (probs * (dot_last(g, v_all) - delta)).astype(BF16)
    dq = jnp.dot(dscores, k_all, preferred_element_type=F32) * score_scale
    dq_ref[...] = dq.astype(BF16)
    dk_ref[...] = dot_first(dscores[:, :cols], q) * score_scale
    dv_ref[...] = dot_first(weights[:, :cols], g)


def landing_kernel(plan_ref, landed_ref, out_ref, sum_ref, *, first):
    sum_ref[...] = jnp.zeros_like(sum_ref)
    for group in range(landed_ref.shape[0]):
        place = plan_ref[first + group]

        @pl.when(place >= 0)
        def _():
            sum_ref[place] = sum_ref[place] + landed_ref[group].astype(F32)

    out_ref[...] = sum_ref[...].astype(out_ref.dtype)


def own_half_kernel(
    plan_ref, landed_ref, dk_near_ref, dv_near_ref, out_ref, sum_ref, *, kv_heads
):
    sum_ref[...] = jnp.zeros_like(sum_ref)
    for group in range(landed_ref.shape[0]):
        place = plan_ref[group]

        @pl.when(place >= 0)
        def _():
            sum_ref[place] = sum_ref[place] + landed_ref[group].astype(F32)

    blocks, _, half, _ = out_ref.shape
    order = token_major(half, kv_heads)
    mine = lax.axis_index("uly")
    for block in range(blocks):
        span = pl.ds(pl.multiple_of((2 * block + mine) * half, half), half)
        for which, near_ref in enumerate((dk_near_ref, dv_near_ref)):
            summed = (near_ref[span] + sum_ref[block, which]).astype(BF16)
            out_ref[block, which] = reorder(order, summed)


def finish_kernel(
    dk_near_ref, dv_near_ref, own_ref, back_ref, dk_ref, dv_ref, *, kv_heads
):
    blocks, _, half, _ = back_ref.shape
    order = token_major(half, kv_heads)
    mine = lax.axis_index("uly")
    for which, (near_ref, out_ref) in enumerate(((dk_near_ref, dk_ref), (dv_near_ref, dv_ref))):
        for block in range(blocks):
            here = pl.ds(pl.multiple_of((2 * block + mine) * half, half), half)
            there = pl.ds(pl.multiple_of((2 * block + 1 - mine) * half, half), half)
            summed = (near_ref[there] + back_ref[block, which].astype(F32)).astype(BF16)
            out_ref[here] = own_ref[block, which]
            out_ref[there] = reorder(order, summed)


def take_rows(array, index):
    return array.at[index].get(mode="promise_in_bounds")


def whole_blocks(queries, keys, values, output_cotangent, block_lists, list_counts):
    grp_count = lax.axis_size("grp")
    uly_count = lax.axis_size("uly")
    tokens, heads, width = queries.shape
    kv_heads = keys.shape[1]
    per_group = block_lists.shape[0] // grp_count
    block_tok = tokens * uly_count // per_group
    mine_blocks = tokens // block_tok
    rows = block_tok * heads
    cols = block_tok * kv_heads
    half = cols // 2
    sizes = dict(heads=heads, kv_heads=kv_heads, score_scale=width ** (-0.5))
    swap = [(0, 1), (1, 0)]

    sib_at, source_at, give_at, seen_at = plan_spans(grp_count, mine_blocks)

    q2 = queries.reshape(tokens * heads, width)
    g2 = output_cotangent.reshape(tokens * heads, width)
    k2 = keys.reshape(tokens * kv_heads, width)
    v2 = values.reshape(tokens * kv_heads, width)

    part_shape = jax.ShapeDtypeStruct((mine_blocks, 2, half, width), BF16)
    slots = (grp_count, 2, half, width)
    stat_shape = jax.ShapeDtypeStruct((mine_blocks, 8, rows), F32)
    row_shape = jax.ShapeDtypeStruct(q2.shape, BF16)
    near_shape = jax.ShapeDtypeStruct(k2.shape, F32)
    small_shape = jax.ShapeDtypeStruct(k2.shape, BF16)
    sum_scratch = [pltpu.VMEM((mine_blocks, 2, half, width), F32)]
    limit = pltpu.CompilerParams(vmem_limit_bytes=24 * 1024 * 1024)
    vmem = pl.BlockSpec(memory_space=pltpu.VMEM)
    smem = pl.BlockSpec(memory_space=pltpu.SMEM)
    anywhere = pl.BlockSpec(memory_space=pltpu.HBM)

    def call(kernel, name, scalars, operands, out_shape, scratch=(), into=None, out_spec=vmem):
        extra = () if into is None else (into,)
        return pl.pallas_call(
            kernel,
            in_specs=[smem] * len(scalars) + [vmem] * (len(operands) + len(extra)),
            out_specs=jax.tree.map(lambda _: out_spec, out_shape),
            out_shape=out_shape,
            scratch_shapes=scratch,
            input_output_aliases={len(scalars) + len(operands): 0} if extra else {},
            compiler_params=limit,
            name=name,
        )(*scalars, *operands, *extra)

    def step_rows(i, *_):
        return (i, 0)

    def step_part(i, *_):
        return (i, 0, 0, 0)

    def in_hbm(array):
        return pltpu.with_memory_space_constraint(array, pltpu.HBM)

    kept, given = pl.pallas_call(
        partial(pack_kernel, kv_heads=kv_heads),
        in_specs=[anywhere, anywhere],
        out_specs=[vmem, vmem],
        out_shape=[part_shape, part_shape],
        scratch_shapes=[
            pltpu.VMEM(k2.shape, BF16), pltpu.VMEM(k2.shape, BF16),
            pltpu.SemaphoreType.DMA((2,)),
        ],
        compiler_params=limit,
        name="pack",
    )(in_hbm(k2), in_hbm(v2))
    plan = pl.pallas_call(
        partial(plan_kernel, grp_count=grp_count, blocks=mine_blocks),
        in_specs=[smem, smem],
        out_specs=smem,
        out_shape=pltpu.SMEM((seen_at + mine_blocks,), jnp.int32),
        compiler_params=limit,
        name="plan",
    )(in_hbm(block_lists.reshape(-1)), in_hbm(list_counts))
    gotten = lax.ppermute(given, "uly", swap)
    row_spec = pl.BlockSpec((rows, width), step_rows)
    part_spec = pl.BlockSpec((1, 2, half, width), step_part)
    stats = pl.pallas_call(
        partial(near_kernel, **sizes),
        grid=(mine_blocks,),
        in_specs=[row_spec, row_spec, part_spec, part_spec],
        out_specs=pl.BlockSpec((1, 8, rows), lambda i: (i, 0, 0)),
        out_shape=stat_shape,
        compiler_params=limit,
        name="near",
    )(in_hbm(q2), in_hbm(g2), kept, given)
    outgoing = call(
        send_own_kernel, "send_own", (plan,), (kept,),
        jax.ShapeDtypeStruct(slots, BF16),
    )
    gotten, stats = lax.optimization_barrier((gotten, stats))
    outgoing = call(
        partial(send_sibling_kernel, first=sib_at), "send_sibling", (plan,), (gotten,),
        jax.ShapeDtypeStruct(slots, BF16), into=outgoing,
    )
    arrived = lax.all_to_all(outgoing, "grp", split_axis=0, concat_axis=0, tiled=True)
    chunks = 2 if mine_blocks % 2 == 0 else 1
    chunk = mine_blocks // chunks
    chunk_shape = jax.ShapeDtypeStruct((chunk, 2, half, width), BF16)
    giving = call(
        partial(giving_kernel, give_at=give_at), "give", (plan,), (arrived,),
        [chunk_shape] * chunks,
    )
    stats = call(
        partial(mid_kernel, source_at=source_at, seen_at=seen_at, **sizes), "mid", (plan,),
        (q2, g2, stats, arrived), stat_shape,
    )
    others = []
    for part in giving:
        if others:
            part, stats = lax.optimization_barrier((part, stats))
        others.append(lax.ppermute(part, "uly", swap))
    grads, final = [], []
    for at, other in enumerate(others):
        grad, stat = call(
            partial(far_kernel, seen_at=seen_at, first=at * chunk, **sizes), "far", (plan,),
            (q2, g2, stats, other),
            [chunk_shape, jax.ShapeDtypeStruct((chunk, 8, rows), F32)],
        )
        grads.append(grad)
        final.append(stat)
    from_sib = [lax.ppermute(part, "uly", swap) for part in grads]
    mine = [None] * chunks
    for at in reversed(range(chunks)):
        if at + 1 < chunks:
            from_sib[at], final[at] = lax.optimization_barrier((from_sib[at], final[at]))
        mine[at] = call(
            partial(
                mine_kernel, source_at=source_at, seen_at=seen_at, rows=rows, first=at * chunk,
                **sizes,
            ),
            "mine", (plan,), (q2, g2, arrived, final[at]), chunk_shape,
        )
    returning = call(
        partial(returning_kernel, source_at=source_at), "return", (plan,), mine + from_sib,
        pltpu.HBM(slots, BF16), [pltpu.SemaphoreType.DMA((per_group,))], out_spec=anywhere,
    )
    other = jnp.concatenate(others)
    returning, k2l = lax.optimization_barrier((returning, k2))
    landed = lax.all_to_all(returning, "grp", split_axis=0, concat_axis=0, tiled=True)

    def from_source(i, plan_ref):
        return (plan_ref[source_at + i], 0, 0, 0)

    col_spec = pl.BlockSpec((cols, width), step_rows)
    attended, dq, dk_near, dv_near = pl.pallas_call(
        partial(local_kernel, seen_at=seen_at, **sizes),
        grid_spec=pltpu.PrefetchScalarGridSpec(
            num_scalar_prefetch=1,
            grid=(mine_blocks,),
            in_specs=[
                row_spec, row_spec, col_spec, col_spec,
                pl.BlockSpec((1, 2, half, width), from_source),
                part_spec,
            ],
            out_specs=[row_spec, row_spec, col_spec, col_spec],
            scratch_shapes=[pltpu.VMEM((rows, 2 * cols), F32)],
        ),
        out_shape=[row_shape, row_shape, near_shape, near_shape],
        compiler_params=limit,
        name="local",
    )(plan, q2, g2, k2l, v2, arrived, other)
    landed, dk_near = lax.optimization_barrier((landed, dk_near))
    give = call(
        partial(landing_kernel, first=sib_at), "land_sibling", (plan,), (landed,), part_shape,
        sum_scratch,
    )
    back = lax.ppermute(give, "uly", swap)
    own = call(
        partial(own_half_kernel, kv_heads=kv_heads), "land_own", (plan,),
        (landed, dk_near, dv_near), part_shape, sum_scratch,
    )
    dk, dv = call(
        partial(finish_kernel, kv_heads=kv_heads), "finish", (),
        (dk_near, dv_near, own, back), [small_shape, small_shape],
    )
    return (
        attended.reshape(queries.shape), dq.reshape(queries.shape),
        dk.reshape(keys.shape), dv.reshape(keys.shape),
    )


def on_device(queries, keys, values, output_cotangent, block_lists, list_counts):
    uly_count = lax.axis_size("uly")
    grp_count = lax.axis_size("grp")
    blocks_all, remote = block_lists.shape
    block_tok = queries.shape[0] * uly_count * grp_count // blocks_all
    held_whole = queries.shape[0] % block_tok == 0
    run = whole_blocks if held_whole and remote == 1 and uly_count == 2 else spread_blocks
    return run(queries, keys, values, output_cotangent, block_lists, list_counts)


def solution(mesh):
    placed = (
        P(("grp", "uly"), None, None),
        P(("grp", "uly"), None, None),
        P(("grp", "uly"), None, None),
        P(("grp", "uly"), None, None),
        P(),
        P(),
    )
    return jax.shard_map(
        on_device,
        mesh=mesh,
        in_specs=placed,
        out_specs=(
            P(("grp", "uly"), None, None),
            P(("grp", "uly"), None, None),
            P(("grp", "uly"), None, None),
            P(("grp", "uly"), None, None),
        ),
        check_vma=False,
    )
```

```python
from functools import partial

import jax
import jax.numpy as jnp
from jax import lax
from jax.experimental import pallas as pl
from jax.experimental.pallas import tpu as pltpu
from jax.sharding import PartitionSpec as P


def spread_blocks(queries, keys, values, output_cotangent, block_lists, list_counts):
    uly_count = lax.axis_size("uly")
    grp_count = lax.axis_size("grp")
    my_group = lax.axis_index("grp")
    tokens, head_count, head_width = queries.shape
    kv_heads = keys.shape[1]
    copies = max(1, uly_count // kv_heads)
    blocks_all, remote = block_lists.shape
    per_group = blocks_all // grp_count
    block_tok = tokens * uly_count // per_group
    group_tok = tokens * uly_count
    score_scale = head_width ** (-0.5)
    lists = block_lists.reshape(grp_count, per_group, remote)
    counted = (jnp.arange(remote)[None, :] < list_counts[:, None]).reshape(
        grp_count, per_group, remote
    )
    wanted = (lists // per_group == my_group) & counted
    send_place = jnp.sum(jnp.where(wanted, lists % per_group, 0), axis=(1, 2))
    sending = jnp.any(wanted, axis=(1, 2))
    mine_source = lax.dynamic_index_in_dim(lists, my_group, 0, keepdims=False) // per_group
    mine_counted = lax.dynamic_index_in_dim(counted, my_group, 0, keepdims=False)
    trip_count = jnp.max(jnp.sum(mine_counted.astype(jnp.int32), axis=1))

    def to_blocks(array_in):
        return array_in.reshape((per_group, block_tok) + array_in.shape[1:])

    keys_wide = jnp.repeat(keys, copies, axis=1)
    values_wide = jnp.repeat(values, copies, axis=1)
    query_heads, grad_heads, key_heads, value_heads = (
        lax.all_to_all(queries, "uly", split_axis=1, concat_axis=0, tiled=True),
        lax.all_to_all(output_cotangent, "uly", split_axis=1, concat_axis=0, tiled=True),
        lax.all_to_all(keys_wide, "uly", split_axis=1, concat_axis=0, tiled=True),
        lax.all_to_all(values_wide, "uly", split_axis=1, concat_axis=0, tiled=True),
    )
    stacked = jnp.stack([to_blocks(key_heads), to_blocks(value_heads)])
    outgoing = jnp.take(stacked, send_place, axis=1)
    arrived = lax.all_to_all(outgoing, "grp", split_axis=1, concat_axis=1, tiled=True)
    kv_local = key_heads.shape[1]
    heads_local = query_heads.shape[1]
    heads_per_group = heads_local // kv_local
    query_blk = query_heads.reshape(per_group, block_tok, kv_local, heads_per_group, head_width)
    grad_blk = grad_heads.reshape(per_group, block_tok, kv_local, heads_per_group, head_width)
    key_blk = to_blocks(key_heads)
    value_blk = to_blocks(value_heads)
    far_keys = arrived[0]
    far_values = arrived[1]
    causal = jnp.arange(block_tok)[:, None] >= jnp.arange(block_tok)[None, :]

    def logits(key_rows):
        return (
            jnp.einsum("pqkgd,pjkd->pkgqj", query_blk, key_rows, preferred_element_type=jnp.float32)
            * score_scale
        )

    def slot_rows(slot_index):
        source = lax.dynamic_index_in_dim(mine_source, slot_index, 1, keepdims=False)
        counted_slot = lax.dynamic_index_in_dim(mine_counted, slot_index, 1, keepdims=False)
        return (
            jnp.take(far_keys, source, axis=0),
            jnp.take(far_values, source, axis=0),
            counted_slot,
            source,
        )

    def masked(scores, counted_slot):
        return jnp.where(counted_slot[:, None, None, None, None], scores, -jnp.inf)

    near_scores = jnp.where(causal, logits(key_blk), -jnp.inf)
    highest = jnp.max(near_scores, axis=-1)
    denominator = jnp.sum(jnp.exp(near_scores - highest[..., None]), axis=-1)

    def max_sweep(slot_index, state_pair):
        highest, denominator = state_pair
        key_rows, value_rows, counted_slot, source = slot_rows(slot_index)
        scores = masked(logits(key_rows), counted_slot)
        new_highest = jnp.maximum(highest, jnp.max(scores, axis=-1))
        denominator = denominator * jnp.exp(highest - new_highest) + jnp.sum(
            jnp.exp(scores - new_highest[..., None]), axis=-1
        )
        return (new_highest, denominator)

    highest, denominator = lax.fori_loop(0, trip_count, max_sweep, (highest, denominator))
    log_total = highest + jnp.log(denominator)

    def softmax_weights(scores):
        return jnp.exp(scores - log_total[..., None])

    summed = jnp.einsum(
        "pkgqj,pjkd->pqkgd",
        softmax_weights(near_scores).astype(jnp.bfloat16),
        value_blk,
        preferred_element_type=jnp.float32,
    )

    def value_sweep(slot_index, summed):
        key_rows, value_rows, counted_slot, source = slot_rows(slot_index)
        weights = softmax_weights(masked(logits(key_rows), counted_slot)).astype(jnp.bfloat16)
        return summed + jnp.einsum(
            "pkgqj,pjkd->pqkgd", weights, value_rows, preferred_element_type=jnp.float32
        )

    summed = lax.fori_loop(0, trip_count, value_sweep, summed)
    attended_blk = summed.astype(jnp.bfloat16)
    row_delta = jnp.transpose(
        jnp.sum(grad_blk.astype(jnp.float32) * attended_blk.astype(jnp.float32), axis=-1),
        (0, 2, 3, 1),
    )

    def backward(scores, key_rows, value_rows):
        probs = softmax_weights(scores)
        weights = probs.astype(jnp.bfloat16)
        dprobs = jnp.einsum(
            "pqkgd,pjkd->pkgqj", grad_blk, value_rows, preferred_element_type=jnp.float32
        )
        dscores = (probs * (dprobs - row_delta[..., None])).astype(jnp.bfloat16)
        query_term = jnp.einsum(
            "pkgqj,pjkd->pqkgd", dscores, key_rows, preferred_element_type=jnp.float32
        )
        key_term = (
            jnp.einsum("pkgqj,pqkgd->pjkd", dscores, query_blk, preferred_element_type=jnp.float32)
            * score_scale
        )
        value_term = jnp.einsum(
            "pkgqj,pqkgd->pjkd", weights, grad_blk, preferred_element_type=jnp.float32
        )
        return (query_term, key_term, value_term)

    query_sum, key_near, value_near = backward(near_scores, key_blk, value_blk)
    far_grads = jnp.zeros((2, grp_count, block_tok, kv_local, head_width), jnp.float32)

    def grad_sweep(slot_index, state_pair):
        query_sum, far_grads = state_pair
        key_rows, value_rows, counted_slot, source = slot_rows(slot_index)
        query_term, key_term, value_term = backward(
            masked(logits(key_rows), counted_slot), key_rows, value_rows
        )
        routing = (
            (source[:, None] == jnp.arange(grp_count)[None, :]) & counted_slot[:, None]
        ).astype(jnp.float32)
        routed = jnp.einsum(
            "ps,xpjkd->xsjkd",
            routing,
            jnp.stack([key_term, value_term]),
            precision=lax.Precision.HIGHEST,
        )
        return (query_sum + query_term, far_grads + routed)

    query_sum, far_grads = lax.fori_loop(0, trip_count, grad_sweep, (query_sum, far_grads))
    owners = ((send_place[:, None] == jnp.arange(per_group)[None, :]) & sending[:, None]).astype(
        jnp.float32
    )
    returned = lax.all_to_all(far_grads, "grp", split_axis=1, concat_axis=1, tiled=True)
    landed = jnp.einsum("sp,xsjkd->xpjkd", owners, returned, precision=lax.Precision.HIGHEST)
    key_local = (key_near + landed[0]).reshape(group_tok, kv_local, head_width)
    value_local = (value_near + landed[1]).reshape(group_tok, kv_local, head_width)
    attended_rows = attended_blk.reshape(group_tok, heads_local, head_width)
    query_rows = (
        (query_sum * score_scale).astype(jnp.bfloat16).reshape(group_tok, heads_local, head_width)
    )
    attended, query_grad = (
        lax.all_to_all(attended_rows, "uly", split_axis=0, concat_axis=1, tiled=True),
        lax.all_to_all(query_rows, "uly", split_axis=0, concat_axis=1, tiled=True),
    )
    key_parts, value_parts = (
        lax.all_to_all(key_local, "uly", split_axis=0, concat_axis=1, tiled=True),
        lax.all_to_all(value_local, "uly", split_axis=0, concat_axis=1, tiled=True),
    )
    key_gradient = jnp.sum(key_parts.reshape(tokens, kv_heads, copies, head_width), axis=2).astype(
        jnp.bfloat16
    )
    value_gradient = jnp.sum(
        value_parts.reshape(tokens, kv_heads, copies, head_width), axis=2
    ).astype(jnp.bfloat16)
    return (attended, query_grad, key_gradient, value_gradient)


HIDDEN = -1e30
LAST = (((1,), (1,)), ((), ()))
FIRST = (((0,), (0,)), ((), ()))
F32 = jnp.float32
BF16 = jnp.bfloat16


def dot_last(left, right):
    return lax.dot_general(left, right, LAST, preferred_element_type=F32)


def dot_first(left, right):
    return lax.dot_general(left, right, FIRST, preferred_element_type=F32)


def head_major(cols, kv_heads):
    half = cols // 2
    place = half // kv_heads
    row = lax.broadcasted_iota(jnp.int32, (cols, cols), 0)
    col = lax.broadcasted_iota(jnp.int32, (cols, cols), 1)
    token = row // half * place + row % place
    return jnp.where(col == token * kv_heads + row % half // place, 1.0, 0.0).astype(BF16)


def token_major(half, kv_heads):
    place = half // kv_heads
    row = lax.broadcasted_iota(jnp.int32, (half, half), 0)
    col = lax.broadcasted_iota(jnp.int32, (half, half), 1)
    return jnp.where(col == row % kv_heads * place + row // kv_heads, 1.0, 0.0).astype(BF16)


def reorder(one_hot, array):
    return jnp.dot(one_hot, array, preferred_element_type=F32).astype(BF16)


def own_head(scores, lane_head, kv_heads):
    place = scores.shape[0] // kv_heads
    kept = scores[:place]
    for head in range(1, kv_heads):
        kept = jnp.where(lane_head == head, scores[head * place:(head + 1) * place], kept)
    return kept


def all_heads(kept, lane_head, kv_heads):
    none = jnp.zeros_like(kept)
    return jnp.concatenate(
        [jnp.where(lane_head == head, kept, none) for head in range(kv_heads)], axis=0
    )


def lanes(rows, heads, kv_heads):
    lane = lax.broadcasted_iota(jnp.int32, (1, rows), 1)
    return lane // heads, lane % heads // (heads // kv_heads)


def plan_spans(grp_count, blocks):
    return grp_count, 2 * grp_count, 2 * grp_count + blocks, 2 * grp_count + 2 * blocks


def plan_kernel(lists_ref, counts_ref, plan_ref, *, grp_count, blocks):
    group, mine = lax.axis_index("grp"), lax.axis_index("uly")
    per_group = 2 * blocks
    low = group * per_group
    sib_at, source_at, give_at, seen_at = plan_spans(grp_count, blocks)
    for other in range(grp_count):
        place = jnp.int32(-1)
        for at in range(other * per_group, (other + 1) * per_group):
            here = lists_ref[at] - low
            wanted = (here >= 0) & (here < per_group) & (counts_ref[at] > 0)
            place = jnp.where(wanted, here, place)
        own = place - mine * blocks
        sib = place - (1 - mine) * blocks
        plan_ref[other] = jnp.where((own >= 0) & (own < blocks), own, -1)
        plan_ref[sib_at + other] = jnp.where((sib >= 0) & (sib < blocks), sib, -1)
    for block in range(blocks):
        at = low + mine * blocks + block
        plan_ref[source_at + block] = lax.div(lists_ref[at], per_group)
        plan_ref[seen_at + block] = counts_ref[at]
        at = low + (1 - mine) * blocks + block
        plan_ref[give_at + block] = lax.div(lists_ref[at], per_group)


def pack_kernel(k_hbm, v_hbm, kept_ref, given_ref, k_ref, v_ref, sems, *, kv_heads):
    blocks, _, half, _ = kept_ref.shape
    copies = [
        pltpu.make_async_copy(k_hbm, k_ref, sems.at[0]),
        pltpu.make_async_copy(v_hbm, v_ref, sems.at[1]),
    ]
    for copy in copies:
        copy.start()
    first = lax.axis_index("uly") == 0
    order = head_major(2 * half, kv_heads)
    for which, ref in enumerate((k_ref, v_ref)):
        copies[which].wait()
        for block in range(blocks):
            ordered = reorder(order, ref[block * 2 * half:(block + 1) * 2 * half])
            kept_ref[block, which] = jnp.where(first, ordered[:half], ordered[half:])
            given_ref[block, which] = jnp.where(first, ordered[half:], ordered[:half])


def send_own_kernel(plan_ref, blocks_ref, out_ref):
    for group in range(out_ref.shape[0]):
        out_ref[group] = blocks_ref[jnp.maximum(plan_ref[group], 0)]


def send_sibling_kernel(plan_ref, blocks_ref, _, out_ref, *, first):
    for group in range(out_ref.shape[0]):
        place = plan_ref[first + group]

        @pl.when(place >= 0)
        def _():
            out_ref[group] = blocks_ref[place]


def giving_kernel(plan_ref, arrived_ref, *out_refs, give_at):
    block = 0
    for out_ref in out_refs:
        for at in range(out_ref.shape[0]):
            out_ref[at] = arrived_ref[plan_ref[give_at + block]]
            block += 1


def returning_kernel(plan_ref, *refs, source_at):
    part_refs, (out_ref, sems) = refs[:-2], refs[-2:]
    copies = []
    for part_ref in part_refs:
        for at in range(part_ref.shape[0]):
            block = len(copies)
            target = out_ref.at[plan_ref[source_at + block]]
            copies.append(pltpu.make_async_copy(part_ref.at[at], target, sems.at[block]))
            copies[-1].start()
    for copy in copies:
        copy.wait()


def near_kernel(
    q_ref, g_ref, kept_ref, given_ref, stat_ref, *, heads, kv_heads, score_scale
):
    rows = q_ref.shape[0]
    place = kept_ref.shape[2] // kv_heads
    token, lane_head = lanes(rows, heads, kv_heads)
    key = lax.broadcasted_iota(jnp.int32, (2 * place, rows), 0)
    mine = lax.axis_index("uly")
    part = jnp.where(key < place, mine, 1 - mine)
    causal = key % place + part * place <= token
    pieces = []
    for which, ref in enumerate((q_ref, g_ref)):
        both = jnp.concatenate([kept_ref[0, which], given_ref[0, which]], axis=0)
        full = dot_last(both, ref[...])
        half = full.shape[0] // 2
        pieces.append(
            jnp.concatenate(
                [
                    own_head(full[:half], lane_head, kv_heads),
                    own_head(full[half:], lane_head, kv_heads),
                ],
                axis=0,
            )
        )
    scores = jnp.where(causal, pieces[0] * score_scale, HIDDEN)
    highest = jnp.max(scores, axis=0, keepdims=True)
    raised = jnp.exp(scores - highest)
    stat_ref[0, 0:1] = highest
    stat_ref[0, 1:2] = jnp.sum(raised, axis=0, keepdims=True)
    stat_ref[0, 2:3] = jnp.sum(raised * pieces[1], axis=0, keepdims=True)


def far_scores(part_ref, at, q, g, seen, lane_head, kv_heads, score_scale):
    hidden = jnp.where(seen > 0, 0.0, HIDDEN)
    scores = own_head(dot_last(part_ref[at, 0], q), lane_head, kv_heads) * score_scale + hidden
    return scores, own_head(dot_last(part_ref[at, 1], g), lane_head, kv_heads)


def merged(stat_ref, block, scores, dprobs):
    before = stat_ref[block, 0:1]
    highest = jnp.maximum(before, jnp.max(scores, axis=0, keepdims=True))
    raised = jnp.exp(scores - highest)
    shrink = jnp.exp(before - highest)
    total = shrink * stat_ref[block, 1:2] + jnp.sum(raised, axis=0, keepdims=True)
    delta = shrink * stat_ref[block, 2:3] + jnp.sum(raised * dprobs, axis=0, keepdims=True)
    return highest, raised, total, delta


def far_gradients(probs, dprobs, delta, q, g, lane_head, kv_heads, score_scale):
    dscores = (probs * (dprobs - delta)).astype(BF16)
    dk = jnp.dot(all_heads(dscores, lane_head, kv_heads), q, preferred_element_type=F32)
    dv = jnp.dot(all_heads(probs.astype(BF16), lane_head, kv_heads), g, preferred_element_type=F32)
    return (dk * score_scale).astype(BF16), dv.astype(BF16)


def mid_kernel(
    plan_ref, q_ref, g_ref, stat_ref, arrived_ref, out_ref,
    *, heads, kv_heads, score_scale, source_at, seen_at
):
    blocks = stat_ref.shape[0]
    rows = q_ref.shape[0] // blocks
    _, lane_head = lanes(rows, heads, kv_heads)
    for block in range(blocks):
        span = slice(block * rows, (block + 1) * rows)
        scores, dprobs = far_scores(
            arrived_ref, plan_ref[source_at + block], q_ref[span], g_ref[span],
            plan_ref[seen_at + block],            lane_head, kv_heads, score_scale,
        )
        highest, _, total, delta = merged(stat_ref, block, scores, dprobs)
        out_ref[block, 0:1] = highest
        out_ref[block, 1:2] = total
        out_ref[block, 2:3] = delta


def far_kernel(
    plan_ref, q_ref, g_ref, stat_ref, other_ref, grad_ref, out_ref,
    *, heads, kv_heads, score_scale, seen_at, first
):
    rows = q_ref.shape[0] // stat_ref.shape[0]
    _, lane_head = lanes(rows, heads, kv_heads)
    for at in range(other_ref.shape[0]):
        block = first + at
        span = slice(block * rows, (block + 1) * rows)
        q = q_ref[span]
        g = g_ref[span]
        scores, dprobs = far_scores(
            other_ref, at, q, g, plan_ref[seen_at + block], lane_head, kv_heads, score_scale
        )
        highest, raised, total, delta = merged(stat_ref, block, scores, dprobs)
        inverse = 1.0 / total
        delta = delta * inverse
        grad_ref[at, 0], grad_ref[at, 1] = far_gradients(
            raised * inverse, dprobs, delta, q, g, lane_head, kv_heads, score_scale
        )
        out_ref[at, 0:1] = highest
        out_ref[at, 1:2] = inverse
        out_ref[at, 2:3] = delta


def mine_kernel(
    plan_ref, q_ref, g_ref, arrived_ref, stat_ref, grad_ref,
    *, heads, kv_heads, score_scale, source_at, seen_at, rows, first
):
    _, lane_head = lanes(rows, heads, kv_heads)
    for at in range(stat_ref.shape[0]):
        block = first + at
        span = slice(block * rows, (block + 1) * rows)
        q = q_ref[span]
        g = g_ref[span]
        scores, dprobs = far_scores(
            arrived_ref, plan_ref[source_at + block], q, g, plan_ref[seen_at + block],
            lane_head, kv_heads, score_scale,
        )
        probs = jnp.exp(scores - stat_ref[at, 0:1]) * stat_ref[at, 1:2]
        grad_ref[at, 0], grad_ref[at, 1] = far_gradients(
            probs, dprobs, stat_ref[at, 2:3], q, g, lane_head, kv_heads, score_scale
        )


def local_kernel(
    plan_ref, q_ref, g_ref, k_ref, v_ref, mine_ref, other_ref,
    att_ref, dq_ref, dk_ref, dv_ref, bias_ref, *, heads, kv_heads, score_scale, seen_at
):
    step = pl.program_id(0)
    rows = q_ref.shape[0]
    cols = k_ref.shape[0]

    @pl.when(step == 0)
    def _():
        half = cols // 2
        place = half // kv_heads
        row = lax.broadcasted_iota(jnp.int32, (rows, cols), 0)
        col = lax.broadcasted_iota(jnp.int32, (rows, cols), 1)
        same = row % heads // (heads // kv_heads) == col % half // place
        causal = col // half * place + col % place <= row // heads
        bias_ref[:, :cols] = jnp.where(same & causal, 0.0, HIDDEN)
        bias_ref[:, cols:] = jnp.where(same, 0.0, HIDDEN)

    far_bias = jnp.where(plan_ref[seen_at + step] > 0, 0.0, HIDDEN)
    order = head_major(cols, kv_heads)
    k_near = reorder(order, k_ref[...])
    v_near = reorder(order, v_ref[...])
    k_all = jnp.concatenate([k_near, mine_ref[0, 0], other_ref[0, 0]], axis=0)
    v_all = jnp.concatenate([v_near, mine_ref[0, 1], other_ref[0, 1]], axis=0)
    q = q_ref[...]
    g = g_ref[...]
    scores = dot_last(q, k_all) * score_scale + bias_ref[...]
    scores = jnp.concatenate([scores[:, :cols], scores[:, cols:] + far_bias], axis=1)
    highest = jnp.max(scores, axis=1, keepdims=True)
    raised = jnp.exp(scores - highest)
    total = jnp.sum(raised, axis=1, keepdims=True)
    probs = raised * (1.0 / total)
    weights = probs.astype(BF16)
    attended = jnp.dot(weights, v_all, preferred_element_type=F32).astype(BF16)
    att_ref[...] = attended
    delta = jnp.sum(g.astype(F32) * attended.astype(F32), axis=1, keepdims=True)
    dscores = (probs * (dot_last(g, v_all) - delta)).astype(BF16)
    dq = jnp.dot(dscores, k_all, preferred_element_type=F32) * score_scale
    dq_ref[...] = dq.astype(BF16)
    dk_ref[...] = dot_first(dscores[:, :cols], q) * score_scale
    dv_ref[...] = dot_first(weights[:, :cols], g)


def landing_kernel(plan_ref, landed_ref, out_ref, sum_ref, *, first):
    sum_ref[...] = jnp.zeros_like(sum_ref)
    for group in range(landed_ref.shape[0]):
        place = plan_ref[first + group]

        @pl.when(place >= 0)
        def _():
            sum_ref[place] = sum_ref[place] + landed_ref[group].astype(F32)

    out_ref[...] = sum_ref[...].astype(out_ref.dtype)


def own_half_kernel(
    plan_ref, landed_ref, dk_near_ref, dv_near_ref, out_ref, sum_ref, *, kv_heads
):
    sum_ref[...] = jnp.zeros_like(sum_ref)
    for group in range(landed_ref.shape[0]):
        place = plan_ref[group]

        @pl.when(place >= 0)
        def _():
            sum_ref[place] = sum_ref[place] + landed_ref[group].astype(F32)

    blocks, _, half, _ = out_ref.shape
    order = token_major(half, kv_heads)
    mine = lax.axis_index("uly")
    for block in range(blocks):
        span = pl.ds(pl.multiple_of((2 * block + mine) * half, half), half)
        for which, near_ref in enumerate((dk_near_ref, dv_near_ref)):
            summed = (near_ref[span] + sum_ref[block, which]).astype(BF16)
            out_ref[block, which] = reorder(order, summed)


def finish_kernel(
    dk_near_ref, dv_near_ref, own_ref, back_ref, dk_ref, dv_ref, *, kv_heads
):
    blocks, _, half, _ = back_ref.shape
    order = token_major(half, kv_heads)
    mine = lax.axis_index("uly")
    for which, (near_ref, out_ref) in enumerate(((dk_near_ref, dk_ref), (dv_near_ref, dv_ref))):
        for block in range(blocks):
            here = pl.ds(pl.multiple_of((2 * block + mine) * half, half), half)
            there = pl.ds(pl.multiple_of((2 * block + 1 - mine) * half, half), half)
            summed = (near_ref[there] + back_ref[block, which].astype(F32)).astype(BF16)
            out_ref[here] = own_ref[block, which]
            out_ref[there] = reorder(order, summed)


def take_rows(array, index):
    return array.at[index].get(mode="promise_in_bounds")


def whole_blocks(queries, keys, values, output_cotangent, block_lists, list_counts):
    grp_count = lax.axis_size("grp")
    uly_count = lax.axis_size("uly")
    tokens, heads, width = queries.shape
    kv_heads = keys.shape[1]
    per_group = block_lists.shape[0] // grp_count
    block_tok = tokens * uly_count // per_group
    mine_blocks = tokens // block_tok
    rows = block_tok * heads
    cols = block_tok * kv_heads
    half = cols // 2
    sizes = dict(heads=heads, kv_heads=kv_heads, score_scale=width ** (-0.5))
    swap = [(0, 1), (1, 0)]

    sib_at, source_at, give_at, seen_at = plan_spans(grp_count, mine_blocks)

    q2 = queries.reshape(tokens * heads, width)
    g2 = output_cotangent.reshape(tokens * heads, width)
    k2 = keys.reshape(tokens * kv_heads, width)
    v2 = values.reshape(tokens * kv_heads, width)

    part_shape = jax.ShapeDtypeStruct((mine_blocks, 2, half, width), BF16)
    slots = (grp_count, 2, half, width)
    stat_shape = jax.ShapeDtypeStruct((mine_blocks, 8, rows), F32)
    row_shape = jax.ShapeDtypeStruct(q2.shape, BF16)
    near_shape = jax.ShapeDtypeStruct(k2.shape, F32)
    small_shape = jax.ShapeDtypeStruct(k2.shape, BF16)
    sum_scratch = [pltpu.VMEM((mine_blocks, 2, half, width), F32)]
    limit = pltpu.CompilerParams(vmem_limit_bytes=24 * 1024 * 1024)
    vmem = pl.BlockSpec(memory_space=pltpu.VMEM)
    smem = pl.BlockSpec(memory_space=pltpu.SMEM)
    anywhere = pl.BlockSpec(memory_space=pltpu.HBM)

    def call(kernel, name, scalars, operands, out_shape, scratch=(), into=None, out_spec=vmem):
        extra = () if into is None else (into,)
        return pl.pallas_call(
            kernel,
            in_specs=[smem] * len(scalars) + [vmem] * (len(operands) + len(extra)),
            out_specs=jax.tree.map(lambda _: out_spec, out_shape),
            out_shape=out_shape,
            scratch_shapes=scratch,
            input_output_aliases={len(scalars) + len(operands): 0} if extra else {},
            compiler_params=limit,
            name=name,
        )(*scalars, *operands, *extra)

    def step_rows(i, *_):
        return (i, 0)

    def step_part(i, *_):
        return (i, 0, 0, 0)

    def in_hbm(array):
        return pltpu.with_memory_space_constraint(array, pltpu.HBM)

    kept, given = pl.pallas_call(
        partial(pack_kernel, kv_heads=kv_heads),
        in_specs=[anywhere, anywhere],
        out_specs=[vmem, vmem],
        out_shape=[part_shape, part_shape],
        scratch_shapes=[
            pltpu.VMEM(k2.shape, BF16), pltpu.VMEM(k2.shape, BF16),
            pltpu.SemaphoreType.DMA((2,)),
        ],
        compiler_params=limit,
        name="pack",
    )(in_hbm(k2), in_hbm(v2))
    plan = pl.pallas_call(
        partial(plan_kernel, grp_count=grp_count, blocks=mine_blocks),
        in_specs=[smem, smem],
        out_specs=smem,
        out_shape=pltpu.SMEM((seen_at + mine_blocks,), jnp.int32),
        compiler_params=limit,
        name="plan",
    )(in_hbm(block_lists.reshape(-1)), in_hbm(list_counts))
    gotten = lax.ppermute(given, "uly", swap)
    row_spec = pl.BlockSpec((rows, width), step_rows)
    part_spec = pl.BlockSpec((1, 2, half, width), step_part)
    stats = pl.pallas_call(
        partial(near_kernel, **sizes),
        grid=(mine_blocks,),
        in_specs=[row_spec, row_spec, part_spec, part_spec],
        out_specs=pl.BlockSpec((1, 8, rows), lambda i: (i, 0, 0)),
        out_shape=stat_shape,
        compiler_params=limit,
        name="near",
    )(in_hbm(q2), in_hbm(g2), kept, given)
    outgoing = call(
        send_own_kernel, "send_own", (plan,), (kept,),
        jax.ShapeDtypeStruct(slots, BF16),
    )
    gotten, stats = lax.optimization_barrier((gotten, stats))
    outgoing = call(
        partial(send_sibling_kernel, first=sib_at), "send_sibling", (plan,), (gotten,),
        jax.ShapeDtypeStruct(slots, BF16), into=outgoing,
    )
    arrived = lax.all_to_all(outgoing, "grp", split_axis=0, concat_axis=0, tiled=True)
    chunks = 2 if mine_blocks % 2 == 0 else 1
    chunk = mine_blocks // chunks
    chunk_shape = jax.ShapeDtypeStruct((chunk, 2, half, width), BF16)
    giving = call(
        partial(giving_kernel, give_at=give_at), "give", (plan,), (arrived,),
        [chunk_shape] * chunks,
    )
    stats = call(
        partial(mid_kernel, source_at=source_at, seen_at=seen_at, **sizes), "mid", (plan,),
        (q2, g2, stats, arrived), stat_shape,
    )
    others = []
    for part in giving:
        others.append(lax.ppermute(part, "uly", swap))
    grads, final = [], []
    for at, other in enumerate(others):
        grad, stat = call(
            partial(far_kernel, seen_at=seen_at, first=at * chunk, **sizes), "far", (plan,),
            (q2, g2, stats, other),
            [chunk_shape, jax.ShapeDtypeStruct((chunk, 8, rows), F32)],
        )
        grads.append(grad)
        final.append(stat)
    from_sib = [lax.ppermute(part, "uly", swap) for part in grads]
    mine = [None] * chunks
    for at in reversed(range(chunks)):
        if at + 1 < chunks:
            from_sib[at], final[at] = lax.optimization_barrier((from_sib[at], final[at]))
        mine[at] = call(
            partial(
                mine_kernel, source_at=source_at, seen_at=seen_at, rows=rows, first=at * chunk,
                **sizes,
            ),
            "mine", (plan,), (q2, g2, arrived, final[at]), chunk_shape,
        )
    returning = call(
        partial(returning_kernel, source_at=source_at), "return", (plan,), mine + from_sib,
        pltpu.HBM(slots, BF16), [pltpu.SemaphoreType.DMA((per_group,))], out_spec=anywhere,
    )
    other = jnp.concatenate(others)
    returning, k2l = lax.optimization_barrier((returning, k2))
    landed = lax.all_to_all(returning, "grp", split_axis=0, concat_axis=0, tiled=True)

    def from_source(i, plan_ref):
        return (plan_ref[source_at + i], 0, 0, 0)

    col_spec = pl.BlockSpec((cols, width), step_rows)
    attended, dq, dk_near, dv_near = pl.pallas_call(
        partial(local_kernel, seen_at=seen_at, **sizes),
        grid_spec=pltpu.PrefetchScalarGridSpec(
            num_scalar_prefetch=1,
            grid=(mine_blocks,),
            in_specs=[
                row_spec, row_spec, col_spec, col_spec,
                pl.BlockSpec((1, 2, half, width), from_source),
                part_spec,
            ],
            out_specs=[row_spec, row_spec, col_spec, col_spec],
            scratch_shapes=[pltpu.VMEM((rows, 2 * cols), F32)],
        ),
        out_shape=[row_shape, row_shape, near_shape, near_shape],
        compiler_params=limit,
        name="local",
    )(plan, q2, g2, k2l, v2, arrived, other)
    landed, dk_near = lax.optimization_barrier((landed, dk_near))
    give = call(
        partial(landing_kernel, first=sib_at), "land_sibling", (plan,), (landed,), part_shape,
        sum_scratch,
    )
    back = lax.ppermute(give, "uly", swap)
    own = call(
        partial(own_half_kernel, kv_heads=kv_heads), "land_own", (plan,),
        (landed, dk_near, dv_near), part_shape, sum_scratch,
    )
    dk, dv = call(
        partial(finish_kernel, kv_heads=kv_heads), "finish", (),
        (dk_near, dv_near, own, back), [small_shape, small_shape],
    )
    return (
        attended.reshape(queries.shape), dq.reshape(queries.shape),
        dk.reshape(keys.shape), dv.reshape(keys.shape),
    )


def on_device(queries, keys, values, output_cotangent, block_lists, list_counts):
    uly_count = lax.axis_size("uly")
    grp_count = lax.axis_size("grp")
    blocks_all, remote = block_lists.shape
    block_tok = queries.shape[0] * uly_count * grp_count // blocks_all
    held_whole = queries.shape[0] % block_tok == 0
    run = whole_blocks if held_whole and remote == 1 and uly_count == 2 else spread_blocks
    return run(queries, keys, values, output_cotangent, block_lists, list_counts)


def solution(mesh):
    placed = (
        P(("grp", "uly"), None, None),
        P(("grp", "uly"), None, None),
        P(("grp", "uly"), None, None),
        P(("grp", "uly"), None, None),
        P(),
        P(),
    )
    return jax.shard_map(
        on_device,
        mesh=mesh,
        in_specs=placed,
        out_specs=(
            P(("grp", "uly"), None, None),
            P(("grp", "uly"), None, None),
            P(("grp", "uly"), None, None),
            P(("grp", "uly"), None, None),
        ),
        check_vma=False,
    )
```
